32 devices in a mesh: batch: 4 (over y, x), seq: 8 (over z, core).
Axes of the slice: x: 2, y: 2, z: 4, core: 2. Of those that a mesh axis runs over, the one named last changes fastest.
Arguments:
- tokens_in: bfloat16 [4, 4096, 1024], P('batch', 'seq'), may hold values from -6 to 6
- skip_in: bfloat16 [4, 4096, 1024], P('batch', 'seq'), may hold values from -6 to 6
- condition: bfloat16 [4, 4096, 1024], P('batch', 'seq'), may hold values from -3 to 3
- cotangent: bfloat16 [4, 4096, 1024], P('batch', 'seq'), may hold values from -6 to 6
- time_embed: float32 [4, 8, 1024], P('batch'), may hold values from -6 to 6
- lengths: int32 [4, 8], P('batch'), may hold values from 1 to 2048, 4096 in all within a row
- key_mask: int32 [4, 4096], P('batch'), may hold values 0 or 1
- drop_mask: int32 [4, 8], P('batch'), may hold values 0 or 1
- loss_mask: int32 [4, 4096], P('batch', 'seq'), may hold values from 0 to 1, as said below
- w_skip: bfloat16 [2048, 1024], replicated, may hold values from -0.125 to 0.125
- b_skip: bfloat16 [1024], replicated, may hold values from -2 to 2
- w_ada: bfloat16 [1024, 6144], replicated, may hold values from -0.1875 to 0.1875
- b_ada: bfloat16 [6144], replicated, may hold values from -3 to 3
- w_qkv: bfloat16 [1024, 3072], replicated, may hold values from -0.1875 to 0.1875
- b_qkv: bfloat16 [3072], replicated, may hold values from -2 to 2
- w_out: bfloat16 [1024, 1024], replicated, may hold values from -1.5 to 1.5
- b_out: bfloat16 [1024], replicated, may hold values from -2 to 2
- w_up: bfloat16 [1024, 4096], replicated, may hold values from -0.1875 to 0.1875
- b_up: bfloat16 [4096], replicated, may hold values from -2 to 2
- w_down: bfloat16 [4096, 1024], replicated, may hold values from -0.09375 to 0.09375
- b_down: bfloat16 [1024], replicated, may hold values from -2 to 2
Outputs:
- output: bfloat16 [4, 4096, 1024], P('batch', 'seq')
- grad_tokens: float32 [4, 4096, 1024], P('batch', 'seq')
- grad_skip: float32 [4, 4096, 1024], P('batch', 'seq')
- grad_w_skip: float32 [2048, 1024], P('seq')
- grad_b_skip: float32 [1024], P('seq')
- grad_w_ada: float32 [1024, 6144], P('seq')
- grad_b_ada: float32 [6144], P('seq')
- grad_w_qkv: float32 [1024, 3072], P('seq')
- grad_b_qkv: float32 [3072], P('seq')
- grad_w_out: float32 [1024, 1024], P('seq')
- grad_b_out: float32 [1024], P('seq')
- grad_w_up: float32 [1024, 4096], P('seq')
- grad_b_up: float32 [4096], P('seq')
- grad_w_down: float32 [4096, 1024], P('seq')
- grad_b_down: float32 [1024], P('seq')
The draws below stay inside these ranges and needn't reach their ends.
Inputs may be any that keep to these rules, and one draw needn't show every extreme that they name: Each group's 8 lengths sum to 4096; in every group the longest is exactly 2048. `loss_mask`: the last frame of every group is a loss frame.
All inputs are finite; a program needn't handle non-finite values. No bound on the sum of `key_mask` or of `drop_mask` on one device may be relied on, other than what follows from the above.
Results may differ from the reference program's by a relative error of at most 0.02.
Values may be sent and summed in bfloat16 or wider, within the bound.
No kernel may reach another device: no remote copies, remote signals or barrier semaphores. Data moves between devices by JAX's collectives and lax.ppermute only.
A program may use at most 320 MiB of HBM per device.

```python
import math
import jax
import jax.numpy as jnp
import numpy as np
from jax import lax

D = 1024
HEADS = 16
HEAD_DIM = 64
FF = 4096
GROUP_FRAMES = 4096
NGROUP = 4
MOST_LEN = 2048
UTTS = 8


def draw_loss_mask(key, part):
    frame_ids = jnp.arange(GROUP_FRAMES, dtype=jnp.int32)[None, :]
    group_ids = jnp.arange(NGROUP, dtype=jnp.int32)[:, None]
    flat_ids = group_ids * GROUP_FRAMES + frame_ids
    threshold = 200 + 500 * flat_ids // (NGROUP * GROUP_FRAMES)
    draw_rolls = jax.random.randint(key, (NGROUP, GROUP_FRAMES), 0, 1000, dtype=jnp.int32)
    chosen = (draw_rolls < threshold).astype(jnp.int32)
    return jnp.where(frame_ids == GROUP_FRAMES - 1, 1, chosen).astype(jnp.int32)


def plant(result, key, smallest, top_value):
    longest = result.shape.index(max(result.shape))
    spots = []
    for shift in (0, 1):
        where = [jax.random.randint(jax.random.fold_in(key, axis), (), 0, length) for axis, length in enumerate(result.shape)]
        where[longest] = (where[longest] + shift) % result.shape[longest]
        spots.append(tuple(where))
    return result.at[spots[0]].set(smallest).at[spots[1]].set(top_value)


def shard_levels(key, extent, cuts, smallest, largest):
    def one(axis_at, parts):
        steps = jax.random.uniform(jax.random.fold_in(jax.random.fold_in(key, 6), axis_at), (parts,), jnp.float32, smallest / len(cuts), largest / len(cuts))
        return jnp.repeat(jnp.exp(steps), extent[axis_at] // parts).reshape((-1,) + (1,) * (len(extent) - axis_at - 1))

    gain = one(*cuts[0])
    for cut in cuts[1:]:
        gain = gain * one(*cut)
    return gain


def profile(number_of, total, most, slope):
    loads = [(1 << 20) // math.isqrt(standing ** slope) + 1 for standing in range(2, number_of + 1)]
    rest, given = total - most - (number_of - 1), [1] * (number_of - 1)
    while rest > 0:
        free = [i for i in range(number_of - 1) if given[i] < most]
        pool, left = sum([loads[i] for i in free]), rest
        for i in free:
            addition = min(most - given[i], max(1, left * loads[i] // pool), rest)
            given[i] = given[i] + addition
            rest = rest - addition
    return np.array([most] + given)


def uneven_parts(key, number_of, total, reach, lean):
    if number_of == 2:
        one = jax.random.randint(key, (), max(1, total - reach), min(reach, total - 1) + 1)
        return jnp.stack([one, total - one])
    sizes = jnp.asarray(profile(number_of, total, reach, lean), jnp.int32)
    couples = (number_of - 1) // 2
    source_of, receiver = sizes[1:1 + 2 * couples:2], sizes[2:2 + 2 * couples:2]
    margin = jnp.minimum(source_of - 1, reach - receiver)
    shifted = jax.random.randint(jax.random.fold_in(key, 1), (couples,), 0, 1 << 20) % (margin + 1)
    sizes = sizes.at[1:1 + 2 * couples:2].set(source_of - shifted).at[2:2 + 2 * couples:2].set(receiver + shifted)
    return sizes[jax.random.permutation(jax.random.fold_in(key, 2), number_of)]


def normal_values(key, shape, scale, bound, cuts=(), held_as=jnp.bfloat16):
    entries = jax.random.normal(key, shape, jnp.float32) * scale
    if len(cuts) > 0:
        entries = shard_levels(key, shape, cuts, -0.22, 0.18) * entries
    return jnp.clip(entries, min=-bound, max=bound).astype(held_as)


def setup_inputs(seed: int = 0) -> dict:
    key_of = jax.random.split(jax.random.key(seed), 22)
    return {
        "tokens_in": normal_values(key_of[0], (NGROUP, GROUP_FRAMES, D), 1.0, 6.0, ((0, 4), (1, 8))),
        "skip_in": normal_values(key_of[1], (NGROUP, GROUP_FRAMES, D), 1.0, 6.0, ((0, 4), (1, 8))),
        "condition": normal_values(key_of[2], (NGROUP, GROUP_FRAMES, D), 0.5, 3.0, ((0, 4), (1, 8))),
        "cotangent": normal_values(key_of[3], (NGROUP, GROUP_FRAMES, D), 1.0, 6.0, ((0, 4), (1, 8))),
        "time_embed": normal_values(key_of[4], (NGROUP, UTTS, D), 1.0, 6.0, ((0, 4),), jnp.float32),
        "lengths": jax.vmap(lambda own: uneven_parts(own, UTTS, GROUP_FRAMES, MOST_LEN, 2))(jax.random.split(key_of[5], NGROUP)).reshape((NGROUP, UTTS)).astype(jnp.int32),
        "key_mask": plant((jax.random.randint(key_of[6], (NGROUP, GROUP_FRAMES), 0, 8) < 7).astype(jnp.int32), jax.random.fold_in(key_of[6], 1), 0, 1),
        "drop_mask": plant((jax.random.randint(key_of[7], (NGROUP, UTTS), 0, 4) < 1).astype(jnp.int32), jax.random.fold_in(key_of[7], 1), 0, 1),
        "loss_mask": draw_loss_mask(jax.random.fold_in(key_of[21], 71), 0),
        "w_skip": normal_values(key_of[9], (2 * D, D), (2 * D) ** -0.5, 0.125),
        "b_skip": normal_values(key_of[10], (D,), 0.3, 2.0),
        "w_ada": normal_values(key_of[11], (D, 6 * D), D ** -0.5, 0.1875),
        "b_ada": normal_values(key_of[12], (6 * D,), 0.5, 3.0),
        "w_qkv": normal_values(key_of[13], (D, 3 * D), D ** -0.5, 0.1875),
        "b_qkv": normal_values(key_of[14], (3 * D,), 0.3, 2.0),
        "w_out": normal_values(key_of[15], (D, D), (D // 64) ** -0.5, 1.5),
        "b_out": normal_values(key_of[16], (D,), 0.3, 2.0),
        "w_up": normal_values(key_of[17], (D, FF), D ** -0.5, 0.1875),
        "b_up": normal_values(key_of[18], (FF,), 0.3, 2.0),
        "w_down": normal_values(key_of[19], (FF, D), FF ** -0.5, 0.09375),
        "b_down": normal_values(key_of[20], (D,), 0.3, 2.0),
    }


@jax.custom_vjp
def low(v):
    return lax.optimization_barrier(v.astype(jnp.bfloat16)).astype(jnp.float32)

@jax.custom_vjp
def low_back(v):
    return v

def low_keep(v):
    return (low(v), None)

def low_pass(kept, grad):
    return (grad,)

def back_keep(v):
    return (v, None)

def back_low(kept, grad):
    return (low(grad),)
low.defvjp(low_keep, low_pass)
low_back.defvjp(back_keep, back_low)
epsilon = 1e-06
masked_score = -1e+30

def matmul(left_op, right_op):
    return jnp.dot(left_op, right_op, precision=lax.Precision.HIGHEST)

def both_round(tensor):
    return low_back(low(tensor))

def norm_rows(tensor):
    centred = tensor - lax.optimization_barrier(jnp.mean(tensor, axis=-1, keepdims=True))
    spread = lax.optimization_barrier(jnp.mean(centred * centred, axis=-1, keepdims=True))
    return centred * lax.rsqrt(spread + epsilon)

def rotary_tables(position, head_size):
    halfway = head_size // 2
    inverse = 10000.0 ** (-(2.0 * jnp.arange(halfway, dtype=jnp.float32)) / head_size)
    angles = position.astype(jnp.float32)[:, None] * inverse[None, :]
    return (jnp.cos(angles)[:, None, :], jnp.sin(angles)[:, None, :])

def rotate(tensor, cosine_table, sine_table):
    halfway = tensor.shape[-1] // 2
    first_half = tensor[..., :halfway]
    second_half = tensor[..., halfway:]
    return jnp.concatenate([first_half * cosine_table - second_half * sine_table, second_half * cosine_table + first_half * sine_table], axis=-1)

def group_layout(lengths_row, frame_ids):
    ends_at = jnp.cumsum(lengths_row).astype(jnp.int32)
    starts_at = (ends_at - lengths_row).astype(jnp.int32)
    member = (frame_ids[:, None] >= starts_at[None, :]) & (frame_ids[:, None] < ends_at[None, :])
    utter_ids = jnp.arange(lengths_row.shape[0], dtype=jnp.int32)
    segment = lax.optimization_barrier(jnp.sum(jnp.where(member, utter_ids[None, :], 0), axis=1)).astype(jnp.int32)
    position = (frame_ids - lax.optimization_barrier(jnp.sum(jnp.where(member, starts_at[None, :], 0), axis=1))).astype(jnp.int32)
    return (member, segment, position)

def block_mask(segment_all, key_ok, row_start, block_rows):
    key_ids = jnp.arange(segment_all.shape[0], dtype=jnp.int32)
    row_ids = row_start + jnp.arange(block_rows, dtype=jnp.int32)
    row_segment = lax.dynamic_slice_in_dim(segment_all, row_start, block_rows)
    return (row_segment[:, None] == segment_all[None, :]) & ((key_ok[None, :] > 0) | (row_ids[:, None] == key_ids[None, :]))

def attention(queries, keys_all, values_all, segment, key_ok):
    frames_all = queries.shape[0]
    block_rows = min(512, frames_all)
    blocks = frames_all // block_rows
    query_blocks = queries.reshape(blocks, block_rows, queries.shape[1], queries.shape[2])
    block_starts = (jnp.arange(blocks, dtype=jnp.int32) * block_rows).astype(jnp.int32)

    def one_block(block_args):
        query_block, row_start = block_args
        allowed = block_mask(segment, key_ok, row_start, block_rows)
        scores = low_back(jnp.einsum('qhd,khd->hqk', query_block, keys_all, precision=lax.Precision.HIGHEST) * 0.125)
        scores = jnp.where(allowed[None], scores, masked_score)
        row_peak = lax.optimization_barrier(jnp.max(scores, axis=-1, keepdims=True))
        log_total = row_peak + jnp.log(lax.optimization_barrier(jnp.sum(jnp.exp(scores - row_peak), axis=-1, keepdims=True)))
        attn_probs = low(jnp.exp(scores - log_total))
        mixed_block = jnp.einsum('hqk,khd->qhd', attn_probs, values_all, precision=lax.Precision.HIGHEST)
        return both_round(mixed_block).reshape(block_rows, -1)
    outputs = lax.map(jax.checkpoint(one_block), (query_blocks, block_starts))
    return outputs.reshape(frames_all, -1)

def group_forward(weight_set, tokens_f, skip_f, cond_f, keep_frame, time_g, segment, cosine_table, sine_table, key_ok):
    w_skip, b_skip, w_ada, b_ada, w_qkv, b_qkv, w_out, b_out, w_up, b_up, w_down, b_down = weight_set
    frames_all = tokens_f.shape[0]
    mixed_in = tokens_f + keep_frame[:, None] * cond_f
    joined = low(jnp.concatenate([mixed_in, skip_f], axis=1))
    hidden = low_back(matmul(joined, w_skip) + b_skip)
    time_act = low(jax.nn.silu(time_g))
    modulation = matmul(time_act, w_ada) + b_ada
    frame_mods = modulation[segment]
    shift_a, scale_a, gate_a, shift_f, scale_f, gate_f = jnp.split(frame_mods, 6, axis=1)
    normed_a = low(norm_rows(hidden) * (1.0 + scale_a) + shift_a)
    projected = low_back(matmul(normed_a, w_qkv) + b_qkv)
    query_raw, key_raw, value_raw = jnp.split(projected, 3, axis=1)
    query_rot = both_round(rotate(query_raw.reshape(frames_all, HEADS, HEAD_DIM), cosine_table, sine_table))
    key_rot = both_round(rotate(key_raw.reshape(frames_all, HEADS, HEAD_DIM), cosine_table, sine_table))
    value_rot = both_round(value_raw.reshape(frames_all, HEADS, HEAD_DIM))
    attended = attention(query_rot, key_rot, value_rot, segment, key_ok)
    attn_proj = low_back(matmul(attended, w_out) + b_out)
    after_attn = hidden + gate_a * attn_proj
    normed_f = low(norm_rows(after_attn) * (1.0 + scale_f) + shift_f)
    up_proj = low_back(matmul(normed_f, w_up) + b_up)
    activated = low(jax.nn.gelu(up_proj, approximate=True))
    ff_out = low_back(matmul(activated, w_down) + b_down)
    return after_attn + gate_f * ff_out

def reference(tokens_in, skip_in, condition, cotangent, time_embed, lengths, key_mask, drop_mask, loss_mask, w_skip, b_skip, w_ada, b_ada, w_qkv, b_qkv, w_out, b_out, w_up, b_up, w_down, b_down):
    weight_set = tuple((weight_arg.astype(jnp.float32) for weight_arg in (w_skip, b_skip, w_ada, b_ada, w_qkv, b_qkv, w_out, b_out, w_up, b_up, w_down, b_down)))
    frame_count = jnp.sum(loss_mask.astype(jnp.float32))
    grad_scale = NGROUP * GROUP_FRAMES / frame_count
    frame_ids = jnp.arange(GROUP_FRAMES, dtype=jnp.int32)

    def per_group(running, group_args):
        tokens_g, skip_g, cond_g, cot_g, time_g, lengths_g, keys_g, drop_g, loss_g = group_args
        member, segment, position = group_layout(lengths_g, frame_ids)
        keep_frame = (1 - drop_g).astype(jnp.float32)[segment]
        cosine_table, sine_table = rotary_tables(position, HEAD_DIM)
        cond_f = cond_g.astype(jnp.float32)

        def forward(weights_in, tokens_f, skip_f):
            return group_forward(weights_in, tokens_f, skip_f, cond_f, keep_frame, time_g, segment, cosine_table, sine_table, keys_g)
        output, pullback = jax.vjp(forward, weight_set, tokens_g.astype(jnp.float32), skip_g.astype(jnp.float32))
        grad_output = cot_g.astype(jnp.float32) * loss_g.astype(jnp.float32)[:, None] * grad_scale
        grad_weights, grad_tokens, grad_skip = pullback(grad_output)
        running = jax.tree.map(lambda summed, addend: summed + addend, running, grad_weights)
        return (running, (output.astype(jnp.bfloat16), grad_tokens, grad_skip))
    start_sums = jax.tree.map(jnp.zeros_like, weight_set)
    totals, (outputs, grad_tokens, grad_skips) = lax.scan(per_group, start_sums, (tokens_in, skip_in, condition, cotangent, time_embed, lengths, key_mask, drop_mask, loss_mask))
    return (outputs, grad_tokens, grad_skips, totals[0], totals[1], totals[2], totals[3], totals[4], totals[5], totals[6], totals[7], totals[8], totals[9], totals[10], totals[11])
```

```python
import functools

import jax
import jax.numpy as jnp
from jax import lax
from jax.experimental import pallas as pl
from jax.experimental.pallas import tpu as pltpu
from jax.sharding import PartitionSpec as P

HEADS = 16


epsilon = 1e-06


def norm_rows(tensor):
    centred = tensor - jnp.mean(tensor, axis=-1, keepdims=True)
    spread = jnp.mean(centred * centred, axis=-1, keepdims=True)
    return centred * lax.rsqrt(spread + epsilon)


def modulate(hidden, shift_in, scale_in):
    return norm_rows(hidden) * (1.0 + scale_in) + shift_in


def gelu_tanh(tensor):
    return jax.nn.gelu(tensor, approximate=True)


def group_layout(lengths_row, frame_ids):
    ends_at = jnp.cumsum(lengths_row)
    starts_at = ends_at - lengths_row
    member = (frame_ids[:, None] >= starts_at[None, :]) & (frame_ids[:, None] < ends_at[None, :])
    utter_ids = jnp.arange(lengths_row.shape[0], dtype=jnp.int32)
    segment = jnp.sum(jnp.where(member, utter_ids[None, :], 0), axis=1)
    position = frame_ids - jnp.sum(jnp.where(member, starts_at[None, :], 0), axis=1)
    return (member, segment, position)


def transpose_dot(left_op, right_op):
    return lax.dot_general(
        left_op, right_op, (((0,), (0,)), ((), ())), preferred_element_type=jnp.float32
    )


def back_dot(left_op, right_op):
    return lax.dot_general(
        left_op, right_op, (((1,), (1,)), ((), ())), preferred_element_type=jnp.float32
    )


def precise_dot(left_op, right_op):
    return jnp.dot(left_op, right_op, precision=lax.Precision.HIGHEST)

BIG = 1e30
DH = 64
BQ = 512
BK = 512


def onehot_rows(lengths_ref, utts, rows, base, width):
    row = lax.broadcasted_iota(jnp.int32, (rows, width), 0)
    col = base + lax.broadcasted_iota(jnp.int32, (rows, width), 1)
    start = jnp.int32(0)
    hot = jnp.zeros((rows, width), jnp.float32)
    for u in range(utts):
        end = start + lengths_ref[u]
        hot = jnp.where((row == u) & (col >= start) & (col < end), 1.0, hot)
        start = end
    return hot


def key_range(lengths_ref, utts, first, last):
    start = jnp.int32(0)
    low, high = jnp.int32(0), jnp.int32(0)
    for u in range(utts):
        end = start + lengths_ref[u]
        low = jnp.where((start <= first) & (first < end), start, low)
        high = jnp.where((start <= last) & (last < end), end, high)
        start = end
    return low // BK, (high + BK - 1) // BK


def aug_rows(utts):
    return -(-utts // 16) * 16


def split3(row):
    a = row.astype(jnp.bfloat16)
    rest = row - a.astype(jnp.float32)
    b = rest.astype(jnp.bfloat16)
    c = (rest - b.astype(jnp.float32)).astype(jnp.bfloat16)
    return a, b, c


def pad_rows(parts, total):
    have = sum(p.shape[0] for p in parts)
    if have < total:
        parts = parts + [jnp.zeros((total - have, parts[0].shape[1]), parts[0].dtype)]
    return jnp.concatenate(parts, axis=0)


def rows16(rows, width):
    idx = lax.broadcasted_iota(jnp.int32, (16, width), 0)
    out = jnp.zeros((16, width), jnp.float32)
    for i, r in enumerate(rows):
        out = jnp.where(idx == i, r, out)
    return out.astype(jnp.bfloat16)


def fwd_kernel(utts, lengths_ref, qkv_ref, ok_ref, out_ref, lse_ref, kaug, vaug):
    sources, _, frames = qkv_ref.shape
    per = frames // BQ
    pad_u = aug_rows(utts)
    step = pl.program_id(0)

    @pl.when(step == 0)
    def _():
        def build(s, c):
            hot = onehot_rows(lengths_ref, utts, pad_u, s * frames, frames)
            ok = ok_ref[s].astype(jnp.float32)
            block = qkv_ref[s]
            one = jnp.ones((1, frames), jnp.float32)
            kT = pad_rows(
                [block[DH : 2 * DH], (1.0 - hot).astype(jnp.bfloat16), rows16([1.0 - ok], frames)], 128
            )
            kaug[pl.ds(pl.multiple_of(s * frames, frames), frames), :] = kT.T
            vT = jnp.concatenate([block[2 * DH :], rows16([one], frames)], axis=0)
            for t in range(frames // BK):
                vaug[s * (frames // BK) + t] = vT[:, t * BK : (t + 1) * BK]
            return c

        lax.fori_loop(0, sources, build, 0)

    block = qkv_ref[step]
    hot_q = onehot_rows(lengths_ref, utts, pad_u, step * frames, frames)
    qT = (block[:DH].astype(jnp.float32) * 0.125)
    one = jnp.ones((1, frames), jnp.float32)
    qaug = pad_rows(
        [qT.astype(jnp.bfloat16), (hot_q * -BIG).astype(jnp.bfloat16), rows16([one * -BIG], frames)], 128
    )
    kT = block[DH : 2 * DH].astype(jnp.float32)
    vT = block[2 * DH :].astype(jnp.float32)
    ok = ok_ref[step] > 0
    s_self = jnp.sum(qT * kT, axis=0, keepdims=True)
    m0 = jnp.where(ok, -3e38, s_self)
    acc0 = jnp.concatenate([jnp.where(ok, 0.0, vT), jnp.where(ok, 0.0, jnp.ones((16, frames), jnp.float32))], axis=0)
    for t in range(per):
        cols = slice(t * BQ, (t + 1) * BQ)
        low, high = key_range(lengths_ref, utts, step * frames + t * BQ, step * frames + (t + 1) * BQ - 1)
        q_b = qaug[:, cols]

        def body(j, carry):
            m, acc = carry
            s = jnp.dot(kaug[pl.ds(pl.multiple_of(j * BK, BK), BK), :], q_b, preferred_element_type=jnp.float32)
            m_new = jnp.maximum(m, jnp.max(s, axis=0, keepdims=True))
            p = jnp.exp(s - m_new).astype(jnp.bfloat16)
            alpha = jnp.exp(m - m_new)
            acc = acc * alpha + jnp.dot(vaug[j], p, preferred_element_type=jnp.float32)
            return m_new, acc

        m, acc = lax.fori_loop(low, high, body, (m0[:, cols], acc0[:, cols]))
        total = acc[DH : DH + 1]
        out_ref[0, :, cols] = (acc[:DH] / total).astype(jnp.bfloat16)
        lse_ref[0, :, cols] = m + jnp.log(total)


def attend(lengths, qkv, ok):
    sources, _, frames = qkv.shape
    total = sources * frames
    utts = lengths.shape[0]
    whole = lambda shape: pl.BlockSpec(shape, lambda i, *_: (0,) * len(shape))
    return pl.pallas_call(
        functools.partial(fwd_kernel, utts),
        out_shape=(
            jax.ShapeDtypeStruct((sources, DH, frames), jnp.bfloat16),
            jax.ShapeDtypeStruct((sources, 1, frames), jnp.float32),
        ),
        grid_spec=pltpu.PrefetchScalarGridSpec(
            num_scalar_prefetch=1,
            grid=(sources,),
            in_specs=[whole(qkv.shape), whole(ok.shape)],
            out_specs=(
                pl.BlockSpec((1, DH, frames), lambda i, *_: (i, 0, 0)),
                pl.BlockSpec((1, 1, frames), lambda i, *_: (i, 0, 0)),
            ),
            scratch_shapes=[
                pltpu.VMEM((total, 128), jnp.bfloat16),
                pltpu.VMEM((total // BK, DH + 16, BK), jnp.bfloat16),
            ],
        ),
        name="attend",
    )(lengths, qkv, ok)


def bwd_kernel(utts, lengths_ref, qkv_ref, ok_ref, o_ref, do_ref, lse_ref, out_ref, kaug, vnat, kT_s, dk, dv):
    sources, _, frames = qkv_ref.shape
    per = frames // BK
    pad_u = aug_rows(utts)
    step = pl.program_id(0)
    f32 = jnp.float32

    @pl.when(step == 0)
    def _():
        def build(s, c):
            hot = onehot_rows(lengths_ref, utts, pad_u, s * frames, frames)
            ok = ok_ref[s]
            block = qkv_ref[s]
            one = jnp.ones((1, frames), f32)
            kT = block[DH : 2 * DH]
            vT = block[2 * DH :]
            kA = pad_rows(
                [kT, (1.0 - hot).astype(jnp.bfloat16), rows16([1.0 - ok.astype(f32), one, one, one], frames)], 128
            )
            rows = pl.ds(pl.multiple_of(s * frames, frames), frames)
            kaug[rows, :] = kA.T
            vnat[rows, :] = pad_rows([vT, rows16([one, one, one], frames)], 128).T
            qT = block[:DH].astype(f32) * 0.125
            do = do_ref[s].astype(f32)
            s_self = jnp.sum(qT * kT.astype(f32), axis=0, keepdims=True)
            delta = jnp.sum(do * o_ref[s].astype(f32), axis=0, keepdims=True)
            p_self = jnp.where(ok > 0, 0.0, jnp.exp(s_self - lse_ref[s]))
            ds_self = p_self * (jnp.sum(do * vT.astype(f32), axis=0, keepdims=True) - delta)
            dk0 = ds_self * qT
            dv0 = p_self * do
            for t in range(per):
                cols = slice(t * BK, (t + 1) * BK)
                kT_s[s * per + t] = kT[:, cols]
                dk[s * per + t] = dk0[:, cols]
                dv[s * per + t] = dv0[:, cols]
            return c

        lax.fori_loop(0, sources, build, 0)

    block = qkv_ref[step]
    one = jnp.ones((1, frames), f32)
    hot_q = onehot_rows(lengths_ref, utts, pad_u, step * frames, frames)
    qT = block[:DH].astype(f32) * 0.125
    qTb = qT.astype(jnp.bfloat16)
    kT = block[DH : 2 * DH].astype(f32)
    vT = block[2 * DH :].astype(f32)
    ok = ok_ref[step]
    dob = do_ref[step]
    do = dob.astype(f32)
    lse = lse_ref[step]
    delta = jnp.sum(do * o_ref[step].astype(f32), axis=0, keepdims=True)
    l3 = [-r.astype(f32) for r in split3(lse)]
    d3 = [-r.astype(f32) for r in split3(delta)]
    qaug = pad_rows([qTb, (hot_q * -BIG).astype(jnp.bfloat16), rows16([one * -BIG] + l3, frames)], 128)
    doaug = pad_rows([dob, rows16(d3, frames)], 128)
    s_self = jnp.sum(qT * kT, axis=0, keepdims=True)
    p_self = jnp.where(ok > 0, 0.0, jnp.exp(s_self - lse))
    ds_self = p_self * (jnp.sum(do * vT, axis=0, keepdims=True) - delta)
    dq0 = ds_self * kT
    nt = (((1,), (1,)), ((), ()))
    for t in range(frames // BQ):
        cols = slice(t * BQ, (t + 1) * BQ)
        low, high = key_range(lengths_ref, utts, step * frames + t * BQ, step * frames + (t + 1) * BQ - 1)
        q_a = qaug[:, cols]
        q_b = qTb[:, cols]
        do_a = doaug[:, cols]
        do_b = dob[:, cols]

        def body(j, dq):
            rows = pl.ds(pl.multiple_of(j * BK, BK), BK)
            s = jnp.dot(kaug[rows, :], q_a, preferred_element_type=f32)
            dp = jnp.dot(vnat[rows, :], do_a, preferred_element_type=f32)
            p = jnp.exp(s)
            ds = (p * dp).astype(jnp.bfloat16)
            dv[j] += lax.dot_general(do_b, p.astype(jnp.bfloat16), nt, preferred_element_type=f32)
            dk[j] += lax.dot_general(q_b, ds, nt, preferred_element_type=f32)
            return dq + jnp.dot(kT_s[j], ds, preferred_element_type=f32)

        dq = lax.fori_loop(low, high, body, dq0[:, cols])
        out_ref[step, :DH, cols] = (dq * 0.125).astype(jnp.bfloat16)

    @pl.when(step == sources - 1)
    def _():
        def finish(s, c):
            for t in range(per):
                cols = slice(t * BK, (t + 1) * BK)
                out_ref[s, DH : 2 * DH, cols] = dk[s * per + t].astype(jnp.bfloat16)
                out_ref[s, 2 * DH :, cols] = dv[s * per + t].astype(jnp.bfloat16)
            return c

        lax.fori_loop(0, sources, finish, 0)


def attend_back(lengths, qkv, ok, out, grad, lse):
    sources, _, frames = qkv.shape
    total = sources * frames
    utts = lengths.shape[0]
    whole = lambda shape: pl.BlockSpec(shape, lambda i, *_: (0,) * len(shape))
    return pl.pallas_call(
        functools.partial(bwd_kernel, utts),
        out_shape=jax.ShapeDtypeStruct(qkv.shape, jnp.bfloat16),
        grid_spec=pltpu.PrefetchScalarGridSpec(
            num_scalar_prefetch=1,
            grid=(sources,),
            in_specs=[whole(a.shape) for a in (qkv, ok, out, grad, lse)],
            out_specs=whole(qkv.shape),
            scratch_shapes=[
                pltpu.VMEM((total, 128), jnp.bfloat16),
                pltpu.VMEM((total, 128), jnp.bfloat16),
                pltpu.VMEM((total // BK, DH, BK), jnp.bfloat16),
                pltpu.VMEM((total // BK, DH, BK), jnp.float32),
                pltpu.VMEM((total // BK, DH, BK), jnp.float32),
            ],
        ),
        name="attend_back",
    )(lengths, qkv, ok, out, grad, lse)


def shards(
    tokens_in,
    skip_in,
    condition,
    cotangent,
    time_embed,
    lengths,
    key_mask,
    drop_mask,
    loss_mask,
    w_skip,
    b_skip,
    w_ada,
    b_ada,
    w_qkv,
    b_qkv,
    w_out,
    b_out,
    w_up,
    b_up,
    w_down,
    b_down,
):
    seq_ways = lax.axis_size("seq")
    seq_rank = lax.axis_index("seq")
    frames = tokens_in.shape[1]
    model_width = tokens_in.shape[2]
    group_frames = frames * seq_ways
    local_heads = HEADS // seq_ways
    head_size = model_width // HEADS
    lengths_row = lengths[0]
    key_ok = key_mask[0]
    local_ids = seq_rank * frames + jnp.arange(frames, dtype=jnp.int32)
    member, segment_local, position = group_layout(lengths_row, local_ids)
    onehot = member.astype(jnp.float32)
    keep_frame = precise_dot(onehot, (1 - drop_mask[0]).astype(jnp.float32))
    mixed_in = tokens_in[0].astype(jnp.float32) + keep_frame[:, None] * condition[0].astype(
        jnp.float32
    )
    joined = jnp.concatenate([mixed_in.astype(jnp.bfloat16), skip_in[0]], axis=1)
    hidden = jnp.dot(joined, w_skip, preferred_element_type=jnp.float32) + b_skip.astype(
        jnp.float32
    )
    time_act = jax.nn.silu(time_embed[0]).astype(jnp.bfloat16)
    modulation = jnp.dot(time_act, w_ada, preferred_element_type=jnp.float32) + b_ada.astype(
        jnp.float32
    )
    frame_mods = precise_dot(onehot, modulation)
    shift_a, scale_a, gate_a, shift_f, scale_f, gate_f = jnp.split(frame_mods, 6, axis=1)
    normed_a, pull_norm_a = jax.vjp(modulate, hidden, shift_a, scale_a)
    normed_a = normed_a.astype(jnp.bfloat16)
    half = head_size // 2
    projected = lax.dot_general(
        w_qkv, normed_a, (((0,), (1,)), ((), ())), preferred_element_type=jnp.float32
    ) + b_qkv.astype(jnp.float32)[:, None]
    projected = projected.reshape(3, HEADS, head_size, frames)
    inverse = 10000.0 ** (-(2.0 * jnp.arange(half, dtype=jnp.float32)) / head_size)
    angles = inverse[:, None] * position.astype(jnp.float32)[None, :]
    cosine, sine = jnp.cos(angles)[None], jnp.sin(angles)[None]

    def turn(tensor, sign):
        first, second = tensor[:, :half], tensor[:, half:]
        return jnp.concatenate(
            [first * cosine - sign * second * sine, second * cosine + sign * first * sine], axis=1
        )

    packed = jnp.concatenate(
        [turn(projected[0], 1.0), turn(projected[1], 1.0), projected[2]], axis=1
    ).astype(jnp.bfloat16)
    packed = packed.reshape(seq_ways, local_heads, 3 * head_size, frames)
    ok = key_ok.reshape(seq_ways, 1, frames)
    exchange = functools.partial(
        lax.all_to_all, axis_name="seq", split_axis=0, concat_axis=0, tiled=True
    )
    received, head_out, log_totals, returned = [], [], [], []
    for h in range(local_heads):
        received.append(exchange(packed[:, h]))
    for h in range(local_heads):
        out, log_total = attend(lengths_row, received[h], ok)
        head_out.append(out)
        log_totals.append(log_total)
        returned.append(exchange(out))
    attended = jnp.stack(returned, axis=1).reshape(model_width, frames)
    attn_proj = transpose_dot(attended, w_out) + b_out.astype(jnp.float32)
    after_attn = hidden + gate_a * attn_proj
    normed_f, pull_norm_f = jax.vjp(modulate, after_attn, shift_f, scale_f)
    normed_f = normed_f.astype(jnp.bfloat16)
    up_proj = jnp.dot(normed_f, w_up, preferred_element_type=jnp.float32) + b_up.astype(jnp.float32)
    activated, pull_gelu = jax.vjp(gelu_tanh, up_proj)
    activated = activated.astype(jnp.bfloat16)
    ff_out = jnp.dot(activated, w_down, preferred_element_type=jnp.float32) + b_down.astype(
        jnp.float32
    )
    output = after_attn + gate_f * ff_out
    frame_count = lax.psum(jnp.sum(loss_mask[0].astype(jnp.float32)), ("batch", "seq"))
    grad_scale = group_frames * lax.axis_size("batch") / frame_count
    grad_out = (
        cotangent[0].astype(jnp.float32) * loss_mask[0].astype(jnp.float32)[:, None] * grad_scale
    )
    grad_ff = (grad_out * gate_f).astype(jnp.bfloat16)
    grad_gate_f = grad_out * ff_out
    grad_w_down = transpose_dot(activated, grad_ff)
    grad_b_down = jnp.sum(grad_ff.astype(jnp.float32), axis=0)
    grad_act = back_dot(grad_ff, w_down)
    grad_up = pull_gelu(grad_act)[0].astype(jnp.bfloat16)
    grad_w_up = transpose_dot(normed_f, grad_up)
    grad_b_up = jnp.sum(grad_up.astype(jnp.float32), axis=0)
    grad_normed_f = back_dot(grad_up, w_up)
    grad_after_norm, grad_shift_f, grad_scale_f = pull_norm_f(grad_normed_f)
    grad_after = grad_out + grad_after_norm
    grad_attn = (grad_after * gate_a).astype(jnp.bfloat16)
    grad_gate_a = grad_after * attn_proj
    grad_w_out = jnp.dot(attended, grad_attn, preferred_element_type=jnp.float32)
    grad_b_out = jnp.sum(grad_attn.astype(jnp.float32), axis=0)
    grad_attended = back_dot(w_out, grad_attn).astype(jnp.bfloat16)
    grad_attended = grad_attended.reshape(seq_ways, local_heads, head_size, frames)
    grad_heads = [exchange(grad_attended[:, h]) for h in range(local_heads)]
    grad_local = []
    for h in range(local_heads):
        grad_packed = attend_back(
            lengths_row, received[h], ok, head_out[h], grad_heads[h], log_totals[h]
        )
        grad_local.append(exchange(grad_packed))
    grad_local = jnp.stack(grad_local, axis=1).reshape(HEADS, 3, head_size, frames)
    grad_local = grad_local.astype(jnp.float32)
    grad_projected = jnp.stack(
        [turn(grad_local[:, 0], -1.0), turn(grad_local[:, 1], -1.0), grad_local[:, 2]]
    )
    grad_projected = grad_projected.reshape(3 * model_width, frames).astype(jnp.bfloat16)
    grad_w_qkv = lax.dot_general(
        normed_a, grad_projected, (((0,), (1,)), ((), ())), preferred_element_type=jnp.float32
    )
    grad_b_qkv = jnp.sum(grad_projected.astype(jnp.float32), axis=1)
    grad_normed_a = lax.dot_general(
        grad_projected, w_qkv, (((0,), (1,)), ((), ())), preferred_element_type=jnp.float32
    )
    grad_hidden_norm, grad_shift_a, grad_scale_a = pull_norm_a(grad_normed_a)
    grad_hidden = (grad_after + grad_hidden_norm).astype(jnp.bfloat16)
    grad_w_skip = transpose_dot(joined, grad_hidden)
    grad_b_skip = jnp.sum(grad_hidden.astype(jnp.float32), axis=0)
    grad_joined = back_dot(grad_hidden, w_skip)
    grad_tokens = grad_joined[:, :model_width]
    grad_skip = grad_joined[:, model_width:]
    grad_frame_mods = jnp.concatenate(
        [grad_shift_a, grad_scale_a, grad_gate_a, grad_shift_f, grad_scale_f, grad_gate_f], axis=1
    )
    grad_modulation = lax.dot_general(
        onehot, grad_frame_mods, (((0,), (0,)), ((), ())), precision=lax.Precision.HIGHEST
    )
    grad_modulation = lax.psum(grad_modulation, "seq")
    all_modulation = lax.all_gather(grad_modulation, "batch", axis=0, tiled=True)
    all_time = lax.all_gather(time_act, "batch", axis=0, tiled=True)
    ada_rows = model_width // seq_ways
    own_time = lax.dynamic_slice_in_dim(all_time, seq_rank * ada_rows, ada_rows, axis=1)
    grad_w_ada = lax.dot_general(
        own_time.astype(jnp.float32),
        all_modulation,
        (((0,), (0,)), ((), ())),
        precision=lax.Precision.HIGHEST,
    )
    bias_rows = all_modulation.shape[1] // seq_ways
    grad_b_ada = jnp.sum(
        lax.dynamic_slice_in_dim(all_modulation, seq_rank * bias_rows, bias_rows, axis=1), axis=0
    )
    def reduce_grad(grad):
        shard = lax.psum_scatter(
            grad.astype(jnp.bfloat16), "seq", scatter_dimension=0, tiled=True
        )
        return lax.psum(shard, "batch").astype(jnp.float32)

    reduced = [
        reduce_grad(g)
        for g in (
            grad_w_skip,
            grad_b_skip,
            grad_w_qkv,
            grad_b_qkv,
            grad_w_out,
            grad_b_out,
            grad_w_up,
            grad_b_up,
            grad_w_down,
            grad_b_down,
        )
    ]
    reduced = reduced[:2] + [grad_w_ada, grad_b_ada] + reduced[2:]
    return (
        output.astype(jnp.bfloat16)[None],
        grad_tokens[None],
        grad_skip[None],
        reduced[0],
        reduced[1],
        reduced[2],
        reduced[3],
        reduced[4],
        reduced[5],
        reduced[6],
        reduced[7],
        reduced[8],
        reduced[9],
        reduced[10],
        reduced[11],
    )


def solution(mesh):
    in_specs = (
        P("batch", "seq", None),
        P("batch", "seq", None),
        P("batch", "seq", None),
        P("batch", "seq", None),
        P("batch", None, None),
        P("batch", None),
        P("batch", None),
        P("batch", None),
        P("batch", "seq"),
        P(),
        P(),
        P(),
        P(),
        P(),
        P(),
        P(),
        P(),
        P(),
        P(),
        P(),
        P(),
    )
    out_specs = (
        P("batch", "seq", None),
        P("batch", "seq", None),
        P("batch", "seq", None),
        P("seq", None),
        P("seq"),
        P("seq", None),
        P("seq"),
        P("seq", None),
        P("seq"),
        P("seq", None),
        P("seq"),
        P("seq", None),
        P("seq"),
        P("seq", None),
        P("seq"),
    )
    return jax.shard_map(shards, mesh=mesh, in_specs=in_specs, out_specs=out_specs, check_vma=False)
```

```python
import functools

import jax
import jax.numpy as jnp
from jax import lax
from jax.experimental import pallas as pl
from jax.experimental.pallas import tpu as pltpu
from jax.sharding import PartitionSpec as P

HEADS = 16
HEAD_DIM = 64
PARTS = 8
BIG = 1e30
DH = 64
BQ = 512
BK = 512


def onehot_rows(lengths_ref, utts, rows, base, width):
    row = lax.broadcasted_iota(jnp.int32, (rows, width), 0)
    col = base + lax.broadcasted_iota(jnp.int32, (rows, width), 1)
    start = jnp.int32(0)
    hot = jnp.zeros((rows, width), jnp.float32)
    for u in range(utts):
        end = start + lengths_ref[u]
        hot = jnp.where((row == u) & (col >= start) & (col < end), 1.0, hot)
        start = end
    return hot


def key_range(lengths_ref, utts, first, last):
    start = jnp.int32(0)
    low, high = jnp.int32(0), jnp.int32(0)
    for u in range(utts):
        end = start + lengths_ref[u]
        low = jnp.where((start <= first) & (first < end), start, low)
        high = jnp.where((start <= last) & (last < end), end, high)
        start = end
    return low // BK, (high + BK - 1) // BK


def aug_rows(utts):
    return -(-utts // 16) * 16


def split3(row):
    a = row.astype(jnp.bfloat16)
    rest = row - a.astype(jnp.float32)
    b = rest.astype(jnp.bfloat16)
    c = (rest - b.astype(jnp.float32)).astype(jnp.bfloat16)
    return a, b, c


def pad_rows(parts, total):
    have = sum(p.shape[0] for p in parts)
    if have < total:
        parts = parts + [jnp.zeros((total - have, parts[0].shape[1]), parts[0].dtype)]
    return jnp.concatenate(parts, axis=0)


def rows16(rows, width):
    idx = lax.broadcasted_iota(jnp.int32, (16, width), 0)
    out = jnp.zeros((16, width), jnp.float32)
    for i, r in enumerate(rows):
        out = jnp.where(idx == i, r, out)
    return out.astype(jnp.bfloat16)


def fwd_kernel(utts, lengths_ref, qkv_ref, ok_ref, out_ref, lse_ref, kaug, vaug):
    sources, _, frames = qkv_ref.shape
    per = frames // BQ
    pad_u = aug_rows(utts)
    step = pl.program_id(0)

    @pl.when(step == 0)
    def _():
        def build(s, c):
            hot = onehot_rows(lengths_ref, utts, pad_u, s * frames, frames)
            ok = ok_ref[s].astype(jnp.float32)
            block = qkv_ref[s]
            one = jnp.ones((1, frames), jnp.float32)
            kT = pad_rows(
                [block[DH : 2 * DH], (1.0 - hot).astype(jnp.bfloat16), rows16([1.0 - ok], frames)], 128
            )
            kaug[pl.ds(pl.multiple_of(s * frames, frames), frames), :] = kT.T
            vT = jnp.concatenate([block[2 * DH :], rows16([one], frames)], axis=0)
            for t in range(frames // BK):
                vaug[s * (frames // BK) + t] = vT[:, t * BK : (t + 1) * BK]
            return c

        lax.fori_loop(0, sources, build, 0)

    block = qkv_ref[step]
    hot_q = onehot_rows(lengths_ref, utts, pad_u, step * frames, frames)
    qT = (block[:DH].astype(jnp.float32) * 0.125)
    one = jnp.ones((1, frames), jnp.float32)
    qaug = pad_rows(
        [qT.astype(jnp.bfloat16), (hot_q * -BIG).astype(jnp.bfloat16), rows16([one * -BIG], frames)], 128
    )
    kT = block[DH : 2 * DH].astype(jnp.float32)
    vT = block[2 * DH :].astype(jnp.float32)
    ok = ok_ref[step] > 0
    s_self = jnp.sum(qT * kT, axis=0, keepdims=True)
    m0 = jnp.where(ok, -3e38, s_self)
    acc0 = jnp.concatenate([jnp.where(ok, 0.0, vT), jnp.where(ok, 0.0, jnp.ones((16, frames), jnp.float32))], axis=0)
    for t in range(per):
        cols = slice(t * BQ, (t + 1) * BQ)
        low, high = key_range(lengths_ref, utts, step * frames + t * BQ, step * frames + (t + 1) * BQ - 1)
        q_b = qaug[:, cols]

        def body(j, carry):
            m, acc = carry
            s = jnp.dot(kaug[pl.ds(pl.multiple_of(j * BK, BK), BK), :], q_b, preferred_element_type=jnp.float32)
            m_new = jnp.maximum(m, jnp.max(s, axis=0, keepdims=True))
            p = jnp.exp(s - m_new).astype(jnp.bfloat16)
            alpha = jnp.exp(m - m_new)
            acc = acc * alpha + jnp.dot(vaug[j], p, preferred_element_type=jnp.float32)
            return m_new, acc

        m, acc = lax.fori_loop(low, high, body, (m0[:, cols], acc0[:, cols]))
        total = acc[DH : DH + 1]
        out_ref[0, :, cols] = (acc[:DH] / total).astype(jnp.bfloat16)
        lse_ref[0, :, cols] = m + jnp.log(total)


def attend(lengths, qkv, ok):
    sources, _, frames = qkv.shape
    total = sources * frames
    utts = lengths.shape[0]
    whole = lambda shape: pl.BlockSpec(shape, lambda i, *_: (0,) * len(shape))
    return pl.pallas_call(
        functools.partial(fwd_kernel, utts),
        out_shape=(
            jax.ShapeDtypeStruct((sources, DH, frames), jnp.bfloat16),
            jax.ShapeDtypeStruct((sources, 1, frames), jnp.float32),
        ),
        grid_spec=pltpu.PrefetchScalarGridSpec(
            num_scalar_prefetch=1,
            grid=(sources,),
            in_specs=[whole(qkv.shape), whole(ok.shape)],
            out_specs=(
                pl.BlockSpec((1, DH, frames), lambda i, *_: (i, 0, 0)),
                pl.BlockSpec((1, 1, frames), lambda i, *_: (i, 0, 0)),
            ),
            scratch_shapes=[
                pltpu.VMEM((total, 128), jnp.bfloat16),
                pltpu.VMEM((total // BK, DH + 16, BK), jnp.bfloat16),
            ],
        ),
        name="attend",
    )(lengths, qkv, ok)


def bwd_kernel(utts, lengths_ref, qkv_ref, ok_ref, o_ref, do_ref, lse_ref, out_ref, kaug, vnat, kT_s, dk, dv):
    sources, _, frames = qkv_ref.shape
    per = frames // BK
    pad_u = aug_rows(utts)
    step = pl.program_id(0)
    f32 = jnp.float32

    @pl.when(step == 0)
    def _():
        def build(s, c):
            hot = onehot_rows(lengths_ref, utts, pad_u, s * frames, frames)
            ok = ok_ref[s]
            block = qkv_ref[s]
            one = jnp.ones((1, frames), f32)
            kT = block[DH : 2 * DH]
            vT = block[2 * DH :]
            kA = pad_rows(
                [kT, (1.0 - hot).astype(jnp.bfloat16), rows16([1.0 - ok.astype(f32), one, one, one], frames)], 128
            )
            rows = pl.ds(pl.multiple_of(s * frames, frames), frames)
            kaug[rows, :] = kA.T
            vnat[rows, :] = pad_rows([vT, rows16([one, one, one], frames)], 128).T
            qT = block[:DH].astype(f32) * 0.125
            do = do_ref[s].astype(f32)
            s_self = jnp.sum(qT * kT.astype(f32), axis=0, keepdims=True)
            delta = jnp.sum(do * o_ref[s].astype(f32), axis=0, keepdims=True)
            p_self = jnp.where(ok > 0, 0.0, jnp.exp(s_self - lse_ref[s]))
            ds_self = p_self * (jnp.sum(do * vT.astype(f32), axis=0, keepdims=True) - delta)
            dk0 = ds_self * qT
            dv0 = p_self * do
            for t in range(per):
                cols = slice(t * BK, (t + 1) * BK)
                kT_s[s * per + t] = kT[:, cols]
                dk[s * per + t] = dk0[:, cols]
                dv[s * per + t] = dv0[:, cols]
            return c

        lax.fori_loop(0, sources, build, 0)

    block = qkv_ref[step]
    one = jnp.ones((1, frames), f32)
    hot_q = onehot_rows(lengths_ref, utts, pad_u, step * frames, frames)
    qT = block[:DH].astype(f32) * 0.125
    qTb = qT.astype(jnp.bfloat16)
    kT = block[DH : 2 * DH].astype(f32)
    vT = block[2 * DH :].astype(f32)
    ok = ok_ref[step]
    dob = do_ref[step]
    do = dob.astype(f32)
    lse = lse_ref[step]
    delta = jnp.sum(do * o_ref[step].astype(f32), axis=0, keepdims=True)
    l3 = [-r.astype(f32) for r in split3(lse)]
    d3 = [-r.astype(f32) for r in split3(delta)]
    qaug = pad_rows([qTb, (hot_q * -BIG).astype(jnp.bfloat16), rows16([one * -BIG] + l3, frames)], 128)
    doaug = pad_rows([dob, rows16(d3, frames)], 128)
    s_self = jnp.sum(qT * kT, axis=0, keepdims=True)
    p_self = jnp.where(ok > 0, 0.0, jnp.exp(s_self - lse))
    ds_self = p_self * (jnp.sum(do * vT, axis=0, keepdims=True) - delta)
    dq0 = ds_self * kT
    nt = (((1,), (1,)), ((), ()))
    for t in range(frames // BQ):
        cols = slice(t * BQ, (t + 1) * BQ)
        low, high = key_range(lengths_ref, utts, step * frames + t * BQ, step * frames + (t + 1) * BQ - 1)
        q_a = qaug[:, cols]
        q_b = qTb[:, cols]
        do_a = doaug[:, cols]
        do_b = dob[:, cols]

        def body(j, dq):
            rows = pl.ds(pl.multiple_of(j * BK, BK), BK)
            s = jnp.dot(kaug[rows, :], q_a, preferred_element_type=f32)
            dp = jnp.dot(vnat[rows, :], do_a, preferred_element_type=f32)
            p = jnp.exp(s)
            ds = (p * dp).astype(jnp.bfloat16)
            dv[j] += lax.dot_general(do_b, p.astype(jnp.bfloat16), nt, preferred_element_type=f32)
            dk[j] += lax.dot_general(q_b, ds, nt, preferred_element_type=f32)
            return dq + jnp.dot(kT_s[j], ds, preferred_element_type=f32)

        dq = lax.fori_loop(low, high, body, dq0[:, cols])
        out_ref[step, :DH, cols] = (dq * 0.125).astype(jnp.bfloat16)

    @pl.when(step == sources - 1)
    def _():
        def finish(s, c):
            for t in range(per):
                cols = slice(t * BK, (t + 1) * BK)
                out_ref[s, DH : 2 * DH, cols] = dk[s * per + t].astype(jnp.bfloat16)
                out_ref[s, 2 * DH :, cols] = dv[s * per + t].astype(jnp.bfloat16)
            return c

        lax.fori_loop(0, sources, finish, 0)


def attend_back(lengths, qkv, ok, out, grad, lse):
    sources, _, frames = qkv.shape
    total = sources * frames
    utts = lengths.shape[0]
    whole = lambda shape: pl.BlockSpec(shape, lambda i, *_: (0,) * len(shape))
    return pl.pallas_call(
        functools.partial(bwd_kernel, utts),
        out_shape=jax.ShapeDtypeStruct(qkv.shape, jnp.bfloat16),
        grid_spec=pltpu.PrefetchScalarGridSpec(
            num_scalar_prefetch=1,
            grid=(sources,),
            in_specs=[whole(a.shape) for a in (qkv, ok, out, grad, lse)],
            out_specs=whole(qkv.shape),
            scratch_shapes=[
                pltpu.VMEM((total, 128), jnp.bfloat16),
                pltpu.VMEM((total, 128), jnp.bfloat16),
                pltpu.VMEM((total // BK, DH, BK), jnp.bfloat16),
                pltpu.VMEM((total // BK, DH, BK), jnp.float32),
                pltpu.VMEM((total // BK, DH, BK), jnp.float32),
            ],
        ),
        name="attend_back",
    )(lengths, qkv, ok, out, grad, lse)


FF_TILE = 512
EPS = 1e-06


def dot(left, right):
    return jnp.dot(left, right, preferred_element_type=jnp.float32)


def dot_nt(left, right):
    return lax.dot_general(left, right, (((1,), (1,)), ((), ())), preferred_element_type=jnp.float32)


def norm_stats(x):
    mean = jnp.mean(x, axis=1, keepdims=True)
    centred = x - mean
    rstd = lax.rsqrt(jnp.mean(centred * centred, axis=1, keepdims=True) + EPS)
    return centred * rstd, rstd


def norm_back(grad, normed, rstd):
    first = jnp.mean(grad, axis=1, keepdims=True)
    second = jnp.mean(grad * normed, axis=1, keepdims=True)
    return rstd * (grad - first - normed * second)


def mods_operand(mods_ref):
    rows = mods_ref[...]
    return pad_rows(list(split3(rows)), 128)


def sum_rows(hot, utts_pad, frames):
    idx = lax.broadcasted_iota(jnp.int32, (16, frames), 0)
    ones = jnp.where(idx == 0, 1.0, 0.0).astype(jnp.bfloat16)
    return jnp.concatenate([hot.astype(jnp.bfloat16), ones], axis=0)


def mid_kernel(
    dims,
    lengths_ref,
    ids_ref,
    scale_ref,
    *refs,
):
    seq_ways, heads_local, utts = dims
    att_refs = refs[:heads_local]
    (
        hidden_ref,
        mods_ref,
        cot_ref,
        loss_ref,
        w_out_ref,
        b_out_ref,
        w_up_ref,
        b_up_ref,
        w_down_ref,
        b_down_ref,
    ) = refs[heads_local : heads_local + 10]
    outs = refs[heads_local + 10 :]
    output_ref, after_grad_ref, tables_ref, b_up_grad_ref = outs[:4]
    gatt_refs = outs[4 : 4 + heads_local]
    keep_ref, send_ref = outs[4 + heads_local : 6 + heads_local]
    (
        attT,
        attn_proj,
        after,
        nf,
        nfT,
        gff,
        ff_acc,
        gnf_acc,
        sums,
        cols,
        madd,
        grads,
        sems,
    ) = outs[6 + heads_local :]
    f32, bf16 = jnp.float32, jnp.bfloat16
    step = pl.program_id(0)
    steps = pl.num_programs(0)
    core = ids_ref[0]
    rank = ids_ref[1]
    frames, width = hidden_ref.shape
    up_rows = width // seq_ways
    down_rows = FF_TILE
    z_ways = seq_ways // 2
    parts = grads.shape[1]
    ff_total = b_up_grad_ref.shape[1]
    up_part = ff_total // width * up_rows // parts
    down_block = ff_total // seq_ways
    down_part = down_block // parts
    out_part = up_rows // parts

    def mod(index):
        return dot(cols[...], madd[:, index * width : (index + 1) * width])

    def grad_out():
        loss = cols[:, 48:49].astype(f32)
        return cot_ref[...].astype(f32) * (loss * scale_ref[0])

    @pl.when(step == 0)
    def _():
        hot = onehot_rows(lengths_ref, utts, 16, rank * frames, frames)
        hotb = hot.astype(bf16)
        idx = lax.broadcasted_iota(jnp.int32, (16, frames), 0)
        loss = jnp.where(idx == 0, loss_ref[...].astype(f32), 0.0).astype(bf16)
        cols[...] = pad_rows([hotb, hotb, hotb, loss], 128).T
        sums[...] = sum_rows(hot, 16, frames)
        madd[...] = mods_operand(mods_ref)
        for c in range(heads_local):
            for s in range(seq_ways):
                attT[(c * seq_ways + s) * DH : (c * seq_ways + s + 1) * DH, :] = att_refs[c][s]
        proj = dot(attT[...].T, w_out_ref[...]) + b_out_ref[...].astype(f32)
        attn_proj[...] = proj
        mixed = hidden_ref[...] + mod(0) * proj
        after[...] = mixed
        normed, _ = norm_stats(mixed)
        value = (normed * (1.0 + mod(2)) + mod(1)).astype(bf16)
        nf[...] = value
        nfT[...] = value.T
        gff[...] = (grad_out() * mod(3)).astype(bf16)

    up = dot(nf[...], w_up_ref[...]) + b_up_ref[...].astype(f32)
    inner = 0.7978845608028654 * (up + 0.044715 * (up * up * up))
    tanh = jnp.tanh(inner)
    cdf = 0.5 * (1.0 + tanh)
    act = (up * cdf).astype(bf16)
    slope = cdf + 0.5 * up * (1.0 - tanh * tanh) * (
        0.7978845608028654 * (1.0 + (3 * 0.044715) * (up * up))
    )
    ff_part = dot(act, w_down_ref[...])
    gup = (dot_nt(gff[...], w_down_ref[...]) * slope).astype(bf16)
    gnf_part = dot_nt(gup, w_up_ref[...])

    @pl.when(step == 0)
    def _():
        ff_acc[...] = ff_part
        gnf_acc[...] = gnf_part

    @pl.when(step > 0)
    def _():
        ff_acc[...] += ff_part
        gnf_acc[...] += gnf_part

    b_up_grad_ref[:, pl.ds(pl.multiple_of(step * FF_TILE, FF_TILE), FF_TILE)] = dot(
        sums[16:32, :], gup
    )[:8]
    halves = width // FF_TILE
    chunk = step // halves
    half = step % halves
    col = pl.ds(pl.multiple_of(half * FF_TILE, FF_TILE), FF_TILE)
    per_chunk = up_rows // up_part
    grad_w_up = dot(nfT[...], gup).astype(bf16)
    for s in range(seq_ways):
        side = jnp.where(core == s % 2, 0, 1)
        for h in range(per_chunk):
            lo = s * up_rows + h * up_part
            grads[side, chunk * per_chunk + h, s // 2, 0:up_part, col] = grad_w_up[lo : lo + up_part]
    grad_w_down = dot(act.T, gff[...]).astype(bf16)
    blocks = FF_TILE // down_block
    copies = []
    for b in range(blocks):
        s = step * blocks + b
        side = jnp.where(core == s % 2, 0, 1)
        for k in range(parts):
            lo = b * down_block + k * down_part
            grads[side, k, s // 2, up_part : up_part + down_part, :] = grad_w_down[lo : lo + down_part]

    def up_copy(side, j):
        target = (keep_ref, send_ref)[side]
        where = (
            pl.ds((j // halves) * per_chunk, per_chunk),
            slice(None),
            pl.ds(0, up_part),
            pl.ds(pl.multiple_of((j % halves) * FF_TILE, FF_TILE), FF_TILE),
        )
        return pltpu.make_async_copy(grads.at[side].at[where], target.at[where], sems.at[side, j])

    def down_copy(side, z, index):
        target = (keep_ref, send_ref)[side]
        where = (slice(None), pl.ds(z, 1), pl.ds(up_part, down_part), slice(None))
        return pltpu.make_async_copy(grads.at[side].at[where], target.at[where], sems.at[side, index])

    def out_copy(side):
        target = (keep_ref, send_ref)[side]
        where = (slice(None), slice(None), pl.ds(up_part + down_part, out_part), slice(None))
        return pltpu.make_async_copy(
            grads.at[side].at[where], target.at[where], sems.at[side, ff_total // FF_TILE + z_ways]
        )

    base = ff_total // FF_TILE
    for side in range(2):
        up_copy(side, step).start()
    for b in range(blocks):
        s = step * blocks + b
        for side in range(2):

            @pl.when(lax.rem(s + core, 2) == side)
            def _():
                down_copy(side, s // 2, base + s // 2).start()

    @pl.when(step == steps - 1)
    def _():
        ff_out = ff_acc[...] + b_down_ref[...].astype(f32)
        mixed = after[...]
        go = grad_out()
        output_ref[...] = (mixed + mod(3) * ff_out).astype(bf16)
        rows = sums[...]
        tables_ref[:, 3 * width : 4 * width] = dot(rows, (go * ff_out).astype(bf16))
        normed, rstd = norm_stats(mixed)
        gnf = gnf_acc[...]
        tables_ref[:, width : 2 * width] = dot(rows, gnf.astype(bf16))
        tables_ref[:, 2 * width : 3 * width] = dot(rows, (gnf * normed).astype(bf16))
        g_after = go + norm_back(gnf * (1.0 + mod(2)), normed, rstd)
        after_grad_ref[...] = g_after
        tables_ref[:, 0:width] = dot(rows, (g_after * attn_proj[...]).astype(bf16))
        gattn = (g_after * mod(0)).astype(bf16)
        tables_ref[:, 4 * width : 5 * width] = dot(rows, gattn)
        tables_ref[:, 5 * width : 6 * width] = dot(rows, gff[...])
        gattT = dot_nt(w_out_ref[...], gattn).astype(bf16)
        for c in range(heads_local):
            for s in range(seq_ways):
                lo = (c * seq_ways + s) * DH
                gatt_refs[c][s] = gattT[lo : lo + DH]
        grad_w_out = dot(attT[...], gattn).astype(bf16)
        for s in range(seq_ways):
            side = jnp.where(core == s % 2, 0, 1)
            for k in range(parts):
                lo = s * up_rows + k * out_part
                grads[side, k, s // 2, up_part + down_part : up_part + down_part + out_part, :] = grad_w_out[
                    lo : lo + out_part
                ]
        for side in range(2):
            out_copy(side).start()
        for side in range(2):
            for j in range(ff_total // FF_TILE):
                up_copy(side, j).wait()
            for z in range(z_ways):
                down_copy(side, z, base + z).wait()
            out_copy(side).wait()


def mid_block(
    lengths, ids, scale, att, hidden, mods, cot, loss, w_out, b_out, w_up, b_up, w_down, b_down, parts
):
    frames, width = hidden.shape
    heads_local = len(att)
    seq_ways = att[0].shape[0]
    ff = w_up.shape[1]
    up_rows = width // seq_ways
    rows = (ff // width * up_rows + ff // seq_ways + up_rows) // parts
    utts = lengths.shape[0]
    f32, bf16 = jnp.float32, jnp.bfloat16
    steps = ff // FF_TILE

    def whole(shape):
        return pl.BlockSpec(shape, lambda j, *_: (0,) * len(shape), pipeline_mode=pl.Buffered(1))

    hbm = pl.BlockSpec(memory_space=pl.ANY)
    gshape = (parts, seq_ways // 2, rows, width)
    out_shape = [
        jax.ShapeDtypeStruct((frames, width), bf16),
        jax.ShapeDtypeStruct((frames, width), f32),
        jax.ShapeDtypeStruct((32, 6 * width), f32),
        jax.ShapeDtypeStruct((8, ff), f32),
    ]
    out_shape += [jax.ShapeDtypeStruct(a.shape, bf16) for a in att]
    out_specs = [whole(o.shape) for o in out_shape] + [hbm, hbm]
    out_shape += [jax.ShapeDtypeStruct(gshape, bf16)] * 2
    ins = list(att) + [hidden, mods, cot, loss, w_out, b_out]
    return pl.pallas_call(
        functools.partial(mid_kernel, (seq_ways, heads_local, utts)),
        out_shape=out_shape,
        grid_spec=pltpu.PrefetchScalarGridSpec(
            num_scalar_prefetch=3,
            grid=(steps,),
            in_specs=[whole(a.shape) for a in ins]
            + [
                pl.BlockSpec((width, FF_TILE), lambda j, *_: (0, j)),
                pl.BlockSpec((1, FF_TILE), lambda j, *_: (0, j)),
                pl.BlockSpec((FF_TILE, width), lambda j, *_: (j, 0)),
                whole((1, width)),
            ],
            out_specs=out_specs,
            scratch_shapes=[
                pltpu.VMEM((width, frames), bf16),
                pltpu.VMEM((frames, width), f32),
                pltpu.VMEM((frames, width), f32),
                pltpu.VMEM((frames, width), bf16),
                pltpu.VMEM((width, frames), bf16),
                pltpu.VMEM((frames, width), bf16),
                pltpu.VMEM((frames, width), f32),
                pltpu.VMEM((frames, width), f32),
                pltpu.VMEM((32, frames), bf16),
                pltpu.VMEM((frames, 128), bf16),
                pltpu.VMEM((128, 4 * width), bf16),
                pltpu.VMEM((2,) + gshape, bf16),
                pltpu.SemaphoreType.DMA((2, steps + seq_ways // 2 + 1)),
            ],
        ),
        compiler_params=pltpu.CompilerParams(vmem_limit_bytes=63 << 20),
        cost_estimate=pl.CostEstimate(
            flops=2 * frames * width * (6 * ff + 3 * width),
            bytes_accessed=4 * width * ff * 2 + 16 * frames * width,
            transcendentals=frames * ff,
        ),
        name="mid_block",
    )(lengths, ids, scale, *ins, w_up, b_up, w_down, b_down)


def segment_rows(lengths_ref, drop_ref, utts, base, width):
    col = base + lax.broadcasted_iota(jnp.int32, (1, width), 1)
    start = jnp.int32(0)
    kept = jnp.zeros((1, width), jnp.float32)
    place = jnp.zeros((1, width), jnp.int32)
    for u in range(utts):
        end = start + lengths_ref[u]
        inside = (col >= start) & (col < end)
        kept = jnp.where(inside, (1 - drop_ref[u]).astype(jnp.float32), kept)
        place = jnp.where(inside, col - start, place)
        start = end
    return kept, place.astype(jnp.float32)


def rotary_rows(place, half):
    index = lax.broadcasted_iota(jnp.int32, (half, 1), 0).astype(jnp.float32)
    inverse = jnp.exp(index * (-9.210340371976184 / half))
    angles = inverse * place
    return jnp.cos(angles), jnp.sin(angles)


def frame_columns(hot, extra):
    hotb = hot.astype(jnp.bfloat16)
    idx = lax.broadcasted_iota(jnp.int32, hot.shape, 0)
    last = jnp.where(idx == 0, extra, 0.0).astype(jnp.bfloat16)
    return pad_rows([hotb, hotb, hotb, last], 128).T


def head_kernel(
    utts,
    lengths_ref,
    ids_ref,
    drop_ref,
    tokens_ref,
    skip_ref,
    cond_ref,
    mods_ref,
    w_skip_ref,
    b_skip_ref,
    hidden_ref,
    joinedT_ref,
    naT_ref,
    na_ref,
    cols,
):
    f32, bf16 = jnp.float32, jnp.bfloat16
    step = pl.program_id(0)
    frames, width = tokens_ref.shape
    rank = ids_ref[1]

    @pl.when(step == 0)
    def _():
        hot = onehot_rows(lengths_ref, utts, 16, rank * frames, frames)
        kept, _ = segment_rows(lengths_ref, drop_ref, utts, rank * frames, frames)
        cols[...] = frame_columns(hot, kept)
        keep = cols[:, 48:49].astype(f32)
        mixed = (tokens_ref[...].astype(f32) + keep * cond_ref[...].astype(f32)).astype(bf16)
        joinedT_ref[0:width, :] = mixed.T
        hidden_ref[...] = dot(mixed, w_skip_ref[...]) + b_skip_ref[...].astype(f32)

    @pl.when(step == 1)
    def _():
        skip = skip_ref[...]
        joinedT_ref[width : 2 * width, :] = skip.T
        hidden = hidden_ref[...] + dot(skip, w_skip_ref[...])
        hidden_ref[...] = hidden
        madd = mods_operand(mods_ref)
        shift = dot(cols[...], madd[:, :width])
        scale = dot(cols[...], madd[:, width:])
        normed, _ = norm_stats(hidden)
        value = (normed * (1.0 + scale) + shift).astype(bf16)
        na_ref[...] = value
        naT_ref[...] = value.T


def head_block(lengths, ids, drop, tokens, skip, cond, mods, w_skip, b_skip):
    frames, width = tokens.shape
    utts = lengths.shape[0]
    f32, bf16 = jnp.float32, jnp.bfloat16

    def whole(shape):
        return pl.BlockSpec(shape, lambda j, *_: (0,) * len(shape), pipeline_mode=pl.Buffered(1))

    out_shape = [
        jax.ShapeDtypeStruct((frames, width), f32),
        jax.ShapeDtypeStruct((2 * width, frames), bf16),
        jax.ShapeDtypeStruct((width, frames), bf16),
        jax.ShapeDtypeStruct((frames, width), bf16),
    ]
    return pl.pallas_call(
        functools.partial(head_kernel, utts),
        out_shape=out_shape,
        grid_spec=pltpu.PrefetchScalarGridSpec(
            num_scalar_prefetch=3,
            grid=(2,),
            in_specs=[whole(a.shape) for a in (tokens, skip, cond, mods)]
            + [pl.BlockSpec((width, width), lambda j, *_: (j, 0)), whole((1, width))],
            out_specs=[whole(o.shape) for o in out_shape],
            scratch_shapes=[pltpu.VMEM((frames, 128), bf16)],
        ),
        compiler_params=pltpu.CompilerParams(vmem_limit_bytes=48 << 20),
        cost_estimate=pl.CostEstimate(
            flops=4 * frames * width * width, bytes_accessed=20 * frames * width, transcendentals=0
        ),
        name="head_block",
    )(lengths, ids, drop, tokens, skip, cond, mods, w_skip, b_skip)


def turn_heads(tensor, cosine, sine):
    half = DH // 2
    first, second = tensor[:, :half], tensor[:, half:]
    return jnp.concatenate([first * cosine - second * sine, second * cosine + first * sine], axis=1)


def qkv_kernel(utts, seq_ways, lengths_ref, ids_ref, drop_ref, na_ref, w_ref, b_ref, out_ref, trig):
    f32, bf16 = jnp.float32, jnp.bfloat16
    part = pl.program_id(0)
    frames = na_ref.shape[0]

    @pl.when(part == 0)
    def _():
        _, place = segment_rows(lengths_ref, drop_ref, utts, ids_ref[1] * frames, frames)
        cosine, sine = rotary_rows(place, DH // 2)
        trig[0] = cosine
        trig[1] = sine

    raw = dot(na_ref[...], w_ref[...]) + b_ref[...].astype(f32)
    rawT = raw.T.reshape(seq_ways, DH, frames)
    turned = part < 2
    cosine = jnp.where(turned, trig[0], 1.0)[None]
    sine = jnp.where(turned, trig[1], 0.0)[None]
    out_ref[:, pl.ds(pl.multiple_of(part * DH, DH), DH), :] = turn_heads(rawT, cosine, sine).astype(bf16)


def qkv_block(lengths, ids, drop, na, w_qkv, b_qkv, chunk, seq_ways):
    frames, width = na.shape
    cols = seq_ways * DH
    chunks = width // cols
    utts = lengths.shape[0]

    def whole(shape):
        return pl.BlockSpec(shape, lambda j, *_: (0,) * len(shape), pipeline_mode=pl.Buffered(1))

    shape = (seq_ways, 3 * DH, frames)
    return pl.pallas_call(
        functools.partial(qkv_kernel, utts, seq_ways),
        out_shape=jax.ShapeDtypeStruct(shape, jnp.bfloat16),
        grid_spec=pltpu.PrefetchScalarGridSpec(
            num_scalar_prefetch=3,
            grid=(3,),
            in_specs=[
                whole(na.shape),
                pl.BlockSpec((width, cols), lambda j, *_: (0, j * chunks + chunk)),
                pl.BlockSpec((1, cols), lambda j, *_: (0, j * chunks + chunk)),
            ],
            out_specs=whole(shape),
            scratch_shapes=[pltpu.VMEM((2, DH // 2, frames), jnp.float32)],
        ),
        cost_estimate=pl.CostEstimate(
            flops=6 * frames * width * cols, bytes_accessed=10 * frames * width, transcendentals=0
        ),
        name="qkv_block",
    )(lengths, ids, drop, na, w_qkv, b_qkv)


def back_kernel(utts, seq_ways, first, lengths_ref, ids_ref, drop_ref, grad_ref, naT_ref, w_ref, *refs):
    if first:
        acc_in = None
        acc_ref, bias_ref, keep_ref, send_ref, trig = refs
    else:
        acc_in, acc_ref, bias_ref, keep_ref, send_ref, trig = refs
    f32, bf16 = jnp.float32, jnp.bfloat16
    part = pl.program_id(0)
    width, frames = naT_ref.shape
    core = ids_ref[0]
    parts = keep_ref.shape[0]
    own = width // seq_ways
    rows = own // parts

    @pl.when(part == 0)
    def _():
        _, place = segment_rows(lengths_ref, drop_ref, utts, ids_ref[1] * frames, frames)
        cosine, sine = rotary_rows(place, DH // 2)
        trig[0] = cosine
        trig[1] = sine

    turned = part < 2
    cosine = jnp.where(turned, trig[0], 1.0)[None]
    sine = jnp.where(turned, trig[1], 0.0)[None]
    raw = grad_ref[:, pl.ds(pl.multiple_of(part * DH, DH), DH), :].astype(f32)
    gpT = turn_heads(raw, cosine, -sine).astype(bf16).reshape(seq_ways * DH, frames)
    gna = dot(w_ref[...], gpT)

    @pl.when(part == 0)
    def _():
        acc_ref[...] = gna if first else acc_in[...] + gna

    @pl.when(part > 0)
    def _():
        acc_ref[...] += gna

    ones = jnp.ones((8, frames), bf16)
    bias_ref[0] = dot_nt(ones, gpT)
    grad_w = dot_nt(naT_ref[...], gpT).astype(bf16)
    for s in range(seq_ways):
        for k in range(parts):
            tile = grad_w[s * own + k * rows : s * own + (k + 1) * rows]

            @pl.when(core == s % 2)
            def _():
                keep_ref[k, s // 2] = tile

            @pl.when(core != s % 2)
            def _():
                send_ref[k, s // 2] = tile


def back_block(lengths, ids, drop, grad, naT, w_qkv, acc, chunk, parts):
    seq_ways, _, frames = grad.shape
    width = naT.shape[0]
    cols = seq_ways * DH
    chunks = width // cols
    utts = lengths.shape[0]
    f32, bf16 = jnp.float32, jnp.bfloat16
    rows = width // seq_ways // parts

    def whole(shape):
        return pl.BlockSpec(shape, lambda j, *_: (0,) * len(shape), pipeline_mode=pl.Buffered(1))

    gblock = (parts, seq_ways // 2, rows, cols)
    gspec = pl.BlockSpec(gblock, lambda j, *_: (0, 0, 0, j))
    gshape = jax.ShapeDtypeStruct((parts, seq_ways // 2, rows, 3 * cols), bf16)
    ins = [grad, naT, w_qkv] + ([] if acc is None else [acc])
    in_specs = [whole(grad.shape), whole(naT.shape)]
    in_specs += [pl.BlockSpec((width, cols), lambda j, *_: (0, j * chunks + chunk))]
    if acc is not None:
        in_specs += [whole(acc.shape)]
    return pl.pallas_call(
        functools.partial(back_kernel, utts, seq_ways, acc is None),
        out_shape=[
            jax.ShapeDtypeStruct((width, frames), f32),
            jax.ShapeDtypeStruct((3, 8, cols), f32),
            gshape,
            gshape,
        ],
        grid_spec=pltpu.PrefetchScalarGridSpec(
            num_scalar_prefetch=3,
            grid=(3,),
            in_specs=in_specs,
            out_specs=[
                whole((width, frames)),
                pl.BlockSpec((1, 8, cols), lambda j, *_: (j, 0, 0)),
                gspec,
                gspec,
            ],
            scratch_shapes=[pltpu.VMEM((2, DH // 2, frames), f32)],
        ),
        cost_estimate=pl.CostEstimate(
            flops=12 * frames * width * cols, bytes_accessed=20 * frames * width, transcendentals=0
        ),
        name="back_block",
    )(lengths, ids, drop, *ins)


def tail_kernel(
    utts,
    seq_ways,
    lengths_ref,
    ids_ref,
    acc_ref,
    hidden_ref,
    after_ref,
    mods_ref,
    joinedT_ref,
    w_skip_ref,
    tables_ref,
    grad_a_ref,
    grad_b_ref,
    keep_ref,
    send_ref,
    gh_ref,
):
    f32, bf16 = jnp.float32, jnp.bfloat16
    step = pl.program_id(0)
    frames, width = hidden_ref.shape
    core = ids_ref[0]
    parts = keep_ref.shape[0]
    block = 2 * width // seq_ways
    rows = block // parts

    @pl.when(step == 0)
    def _():
        hot = onehot_rows(lengths_ref, utts, 16, ids_ref[1] * frames, frames)
        cols = frame_columns(hot, jnp.zeros((1, frames), f32))
        madd = mods_operand(mods_ref)
        scale = dot(cols, madd[:, width:])
        gna = acc_ref[...].T
        normed, rstd = norm_stats(hidden_ref[...])
        sums = sum_rows(hot, 16, frames)
        tables_ref[:, 0:width] = dot(sums, gna.astype(bf16))
        tables_ref[:, width : 2 * width] = dot(sums, (gna * normed).astype(bf16))
        gh = (after_ref[...] + norm_back(gna * (1.0 + scale), normed, rstd)).astype(bf16)
        gh_ref[...] = gh
        tables_ref[:, 2 * width : 3 * width] = dot(sums, gh)

    gh = gh_ref[...]
    grad_w = dot(joinedT_ref[...], gh).astype(bf16)
    blocks = width // block
    for b in range(blocks):
        for k in range(parts):
            tile = grad_w[b * block + k * rows : b * block + (k + 1) * rows]

            @pl.when(core == b % 2)
            def _():
                keep_ref[k, b // 2] = tile

            @pl.when(core != b % 2)
            def _():
                send_ref[k, b // 2] = tile

    joined = dot_nt(gh, w_skip_ref[...])

    @pl.when(step == 0)
    def _():
        grad_a_ref[...] = joined

    @pl.when(step == 1)
    def _():
        grad_b_ref[...] = joined


def tail_block(lengths, ids, acc, hidden, after, mods, joinedT, w_skip, seq_ways, parts):
    frames, width = hidden.shape
    utts = lengths.shape[0]
    f32, bf16 = jnp.float32, jnp.bfloat16
    rows = 2 * width // seq_ways // parts

    def whole(shape):
        return pl.BlockSpec(shape, lambda j, *_: (0,) * len(shape), pipeline_mode=pl.Buffered(1))

    gspec = pl.BlockSpec((parts, seq_ways // 4, rows, width), lambda j, *_: (0, j, 0, 0))
    gshape = jax.ShapeDtypeStruct((parts, seq_ways // 2, rows, width), bf16)
    out_shape = [
        jax.ShapeDtypeStruct((32, 3 * width), f32),
        jax.ShapeDtypeStruct((frames, width), f32),
        jax.ShapeDtypeStruct((frames, width), f32),
        gshape,
        gshape,
    ]
    return pl.pallas_call(
        functools.partial(tail_kernel, utts, seq_ways),
        out_shape=out_shape,
        grid_spec=pltpu.PrefetchScalarGridSpec(
            num_scalar_prefetch=2,
            grid=(2,),
            in_specs=[whole(a.shape) for a in (acc, hidden, after, mods)]
            + [
                pl.BlockSpec((width, frames), lambda j, *_: (j, 0)),
                pl.BlockSpec((width, width), lambda j, *_: (j, 0)),
            ],
            out_specs=[whole(o.shape) for o in out_shape[:3]] + [gspec, gspec],
            scratch_shapes=[pltpu.VMEM((frames, width), bf16)],
        ),
        compiler_params=pltpu.CompilerParams(vmem_limit_bytes=48 << 20),
        cost_estimate=pl.CostEstimate(
            flops=8 * frames * width * width, bytes_accessed=30 * frames * width, transcendentals=0
        ),
        name="tail_block",
    )(lengths, ids, acc, hidden, after, mods, joinedT, w_skip)


def sum_exchange(value, axis, bit):
    ways = lax.axis_size(axis)
    return lax.ppermute(value, axis, [(i, i ^ bit) for i in range(ways)])


def add_pair(left, right):
    return (left.astype(jnp.float32) + right.astype(jnp.float32)).astype(jnp.bfloat16)


def pick(value, bit, axis=0):
    return lax.dynamic_index_in_dim(value, bit, axis, keepdims=False)


def axis_bits(ways):
    return [1 << i for i in range(ways.bit_length() - 1)]


def reduce_blocks(keep, send):
    seq_ways, batch_ways = lax.axis_size("seq"), lax.axis_size("batch")
    seq_rank, batch_rank = lax.axis_index("seq"), lax.axis_index("batch")
    side = 1 << ((batch_ways.bit_length() - 1) // 2)
    x_bit, y_bit = 1, side
    x = lax.rem(batch_rank, 2)
    y = lax.rem(batch_rank // side, 2)
    _, z_ways, rows, width = keep.shape
    total = add_pair(keep, sum_exchange(send, "seq", 1)).reshape(2, 2, 2, z_ways, rows, width)
    first = []
    for block, mine, bit in ((total[0], x, x_bit), (total[1], y, y_bit)):
        got = sum_exchange(pick(block, 1 - mine), "batch", bit)
        first.append(add_pair(pick(block, mine), got))
    second = []
    for block, mine, bit in ((first[0], y, y_bit), (first[1], x, x_bit)):
        got = sum_exchange(pick(block, 1 - mine), "batch", bit)
        second.append(add_pair(pick(block, mine), got))
    block = jnp.stack(second)
    for bit in axis_bits(batch_ways):
        if bit not in (x_bit, y_bit):
            block = add_pair(block, sum_exchange(block, "batch", bit))
    z = seq_rank // 2
    for i, bit in enumerate(axis_bits(z_ways)):
        mine = lax.rem(z // bit, 2)
        block = block.reshape(2, block.shape[1] // 2, 2, rows, width)
        got = sum_exchange(pick(block, 1 - mine, 2), "seq", 2 * bit)
        block = add_pair(pick(block, mine, 2), got)
    block = block.reshape(2, rows, width)
    got_x = sum_exchange(block, "batch", x_bit)
    got_y = sum_exchange(block, "batch", y_bit)
    got_xy = sum_exchange(block, "batch", x_bit | y_bit)
    table = jnp.stack([jnp.stack([block, got_y]), jnp.stack([got_x, got_xy])])
    table = jnp.where(x == 1, table[::-1], table)
    table = jnp.where(y == 1, table[:, ::-1], table)
    return jnp.concatenate(
        [table[:, :, 0].reshape(4, rows, width), jnp.swapaxes(table[:, :, 1], 0, 1).reshape(4, rows, width)]
    ).astype(jnp.float32)


def gather_groups(value):
    return [value] + [sum_exchange(value, "batch", i) for i in range(1, lax.axis_size("batch"))]


def sum_seq(value):
    for bit in axis_bits(lax.axis_size("seq")):
        value = value + sum_exchange(value, "seq", bit)
    return value


def shards(
    tokens_in,
    skip_in,
    condition,
    cotangent,
    time_embed,
    lengths,
    key_mask,
    drop_mask,
    loss_mask,
    w_skip,
    b_skip,
    w_ada,
    b_ada,
    w_qkv,
    b_qkv,
    w_out,
    b_out,
    w_up,
    b_up,
    w_down,
    b_down,
):
    f32, bf16 = jnp.float32, jnp.bfloat16
    seq_ways, batch_ways = lax.axis_size("seq"), lax.axis_size("batch")
    seq_rank = lax.axis_index("seq")
    frames, width = tokens_in.shape[1:]
    group_frames = frames * seq_ways
    heads_local = HEADS // seq_ways
    utts = lengths.shape[1]
    lengths_row, drop = lengths[0], drop_mask[0]
    ids = jnp.stack([lax.rem(seq_rank, 2), seq_rank]).astype(jnp.int32)
    ok = key_mask.reshape(seq_ways, 1, frames)
    exchange = functools.partial(lax.all_to_all, axis_name="seq", split_axis=0, concat_axis=0, tiled=True)

    time_act = jax.nn.silu(time_embed[0]).astype(bf16)
    time_rows = jnp.pad(time_act, ((0, 16 - utts), (0, 0)))

    def modulation(first, last):
        return jnp.dot(time_rows, w_ada[:, first:last], preferred_element_type=f32) + b_ada[
            first:last
        ].astype(f32)

    mods_a = modulation(0, 2 * width)
    hidden, joinedT, naT, na = head_block(
        lengths_row, ids, drop, tokens_in[0], skip_in[0], condition[0], mods_a, w_skip, b_skip[None]
    )
    received = []
    for c in range(heads_local):
        packed = qkv_block(lengths_row, ids, drop, na, w_qkv, b_qkv[None], c, seq_ways)
        received.append(exchange(packed))

    count = jnp.sum(loss_mask.astype(f32))
    count = sum_seq(jnp.full((8, 128), count))
    for bit in axis_bits(batch_ways):
        count = count + sum_exchange(count, "batch", bit)
    scale = (group_frames * batch_ways) / count[0, :1]
    mods_rest = modulation(2 * width, 6 * width)
    time_all = jnp.concatenate(gather_groups(time_act))

    head_out, log_totals, returned = [], [], []
    for c in range(heads_local):
        out, log_total = attend(lengths_row, received[c], ok)
        head_out.append(out)
        log_totals.append(log_total)
        returned.append(exchange(out))
    mid = mid_block(
        lengths_row,
        ids,
        scale,
        returned,
        hidden,
        mods_rest,
        cotangent[0],
        loss_mask,
        w_out,
        b_out[None],
        w_up,
        b_up[None],
        w_down,
        b_down[None],
        PARTS,
    )
    output, after_grad, tables, b_up_grad = mid[:4]
    grad_att = mid[4 : 4 + heads_local]
    keep_f, send_f = mid[4 + heads_local :]
    grad_heads = [exchange(g) for g in grad_att]
    feed = reduce_blocks(keep_f, send_f)
    early = jnp.concatenate([tables[:utts, : 4 * width].reshape(-1), b_up_grad[0], tables[16, 4 * width :]])
    early = early.reshape(-1, 2 * width)
    early = gather_groups(sum_seq(early))

    acc, part_biases, part_blocks = None, [], []
    grad_local = []
    for c in range(heads_local):
        grad = attend_back(lengths_row, received[c], ok, head_out[c], grad_heads[c], log_totals[c])
        grad_local.append(exchange(grad))
    for c in range(heads_local):
        acc, bias, keep, send = back_block(
            lengths_row, ids, drop, grad_local[c], naT, w_qkv, acc, c, PARTS
        )
        part_biases.append(bias[:, 0])
        part_blocks.append(reduce_blocks(keep, send))
    late_tables, grad_tokens, grad_skip, keep, send = tail_block(
        lengths_row, ids, acc, hidden, after_grad, mods_a, joinedT, w_skip, seq_ways, PARTS
    )
    skip_blocks = reduce_blocks(keep, send)
    late = jnp.concatenate(
        [
            late_tables[:utts, : 2 * width].reshape(-1),
            jnp.stack(part_biases, axis=1).reshape(-1),
            late_tables[16, 2 * width :],
        ]
    ).reshape(-1, 2 * width)
    late = gather_groups(sum_seq(late))

    ada_rows = width // seq_ways
    own_time = lax.dynamic_slice_in_dim(time_all, seq_rank * ada_rows, ada_rows, axis=1).astype(f32)

    def own_slice(vector):
        size = vector.shape[0] // seq_ways
        return lax.dynamic_slice_in_dim(vector, seq_rank * size, size)

    def ada_part(groups, tables_count):
        rows = jnp.concatenate(
            [g.reshape(-1)[: utts * tables_count * width].reshape(utts, -1) for g in groups]
        )
        weight = lax.dot_general(
            own_time, rows, (((0,), (0,)), ((), ())), precision=lax.Precision.HIGHEST
        )
        return weight, jnp.sum(rows, axis=0)

    early_weight, early_bias = ada_part(early, 4)
    late_weight, late_bias = ada_part(late, 2)
    grad_w_ada = jnp.concatenate([late_weight, early_weight], axis=1)
    grad_b_ada = own_slice(jnp.concatenate([late_bias, early_bias]))
    early_vec = sum(g.reshape(-1)[utts * 4 * width :] for g in early)
    late_vec = sum(g.reshape(-1)[utts * 2 * width :] for g in late)
    ff = w_up.shape[1]
    grad_b_up = own_slice(early_vec[:ff])
    grad_b_out = own_slice(early_vec[ff : ff + width])
    grad_b_down = own_slice(early_vec[ff + width :])
    grad_b_qkv = own_slice(late_vec[: 3 * width])
    grad_b_skip = own_slice(late_vec[3 * width :])

    own = width // seq_ways
    chunks = ff // width
    up_part = chunks * own // PARTS
    down_part = ff // seq_ways // PARTS
    halves = own // up_part
    grad_w_up = (
        feed[:, :up_part]
        .reshape(chunks, halves, up_part, width)
        .transpose(1, 2, 0, 3)
        .reshape(own, ff)
    )
    grad_w_down = feed[:, up_part : up_part + down_part].reshape(ff // seq_ways, width)
    grad_w_out = feed[:, up_part + down_part :].reshape(own, width)
    cols = seq_ways * HEAD_DIM
    grad_w_qkv = jnp.stack([b.reshape(own, 3, cols) for b in part_blocks], axis=2).reshape(own, 3 * width)
    grad_w_skip = skip_blocks.reshape(2 * own, width)
    return (
        output[None],
        grad_tokens[None],
        grad_skip[None],
        grad_w_skip,
        grad_b_skip,
        grad_w_ada,
        grad_b_ada,
        grad_w_qkv,
        grad_b_qkv,
        grad_w_out,
        grad_b_out,
        grad_w_up,
        grad_b_up,
        grad_w_down,
        grad_b_down,
    )


def solution(mesh):
    in_specs = (
        P("batch", "seq", None),
        P("batch", "seq", None),
        P("batch", "seq", None),
        P("batch", "seq", None),
        P("batch", None, None),
        P("batch", None),
        P("batch", None),
        P("batch", None),
        P("batch", "seq"),
        P(),
        P(),
        P(),
        P(),
        P(),
        P(),
        P(),
        P(),
        P(),
        P(),
        P(),
        P(),
    )
    out_specs = (
        P("batch", "seq", None),
        P("batch", "seq", None),
        P("batch", "seq", None),
        P("seq", None),
        P("seq"),
        P("seq", None),
        P("seq"),
        P("seq", None),
        P("seq"),
        P("seq", None),
        P("seq"),
        P("seq", None),
        P("seq"),
        P("seq", None),
        P("seq"),
    )
    return jax.shard_map(shards, mesh=mesh, in_specs=in_specs, out_specs=out_specs, check_vma=False)
```

```python
import functools

import jax
import jax.numpy as jnp
from jax import lax
from jax.experimental import pallas as pl
from jax.experimental.pallas import tpu as pltpu
from jax.sharding import PartitionSpec as P

HEADS = 16
HEAD_DIM = 64
PARTS = 8
BIG = 1e30
DH = 64
BQ = 512
BK = 512


def onehot_rows(lengths_ref, utts, rows, base, width):
    row = lax.broadcasted_iota(jnp.int32, (rows, width), 0)
    col = base + lax.broadcasted_iota(jnp.int32, (rows, width), 1)
    start = jnp.int32(0)
    hot = jnp.zeros((rows, width), jnp.float32)
    for u in range(utts):
        end = start + lengths_ref[u]
        hot = jnp.where((row == u) & (col >= start) & (col < end), 1.0, hot)
        start = end
    return hot


def key_range(lengths_ref, utts, first, last):
    start = jnp.int32(0)
    low, high = jnp.int32(0), jnp.int32(0)
    for u in range(utts):
        end = start + lengths_ref[u]
        low = jnp.where((start <= first) & (first < end), start, low)
        high = jnp.where((start <= last) & (last < end), end, high)
        start = end
    return low // BK, (high + BK - 1) // BK


def aug_rows(utts):
    return -(-utts // 16) * 16


def split3(row):
    a = row.astype(jnp.bfloat16)
    rest = row - a.astype(jnp.float32)
    b = rest.astype(jnp.bfloat16)
    c = (rest - b.astype(jnp.float32)).astype(jnp.bfloat16)
    return a, b, c


def pad_rows(parts, total):
    have = sum(p.shape[0] for p in parts)
    if have < total:
        parts = parts + [jnp.zeros((total - have, parts[0].shape[1]), parts[0].dtype)]
    return jnp.concatenate(parts, axis=0)


def rows16(rows, width):
    idx = lax.broadcasted_iota(jnp.int32, (16, width), 0)
    out = jnp.zeros((16, width), jnp.float32)
    for i, r in enumerate(rows):
        out = jnp.where(idx == i, r, out)
    return out.astype(jnp.bfloat16)


def fwd_kernel(utts, lengths_ref, qkv_ref, ok_ref, out_ref, lse_ref, kaug, vaug):
    sources, _, frames = qkv_ref.shape
    per = frames // BQ
    pad_u = aug_rows(utts)
    step = pl.program_id(0)

    @pl.when(step == 0)
    def _():
        def build(s, c):
            hot = onehot_rows(lengths_ref, utts, pad_u, s * frames, frames)
            ok = ok_ref[s].astype(jnp.float32)
            block = qkv_ref[s]
            one = jnp.ones((1, frames), jnp.float32)
            kT = pad_rows(
                [block[DH : 2 * DH], (1.0 - hot).astype(jnp.bfloat16), rows16([1.0 - ok], frames)], 128
            )
            kaug[pl.ds(pl.multiple_of(s * frames, frames), frames), :] = kT.T
            vT = jnp.concatenate([block[2 * DH :], rows16([one], frames)], axis=0)
            for t in range(frames // BK):
                vaug[s * (frames // BK) + t] = vT[:, t * BK : (t + 1) * BK]
            return c

        lax.fori_loop(0, sources, build, 0)

    block = qkv_ref[step]
    hot_q = onehot_rows(lengths_ref, utts, pad_u, step * frames, frames)
    qT = (block[:DH].astype(jnp.float32) * 0.125)
    one = jnp.ones((1, frames), jnp.float32)
    qaug = pad_rows(
        [qT.astype(jnp.bfloat16), (hot_q * -BIG).astype(jnp.bfloat16), rows16([one * -BIG], frames)], 128
    )
    kT = block[DH : 2 * DH].astype(jnp.float32)
    vT = block[2 * DH :].astype(jnp.float32)
    ok = ok_ref[step] > 0
    s_self = jnp.sum(qT * kT, axis=0, keepdims=True)
    m0 = jnp.where(ok, -3e38, s_self)
    acc0 = jnp.concatenate([jnp.where(ok, 0.0, vT), jnp.where(ok, 0.0, jnp.ones((16, frames), jnp.float32))], axis=0)
    for t in range(per):
        cols = slice(t * BQ, (t + 1) * BQ)
        low, high = key_range(lengths_ref, utts, step * frames + t * BQ, step * frames + (t + 1) * BQ - 1)
        q_b = qaug[:, cols]

        def body(j, carry):
            m, acc = carry
            s = jnp.dot(kaug[pl.ds(pl.multiple_of(j * BK, BK), BK), :], q_b, preferred_element_type=jnp.float32)
            m_new = jnp.maximum(m, jnp.max(s, axis=0, keepdims=True))
            p = jnp.exp(s - m_new).astype(jnp.bfloat16)
            alpha = jnp.exp(m - m_new)
            acc = acc * alpha + jnp.dot(vaug[j], p, preferred_element_type=jnp.float32)
            return m_new, acc

        m, acc = lax.fori_loop(low, high, body, (m0[:, cols], acc0[:, cols]))
        total = acc[DH : DH + 1]
        out_ref[0, :, cols] = (acc[:DH] / total).astype(jnp.bfloat16)
        lse_ref[0, :, cols] = m + jnp.log(total)


def attend(lengths, qkv, ok):
    sources, _, frames = qkv.shape
    total = sources * frames
    utts = lengths.shape[0]
    whole = lambda shape: pl.BlockSpec(shape, lambda i, *_: (0,) * len(shape))
    return pl.pallas_call(
        functools.partial(fwd_kernel, utts),
        out_shape=(
            jax.ShapeDtypeStruct((sources, DH, frames), jnp.bfloat16),
            jax.ShapeDtypeStruct((sources, 1, frames), jnp.float32),
        ),
        grid_spec=pltpu.PrefetchScalarGridSpec(
            num_scalar_prefetch=1,
            grid=(sources,),
            in_specs=[whole(qkv.shape), whole(ok.shape)],
            out_specs=(
                pl.BlockSpec((1, DH, frames), lambda i, *_: (i, 0, 0)),
                pl.BlockSpec((1, 1, frames), lambda i, *_: (i, 0, 0)),
            ),
            scratch_shapes=[
                pltpu.VMEM((total, 128), jnp.bfloat16),
                pltpu.VMEM((total // BK, DH + 16, BK), jnp.bfloat16),
            ],
        ),
        cost_estimate=pl.CostEstimate(
            flops=total * total * 1200, bytes_accessed=8 * total * DH, transcendentals=0
        ),
        name="attend",
    )(lengths, qkv, ok)


def bwd_kernel(utts, lengths_ref, qkv_ref, ok_ref, o_ref, do_ref, lse_ref, out_ref, kaug, vnat, kT_s, dk, dv):
    sources, _, frames = qkv_ref.shape
    per = frames // BK
    pad_u = aug_rows(utts)
    step = pl.program_id(0)
    f32 = jnp.float32

    @pl.when(step == 0)
    def _():
        def build(s, c):
            hot = onehot_rows(lengths_ref, utts, pad_u, s * frames, frames)
            ok = ok_ref[s]
            block = qkv_ref[s]
            one = jnp.ones((1, frames), f32)
            kT = block[DH : 2 * DH]
            vT = block[2 * DH :]
            kA = pad_rows(
                [kT, (1.0 - hot).astype(jnp.bfloat16), rows16([1.0 - ok.astype(f32), one, one, one], frames)], 128
            )
            rows = pl.ds(pl.multiple_of(s * frames, frames), frames)
            kaug[rows, :] = kA.T
            vnat[rows, :] = pad_rows([vT, rows16([one, one, one], frames)], 128).T
            qT = block[:DH].astype(f32) * 0.125
            do = do_ref[s].astype(f32)
            s_self = jnp.sum(qT * kT.astype(f32), axis=0, keepdims=True)
            delta = jnp.sum(do * o_ref[s].astype(f32), axis=0, keepdims=True)
            p_self = jnp.where(ok > 0, 0.0, jnp.exp(s_self - lse_ref[s]))
            ds_self = p_self * (jnp.sum(do * vT.astype(f32), axis=0, keepdims=True) - delta)
            dk0 = ds_self * qT
            dv0 = p_self * do
            for t in range(per):
                cols = slice(t * BK, (t + 1) * BK)
                kT_s[s * per + t] = kT[:, cols]
                dk[s * per + t] = dk0[:, cols]
                dv[s * per + t] = dv0[:, cols]
            return c

        lax.fori_loop(0, sources, build, 0)

    block = qkv_ref[step]
    one = jnp.ones((1, frames), f32)
    hot_q = onehot_rows(lengths_ref, utts, pad_u, step * frames, frames)
    qT = block[:DH].astype(f32) * 0.125
    qTb = qT.astype(jnp.bfloat16)
    kT = block[DH : 2 * DH].astype(f32)
    vT = block[2 * DH :].astype(f32)
    ok = ok_ref[step]
    dob = do_ref[step]
    do = dob.astype(f32)
    lse = lse_ref[step]
    delta = jnp.sum(do * o_ref[step].astype(f32), axis=0, keepdims=True)
    l3 = [-r.astype(f32) for r in split3(lse)]
    d3 = [-r.astype(f32) for r in split3(delta)]
    qaug = pad_rows([qTb, (hot_q * -BIG).astype(jnp.bfloat16), rows16([one * -BIG] + l3, frames)], 128)
    doaug = pad_rows([dob, rows16(d3, frames)], 128)
    s_self = jnp.sum(qT * kT, axis=0, keepdims=True)
    p_self = jnp.where(ok > 0, 0.0, jnp.exp(s_self - lse))
    ds_self = p_self * (jnp.sum(do * vT, axis=0, keepdims=True) - delta)
    dq0 = ds_self * kT
    nt = (((1,), (1,)), ((), ()))
    for t in range(frames // BQ):
        cols = slice(t * BQ, (t + 1) * BQ)
        low, high = key_range(lengths_ref, utts, step * frames + t * BQ, step * frames + (t + 1) * BQ - 1)
        q_a = qaug[:, cols]
        q_b = qTb[:, cols]
        do_a = doaug[:, cols]
        do_b = dob[:, cols]

        def body(j, dq):
            rows = pl.ds(pl.multiple_of(j * BK, BK), BK)
            s = jnp.dot(kaug[rows, :], q_a, preferred_element_type=f32)
            dp = jnp.dot(vnat[rows, :], do_a, preferred_element_type=f32)
            p = jnp.exp(s)
            ds = (p * dp).astype(jnp.bfloat16)
            dv[j] += lax.dot_general(do_b, p.astype(jnp.bfloat16), nt, preferred_element_type=f32)
            dk[j] += lax.dot_general(q_b, ds, nt, preferred_element_type=f32)
            return dq + jnp.dot(kT_s[j], ds, preferred_element_type=f32)

        dq = lax.fori_loop(low, high, body, dq0[:, cols])
        out_ref[step, :DH, cols] = (dq * 0.125).astype(jnp.bfloat16)

    @pl.when(step == sources - 1)
    def _():
        def finish(s, c):
            for t in range(per):
                cols = slice(t * BK, (t + 1) * BK)
                out_ref[s, DH : 2 * DH, cols] = dk[s * per + t].astype(jnp.bfloat16)
                out_ref[s, 2 * DH :, cols] = dv[s * per + t].astype(jnp.bfloat16)
            return c

        lax.fori_loop(0, sources, finish, 0)


def attend_back(lengths, qkv, ok, out, grad, lse):
    sources, _, frames = qkv.shape
    total = sources * frames
    utts = lengths.shape[0]
    whole = lambda shape: pl.BlockSpec(shape, lambda i, *_: (0,) * len(shape))
    return pl.pallas_call(
        functools.partial(bwd_kernel, utts),
        out_shape=jax.ShapeDtypeStruct(qkv.shape, jnp.bfloat16),
        grid_spec=pltpu.PrefetchScalarGridSpec(
            num_scalar_prefetch=1,
            grid=(sources,),
            in_specs=[whole(a.shape) for a in (qkv, ok, out, grad, lse)],
            out_specs=whole(qkv.shape),
            scratch_shapes=[
                pltpu.VMEM((total, 128), jnp.bfloat16),
                pltpu.VMEM((total, 128), jnp.bfloat16),
                pltpu.VMEM((total // BK, DH, BK), jnp.bfloat16),
                pltpu.VMEM((total // BK, DH, BK), jnp.float32),
                pltpu.VMEM((total // BK, DH, BK), jnp.float32),
            ],
        ),
        cost_estimate=pl.CostEstimate(
            flops=total * total * 1500, bytes_accessed=16 * total * DH, transcendentals=0
        ),
        name="attend_back",
    )(lengths, qkv, ok, out, grad, lse)


FF_TILE = 512
EPS = 1e-06


def dot(left, right):
    return jnp.dot(left, right, preferred_element_type=jnp.float32)


def dot_nt(left, right):
    return lax.dot_general(left, right, (((1,), (1,)), ((), ())), preferred_element_type=jnp.float32)


def norm_stats(x):
    mean = jnp.mean(x, axis=1, keepdims=True)
    centred = x - mean
    rstd = lax.rsqrt(jnp.mean(centred * centred, axis=1, keepdims=True) + EPS)
    return centred * rstd, rstd


def norm_back(grad, normed, rstd):
    first = jnp.mean(grad, axis=1, keepdims=True)
    second = jnp.mean(grad * normed, axis=1, keepdims=True)
    return rstd * (grad - first - normed * second)


def mods_operand(mods_ref):
    rows = mods_ref[...]
    return pad_rows(list(split3(rows)), 128)


def sum_rows(hot, utts_pad, frames):
    idx = lax.broadcasted_iota(jnp.int32, (16, frames), 0)
    ones = jnp.where(idx == 0, 1.0, 0.0).astype(jnp.bfloat16)
    return jnp.concatenate([hot.astype(jnp.bfloat16), ones], axis=0)


def mid_kernel(
    dims,
    lengths_ref,
    ids_ref,
    *refs,
):
    seq_ways, heads_local, utts = dims
    att_refs = refs[:heads_local]
    (
        hidden_ref,
        mods_ref,
        cot_ref,
        loss_ref,
        w_out_ref,
        b_out_ref,
        w_up_ref,
        b_up_ref,
        w_down_ref,
        b_down_ref,
    ) = refs[heads_local : heads_local + 10]
    outs = refs[heads_local + 10 :]
    output_ref, after_grad_ref, tables_ref, b_up_grad_ref = outs[:4]
    gatt_refs = outs[4 : 4 + heads_local]
    keep_ref, send_ref = outs[4 + heads_local : 6 + heads_local]
    (
        attT,
        attn_proj,
        after,
        nf,
        nfT,
        gff,
        ff_acc,
        gnf_acc,
        sums,
        cols,
        madd,
        grads,
        sems,
    ) = outs[6 + heads_local :]
    f32, bf16 = jnp.float32, jnp.bfloat16
    step = pl.program_id(0)
    steps = pl.num_programs(0)
    core = ids_ref[0]
    rank = ids_ref[1]
    frames, width = hidden_ref.shape
    up_rows = width // seq_ways
    down_rows = FF_TILE
    z_ways = seq_ways // 2
    parts = grads.shape[1]
    ff_total = b_up_grad_ref.shape[1]
    up_part = ff_total // width * up_rows // parts
    down_block = ff_total // seq_ways
    down_part = down_block // parts
    out_part = up_rows // parts

    def mod(index):
        return dot(cols[...], madd[:, index * width : (index + 1) * width])

    def grad_out():
        loss = cols[:, 48:49].astype(f32)
        return cot_ref[...].astype(f32) * loss

    @pl.when(step == 0)
    def _():
        hot = onehot_rows(lengths_ref, utts, 16, rank * frames, frames)
        hotb = hot.astype(bf16)
        idx = lax.broadcasted_iota(jnp.int32, (16, frames), 0)
        loss = jnp.where(idx == 0, loss_ref[...].astype(f32), 0.0).astype(bf16)
        cols[...] = pad_rows([hotb, hotb, hotb, loss], 128).T
        sums[...] = sum_rows(hot, 16, frames)
        madd[...] = mods_operand(mods_ref)
        for c in range(heads_local):
            for s in range(seq_ways):
                attT[(c * seq_ways + s) * DH : (c * seq_ways + s + 1) * DH, :] = att_refs[c][s]
        proj = dot(attT[...].T, w_out_ref[...]) + b_out_ref[...].astype(f32)
        attn_proj[...] = proj
        mixed = hidden_ref[...] + mod(0) * proj
        after[...] = mixed
        normed, _ = norm_stats(mixed)
        value = (normed * (1.0 + mod(2)) + mod(1)).astype(bf16)
        nf[...] = value
        nfT[...] = value.T
        gff[...] = (grad_out() * mod(3)).astype(bf16)

    up = dot(nf[...], w_up_ref[...]) + b_up_ref[...].astype(f32)
    inner = 0.7978845608028654 * (up + 0.044715 * (up * up * up))
    tanh = jnp.tanh(inner)
    cdf = 0.5 * (1.0 + tanh)
    act = (up * cdf).astype(bf16)
    slope = cdf + 0.5 * up * (1.0 - tanh * tanh) * (
        0.7978845608028654 * (1.0 + (3 * 0.044715) * (up * up))
    )
    ff_part = dot(act, w_down_ref[...])
    gup = (dot_nt(gff[...], w_down_ref[...]) * slope).astype(bf16)
    gnf_part = dot_nt(gup, w_up_ref[...])

    @pl.when(step == 0)
    def _():
        ff_acc[...] = ff_part
        gnf_acc[...] = gnf_part

    @pl.when(step > 0)
    def _():
        ff_acc[...] += ff_part
        gnf_acc[...] += gnf_part

    b_up_grad_ref[:, pl.ds(pl.multiple_of(step * FF_TILE, FF_TILE), FF_TILE)] = dot(
        sums[16:32, :], gup
    )[:8]
    halves = width // FF_TILE
    chunk = step // halves
    half = step % halves
    col = pl.ds(pl.multiple_of(half * FF_TILE, FF_TILE), FF_TILE)
    per_chunk = up_rows // up_part
    grad_w_up = dot(nfT[...], gup).astype(bf16)
    for s in range(seq_ways):
        side = jnp.where(core == s % 2, 0, 1)
        for h in range(per_chunk):
            lo = s * up_rows + h * up_part
            grads[side, chunk * per_chunk + h, s // 2, 0:up_part, col] = grad_w_up[lo : lo + up_part]
    grad_w_down = dot(act.T, gff[...]).astype(bf16)
    blocks = FF_TILE // down_block
    copies = []
    for b in range(blocks):
        s = step * blocks + b
        side = jnp.where(core == s % 2, 0, 1)
        for k in range(parts):
            lo = b * down_block + k * down_part
            grads[side, k, s // 2, up_part : up_part + down_part, :] = grad_w_down[lo : lo + down_part]

    def up_copy(side, j):
        target = (keep_ref, send_ref)[side]
        where = (
            pl.ds((j // halves) * per_chunk, per_chunk),
            slice(None),
            pl.ds(0, up_part),
            pl.ds(pl.multiple_of((j % halves) * FF_TILE, FF_TILE), FF_TILE),
        )
        return pltpu.make_async_copy(grads.at[side].at[where], target.at[where], sems.at[side, j])

    def down_copy(side, z, index):
        target = (keep_ref, send_ref)[side]
        where = (slice(None), pl.ds(z, 1), pl.ds(up_part, down_part), slice(None))
        return pltpu.make_async_copy(grads.at[side].at[where], target.at[where], sems.at[side, index])

    def out_copy(side):
        target = (keep_ref, send_ref)[side]
        where = (slice(None), slice(None), pl.ds(up_part + down_part, out_part), slice(None))
        return pltpu.make_async_copy(
            grads.at[side].at[where], target.at[where], sems.at[side, ff_total // FF_TILE + z_ways]
        )

    base = ff_total // FF_TILE
    for side in range(2):
        up_copy(side, step).start()
    for b in range(blocks):
        s = step * blocks + b
        for side in range(2):

            @pl.when(lax.rem(s + core, 2) == side)
            def _():
                down_copy(side, s // 2, base + s // 2).start()

    @pl.when(step == steps - 1)
    def _():
        ff_out = ff_acc[...] + b_down_ref[...].astype(f32)
        mixed = after[...]
        go = grad_out()
        output_ref[...] = (mixed + mod(3) * ff_out).astype(bf16)
        rows = sums[...]
        tables_ref[:, 3 * width : 4 * width] = dot(rows, (go * ff_out).astype(bf16))
        normed, rstd = norm_stats(mixed)
        gnf = gnf_acc[...]
        tables_ref[:, width : 2 * width] = dot(rows, gnf.astype(bf16))
        tables_ref[:, 2 * width : 3 * width] = dot(rows, (gnf * normed).astype(bf16))
        g_after = go + norm_back(gnf * (1.0 + mod(2)), normed, rstd)
        after_grad_ref[...] = g_after
        tables_ref[:, 0:width] = dot(rows, (g_after * attn_proj[...]).astype(bf16))
        gattn = (g_after * mod(0)).astype(bf16)
        tables_ref[:, 4 * width : 5 * width] = dot(rows, gattn)
        tables_ref[:, 5 * width : 6 * width] = dot(rows, gff[...])
        gattT = dot_nt(w_out_ref[...], gattn).astype(bf16)
        for c in range(heads_local):
            for s in range(seq_ways):
                lo = (c * seq_ways + s) * DH
                gatt_refs[c][s] = gattT[lo : lo + DH]
        grad_w_out = dot(attT[...], gattn).astype(bf16)
        for s in range(seq_ways):
            side = jnp.where(core == s % 2, 0, 1)
            for k in range(parts):
                lo = s * up_rows + k * out_part
                grads[side, k, s // 2, up_part + down_part : up_part + down_part + out_part, :] = grad_w_out[
                    lo : lo + out_part
                ]
        for side in range(2):
            out_copy(side).start()
        for side in range(2):
            for j in range(ff_total // FF_TILE):
                up_copy(side, j).wait()
            for z in range(z_ways):
                down_copy(side, z, base + z).wait()
            out_copy(side).wait()


def mid_block(
    lengths, ids, att, hidden, mods, cot, loss, w_out, b_out, w_up, b_up, w_down, b_down, parts
):
    frames, width = hidden.shape
    heads_local = len(att)
    seq_ways = att[0].shape[0]
    ff = w_up.shape[1]
    up_rows = width // seq_ways
    rows = (ff // width * up_rows + ff // seq_ways + up_rows) // parts
    utts = lengths.shape[0]
    f32, bf16 = jnp.float32, jnp.bfloat16
    steps = ff // FF_TILE

    def whole(shape):
        return pl.BlockSpec(shape, lambda j, *_: (0,) * len(shape), pipeline_mode=pl.Buffered(1))

    hbm = pl.BlockSpec(memory_space=pl.ANY)
    gshape = (parts, seq_ways // 2, rows, width)
    out_shape = [
        jax.ShapeDtypeStruct((frames, width), bf16),
        jax.ShapeDtypeStruct((frames, width), f32),
        jax.ShapeDtypeStruct((32, 6 * width), f32),
        jax.ShapeDtypeStruct((8, ff), f32),
    ]
    out_shape += [jax.ShapeDtypeStruct(a.shape, bf16) for a in att]
    out_specs = [whole(o.shape) for o in out_shape] + [hbm, hbm]
    out_shape += [jax.ShapeDtypeStruct(gshape, bf16)] * 2
    ins = list(att) + [hidden, mods, cot, loss, w_out, b_out]
    return pl.pallas_call(
        functools.partial(mid_kernel, (seq_ways, heads_local, utts)),
        out_shape=out_shape,
        grid_spec=pltpu.PrefetchScalarGridSpec(
            num_scalar_prefetch=2,
            grid=(steps,),
            in_specs=[whole(a.shape) for a in ins]
            + [
                pl.BlockSpec((width, FF_TILE), lambda j, *_: (0, j)),
                pl.BlockSpec((1, FF_TILE), lambda j, *_: (0, j)),
                pl.BlockSpec((FF_TILE, width), lambda j, *_: (j, 0)),
                whole((1, width)),
            ],
            out_specs=out_specs,
            scratch_shapes=[
                pltpu.VMEM((width, frames), bf16),
                pltpu.VMEM((frames, width), f32),
                pltpu.VMEM((frames, width), f32),
                pltpu.VMEM((frames, width), bf16),
                pltpu.VMEM((width, frames), bf16),
                pltpu.VMEM((frames, width), bf16),
                pltpu.VMEM((frames, width), f32),
                pltpu.VMEM((frames, width), f32),
                pltpu.VMEM((32, frames), bf16),
                pltpu.VMEM((frames, 128), bf16),
                pltpu.VMEM((128, 4 * width), bf16),
                pltpu.VMEM((2,) + gshape, bf16),
                pltpu.SemaphoreType.DMA((2, steps + seq_ways // 2 + 1)),
            ],
        ),
        compiler_params=pltpu.CompilerParams(vmem_limit_bytes=63 << 20),
        cost_estimate=pl.CostEstimate(
            flops=2 * frames * width * (6 * ff + 3 * width),
            bytes_accessed=4 * width * ff * 2 + 16 * frames * width,
            transcendentals=frames * ff,
        ),
        name="mid_block",
    )(lengths, ids, *ins, w_up, b_up, w_down, b_down)


def segment_rows(lengths_ref, drop_ref, utts, base, width):
    col = base + lax.broadcasted_iota(jnp.int32, (1, width), 1)
    start = jnp.int32(0)
    kept = jnp.zeros((1, width), jnp.float32)
    place = jnp.zeros((1, width), jnp.int32)
    for u in range(utts):
        end = start + lengths_ref[u]
        inside = (col >= start) & (col < end)
        kept = jnp.where(inside, (1 - drop_ref[u]).astype(jnp.float32), kept)
        place = jnp.where(inside, col - start, place)
        start = end
    return kept, place.astype(jnp.float32)


def rotary_rows(place, half):
    index = lax.broadcasted_iota(jnp.int32, (half, 1), 0).astype(jnp.float32)
    inverse = jnp.exp(index * (-9.210340371976184 / half))
    angles = inverse * place
    return jnp.cos(angles), jnp.sin(angles)


def frame_columns(hot, extra):
    hotb = hot.astype(jnp.bfloat16)
    idx = lax.broadcasted_iota(jnp.int32, hot.shape, 0)
    last = jnp.where(idx == 0, extra, 0.0).astype(jnp.bfloat16)
    return pad_rows([hotb, hotb, hotb, last], 128).T


def head_kernel(
    utts,
    lengths_ref,
    ids_ref,
    drop_ref,
    tokens_ref,
    skip_ref,
    cond_ref,
    mods_ref,
    w_skip_ref,
    b_skip_ref,
    hidden_ref,
    joinedT_ref,
    naT_ref,
    na_ref,
    cols,
):
    f32, bf16 = jnp.float32, jnp.bfloat16
    step = pl.program_id(0)
    frames, width = tokens_ref.shape
    rank = ids_ref[1]

    @pl.when(step == 0)
    def _():
        hot = onehot_rows(lengths_ref, utts, 16, rank * frames, frames)
        kept, _ = segment_rows(lengths_ref, drop_ref, utts, rank * frames, frames)
        cols[...] = frame_columns(hot, kept)
        keep = cols[:, 48:49].astype(f32)
        mixed = (tokens_ref[...].astype(f32) + keep * cond_ref[...].astype(f32)).astype(bf16)
        joinedT_ref[0:width, :] = mixed.T
        hidden_ref[...] = dot(mixed, w_skip_ref[...]) + b_skip_ref[...].astype(f32)

    @pl.when(step == 1)
    def _():
        skip = skip_ref[...]
        joinedT_ref[width : 2 * width, :] = skip.T
        hidden = hidden_ref[...] + dot(skip, w_skip_ref[...])
        hidden_ref[...] = hidden
        madd = mods_operand(mods_ref)
        shift = dot(cols[...], madd[:, :width])
        scale = dot(cols[...], madd[:, width:])
        normed, _ = norm_stats(hidden)
        value = (normed * (1.0 + scale) + shift).astype(bf16)
        na_ref[...] = value
        naT_ref[...] = value.T


def head_block(lengths, ids, drop, tokens, skip, cond, mods, w_skip, b_skip):
    frames, width = tokens.shape
    utts = lengths.shape[0]
    f32, bf16 = jnp.float32, jnp.bfloat16

    def whole(shape):
        return pl.BlockSpec(shape, lambda j, *_: (0,) * len(shape), pipeline_mode=pl.Buffered(1))

    out_shape = [
        jax.ShapeDtypeStruct((frames, width), f32),
        jax.ShapeDtypeStruct((2 * width, frames), bf16),
        jax.ShapeDtypeStruct((width, frames), bf16),
        jax.ShapeDtypeStruct((frames, width), bf16),
    ]
    return pl.pallas_call(
        functools.partial(head_kernel, utts),
        out_shape=out_shape,
        grid_spec=pltpu.PrefetchScalarGridSpec(
            num_scalar_prefetch=3,
            grid=(2,),
            in_specs=[whole(a.shape) for a in (tokens, skip, cond, mods)]
            + [pl.BlockSpec((width, width), lambda j, *_: (j, 0)), whole((1, width))],
            out_specs=[whole(o.shape) for o in out_shape],
            scratch_shapes=[pltpu.VMEM((frames, 128), bf16)],
        ),
        compiler_params=pltpu.CompilerParams(vmem_limit_bytes=48 << 20),
        cost_estimate=pl.CostEstimate(
            flops=4 * frames * width * width, bytes_accessed=20 * frames * width, transcendentals=0
        ),
        name="head_block",
    )(lengths, ids, drop, tokens, skip, cond, mods, w_skip, b_skip)


def turn_heads(tensor, cosine, sine):
    half = DH // 2
    first, second = tensor[:, :half], tensor[:, half:]
    return jnp.concatenate([first * cosine - second * sine, second * cosine + first * sine], axis=1)


def qkv_kernel(utts, seq_ways, lengths_ref, ids_ref, drop_ref, na_ref, w_ref, b_ref, out_ref, trig):
    f32, bf16 = jnp.float32, jnp.bfloat16
    part = pl.program_id(0)
    frames = na_ref.shape[0]

    @pl.when(part == 0)
    def _():
        _, place = segment_rows(lengths_ref, drop_ref, utts, ids_ref[1] * frames, frames)
        cosine, sine = rotary_rows(place, DH // 2)
        trig[0] = cosine
        trig[1] = sine

    raw = dot(na_ref[...], w_ref[...]) + b_ref[...].astype(f32)
    rawT = raw.T.reshape(seq_ways, DH, frames)
    turned = part < 2
    cosine = jnp.where(turned, trig[0], 1.0)[None]
    sine = jnp.where(turned, trig[1], 0.0)[None]
    out_ref[:, pl.ds(pl.multiple_of(part * DH, DH), DH), :] = turn_heads(rawT, cosine, sine).astype(bf16)


def qkv_block(lengths, ids, drop, na, w_qkv, b_qkv, chunk, seq_ways):
    frames, width = na.shape
    cols = seq_ways * DH
    chunks = width // cols
    utts = lengths.shape[0]

    def whole(shape):
        return pl.BlockSpec(shape, lambda j, *_: (0,) * len(shape), pipeline_mode=pl.Buffered(1))

    shape = (seq_ways, 3 * DH, frames)
    return pl.pallas_call(
        functools.partial(qkv_kernel, utts, seq_ways),
        out_shape=jax.ShapeDtypeStruct(shape, jnp.bfloat16),
        grid_spec=pltpu.PrefetchScalarGridSpec(
            num_scalar_prefetch=3,
            grid=(3,),
            in_specs=[
                whole(na.shape),
                pl.BlockSpec((width, cols), lambda j, *_: (0, j * chunks + chunk)),
                pl.BlockSpec((1, cols), lambda j, *_: (0, j * chunks + chunk)),
            ],
            out_specs=whole(shape),
            scratch_shapes=[pltpu.VMEM((2, DH // 2, frames), jnp.float32)],
        ),
        cost_estimate=pl.CostEstimate(
            flops=6 * frames * width * cols, bytes_accessed=10 * frames * width, transcendentals=0
        ),
        name="qkv_block",
    )(lengths, ids, drop, na, w_qkv, b_qkv)


def back_kernel(utts, seq_ways, first, lengths_ref, ids_ref, drop_ref, grad_ref, naT_ref, w_ref, *refs):
    if first:
        acc_in = None
        acc_ref, bias_ref, keep_ref, send_ref, trig = refs
    else:
        acc_in, acc_ref, bias_ref, keep_ref, send_ref, trig = refs
    f32, bf16 = jnp.float32, jnp.bfloat16
    part = pl.program_id(0)
    width, frames = naT_ref.shape
    core = ids_ref[0]
    parts = keep_ref.shape[0]
    own = width // seq_ways
    rows = own // parts

    @pl.when(part == 0)
    def _():
        _, place = segment_rows(lengths_ref, drop_ref, utts, ids_ref[1] * frames, frames)
        cosine, sine = rotary_rows(place, DH // 2)
        trig[0] = cosine
        trig[1] = sine

    turned = part < 2
    cosine = jnp.where(turned, trig[0], 1.0)[None]
    sine = jnp.where(turned, trig[1], 0.0)[None]
    raw = grad_ref[:, pl.ds(pl.multiple_of(part * DH, DH), DH), :].astype(f32)
    gpT = turn_heads(raw, cosine, -sine).astype(bf16).reshape(seq_ways * DH, frames)
    gna = dot(w_ref[...], gpT)

    @pl.when(part == 0)
    def _():
        acc_ref[...] = gna if first else acc_in[...] + gna

    @pl.when(part > 0)
    def _():
        acc_ref[...] += gna

    ones = jnp.ones((8, frames), bf16)
    bias_ref[0] = dot_nt(ones, gpT)
    grad_w = dot_nt(naT_ref[...], gpT).astype(bf16)
    for s in range(seq_ways):
        for k in range(parts):
            tile = grad_w[s * own + k * rows : s * own + (k + 1) * rows]

            @pl.when(core == s % 2)
            def _():
                keep_ref[k, s // 2] = tile

            @pl.when(core != s % 2)
            def _():
                send_ref[k, s // 2] = tile


def back_block(lengths, ids, drop, grad, naT, w_qkv, acc, chunk, parts):
    seq_ways, _, frames = grad.shape
    width = naT.shape[0]
    cols = seq_ways * DH
    chunks = width // cols
    utts = lengths.shape[0]
    f32, bf16 = jnp.float32, jnp.bfloat16
    rows = width // seq_ways // parts

    def whole(shape):
        return pl.BlockSpec(shape, lambda j, *_: (0,) * len(shape), pipeline_mode=pl.Buffered(1))

    gblock = (parts, seq_ways // 2, rows, cols)
    gspec = pl.BlockSpec(gblock, lambda j, *_: (0, 0, 0, j))
    gshape = jax.ShapeDtypeStruct((parts, seq_ways // 2, rows, 3 * cols), bf16)
    ins = [grad, naT, w_qkv] + ([] if acc is None else [acc])
    in_specs = [whole(grad.shape), whole(naT.shape)]
    in_specs += [pl.BlockSpec((width, cols), lambda j, *_: (0, j * chunks + chunk))]
    if acc is not None:
        in_specs += [whole(acc.shape)]
    return pl.pallas_call(
        functools.partial(back_kernel, utts, seq_ways, acc is None),
        out_shape=[
            jax.ShapeDtypeStruct((width, frames), f32),
            jax.ShapeDtypeStruct((3, 8, cols), f32),
            gshape,
            gshape,
        ],
        grid_spec=pltpu.PrefetchScalarGridSpec(
            num_scalar_prefetch=3,
            grid=(3,),
            in_specs=in_specs,
            out_specs=[
                whole((width, frames)),
                pl.BlockSpec((1, 8, cols), lambda j, *_: (j, 0, 0)),
                gspec,
                gspec,
            ],
            scratch_shapes=[pltpu.VMEM((2, DH // 2, frames), f32)],
        ),
        cost_estimate=pl.CostEstimate(
            flops=12 * frames * width * cols, bytes_accessed=20 * frames * width, transcendentals=0
        ),
        name="back_block",
    )(lengths, ids, drop, *ins)


def tail_kernel(
    utts,
    seq_ways,
    lengths_ref,
    ids_ref,
    scale_ref,
    acc_ref,
    hidden_ref,
    after_ref,
    mods_ref,
    joinedT_ref,
    w_skip_ref,
    tables_ref,
    grad_a_ref,
    grad_b_ref,
    keep_ref,
    send_ref,
    gh_ref,
):
    f32, bf16 = jnp.float32, jnp.bfloat16
    step = pl.program_id(0)
    frames, width = hidden_ref.shape
    core = ids_ref[0]
    parts = keep_ref.shape[0]
    block = 2 * width // seq_ways
    rows = block // parts

    @pl.when(step == 0)
    def _():
        hot = onehot_rows(lengths_ref, utts, 16, ids_ref[1] * frames, frames)
        cols = frame_columns(hot, jnp.zeros((1, frames), f32))
        madd = mods_operand(mods_ref)
        scale = dot(cols, madd[:, width:])
        gna = acc_ref[...].T
        normed, rstd = norm_stats(hidden_ref[...])
        sums = sum_rows(hot, 16, frames)
        tables_ref[:, 0:width] = dot(sums, gna.astype(bf16))
        tables_ref[:, width : 2 * width] = dot(sums, (gna * normed).astype(bf16))
        gh = (after_ref[...] + norm_back(gna * (1.0 + scale), normed, rstd)).astype(bf16)
        gh_ref[...] = gh
        tables_ref[:, 2 * width : 3 * width] = dot(sums, gh)

    gh = gh_ref[...]
    grad_w = dot(joinedT_ref[...], gh).astype(bf16)
    blocks = width // block
    for b in range(blocks):
        for k in range(parts):
            tile = grad_w[b * block + k * rows : b * block + (k + 1) * rows]

            @pl.when(core == b % 2)
            def _():
                keep_ref[k, b // 2] = tile

            @pl.when(core != b % 2)
            def _():
                send_ref[k, b // 2] = tile

    joined = dot_nt(gh, w_skip_ref[...])

    @pl.when(step == 0)
    def _():
        grad_a_ref[...] = joined * scale_ref[0]

    @pl.when(step == 1)
    def _():
        grad_b_ref[...] = joined * scale_ref[0]


def tail_block(lengths, ids, acc, hidden, after, mods, joinedT, w_skip, scale, seq_ways, parts):
    frames, width = hidden.shape
    utts = lengths.shape[0]
    f32, bf16 = jnp.float32, jnp.bfloat16
    rows = 2 * width // seq_ways // parts

    def whole(shape):
        return pl.BlockSpec(shape, lambda j, *_: (0,) * len(shape), pipeline_mode=pl.Buffered(1))

    gspec = pl.BlockSpec((parts, seq_ways // 4, rows, width), lambda j, *_: (0, j, 0, 0))
    gshape = jax.ShapeDtypeStruct((parts, seq_ways // 2, rows, width), bf16)
    out_shape = [
        jax.ShapeDtypeStruct((32, 3 * width), f32),
        jax.ShapeDtypeStruct((frames, width), f32),
        jax.ShapeDtypeStruct((frames, width), f32),
        gshape,
        gshape,
    ]
    return pl.pallas_call(
        functools.partial(tail_kernel, utts, seq_ways),
        out_shape=out_shape,
        grid_spec=pltpu.PrefetchScalarGridSpec(
            num_scalar_prefetch=3,
            grid=(2,),
            in_specs=[whole(a.shape) for a in (acc, hidden, after, mods)]
            + [
                pl.BlockSpec((width, frames), lambda j, *_: (j, 0)),
                pl.BlockSpec((width, width), lambda j, *_: (j, 0)),
            ],
            out_specs=[whole(o.shape) for o in out_shape[:3]] + [gspec, gspec],
            scratch_shapes=[pltpu.VMEM((frames, width), bf16)],
        ),
        compiler_params=pltpu.CompilerParams(vmem_limit_bytes=48 << 20),
        cost_estimate=pl.CostEstimate(
            flops=8 * frames * width * width, bytes_accessed=30 * frames * width, transcendentals=0
        ),
        name="tail_block",
    )(lengths, ids, scale, acc, hidden, after, mods, joinedT, w_skip)


def sum_exchange(value, axis, bit):
    ways = lax.axis_size(axis)
    return lax.ppermute(value, axis, [(i, i ^ bit) for i in range(ways)])


def add_pair(left, right):
    return (left.astype(jnp.float32) + right.astype(jnp.float32)).astype(jnp.bfloat16)


def pick(value, bit, axis=0):
    return lax.dynamic_index_in_dim(value, bit, axis, keepdims=False)


def axis_bits(ways):
    return [1 << i for i in range(ways.bit_length() - 1)]


def reduce_stages(keep, send):
    seq_ways, batch_ways = lax.axis_size("seq"), lax.axis_size("batch")
    seq_rank, batch_rank = lax.axis_index("seq"), lax.axis_index("batch")
    side = 1 << ((batch_ways.bit_length() - 1) // 2)
    x_bit, y_bit = 1, side
    x = lax.rem(batch_rank, 2)
    y = lax.rem(batch_rank // side, 2)
    _, z_ways, rows, width = keep.shape
    got = sum_exchange(send, "seq", 1)
    total = add_pair(keep, got).reshape(2, 2, 2, z_ways, rows, width)
    blocks = [total[0], total[1]]
    for turn in ((x, x_bit, y, y_bit), (y, y_bit, x, x_bit)):
        sends = [pick(blocks[0], 1 - turn[0]), pick(blocks[1], 1 - turn[2])]
        sends = follow(sends, (yield sends))
        got = [sum_exchange(sends[0], "batch", turn[1]), sum_exchange(sends[1], "batch", turn[3])]
        blocks = [
            add_pair(pick(blocks[0], turn[0]), got[0]),
            add_pair(pick(blocks[1], turn[2]), got[1]),
        ]
    block = jnp.stack(blocks)
    for bit in axis_bits(batch_ways):
        if bit not in (x_bit, y_bit):
            block = add_pair(block, sum_exchange(block, "batch", bit))
    z = seq_rank // 2
    for bit in axis_bits(z_ways):
        mine = lax.rem(z // bit, 2)
        block = block.reshape(2, block.shape[1] // 2, 2, rows, width)
        away = pick(block, 1 - mine, 2)
        (away,) = follow([away], (yield [away]))
        block = add_pair(pick(block, mine, 2), sum_exchange(away, "seq", 2 * bit))
    block = block.reshape(2, rows, width)
    (block,) = follow([block], (yield [block]))
    got_x = sum_exchange(block, "batch", x_bit)
    got_y = sum_exchange(block, "batch", y_bit)
    got_xy = sum_exchange(block, "batch", x_bit | y_bit)
    table = jnp.stack([jnp.stack([block, got_y]), jnp.stack([got_x, got_xy])])
    table = jnp.where(x == 1, table[::-1], table)
    table = jnp.where(y == 1, table[:, ::-1], table)
    yield jnp.concatenate(
        [table[:, :, 0].reshape(4, rows, width), jnp.swapaxes(table[:, :, 1], 0, 1).reshape(4, rows, width)]
    ).astype(jnp.float32)


def last_stage(stages, token=None):
    value = stages.send(token)
    for value in stages:
        pass
    return value


def follow(values, token):
    return values if token is None else [after(v, token) for v in values]


def after(value, *others):
    return lax.optimization_barrier((value,) + others)[0]


def gather_groups(value):
    return [value] + [sum_exchange(value, "batch", i) for i in range(1, lax.axis_size("batch"))]


def sum_seq(value):
    for bit in axis_bits(lax.axis_size("seq")):
        value = value + sum_exchange(value, "seq", bit)
    return value


def shards(
    tokens_in,
    skip_in,
    condition,
    cotangent,
    time_embed,
    lengths,
    key_mask,
    drop_mask,
    loss_mask,
    w_skip,
    b_skip,
    w_ada,
    b_ada,
    w_qkv,
    b_qkv,
    w_out,
    b_out,
    w_up,
    b_up,
    w_down,
    b_down,
):
    f32, bf16 = jnp.float32, jnp.bfloat16
    seq_ways, batch_ways = lax.axis_size("seq"), lax.axis_size("batch")
    seq_rank = lax.axis_index("seq")
    frames, width = tokens_in.shape[1:]
    group_frames = frames * seq_ways
    heads_local = HEADS // seq_ways
    utts = lengths.shape[1]
    lengths_row, drop = lengths[0], drop_mask[0]
    ids = jnp.stack([lax.rem(seq_rank, 2), seq_rank]).astype(jnp.int32)
    ok = key_mask.reshape(seq_ways, 1, frames)
    exchange = functools.partial(lax.all_to_all, axis_name="seq", split_axis=0, concat_axis=0, tiled=True)

    time_act = jax.nn.silu(time_embed[0]).astype(bf16)
    time_rows = jnp.pad(time_act, ((0, 16 - utts), (0, 0)))

    def modulation(first, last):
        return jnp.dot(time_rows, w_ada[:, first:last], preferred_element_type=f32) + b_ada[
            first:last
        ].astype(f32)

    mods_a = modulation(0, 2 * width)
    hidden, joinedT, naT, na = head_block(
        lengths_row, ids, drop, tokens_in[0], skip_in[0], condition[0], mods_a, w_skip, b_skip[None]
    )
    received = []
    for c in range(heads_local):
        packed = qkv_block(lengths_row, ids, drop, na, w_qkv, b_qkv[None], c, seq_ways)
        received.append(exchange(packed))

    mods_rest = modulation(2 * width, 6 * width)
    time_all = jnp.concatenate(gather_groups(time_act))
    hops = [("seq", bit) for bit in axis_bits(seq_ways)] + [("batch", bit) for bit in axis_bits(batch_ways)]
    count = jnp.full((8, 128), jnp.sum(loss_mask.astype(f32)))

    def hop(count):
        if not hops:
            return count
        axis, bit = hops.pop(0)
        return count + sum_exchange(count, axis, bit)

    received[0] = after(received[0], mods_rest, time_all, count)
    head_out, log_totals, returned = [], [], []
    for c in range(heads_local):
        out, log_total = attend(lengths_row, received[c], ok)
        head_out.append(out)
        log_totals.append(log_total)
        returned.append(exchange(out))
        count = hop(count)
        if c < heads_local - 1:
            received[c + 1] = after(received[c + 1], count, out)
    returned[0] = after(returned[0], count)
    mid = mid_block(
        lengths_row,
        ids,
        returned,
        hidden,
        mods_rest,
        cotangent[0],
        loss_mask,
        w_out,
        b_out[None],
        w_up,
        b_up[None],
        w_down,
        b_down[None],
        PARTS,
    )
    output, after_grad, tables, b_up_grad = mid[:4]
    grad_att = mid[4 : 4 + heads_local]
    keep_f, send_f = mid[4 + heads_local :]
    grad_heads = [exchange(g) for g in grad_att]
    feed = reduce_stages(keep_f, send_f)
    count = hop(count)

    acc, part_biases, part_blocks = None, [], []
    grad_local = []
    ahead = list(next(feed)) + [count]
    for c in range(heads_local):
        grad = attend_back(
            lengths_row, received[c], ok, head_out[c], after(grad_heads[c], *ahead), log_totals[c]
        )
        grad_local.append(exchange(after(grad, *grad_heads[c + 1 :])))
        count = hop(count)
        ahead = [grad, count]
    ahead += list(next(feed))
    for c in range(heads_local):
        acc, bias, keep, send = back_block(
            lengths_row, ids, drop, after(grad_local[c], *ahead), naT, w_qkv, acc, c, PARTS
        )
        part_biases.append(bias[:, 0])
        part_blocks.append(reduce_stages(keep, send))
        ahead = list(next(feed))
        for blocks in part_blocks:
            ahead += list(next(blocks))
    while hops:
        count = hop(count)
    scale = (group_frames * batch_ways) / count[0, :1]
    late_tables, grad_tokens, grad_skip, keep, send = tail_block(
        lengths_row, ids, after(acc, *ahead), hidden, after_grad, mods_a, joinedT, w_skip, scale, seq_ways, PARTS
    )
    skip_blocks = reduce_stages(keep, send)
    next(skip_blocks)
    feed = last_stage(feed, late_tables)
    part_blocks = [last_stage(b, late_tables) for b in part_blocks]
    skip_blocks = last_stage(skip_blocks)
    late = jnp.concatenate(
        [
            late_tables[:utts, : 2 * width].reshape(-1),
            tables[:utts, : 4 * width].reshape(-1),
            jnp.stack(part_biases, axis=1).reshape(-1),
            late_tables[16, 2 * width :],
            b_up_grad[0],
            tables[16, 4 * width :],
        ]
    )
    late = gather_groups(sum_seq(late.reshape(-1, 1024)))
    late = [g.reshape(-1) * scale for g in late]

    ada_rows = width // seq_ways
    own_time = lax.dynamic_slice_in_dim(time_all, seq_rank * ada_rows, ada_rows, axis=1).astype(f32)

    def own_slice(vector):
        size = vector.shape[0] // seq_ways
        return lax.dynamic_slice_in_dim(vector, seq_rank * size, size)

    two, six = 2 * utts * width, 6 * utts * width
    rows = jnp.concatenate(
        [
            jnp.concatenate([g[:two].reshape(utts, -1), g[two:six].reshape(utts, -1)], axis=1)
            for g in late
        ]
    )
    grad_w_ada = lax.dot_general(
        own_time, rows, (((0,), (0,)), ((), ())), precision=lax.Precision.HIGHEST
    )
    grad_b_ada = own_slice(jnp.sum(rows, axis=0))
    vector = sum(g[six:] for g in late)
    ff = w_up.shape[1]
    grad_b_qkv = own_slice(vector[: 3 * width])
    grad_b_skip = own_slice(vector[3 * width : 4 * width])
    grad_b_up = own_slice(vector[4 * width : 4 * width + ff])
    grad_b_out = own_slice(vector[4 * width + ff : 5 * width + ff])
    grad_b_down = own_slice(vector[5 * width + ff :])

    feed, skip_blocks = feed * scale, skip_blocks * scale
    part_blocks = [b * scale for b in part_blocks]
    own = width // seq_ways
    chunks = ff // width
    up_part = chunks * own // PARTS
    down_part = ff // seq_ways // PARTS
    halves = own // up_part
    grad_w_up = (
        feed[:, :up_part]
        .reshape(chunks, halves, up_part, width)
        .transpose(1, 2, 0, 3)
        .reshape(own, ff)
    )
    grad_w_down = feed[:, up_part : up_part + down_part].reshape(ff // seq_ways, width)
    grad_w_out = feed[:, up_part + down_part :].reshape(own, width)
    cols = seq_ways * HEAD_DIM
    grad_w_qkv = jnp.stack([b.reshape(own, 3, cols) for b in part_blocks], axis=2).reshape(own, 3 * width)
    grad_w_skip = skip_blocks.reshape(2 * own, width)
    return (
        output[None],
        grad_tokens[None],
        grad_skip[None],
        grad_w_skip,
        grad_b_skip,
        grad_w_ada,
        grad_b_ada,
        grad_w_qkv,
        grad_b_qkv,
        grad_w_out,
        grad_b_out,
        grad_w_up,
        grad_b_up,
        grad_w_down,
        grad_b_down,
    )


def solution(mesh):
    in_specs = (
        P("batch", "seq", None),
        P("batch", "seq", None),
        P("batch", "seq", None),
        P("batch", "seq", None),
        P("batch", None, None),
        P("batch", None),
        P("batch", None),
        P("batch", None),
        P("batch", "seq"),
        P(),
        P(),
        P(),
        P(),
        P(),
        P(),
        P(),
        P(),
        P(),
        P(),
        P(),
        P(),
    )
    out_specs = (
        P("batch", "seq", None),
        P("batch", "seq", None),
        P("batch", "seq", None),
        P("seq", None),
        P("seq"),
        P("seq", None),
        P("seq"),
        P("seq", None),
        P("seq"),
        P("seq", None),
        P("seq"),
        P("seq", None),
        P("seq"),
        P("seq", None),
        P("seq"),
    )
    return jax.shard_map(shards, mesh=mesh, in_specs=in_specs, out_specs=out_specs, check_vma=False)
```

```python
import functools

import jax
import jax.numpy as jnp
from jax import lax
from jax.experimental import pallas as pl
from jax.experimental.pallas import tpu as pltpu
from jax.sharding import PartitionSpec as P

HEADS = 16
HEAD_DIM = 64
PARTS = 8
BIG = 1e30
DH = 64
BQ = 512
BK = 512


def cost(weight):
    return pl.CostEstimate(flops=weight * 100000000, bytes_accessed=weight * 100000, transcendentals=0)


def onehot_rows(lengths_ref, utts, rows, base, width):
    row = lax.broadcasted_iota(jnp.int32, (rows, width), 0)
    col = base + lax.broadcasted_iota(jnp.int32, (rows, width), 1)
    start = jnp.int32(0)
    hot = jnp.zeros((rows, width), jnp.float32)
    for u in range(utts):
        end = start + lengths_ref[u]
        hot = jnp.where((row == u) & (col >= start) & (col < end), 1.0, hot)
        start = end
    return hot


def key_range(lengths_ref, utts, first, last):
    start = jnp.int32(0)
    low, high = jnp.int32(0), jnp.int32(0)
    for u in range(utts):
        end = start + lengths_ref[u]
        low = jnp.where((start <= first) & (first < end), start, low)
        high = jnp.where((start <= last) & (last < end), end, high)
        start = end
    return low // BK, (high + BK - 1) // BK


def aug_rows(utts):
    return -(-utts // 16) * 16


def split3(row):
    a = row.astype(jnp.bfloat16)
    rest = row - a.astype(jnp.float32)
    b = rest.astype(jnp.bfloat16)
    c = (rest - b.astype(jnp.float32)).astype(jnp.bfloat16)
    return a, b, c


def pad_rows(parts, total):
    have = sum(p.shape[0] for p in parts)
    if have < total:
        parts = parts + [jnp.zeros((total - have, parts[0].shape[1]), parts[0].dtype)]
    return jnp.concatenate(parts, axis=0)


def rows16(rows, width):
    idx = lax.broadcasted_iota(jnp.int32, (16, width), 0)
    out = jnp.zeros((16, width), jnp.float32)
    for i, r in enumerate(rows):
        out = jnp.where(idx == i, r, out)
    return out.astype(jnp.bfloat16)


def fwd_kernel(utts, lengths_ref, qkv_ref, ok_ref, out_ref, lse_ref, kaug, vaug):
    sources, _, frames = qkv_ref.shape
    per = frames // BQ
    pad_u = aug_rows(utts)
    step = pl.program_id(0)

    @pl.when(step == 0)
    def _():
        def build(s, c):
            hot = onehot_rows(lengths_ref, utts, pad_u, s * frames, frames)
            ok = ok_ref[s].astype(jnp.float32)
            block = qkv_ref[s]
            one = jnp.ones((1, frames), jnp.float32)
            kT = pad_rows(
                [block[DH : 2 * DH], (1.0 - hot).astype(jnp.bfloat16), rows16([1.0 - ok], frames)], 128
            )
            kaug[pl.ds(pl.multiple_of(s * frames, frames), frames), :] = kT.T
            vT = jnp.concatenate([block[2 * DH :], rows16([one], frames)], axis=0)
            for t in range(frames // BK):
                vaug[s * (frames // BK) + t] = vT[:, t * BK : (t + 1) * BK]
            return c

        lax.fori_loop(0, sources, build, 0)

    block = qkv_ref[step]
    hot_q = onehot_rows(lengths_ref, utts, pad_u, step * frames, frames)
    qT = (block[:DH].astype(jnp.float32) * 0.125)
    one = jnp.ones((1, frames), jnp.float32)
    qaug = pad_rows(
        [qT.astype(jnp.bfloat16), (hot_q * -BIG).astype(jnp.bfloat16), rows16([one * -BIG], frames)], 128
    )
    kT = block[DH : 2 * DH].astype(jnp.float32)
    vT = block[2 * DH :].astype(jnp.float32)
    ok = ok_ref[step] > 0
    s_self = jnp.sum(qT * kT, axis=0, keepdims=True)
    m0 = jnp.where(ok, -3e38, s_self)
    acc0 = jnp.concatenate([jnp.where(ok, 0.0, vT), jnp.where(ok, 0.0, jnp.ones((16, frames), jnp.float32))], axis=0)
    for t in range(per):
        cols = slice(t * BQ, (t + 1) * BQ)
        low, high = key_range(lengths_ref, utts, step * frames + t * BQ, step * frames + (t + 1) * BQ - 1)
        q_b = qaug[:, cols]

        def body(j, carry):
            m, acc = carry
            s = jnp.dot(kaug[pl.ds(pl.multiple_of(j * BK, BK), BK), :], q_b, preferred_element_type=jnp.float32)
            m_new = jnp.maximum(m, jnp.max(s, axis=0, keepdims=True))
            p = jnp.exp(s - m_new).astype(jnp.bfloat16)
            alpha = jnp.exp(m - m_new)
            acc = acc * alpha + jnp.dot(vaug[j], p, preferred_element_type=jnp.float32)
            return m_new, acc

        m, acc = lax.fori_loop(low, high, body, (m0[:, cols], acc0[:, cols]))
        total = acc[DH : DH + 1]
        out_ref[0, :, cols] = (acc[:DH] / total).astype(jnp.bfloat16)
        lse_ref[0, :, cols] = m + jnp.log(total)


def attend(lengths, qkv, ok):
    sources, _, frames = qkv.shape
    total = sources * frames
    utts = lengths.shape[0]
    whole = lambda shape: pl.BlockSpec(shape, lambda i, *_: (0,) * len(shape))
    return pl.pallas_call(
        functools.partial(fwd_kernel, utts),
        out_shape=(
            jax.ShapeDtypeStruct((sources, DH, frames), jnp.bfloat16),
            jax.ShapeDtypeStruct((sources, 1, frames), jnp.float32),
        ),
        grid_spec=pltpu.PrefetchScalarGridSpec(
            num_scalar_prefetch=1,
            grid=(sources,),
            in_specs=[whole(qkv.shape), whole(ok.shape)],
            out_specs=(
                pl.BlockSpec((1, DH, frames), lambda i, *_: (i, 0, 0)),
                pl.BlockSpec((1, 1, frames), lambda i, *_: (i, 0, 0)),
            ),
            scratch_shapes=[
                pltpu.VMEM((total, 128), jnp.bfloat16),
                pltpu.VMEM((total // BK, DH + 16, BK), jnp.bfloat16),
            ],
        ),
        cost_estimate=cost(250),
        name="attend",
    )(lengths, qkv, ok)


def bwd_kernel(utts, lengths_ref, qkv_ref, ok_ref, o_ref, do_ref, lse_ref, out_ref, kaug, vnat, kT_s, dk, dv):
    sources, _, frames = qkv_ref.shape
    per = frames // BK
    pad_u = aug_rows(utts)
    step = pl.program_id(0)
    f32 = jnp.float32

    @pl.when(step == 0)
    def _():
        def build(s, c):
            hot = onehot_rows(lengths_ref, utts, pad_u, s * frames, frames)
            ok = ok_ref[s]
            block = qkv_ref[s]
            one = jnp.ones((1, frames), f32)
            kT = block[DH : 2 * DH]
            vT = block[2 * DH :]
            kA = pad_rows(
                [kT, (1.0 - hot).astype(jnp.bfloat16), rows16([1.0 - ok.astype(f32), one, one, one], frames)], 128
            )
            rows = pl.ds(pl.multiple_of(s * frames, frames), frames)
            kaug[rows, :] = kA.T
            vnat[rows, :] = pad_rows([vT, rows16([one, one, one], frames)], 128).T
            qT = block[:DH].astype(f32) * 0.125
            do = do_ref[s].astype(f32)
            s_self = jnp.sum(qT * kT.astype(f32), axis=0, keepdims=True)
            delta = jnp.sum(do * o_ref[s].astype(f32), axis=0, keepdims=True)
            p_self = jnp.where(ok > 0, 0.0, jnp.exp(s_self - lse_ref[s]))
            ds_self = p_self * (jnp.sum(do * vT.astype(f32), axis=0, keepdims=True) - delta)
            dk0 = ds_self * qT
            dv0 = p_self * do
            for t in range(per):
                cols = slice(t * BK, (t + 1) * BK)
                kT_s[s * per + t] = kT[:, cols]
                dk[s * per + t] = dk0[:, cols]
                dv[s * per + t] = dv0[:, cols]
            return c

        lax.fori_loop(0, sources, build, 0)

    block = qkv_ref[step]
    one = jnp.ones((1, frames), f32)
    hot_q = onehot_rows(lengths_ref, utts, pad_u, step * frames, frames)
    qT = block[:DH].astype(f32) * 0.125
    qTb = qT.astype(jnp.bfloat16)
    kT = block[DH : 2 * DH].astype(f32)
    vT = block[2 * DH :].astype(f32)
    ok = ok_ref[step]
    dob = do_ref[step]
    do = dob.astype(f32)
    lse = lse_ref[step]
    delta = jnp.sum(do * o_ref[step].astype(f32), axis=0, keepdims=True)
    l3 = [-r.astype(f32) for r in split3(lse)]
    d3 = [-r.astype(f32) for r in split3(delta)]
    qaug = pad_rows([qTb, (hot_q * -BIG).astype(jnp.bfloat16), rows16([one * -BIG] + l3, frames)], 128)
    doaug = pad_rows([dob, rows16(d3, frames)], 128)
    s_self = jnp.sum(qT * kT, axis=0, keepdims=True)
    p_self = jnp.where(ok > 0, 0.0, jnp.exp(s_self - lse))
    ds_self = p_self * (jnp.sum(do * vT, axis=0, keepdims=True) - delta)
    dq0 = ds_self * kT
    nt = (((1,), (1,)), ((), ()))
    for t in range(frames // BQ):
        cols = slice(t * BQ, (t + 1) * BQ)
        low, high = key_range(lengths_ref, utts, step * frames + t * BQ, step * frames + (t + 1) * BQ - 1)
        q_a = qaug[:, cols]
        q_b = qTb[:, cols]
        do_a = doaug[:, cols]
        do_b = dob[:, cols]

        def body(j, dq):
            rows = pl.ds(pl.multiple_of(j * BK, BK), BK)
            s = jnp.dot(kaug[rows, :], q_a, preferred_element_type=f32)
            dp = jnp.dot(vnat[rows, :], do_a, preferred_element_type=f32)
            p = jnp.exp(s)
            ds = (p * dp).astype(jnp.bfloat16)
            dv[j] += lax.dot_general(do_b, p.astype(jnp.bfloat16), nt, preferred_element_type=f32)
            dk[j] += lax.dot_general(q_b, ds, nt, preferred_element_type=f32)
            return dq + jnp.dot(kT_s[j], ds, preferred_element_type=f32)

        dq = lax.fori_loop(low, high, body, dq0[:, cols])
        out_ref[step, :DH, cols] = (dq * 0.125).astype(jnp.bfloat16)

    @pl.when(step == sources - 1)
    def _():
        def finish(s, c):
            for t in range(per):
                cols = slice(t * BK, (t + 1) * BK)
                out_ref[s, DH : 2 * DH, cols] = dk[s * per + t].astype(jnp.bfloat16)
                out_ref[s, 2 * DH :, cols] = dv[s * per + t].astype(jnp.bfloat16)
            return c

        lax.fori_loop(0, sources, finish, 0)


def attend_back(lengths, qkv, ok, out, grad, lse):
    sources, _, frames = qkv.shape
    total = sources * frames
    utts = lengths.shape[0]
    whole = lambda shape: pl.BlockSpec(shape, lambda i, *_: (0,) * len(shape))
    return pl.pallas_call(
        functools.partial(bwd_kernel, utts),
        out_shape=jax.ShapeDtypeStruct(qkv.shape, jnp.bfloat16),
        grid_spec=pltpu.PrefetchScalarGridSpec(
            num_scalar_prefetch=1,
            grid=(sources,),
            in_specs=[whole(a.shape) for a in (qkv, ok, out, grad, lse)],
            out_specs=whole(qkv.shape),
            scratch_shapes=[
                pltpu.VMEM((total, 128), jnp.bfloat16),
                pltpu.VMEM((total, 128), jnp.bfloat16),
                pltpu.VMEM((total // BK, DH, BK), jnp.bfloat16),
                pltpu.VMEM((total // BK, DH, BK), jnp.float32),
                pltpu.VMEM((total // BK, DH, BK), jnp.float32),
            ],
        ),
        cost_estimate=cost(320),
        name="attend_back",
    )(lengths, qkv, ok, out, grad, lse)


FF_TILE = 512
EPS = 1e-06


def dot(left, right):
    return jnp.dot(left, right, preferred_element_type=jnp.float32)


def dot_nt(left, right):
    return lax.dot_general(left, right, (((1,), (1,)), ((), ())), preferred_element_type=jnp.float32)


def norm_stats(x):
    mean = jnp.mean(x, axis=1, keepdims=True)
    centred = x - mean
    rstd = lax.rsqrt(jnp.mean(centred * centred, axis=1, keepdims=True) + EPS)
    return centred * rstd, rstd


def norm_back(grad, normed, rstd):
    first = jnp.mean(grad, axis=1, keepdims=True)
    second = jnp.mean(grad * normed, axis=1, keepdims=True)
    return rstd * (grad - first - normed * second)


def mods_operand(mods_ref):
    rows = mods_ref[...]
    return pad_rows(list(split3(rows)), 128)


def table_rows(utts):
    return -(-utts // 8) * 8


def sum_rows(hot, utts_pad, frames):
    idx = lax.broadcasted_iota(jnp.int32, (16, frames), 0)
    ones = jnp.where(idx == 0, 1.0, 0.0).astype(jnp.bfloat16)
    return jnp.concatenate([hot.astype(jnp.bfloat16), ones], axis=0)


def mid_kernel(
    dims,
    lengths_ref,
    ids_ref,
    *refs,
):
    seq_ways, heads_local, utts, ff = dims
    att_refs = refs[:heads_local]
    (
        hidden_ref,
        mods_ref,
        cot_ref,
        loss_ref,
        w_out_ref,
        b_out_ref,
        w_up_ref,
        b_up_ref,
        w_down_ref,
        b_down_ref,
    ) = refs[heads_local : heads_local + 10]
    outs = refs[heads_local + 10 :]
    output_ref, after_grad_ref, small_ref = outs[:3]
    gatt_refs = outs[3 : 3 + heads_local]
    up_refs = outs[3 + heads_local : 5 + heads_local]
    down_refs = outs[5 + heads_local : 7 + heads_local]
    (
        attT,
        attn_proj,
        after,
        nf,
        nfT,
        gff,
        ff_acc,
        gnf_acc,
        sums,
        cols,
        madd,
        grads,
        sems,
    ) = outs[7 + heads_local :]
    f32, bf16 = jnp.float32, jnp.bfloat16
    step = pl.program_id(0)
    steps = pl.num_programs(0)
    core = ids_ref[0]
    rank = ids_ref[1]
    frames, width = hidden_ref.shape
    up_rows = width // seq_ways
    down_rows = FF_TILE
    z_ways = seq_ways // 2
    parts = grads.shape[1]
    pad_u = table_rows(utts)
    ff_total = ff
    up_part = ff_total // width * up_rows // parts
    down_block = ff_total // seq_ways
    down_part = down_block // parts
    out_part = up_rows // parts

    def mod(index):
        return dot(cols[...], madd[:, index * width : (index + 1) * width])

    def grad_out():
        loss = cols[:, 48:49].astype(f32)
        return cot_ref[...].astype(f32) * loss

    @pl.when(step == 0)
    def _():
        hot = onehot_rows(lengths_ref, utts, 16, rank * frames, frames)
        hotb = hot.astype(bf16)
        idx = lax.broadcasted_iota(jnp.int32, (16, frames), 0)
        loss = jnp.where(idx == 0, loss_ref[...].astype(f32), 0.0).astype(bf16)
        cols[...] = pad_rows([hotb, hotb, hotb, loss], 128).T
        sums[...] = sum_rows(hot, 16, frames)
        madd[...] = mods_operand(mods_ref)
        for c in range(heads_local):
            for s in range(seq_ways):
                attT[(c * seq_ways + s) * DH : (c * seq_ways + s + 1) * DH, :] = att_refs[c][s]
        proj = dot(attT[...].T, w_out_ref[...]) + b_out_ref[...].astype(f32)
        attn_proj[...] = proj
        mixed = hidden_ref[...] + mod(0) * proj
        after[...] = mixed
        normed, _ = norm_stats(mixed)
        value = (normed * (1.0 + mod(2)) + mod(1)).astype(bf16)
        nf[...] = value
        nfT[...] = value.T
        gff[...] = (grad_out() * mod(3)).astype(bf16)
        small_ref[4 * pad_u :, :] = jnp.zeros((8, width), f32)

    up = dot(nf[...], w_up_ref[...]) + b_up_ref[...].astype(f32)
    inner = 0.7978845608028654 * (up + 0.044715 * (up * up * up))
    tanh = jnp.tanh(inner)
    cdf = 0.5 * (1.0 + tanh)
    act = (up * cdf).astype(bf16)
    slope = cdf + 0.5 * up * (1.0 - tanh * tanh) * (
        0.7978845608028654 * (1.0 + (3 * 0.044715) * (up * up))
    )
    ff_part = dot(act, w_down_ref[...])
    gup = (dot_nt(gff[...], w_down_ref[...]) * slope).astype(bf16)
    gnf_part = dot_nt(gup, w_up_ref[...])

    @pl.when(step == 0)
    def _():
        ff_acc[...] = ff_part
        gnf_acc[...] = gnf_part

    @pl.when(step > 0)
    def _():
        ff_acc[...] += ff_part
        gnf_acc[...] += gnf_part

    halves = width // FF_TILE
    chunk = step // halves
    half = step % halves
    col = pl.ds(pl.multiple_of(half * FF_TILE, FF_TILE), FF_TILE)
    per_chunk = up_rows // up_part
    small_ref[pl.ds(4 * pad_u + 2 + chunk, 1), col] = dot(sums[16:32, :], gup)[:1]
    grad_w_up = dot(nfT[...], gup).astype(bf16)
    for s in range(seq_ways):
        side = jnp.where(core == s % 2, 0, 1)
        for h in range(per_chunk):
            lo = s * up_rows + h * up_part
            grads[side, chunk * per_chunk + h, s // 2, 0:up_part, col] = grad_w_up[lo : lo + up_part]
    grad_w_down = dot(act.T, gff[...]).astype(bf16)
    blocks = FF_TILE // down_block
    copies = []
    for b in range(blocks):
        s = step * blocks + b
        side = jnp.where(core == s % 2, 0, 1)
        for k in range(parts):
            lo = b * down_block + k * down_part
            grads[side, k, s // 2, up_part : up_part + down_part, :] = grad_w_down[lo : lo + down_part]

    def up_copy(side, j):
        where = (
            pl.ds((j // halves) * per_chunk, per_chunk),
            slice(None),
            slice(None),
            pl.ds(pl.multiple_of((j % halves) * FF_TILE, FF_TILE), FF_TILE),
        )
        source = grads.at[side].at[where[0], where[1], pl.ds(0, up_part), where[3]]
        return pltpu.make_async_copy(source, up_refs[side].at[where], sems.at[side, j])

    def down_copy(side, z, index):
        source = grads.at[side].at[:, pl.ds(z, 1), pl.ds(up_part, down_part)]
        target = down_refs[side].at[:, pl.ds(z, 1), pl.ds(0, down_part)]
        return pltpu.make_async_copy(source, target, sems.at[side, index])

    def out_copy(side):
        source = grads.at[side].at[:, :, pl.ds(up_part + down_part, out_part)]
        target = down_refs[side].at[:, :, pl.ds(down_part, out_part)]
        return pltpu.make_async_copy(source, target, sems.at[side, ff_total // FF_TILE + z_ways])

    base = ff_total // FF_TILE
    for side in range(2):
        up_copy(side, step).start()
    for b in range(blocks):
        s = step * blocks + b
        for side in range(2):

            @pl.when(lax.rem(s + core, 2) == side)
            def _():
                down_copy(side, s // 2, base + s // 2).start()

    @pl.when(step == steps - 1)
    def _():
        ff_out = ff_acc[...] + b_down_ref[...].astype(f32)
        mixed = after[...]
        go = grad_out()
        output_ref[...] = (mixed + mod(3) * ff_out).astype(bf16)
        rows = sums[...]
        small_ref[3 * pad_u : 4 * pad_u, :] = dot(rows, (go * ff_out).astype(bf16))[:pad_u]
        normed, rstd = norm_stats(mixed)
        gnf = gnf_acc[...]
        small_ref[pad_u : 2 * pad_u, :] = dot(rows, gnf.astype(bf16))[:pad_u]
        small_ref[2 * pad_u : 3 * pad_u, :] = dot(rows, (gnf * normed).astype(bf16))[:pad_u]
        g_after = go + norm_back(gnf * (1.0 + mod(2)), normed, rstd)
        after_grad_ref[...] = g_after
        small_ref[0:pad_u, :] = dot(rows, (g_after * attn_proj[...]).astype(bf16))[:pad_u]
        gattn = (g_after * mod(0)).astype(bf16)
        small_ref[4 * pad_u : 4 * pad_u + 1, :] = dot(rows, gattn)[16:17]
        small_ref[4 * pad_u + 1 : 4 * pad_u + 2, :] = dot(rows, gff[...])[16:17]
        gattT = dot_nt(w_out_ref[...], gattn).astype(bf16)
        for c in range(heads_local):
            for s in range(seq_ways):
                lo = (c * seq_ways + s) * DH
                gatt_refs[c][s] = gattT[lo : lo + DH]
        grad_w_out = dot(attT[...], gattn).astype(bf16)
        for s in range(seq_ways):
            side = jnp.where(core == s % 2, 0, 1)
            for k in range(parts):
                lo = s * up_rows + k * out_part
                grads[side, k, s // 2, up_part + down_part : up_part + down_part + out_part, :] = grad_w_out[
                    lo : lo + out_part
                ]
        for side in range(2):
            out_copy(side).start()
        for side in range(2):
            for j in range(ff_total // FF_TILE):
                up_copy(side, j).wait()
            for z in range(z_ways):
                down_copy(side, z, base + z).wait()
            out_copy(side).wait()


def mid_block(
    lengths, ids, att, hidden, mods, cot, loss, w_out, b_out, w_up, b_up, w_down, b_down, parts
):
    frames, width = hidden.shape
    heads_local = len(att)
    seq_ways = att[0].shape[0]
    ff = w_up.shape[1]
    up_rows = width // seq_ways
    rows = (ff // width * up_rows + ff // seq_ways + up_rows) // parts
    utts = lengths.shape[0]
    f32, bf16 = jnp.float32, jnp.bfloat16
    steps = ff // FF_TILE

    def whole(shape):
        return pl.BlockSpec(shape, lambda j, *_: (0,) * len(shape), pipeline_mode=pl.Buffered(1))

    hbm = pl.BlockSpec(memory_space=pl.ANY)
    gshape = (parts, seq_ways // 2, rows, width)
    out_shape = [
        jax.ShapeDtypeStruct((frames, width), bf16),
        jax.ShapeDtypeStruct((frames, width), f32),
        jax.ShapeDtypeStruct((4 * table_rows(utts) + 8, width), f32),
    ]
    out_shape += [jax.ShapeDtypeStruct(a.shape, bf16) for a in att]
    out_specs = [whole(o.shape) for o in out_shape] + [hbm] * 4
    up_part = ff // width * up_rows // parts
    for part in (up_part, rows - up_part):
        out_shape += [jax.ShapeDtypeStruct((parts, seq_ways // 2, part, width), bf16)] * 2
    ins = list(att) + [hidden, mods, cot, loss, w_out, b_out]
    return pl.pallas_call(
        functools.partial(mid_kernel, (seq_ways, heads_local, utts, ff)),
        out_shape=out_shape,
        grid_spec=pltpu.PrefetchScalarGridSpec(
            num_scalar_prefetch=2,
            grid=(steps,),
            in_specs=[whole(a.shape) for a in ins]
            + [
                pl.BlockSpec((width, FF_TILE), lambda j, *_: (0, j)),
                pl.BlockSpec((1, FF_TILE), lambda j, *_: (0, j)),
                pl.BlockSpec((FF_TILE, width), lambda j, *_: (j, 0)),
                whole((1, width)),
            ],
            out_specs=out_specs,
            scratch_shapes=[
                pltpu.VMEM((width, frames), bf16),
                pltpu.VMEM((frames, width), f32),
                pltpu.VMEM((frames, width), f32),
                pltpu.VMEM((frames, width), bf16),
                pltpu.VMEM((width, frames), bf16),
                pltpu.VMEM((frames, width), bf16),
                pltpu.VMEM((frames, width), f32),
                pltpu.VMEM((frames, width), f32),
                pltpu.VMEM((32, frames), bf16),
                pltpu.VMEM((frames, 128), bf16),
                pltpu.VMEM((128, 4 * width), bf16),
                pltpu.VMEM((2,) + gshape, bf16),
                pltpu.SemaphoreType.DMA((2, steps + seq_ways // 2 + 1)),
            ],
        ),
        compiler_params=pltpu.CompilerParams(vmem_limit_bytes=63 << 20),
        cost_estimate=cost(500),
        name="mid_block",
    )(lengths, ids, *ins, w_up, b_up, w_down, b_down)


def whole_block(shape):
    return pl.BlockSpec(shape, lambda *_: (0,) * len(shape), pipeline_mode=pl.Buffered(1))


def segment_rows(lengths_ref, drop_ref, utts, base, width):
    col = base + lax.broadcasted_iota(jnp.int32, (1, width), 1)
    start = jnp.int32(0)
    kept = jnp.zeros((1, width), jnp.float32)
    place = jnp.zeros((1, width), jnp.int32)
    for u in range(utts):
        end = start + lengths_ref[u]
        inside = (col >= start) & (col < end)
        kept = jnp.where(inside, (1 - drop_ref[u]).astype(jnp.float32), kept)
        place = jnp.where(inside, col - start, place)
        start = end
    return kept, place.astype(jnp.float32)


def rotary_rows(place, half):
    index = lax.broadcasted_iota(jnp.int32, (half, 1), 0).astype(jnp.float32)
    inverse = jnp.exp(index * (-9.210340371976184 / half))
    angles = inverse * place
    return jnp.cos(angles), jnp.sin(angles)


def frame_columns(hot, extra):
    hotb = hot.astype(jnp.bfloat16)
    idx = lax.broadcasted_iota(jnp.int32, hot.shape, 0)
    last = jnp.where(idx == 0, extra, 0.0).astype(jnp.bfloat16)
    return pad_rows([hotb, hotb, hotb, last], 128).T


def head_kernel(
    utts,
    lengths_ref,
    ids_ref,
    drop_ref,
    tokens_ref,
    skip_ref,
    cond_ref,
    mods_ref,
    w_skip_ref,
    b_skip_ref,
    hidden_ref,
    joinedT_ref,
    naT_ref,
    na_ref,
    cols,
):
    f32, bf16 = jnp.float32, jnp.bfloat16
    step = pl.program_id(0)
    frames, width = tokens_ref.shape
    rank = ids_ref[1]

    @pl.when(step == 0)
    def _():
        hot = onehot_rows(lengths_ref, utts, 16, rank * frames, frames)
        kept, _ = segment_rows(lengths_ref, drop_ref, utts, rank * frames, frames)
        cols[...] = frame_columns(hot, kept)
        keep = cols[:, 48:49].astype(f32)
        mixed = (tokens_ref[...].astype(f32) + keep * cond_ref[...].astype(f32)).astype(bf16)
        joinedT_ref[0:width, :] = mixed.T
        hidden_ref[...] = dot(mixed, w_skip_ref[...]) + b_skip_ref[...].astype(f32)

    @pl.when(step == 1)
    def _():
        skip = skip_ref[...]
        joinedT_ref[width : 2 * width, :] = skip.T
        hidden = hidden_ref[...] + dot(skip, w_skip_ref[...])
        hidden_ref[...] = hidden
        madd = mods_operand(mods_ref)
        shift = dot(cols[...], madd[:, :width])
        scale = dot(cols[...], madd[:, width:])
        normed, _ = norm_stats(hidden)
        value = (normed * (1.0 + scale) + shift).astype(bf16)
        na_ref[...] = value
        naT_ref[...] = value.T


def head_block(lengths, ids, drop, tokens, skip, cond, mods, w_skip, b_skip):
    frames, width = tokens.shape
    utts = lengths.shape[0]
    f32, bf16 = jnp.float32, jnp.bfloat16

    def whole(shape):
        return pl.BlockSpec(shape, lambda j, *_: (0,) * len(shape), pipeline_mode=pl.Buffered(1))

    out_shape = [
        jax.ShapeDtypeStruct((frames, width), f32),
        jax.ShapeDtypeStruct((2 * width, frames), bf16),
        jax.ShapeDtypeStruct((width, frames), bf16),
        jax.ShapeDtypeStruct((frames, width), bf16),
    ]
    return pl.pallas_call(
        functools.partial(head_kernel, utts),
        out_shape=out_shape,
        grid_spec=pltpu.PrefetchScalarGridSpec(
            num_scalar_prefetch=3,
            grid=(2,),
            in_specs=[whole(a.shape) for a in (tokens, skip, cond, mods)]
            + [pl.BlockSpec((width, width), lambda j, *_: (j, 0)), whole((1, width))],
            out_specs=[whole(o.shape) for o in out_shape],
            scratch_shapes=[pltpu.VMEM((frames, 128), bf16)],
        ),
        compiler_params=pltpu.CompilerParams(vmem_limit_bytes=48 << 20),
        cost_estimate=cost(100),
        name="head_block",
    )(lengths, ids, drop, tokens, skip, cond, mods, w_skip, b_skip)


def turn_heads(tensor, cosine, sine):
    half = DH // 2
    first, second = tensor[:, :half], tensor[:, half:]
    return jnp.concatenate([first * cosine - second * sine, second * cosine + first * sine], axis=1)


def qkv_kernel(utts, seq_ways, lengths_ref, ids_ref, drop_ref, na_ref, w_ref, b_ref, out_ref, trig):
    f32, bf16 = jnp.float32, jnp.bfloat16
    part = pl.program_id(0)
    frames = na_ref.shape[0]

    @pl.when(part == 0)
    def _():
        _, place = segment_rows(lengths_ref, drop_ref, utts, ids_ref[1] * frames, frames)
        cosine, sine = rotary_rows(place, DH // 2)
        trig[0] = cosine
        trig[1] = sine

    raw = dot(na_ref[...], w_ref[...]) + b_ref[...].astype(f32)
    rawT = raw.T.reshape(seq_ways, DH, frames)
    turned = part < 2
    cosine = jnp.where(turned, trig[0], 1.0)[None]
    sine = jnp.where(turned, trig[1], 0.0)[None]
    out_ref[:, pl.ds(pl.multiple_of(part * DH, DH), DH), :] = turn_heads(rawT, cosine, sine).astype(bf16)


def qkv_block(lengths, ids, drop, na, w_qkv, b_qkv, chunk, seq_ways):
    frames, width = na.shape
    cols = seq_ways * DH
    chunks = width // cols
    utts = lengths.shape[0]

    def whole(shape):
        return pl.BlockSpec(shape, lambda j, *_: (0,) * len(shape), pipeline_mode=pl.Buffered(1))

    shape = (seq_ways, 3 * DH, frames)
    return pl.pallas_call(
        functools.partial(qkv_kernel, utts, seq_ways),
        out_shape=jax.ShapeDtypeStruct(shape, jnp.bfloat16),
        grid_spec=pltpu.PrefetchScalarGridSpec(
            num_scalar_prefetch=3,
            grid=(3,),
            in_specs=[
                whole(na.shape),
                pl.BlockSpec((width, cols), lambda j, *_: (0, j * chunks + chunk)),
                pl.BlockSpec((1, cols), lambda j, *_: (0, j * chunks + chunk)),
            ],
            out_specs=whole(shape),
            scratch_shapes=[pltpu.VMEM((2, DH // 2, frames), jnp.float32)],
        ),
        cost_estimate=cost(75),
        name="qkv_block",
    )(lengths, ids, drop, na, w_qkv, b_qkv)


def back_kernel(utts, seq_ways, first, lengths_ref, ids_ref, drop_ref, grad_ref, naT_ref, w_ref, *refs):
    if first:
        acc_in = None
        acc_ref, bias_ref, keep_ref, send_ref, trig, grads, sems = refs
    else:
        acc_in, acc_ref, bias_ref, keep_ref, send_ref, trig, grads, sems = refs
    f32, bf16 = jnp.float32, jnp.bfloat16
    part = pl.program_id(0)
    width, frames = naT_ref.shape
    core = ids_ref[0]
    parts = keep_ref.shape[0]
    own = width // seq_ways
    rows = own // parts

    @pl.when(part == 0)
    def _():
        _, place = segment_rows(lengths_ref, drop_ref, utts, ids_ref[1] * frames, frames)
        cosine, sine = rotary_rows(place, DH // 2)
        trig[0] = cosine
        trig[1] = sine

    turned = part < 2
    cosine = jnp.where(turned, trig[0], 1.0)[None]
    sine = jnp.where(turned, trig[1], 0.0)[None]
    raw = grad_ref[:, pl.ds(pl.multiple_of(part * DH, DH), DH), :].astype(f32)
    gpT = turn_heads(raw, cosine, -sine).astype(bf16).reshape(seq_ways * DH, frames)
    gna = dot(w_ref[...], gpT)

    @pl.when(part == 0)
    def _():
        acc_ref[...] = gna if first else acc_in[...] + gna

    @pl.when(part > 0)
    def _():
        acc_ref[...] += gna

    ones = jnp.ones((8, frames), bf16)
    bias_ref[0] = dot_nt(ones, gpT)
    grad_w = dot_nt(naT_ref[...], gpT).astype(bf16)
    cols = seq_ways * DH
    at = pl.ds(pl.multiple_of(part * cols, cols), cols)
    for s in range(seq_ways):
        side = jnp.where(core == s % 2, 0, 1)
        for k in range(parts):
            lo = s * own + k * rows
            grads[side, k, s // 2, :, at] = grad_w[lo : lo + rows]

    def copy(side, p):
        where = (slice(None), slice(None), slice(None), pl.ds(pl.multiple_of(p * cols, cols), cols))
        return pltpu.make_async_copy(
            grads.at[side].at[where], (keep_ref, send_ref)[side].at[where], sems.at[side, p]
        )

    for side in (1, 0):
        copy(side, part).start()

    @pl.when(part == 2)
    def _():
        for side in (1, 0):
            for p in range(3):
                copy(side, p).wait()


def back_block(lengths, ids, drop, grad, naT, w_qkv, acc, chunk, parts):
    seq_ways, _, frames = grad.shape
    width = naT.shape[0]
    cols = seq_ways * DH
    chunks = width // cols
    utts = lengths.shape[0]
    f32, bf16 = jnp.float32, jnp.bfloat16
    rows = width // seq_ways // parts

    def whole(shape):
        return pl.BlockSpec(shape, lambda j, *_: (0,) * len(shape), pipeline_mode=pl.Buffered(1))

    gspec = pl.BlockSpec(memory_space=pl.ANY)
    gshape = jax.ShapeDtypeStruct((parts, seq_ways // 2, rows, 3 * cols), bf16)
    ins = [grad, naT, w_qkv] + ([] if acc is None else [acc])
    in_specs = [whole(grad.shape), whole(naT.shape)]
    in_specs += [pl.BlockSpec((width, cols), lambda j, *_: (0, j * chunks + chunk))]
    if acc is not None:
        in_specs += [whole(acc.shape)]
    return pl.pallas_call(
        functools.partial(back_kernel, utts, seq_ways, acc is None),
        out_shape=[
            jax.ShapeDtypeStruct((width, frames), f32),
            jax.ShapeDtypeStruct((3, 8, cols), f32),
            gshape,
            gshape,
        ],
        grid_spec=pltpu.PrefetchScalarGridSpec(
            num_scalar_prefetch=3,
            grid=(3,),
            in_specs=in_specs,
            out_specs=[
                whole((width, frames)),
                pl.BlockSpec((1, 8, cols), lambda j, *_: (j, 0, 0)),
                gspec,
                gspec,
            ],
            scratch_shapes=[
                pltpu.VMEM((2, DH // 2, frames), f32),
                pltpu.VMEM((2,) + gshape.shape, bf16),
                pltpu.SemaphoreType.DMA((2, 3)),
            ],
        ),
        compiler_params=pltpu.CompilerParams(vmem_limit_bytes=48 << 20),
        cost_estimate=cost(100),
        name="back_block",
    )(lengths, ids, drop, *ins)


def norm_kernel(
    utts, heads_local, lengths_ref, ids_ref, acc_ref, hidden_ref, after_ref, mods_ref, loss_ref, mid_ref, *refs
):
    f32, bf16 = jnp.float32, jnp.bfloat16
    bias_refs, (gh_ref, small_ref) = refs[:heads_local], refs[heads_local:]
    frames, width = hidden_ref.shape
    pad_u = table_rows(utts)
    base = 6 * pad_u
    hot = onehot_rows(lengths_ref, utts, 16, ids_ref[1] * frames, frames)
    cols = frame_columns(hot, jnp.zeros((1, frames), f32))
    madd = mods_operand(mods_ref)
    scale = dot(cols, madd[:, width:])
    gna = acc_ref[...].T
    normed, rstd = norm_stats(hidden_ref[...])
    sums = sum_rows(hot, 16, frames)
    small_ref[0:pad_u, :] = dot(sums, gna.astype(bf16))[:pad_u]
    small_ref[pad_u : 2 * pad_u, :] = dot(sums, (gna * normed).astype(bf16))[:pad_u]
    gh = (after_ref[...] + norm_back(gna * (1.0 + scale), normed, rstd)).astype(bf16)
    gh_ref[...] = gh
    small_ref[2 * pad_u : base, :] = mid_ref[0 : 4 * pad_u, :]
    cols_local = width // heads_local
    for c in range(heads_local):
        for p in range(3):
            small_ref[base + p : base + p + 1, c * cols_local : (c + 1) * cols_local] = bias_refs[c][p, 0:1, :]
    small_ref[base + 3 : base + 4, :] = dot(sums, gh)[16:17]
    small_ref[base + 4 : base + 12, :] = mid_ref[4 * pad_u : 4 * pad_u + 8, :]
    count = jnp.sum(loss_ref[...].astype(f32), axis=1, keepdims=True)
    small_ref[base + 12 : base + 16, :] = jnp.broadcast_to(count, (4, width))


def norm_block(lengths, ids, acc, hidden, after, mods, loss, mid_small, biases):
    frames, width = hidden.shape
    utts = lengths.shape[0]
    out_shape = [
        jax.ShapeDtypeStruct((frames, width), jnp.bfloat16),
        jax.ShapeDtypeStruct((6 * table_rows(utts) + 16, width), jnp.float32),
    ]
    return pl.pallas_call(
        functools.partial(norm_kernel, utts, len(biases)),
        out_shape=out_shape,
        grid_spec=pltpu.PrefetchScalarGridSpec(
            num_scalar_prefetch=2,
            grid=(1,),
            in_specs=[whole_block(a.shape) for a in (acc, hidden, after, mods, loss, mid_small, *biases)],
            out_specs=[whole_block(o.shape) for o in out_shape],
        ),
        compiler_params=pltpu.CompilerParams(vmem_limit_bytes=48 << 20),
        cost_estimate=cost(50),
        name="norm_block",
    )(lengths, ids, acc, hidden, after, mods, loss, mid_small, *biases)


def skip_kernel(seq_ways, ids_ref, joinedT_ref, gh_ref, keep_ref, send_ref, grads, sems):
    step = pl.program_id(0)
    core = ids_ref[0]
    parts = keep_ref.shape[0]
    width = joinedT_ref.shape[0]
    block = 2 * width // seq_ways
    rows = block // parts
    z_step = seq_ways // 4
    grad_w = dot(joinedT_ref[...], gh_ref[...]).astype(jnp.bfloat16)
    for b in range(width // block):
        side = jnp.where(core == b % 2, 0, 1)
        for k in range(parts):
            lo = b * block + k * rows
            grads[side, k, step * z_step + b // 2] = grad_w[lo : lo + rows]

    def copy(side, at):
        where = (slice(None), pl.ds(at * z_step, z_step))
        return pltpu.make_async_copy(
            grads.at[side].at[where], (keep_ref, send_ref)[side].at[where], sems.at[side, at]
        )

    for side in (1, 0):
        copy(side, step).start()

    @pl.when(step == 1)
    def _():
        for side in (1, 0):
            for at in range(2):
                copy(side, at).wait()


def skip_block(ids, joinedT, gh, seq_ways, parts):
    frames, width = gh.shape
    rows = 2 * width // seq_ways // parts
    gshape = (parts, seq_ways // 2, rows, width)
    return pl.pallas_call(
        functools.partial(skip_kernel, seq_ways),
        out_shape=[jax.ShapeDtypeStruct(gshape, jnp.bfloat16)] * 2,
        grid_spec=pltpu.PrefetchScalarGridSpec(
            num_scalar_prefetch=1,
            grid=(2,),
            in_specs=[pl.BlockSpec((width, frames), lambda j, *_: (j, 0)), whole_block(gh.shape)],
            out_specs=[pl.BlockSpec(memory_space=pl.ANY)] * 2,
            scratch_shapes=[pltpu.VMEM((2,) + gshape, jnp.bfloat16), pltpu.SemaphoreType.DMA((2, 2))],
        ),
        compiler_params=pltpu.CompilerParams(vmem_limit_bytes=32 << 20),
        cost_estimate=cost(50),
        name="skip_block",
    )(ids, joinedT, gh)


def joined_kernel(gh_ref, w_ref, scale_ref, first_ref, second_ref):
    step = pl.program_id(0)
    value = dot_nt(gh_ref[...], w_ref[...]) * scale_ref[0:1, 0:1]

    @pl.when(step == 0)
    def _():
        first_ref[...] = value

    @pl.when(step == 1)
    def _():
        second_ref[...] = value


def joined_block(gh, w_skip, scale):
    frames, width = gh.shape
    out = jax.ShapeDtypeStruct((frames, width), jnp.float32)
    return pl.pallas_call(
        joined_kernel,
        out_shape=[out, out],
        grid_spec=pltpu.PrefetchScalarGridSpec(
            num_scalar_prefetch=0,
            grid=(2,),
            in_specs=[
                whole_block(gh.shape),
                pl.BlockSpec((width, width), lambda j: (j, 0)),
                whole_block(scale.shape),
            ],
            out_specs=[whole_block(out.shape)] * 2,
        ),
        compiler_params=pltpu.CompilerParams(vmem_limit_bytes=32 << 20),
        cost_estimate=cost(50),
        name="joined_block",
    )(gh, w_skip, scale)


def add_bf16(left, right):
    return (left.astype(jnp.float32) + right.astype(jnp.float32)).astype(jnp.bfloat16)


def add_kernel(pairs, ids_ref, *refs):
    for i in range(pairs):
        refs[2 * pairs + i][...] = add_bf16(refs[2 * i][...], refs[2 * i + 1][...]).reshape(
            refs[2 * pairs + i].shape
        )


def first_sum(ids, keep, got):
    _, _, _, z_ways, rows, width = keep.shape

    def source(half, axis, mine):
        def at(g, z, ids):
            bit = ids[axis]
            return half, bit if mine else 1 - bit, g, z, 0, 0

        return pl.BlockSpec((1, 1, 1, 1, rows, width), at)

    order = [(0, 2, False), (1, 3, False), (0, 2, True), (1, 3, True)]
    out = jax.ShapeDtypeStruct((2, z_ways, rows, width), jnp.bfloat16)
    return pl.pallas_call(
        functools.partial(add_kernel, 4),
        out_shape=[out] * 4,
        grid_spec=pltpu.PrefetchScalarGridSpec(
            num_scalar_prefetch=1,
            grid=(2, z_ways),
            in_specs=[source(*o) for o in order for _ in range(2)],
            out_specs=[pl.BlockSpec((1, 1, rows, width), lambda g, z, ids: (g, z, 0, 0))] * 4,
        ),
        cost_estimate=cost(20),
        name="first_sum",
    )(ids, *([keep, got] * 4))


def second_sum(ids, keep_a, got_a, keep_b, got_b):
    _, z_ways, rows, width = keep_a.shape

    def source(axis, mine):
        def at(z, ids):
            bit = ids[axis]
            return bit if mine else 1 - bit, z, 0, 0

        return pl.BlockSpec((1, 1, rows, width), at)

    order = [(3, False), (2, False), (3, True), (2, True)]
    out = jax.ShapeDtypeStruct((z_ways, rows, width), jnp.bfloat16)
    return pl.pallas_call(
        functools.partial(add_kernel, 4),
        out_shape=[out] * 4,
        grid_spec=pltpu.PrefetchScalarGridSpec(
            num_scalar_prefetch=1,
            grid=(z_ways,),
            in_specs=[source(*o) for o in order for _ in range(2)],
            out_specs=[pl.BlockSpec((1, rows, width), lambda z, ids: (z, 0, 0))] * 4,
        ),
        cost_estimate=cost(10),
        name="second_sum",
    )(ids, *([keep_a, got_a, keep_b, got_b] * 2))


def third_kernel(ids_ref, keep_a, got_a, keep_b, got_b, *outs):
    for j, out in enumerate(outs):
        at = ids_ref[4] ^ j
        out[0] = add_bf16(keep_a[at], got_a[at])
        out[1] = add_bf16(keep_b[at], got_b[at])


def third_sum(ids, keep_a, got_a, keep_b, got_b):
    z_ways, rows, width = keep_a.shape
    out = jax.ShapeDtypeStruct((2, rows, width), jnp.bfloat16)
    return pl.pallas_call(
        third_kernel,
        out_shape=[out] * z_ways,
        grid_spec=pltpu.PrefetchScalarGridSpec(
            num_scalar_prefetch=1,
            grid=(1,),
            in_specs=[whole_block(keep_a.shape)] * 4,
            out_specs=[whole_block(out.shape)] * z_ways,
        ),
        cost_estimate=cost(10),
        name="third_sum",
    )(ids, keep_a, got_a, keep_b, got_b)


def fourth_kernel(*refs):
    total = refs[0][...].astype(jnp.float32)
    for r in refs[1:-1]:
        total = total + r[...].astype(jnp.float32)
    refs[-1][...] = total.astype(jnp.bfloat16)


def fourth_sum(terms):
    shape = terms[0].shape
    return pl.pallas_call(
        fourth_kernel,
        out_shape=jax.ShapeDtypeStruct(shape, jnp.bfloat16),
        grid=(1,),
        in_specs=[whole_block(shape)] * len(terms),
        out_specs=whole_block(shape),
        cost_estimate=cost(10),
        name="fourth_sum",
    )(*terms)


def place_kernel(streams, plan, ids_ref, scale_ref, *refs):
    blocks, outs = refs[: 4 * streams], refs[4 * streams :]
    x, y = ids_ref[2], ids_ref[3]
    scale = scale_ref[0:1, 0:1]
    for stream, row, rows, lane, lanes, out, row_of, lane_of in plan:
        for d in range(4):
            own_x, own_y = x ^ (d & 1), y ^ (d >> 1)
            for half in range(2):
                k = own_x * 2 + own_y if half == 0 else 4 + own_y * 2 + own_x
                tile = blocks[4 * stream + d][half, row : row + rows, lane : lane + lanes]
                outs[out][row_of(k), lane_of(k)] = tile.astype(jnp.float32) * scale


def place_blocks(ids, scale, streams, plan, shapes):
    blocks = [b for s in streams for b in s]
    outs = [jax.ShapeDtypeStruct(s, jnp.float32) for s in shapes]
    return pl.pallas_call(
        functools.partial(place_kernel, len(streams), plan),
        out_shape=outs,
        grid_spec=pltpu.PrefetchScalarGridSpec(
            num_scalar_prefetch=1,
            grid=(1,),
            in_specs=[whole_block(a.shape) for a in (scale, *blocks)],
            out_specs=[whole_block(o.shape) for o in outs],
        ),
        compiler_params=pltpu.CompilerParams(vmem_limit_bytes=32 << 20),
        cost_estimate=cost(20),
        name="place_blocks",
    )(ids, scale, *blocks)


def span(start, size):
    return pl.ds(pl.multiple_of(start, size), size)


def ada_kernel(groups, pad_u, numerator, time_ref, *refs):
    f32 = jnp.float32
    parts, (weight_ref, vector_ref, scale_ref) = refs[:groups], refs[groups:]
    table = pl.program_id(0)
    base = 6 * pad_u
    count = parts[0][base + 12 : base + 13, 0:1]
    for p in parts[1:]:
        count = count + p[base + 12 : base + 13, 0:1]
    scale = numerator / count
    rows = jnp.concatenate([p[pl.ds(pl.multiple_of(table * pad_u, 8), pad_u), :] for p in parts], axis=0) * scale
    vector_ref[pl.ds(table, 1), :] = jnp.sum(rows, axis=0, keepdims=True)
    operand = jnp.concatenate(list(split3(rows)), axis=0)
    weight_ref[...] = dot(time_ref[...], operand)

    @pl.when(table == 0)
    def _():
        total = parts[0][base : base + 16, :]
        for p in parts[1:]:
            total = total + p[base : base + 16, :]
        vector_ref[8:24, :] = total * scale
        scale_ref[...] = jnp.broadcast_to(scale, scale_ref.shape)


def ada_block(time3, parts, utts, numerator):
    pad_u = table_rows(utts)
    width = parts[0].shape[1]
    own = time3.shape[0]
    f32 = jnp.float32
    return pl.pallas_call(
        functools.partial(ada_kernel, len(parts), pad_u, numerator),
        out_shape=[
            jax.ShapeDtypeStruct((own, 6 * width), f32),
            jax.ShapeDtypeStruct((24, width), f32),
            jax.ShapeDtypeStruct((8, 128), f32),
        ],
        grid=(6,),
        in_specs=[whole_block(time3.shape)] + [whole_block(p.shape) for p in parts],
        out_specs=[
            pl.BlockSpec((own, width), lambda j: (0, j)),
            whole_block((24, width)),
            whole_block((8, 128)),
        ],
        cost_estimate=cost(50),
        name="ada_block",
    )(time3, *parts)


def sum_exchange(value, axis, bit):
    ways = lax.axis_size(axis)
    return lax.ppermute(value, axis, [(i, i ^ bit) for i in range(ways)])


def axis_bits(ways):
    return [1 << i for i in range(ways.bit_length() - 1)]


def reduce_stages(ids, keep, send):
    batch_ways = lax.axis_size("batch")
    x_bit, y_bit = 1, 1 << ((batch_ways.bit_length() - 1) // 2)
    _, z_ways, rows, width = keep.shape
    shape = (2, 2, 2, z_ways, rows, width)
    got = sum_exchange(send, "seq", 1)
    send_a, send_b, keep_a, keep_b = first_sum(ids, keep.reshape(shape), got.reshape(shape))
    send_a, send_b = follow([send_a, send_b], (yield [send_a, send_b]))
    got = [sum_exchange(send_a, "batch", x_bit), sum_exchange(send_b, "batch", y_bit)]
    got_a, got_b = follow(got, (yield got))
    send_a, send_b, keep_a, keep_b = second_sum(ids, keep_a, got_a, keep_b, got_b)
    send_a, send_b = follow([send_a, send_b], (yield [send_a, send_b]))
    got = [sum_exchange(send_a, "batch", y_bit), sum_exchange(send_b, "batch", x_bit)]
    got_a, got_b = follow(got, (yield got))
    own, *away = third_sum(ids, keep_a, got_a, keep_b, got_b)
    away = follow(away, (yield away))
    got = [sum_exchange(a, "seq", 2 * (j + 1)) for j, a in enumerate(away)]
    got = follow(got, (yield got))
    block = fourth_sum([own] + got)
    for bit in axis_bits(batch_ways):
        if bit not in (x_bit, y_bit):
            block = add_bf16(block, sum_exchange(block, "batch", bit))
    (block,) = follow([block], (yield [block]))
    yield [block] + [sum_exchange(block, "batch", bit) for bit in (x_bit, y_bit, x_bit | y_bit)]


def advance(stages, steps, token=None):
    value = stages.send(token)
    for _ in range(steps - 1):
        value = next(stages)
    return value


def last_stage(stages, token=None):
    value = stages.send(token)
    for value in stages:
        pass
    return value


def follow(values, token):
    return values if token is None else [after(v, token) for v in values]


def after(value, *others):
    return lax.optimization_barrier((value,) + others)[0]


def gather_groups(value):
    return [value] + [sum_exchange(value, "batch", i) for i in range(1, lax.axis_size("batch"))]


def sum_seq(value):
    for bit in axis_bits(lax.axis_size("seq")):
        value = value + sum_exchange(value, "seq", bit)
    return value


def shards(
    tokens_in,
    skip_in,
    condition,
    cotangent,
    time_embed,
    lengths,
    key_mask,
    drop_mask,
    loss_mask,
    w_skip,
    b_skip,
    w_ada,
    b_ada,
    w_qkv,
    b_qkv,
    w_out,
    b_out,
    w_up,
    b_up,
    w_down,
    b_down,
):
    f32, bf16 = jnp.float32, jnp.bfloat16
    seq_ways, batch_ways = lax.axis_size("seq"), lax.axis_size("batch")
    seq_rank = lax.axis_index("seq")
    frames, width = tokens_in.shape[1:]
    group_frames = frames * seq_ways
    heads_local = HEADS // seq_ways
    utts = lengths.shape[1]
    lengths_row, drop = lengths[0], drop_mask[0]
    batch_rank = lax.axis_index("batch")
    side = 1 << ((batch_ways.bit_length() - 1) // 2)
    ids = [lax.rem(seq_rank, 2), seq_rank, lax.rem(batch_rank, 2), lax.rem(batch_rank // side, 2), seq_rank // 2]
    ids = jnp.stack(ids).astype(jnp.int32)
    ok = key_mask.reshape(seq_ways, 1, frames)
    exchange = functools.partial(lax.all_to_all, axis_name="seq", split_axis=0, concat_axis=0, tiled=True)

    time_act = jax.nn.silu(time_embed[0]).astype(bf16)
    time_rows = jnp.pad(time_act, ((0, 16 - utts), (0, 0)))

    def modulation(first, last):
        return jnp.dot(time_rows, w_ada[:, first:last], preferred_element_type=f32) + b_ada[
            first:last
        ].astype(f32)

    mods_a = modulation(0, 2 * width)
    hidden, joinedT, naT, na = head_block(
        lengths_row, ids, drop, tokens_in[0], skip_in[0], condition[0], mods_a, w_skip, b_skip[None]
    )
    received = []
    for c in range(heads_local):
        packed = qkv_block(lengths_row, ids, drop, na, w_qkv, b_qkv[None], c, seq_ways)
        received.append(exchange(packed))

    mods_rest = modulation(2 * width, 6 * width)
    own = width // seq_ways
    pad_u = table_rows(utts)
    time_own = lax.dynamic_slice_in_dim(jnp.concatenate(gather_groups(time_rows[:pad_u])), seq_rank * own, own, axis=1)
    time3 = jnp.tile(time_own.T, (1, 3))

    received[0] = after(received[0], mods_rest)
    head_out, log_totals, returned = [], [], []
    for c in range(heads_local):
        out, log_total = attend(lengths_row, received[c], ok)
        head_out.append(out)
        log_totals.append(log_total)
        returned.append(exchange(after(out, *returned)))
        if c < heads_local - 1:
            received[c + 1] = after(received[c + 1], out)
    mid = mid_block(
        lengths_row,
        ids,
        returned,
        hidden,
        mods_rest,
        cotangent[0],
        loss_mask,
        w_out,
        b_out[None],
        w_up,
        b_up[None],
        w_down,
        b_down[None],
        PARTS,
    )
    output, after_grad, mid_small = mid[:3]
    grad_att = mid[3 : 3 + heads_local]
    grad_heads = [exchange(g) for g in grad_att]
    up = reduce_stages(ids, *mid[3 + heads_local : 5 + heads_local])
    down = reduce_stages(ids, *mid[5 + heads_local :])

    ahead = advance(up, 1) + advance(down, 1)
    grad_local = []
    for c in range(heads_local):
        operand = after(grad_heads[c], *ahead)
        moving = advance(up, 1)
        if c > 0:
            moving = moving + advance(down, 1)
        grad = attend_back(lengths_row, received[c], ok, head_out[c], operand, log_totals[c])
        grad_local.append(exchange(after(grad, *moving, *grad_heads[c + 1 :])))
        ahead = [grad] + advance(up, 1, grad)
    ahead = ahead + (advance(down, 1, grad) if heads_local > 1 else advance(down, 2))
    acc, biases, part_blocks = None, [], []
    for c in range(heads_local):
        acc, bias, keep, send = back_block(
            lengths_row, ids, drop, after(grad_local[c], *ahead), naT, w_qkv, acc, c, PARTS
        )
        biases.append(bias)
        part_blocks.append(reduce_stages(ids, keep, send))
        ahead = advance(down, 2) if c == 0 else []
        ahead = ahead + advance(part_blocks[c], 1)
    if heads_local == 1:
        advance(up, 2)
    gh, small = norm_block(lengths_row, ids, acc, hidden, after_grad, mods_a, loss_mask, mid_small, biases)
    ahead = ahead + [x for blocks in part_blocks[:-1] for x in advance(blocks, 2)]
    keep, send = skip_block(ids, joinedT, after(gh, *ahead), seq_ways, PARTS)
    skip_blocks = reduce_stages(ids, keep, send)
    token = advance(skip_blocks, 1)[0]
    groups = gather_groups(sum_seq(small))
    numerator = float(group_frames * batch_ways)
    grad_w_ada, vectors, scale = ada_block(time3, groups, utts, numerator)
    grad_tokens, grad_skip = joined_block(gh, w_skip, scale)
    up, down = last_stage(up, token), last_stage(down, token)
    part_blocks = [last_stage(b, token) for b in part_blocks]
    skip_blocks = last_stage(skip_blocks)

    ff = w_up.shape[1]
    chunks = ff // width
    up_part = chunks * own // PARTS
    down_part = ff // seq_ways // PARTS
    out_part = own // PARTS
    per_chunk = own // up_part
    whole_lanes = lambda k: span(0, width)
    grad_w_up, grad_w_down, grad_w_out = place_blocks(
        ids,
        scale,
        [up, down],
        [
            (
                *(0, 0, up_part, 0, width, 0),
                lambda k: span(lax.rem(k, per_chunk) * up_part, up_part),
                lambda k: span(k // per_chunk * width, width),
            ),
            (1, 0, down_part, 0, width, 1, lambda k: span(k * down_part, down_part), whole_lanes),
            (1, down_part, out_part, 0, width, 2, lambda k: span(k * out_part, out_part), whole_lanes),
        ],
        [(own, ff), (ff // seq_ways, width), (own, width)],
    )
    cols = seq_ways * HEAD_DIM
    (grad_w_qkv,) = place_blocks(
        ids,
        scale,
        part_blocks,
        [
            (
                *(c, 0, out_part, p * cols, cols, 0),
                lambda k: span(k * out_part, out_part),
                lambda k, at=p * width + c * cols: span(at, cols),
            )
            for c in range(heads_local)
            for p in range(3)
        ],
        [(own, 3 * width)],
    )
    skip_part = 2 * own // PARTS
    (grad_w_skip,) = place_blocks(
        ids,
        scale,
        [skip_blocks],
        [(0, 0, skip_part, 0, width, 0, lambda k: span(k * skip_part, skip_part), whole_lanes)],
        [(2 * own, width)],
    )

    def own_slice(vector):
        vector = vector.reshape(-1)
        size = vector.shape[0] // seq_ways
        return lax.dynamic_slice_in_dim(vector, seq_rank * size, size)

    grad_b_ada = own_slice(vectors[:6])
    grad_b_qkv = own_slice(vectors[8:11])
    grad_b_skip = own_slice(vectors[11])
    grad_b_out = own_slice(vectors[12])
    grad_b_down = own_slice(vectors[13])
    grad_b_up = own_slice(vectors[14 : 14 + chunks])
    return (
        output[None],
        grad_tokens[None],
        grad_skip[None],
        grad_w_skip,
        grad_b_skip,
        grad_w_ada,
        grad_b_ada,
        grad_w_qkv,
        grad_b_qkv,
        grad_w_out,
        grad_b_out,
        grad_w_up,
        grad_b_up,
        grad_w_down,
        grad_b_down,
    )


def solution(mesh):
    in_specs = (
        P("batch", "seq", None),
        P("batch", "seq", None),
        P("batch", "seq", None),
        P("batch", "seq", None),
        P("batch", None, None),
        P("batch", None),
        P("batch", None),
        P("batch", None),
        P("batch", "seq"),
        P(),
        P(),
        P(),
        P(),
        P(),
        P(),
        P(),
        P(),
        P(),
        P(),
        P(),
        P(),
    )
    out_specs = (
        P("batch", "seq", None),
        P("batch", "seq", None),
        P("batch", "seq", None),
        P("seq", None),
        P("seq"),
        P("seq", None),
        P("seq"),
        P("seq", None),
        P("seq"),
        P("seq", None),
        P("seq"),
        P("seq", None),
        P("seq"),
        P("seq", None),
        P("seq"),
    )
    return jax.shard_map(shards, mesh=mesh, in_specs=in_specs, out_specs=out_specs, check_vma=False)
```

```python
import functools

import jax
import jax.numpy as jnp
from jax import lax
from jax.experimental import pallas as pl
from jax.experimental.pallas import tpu as pltpu
from jax.sharding import PartitionSpec as P

HEADS = 16
HEAD_DIM = 64
PARTS = 8
BIG = 1e30
DH = 64
BQ = 512
BK = 512


def cost(weight):
    return pl.CostEstimate(flops=weight * 100000000, bytes_accessed=weight * 100000, transcendentals=0)


def onehot_rows(lengths_ref, utts, rows, base, width):
    row = lax.broadcasted_iota(jnp.int32, (rows, width), 0)
    col = base + lax.broadcasted_iota(jnp.int32, (rows, width), 1)
    start = jnp.int32(0)
    hot = jnp.zeros((rows, width), jnp.float32)
    for u in range(utts):
        end = start + lengths_ref[u]
        hot = jnp.where((row == u) & (col >= start) & (col < end), 1.0, hot)
        start = end
    return hot


def key_range(lengths_ref, utts, first, last):
    start = jnp.int32(0)
    low, high = jnp.int32(0), jnp.int32(0)
    for u in range(utts):
        end = start + lengths_ref[u]
        low = jnp.where((start <= first) & (first < end), start, low)
        high = jnp.where((start <= last) & (last < end), end, high)
        start = end
    return low // BK, (high + BK - 1) // BK


def aug_rows(utts):
    return -(-utts // 16) * 16


def split3(row):
    a = row.astype(jnp.bfloat16)
    rest = row - a.astype(jnp.float32)
    b = rest.astype(jnp.bfloat16)
    c = (rest - b.astype(jnp.float32)).astype(jnp.bfloat16)
    return a, b, c


def pad_rows(parts, total):
    have = sum(p.shape[0] for p in parts)
    if have < total:
        parts = parts + [jnp.zeros((total - have, parts[0].shape[1]), parts[0].dtype)]
    return jnp.concatenate(parts, axis=0)


def rows16(rows, width):
    idx = lax.broadcasted_iota(jnp.int32, (16, width), 0)
    out = jnp.zeros((16, width), jnp.float32)
    for i, r in enumerate(rows):
        out = jnp.where(idx == i, r, out)
    return out.astype(jnp.bfloat16)


def fwd_kernel(utts, lengths_ref, qkv_ref, ok_ref, out_ref, lse_ref, kaug, vaug):
    sources, _, frames = qkv_ref.shape
    per = frames // BQ
    pad_u = aug_rows(utts)
    step = pl.program_id(0)

    @pl.when(step == 0)
    def _():
        def build(s, c):
            hot = onehot_rows(lengths_ref, utts, pad_u, s * frames, frames)
            ok = ok_ref[s].astype(jnp.float32)
            block = qkv_ref[s]
            one = jnp.ones((1, frames), jnp.float32)
            kT = pad_rows(
                [block[DH : 2 * DH], (1.0 - hot).astype(jnp.bfloat16), rows16([1.0 - ok], frames)], 128
            )
            kaug[pl.ds(pl.multiple_of(s * frames, frames), frames), :] = kT.T
            vT = jnp.concatenate([block[2 * DH :], rows16([one], frames)], axis=0)
            for t in range(frames // BK):
                vaug[s * (frames // BK) + t] = vT[:, t * BK : (t + 1) * BK]
            return c

        lax.fori_loop(0, sources, build, 0)

    block = qkv_ref[step]
    hot_q = onehot_rows(lengths_ref, utts, pad_u, step * frames, frames)
    qT = (block[:DH].astype(jnp.float32) * 0.125)
    one = jnp.ones((1, frames), jnp.float32)
    qaug = pad_rows(
        [qT.astype(jnp.bfloat16), (hot_q * -BIG).astype(jnp.bfloat16), rows16([one * -BIG], frames)], 128
    )
    kT = block[DH : 2 * DH].astype(jnp.float32)
    vT = block[2 * DH :].astype(jnp.float32)
    ok = ok_ref[step] > 0
    s_self = jnp.sum(qT * kT, axis=0, keepdims=True)
    m0 = jnp.where(ok, -3e38, s_self)
    acc0 = jnp.concatenate([jnp.where(ok, 0.0, vT), jnp.where(ok, 0.0, jnp.ones((16, frames), jnp.float32))], axis=0)
    for t in range(per):
        cols = slice(t * BQ, (t + 1) * BQ)
        low, high = key_range(lengths_ref, utts, step * frames + t * BQ, step * frames + (t + 1) * BQ - 1)
        q_b = qaug[:, cols]

        def body(j, carry):
            m, acc = carry
            s = jnp.dot(kaug[pl.ds(pl.multiple_of(j * BK, BK), BK), :], q_b, preferred_element_type=jnp.float32)
            m_new = jnp.maximum(m, jnp.max(s, axis=0, keepdims=True))
            p = jnp.exp(s - m_new).astype(jnp.bfloat16)
            alpha = jnp.exp(m - m_new)
            acc = acc * alpha + jnp.dot(vaug[j], p, preferred_element_type=jnp.float32)
            return m_new, acc

        m, acc = lax.fori_loop(low, high, body, (m0[:, cols], acc0[:, cols]))
        total = acc[DH : DH + 1]
        out_ref[0, :, cols] = (acc[:DH] / total).astype(jnp.bfloat16)
        lse_ref[0, :, cols] = m + jnp.log(total)


def attend(lengths, qkv, ok):
    sources, _, frames = qkv.shape
    total = sources * frames
    utts = lengths.shape[0]
    whole = lambda shape: pl.BlockSpec(shape, lambda i, *_: (0,) * len(shape))
    return pl.pallas_call(
        functools.partial(fwd_kernel, utts),
        out_shape=(
            jax.ShapeDtypeStruct((sources, DH, frames), jnp.bfloat16),
            jax.ShapeDtypeStruct((sources, 1, frames), jnp.float32),
        ),
        grid_spec=pltpu.PrefetchScalarGridSpec(
            num_scalar_prefetch=1,
            grid=(sources,),
            in_specs=[whole(qkv.shape), whole(ok.shape)],
            out_specs=(
                pl.BlockSpec((1, DH, frames), lambda i, *_: (i, 0, 0)),
                pl.BlockSpec((1, 1, frames), lambda i, *_: (i, 0, 0)),
            ),
            scratch_shapes=[
                pltpu.VMEM((total, 128), jnp.bfloat16),
                pltpu.VMEM((total // BK, DH + 16, BK), jnp.bfloat16),
            ],
        ),
        cost_estimate=cost(250),
        name="attend",
    )(lengths, qkv, ok)


def bwd_kernel(utts, lengths_ref, qkv_ref, ok_ref, o_ref, do_ref, lse_ref, out_ref, kaug, vnat, kT_s, dk, dv):
    sources, _, frames = qkv_ref.shape
    per = frames // BK
    pad_u = aug_rows(utts)
    step = pl.program_id(0)
    f32 = jnp.float32

    @pl.when(step == 0)
    def _():
        def build(s, c):
            hot = onehot_rows(lengths_ref, utts, pad_u, s * frames, frames)
            ok = ok_ref[s]
            block = qkv_ref[s]
            one = jnp.ones((1, frames), f32)
            kT = block[DH : 2 * DH]
            vT = block[2 * DH :]
            kA = pad_rows(
                [kT, (1.0 - hot).astype(jnp.bfloat16), rows16([1.0 - ok.astype(f32), one, one, one], frames)], 128
            )
            rows = pl.ds(pl.multiple_of(s * frames, frames), frames)
            kaug[rows, :] = kA.T
            vnat[rows, :] = pad_rows([vT, rows16([one, one, one], frames)], 128).T
            qT = block[:DH].astype(f32) * 0.125
            do = do_ref[s].astype(f32)
            s_self = jnp.sum(qT * kT.astype(f32), axis=0, keepdims=True)
            delta = jnp.sum(do * o_ref[s].astype(f32), axis=0, keepdims=True)
            p_self = jnp.where(ok > 0, 0.0, jnp.exp(s_self - lse_ref[s]))
            ds_self = p_self * (jnp.sum(do * vT.astype(f32), axis=0, keepdims=True) - delta)
            dk0 = ds_self * qT
            dv0 = p_self * do
            for t in range(per):
                cols = slice(t * BK, (t + 1) * BK)
                kT_s[s * per + t] = kT[:, cols]
                dk[s * per + t] = dk0[:, cols]
                dv[s * per + t] = dv0[:, cols]
            return c

        lax.fori_loop(0, sources, build, 0)

    block = qkv_ref[step]
    one = jnp.ones((1, frames), f32)
    hot_q = onehot_rows(lengths_ref, utts, pad_u, step * frames, frames)
    qT = block[:DH].astype(f32) * 0.125
    qTb = qT.astype(jnp.bfloat16)
    kT = block[DH : 2 * DH].astype(f32)
    vT = block[2 * DH :].astype(f32)
    ok = ok_ref[step]
    dob = do_ref[step]
    do = dob.astype(f32)
    lse = lse_ref[step]
    delta = jnp.sum(do * o_ref[step].astype(f32), axis=0, keepdims=True)
    l3 = [-r.astype(f32) for r in split3(lse)]
    d3 = [-r.astype(f32) for r in split3(delta)]
    qaug = pad_rows([qTb, (hot_q * -BIG).astype(jnp.bfloat16), rows16([one * -BIG] + l3, frames)], 128)
    doaug = pad_rows([dob, rows16(d3, frames)], 128)
    s_self = jnp.sum(qT * kT, axis=0, keepdims=True)
    p_self = jnp.where(ok > 0, 0.0, jnp.exp(s_self - lse))
    ds_self = p_self * (jnp.sum(do * vT, axis=0, keepdims=True) - delta)
    dq0 = ds_self * kT
    nt = (((1,), (1,)), ((), ()))
    for t in range(frames // BQ):
        cols = slice(t * BQ, (t + 1) * BQ)
        low, high = key_range(lengths_ref, utts, step * frames + t * BQ, step * frames + (t + 1) * BQ - 1)
        q_a = qaug[:, cols]
        q_b = qTb[:, cols]
        do_a = doaug[:, cols]
        do_b = dob[:, cols]

        def body(j, dq):
            rows = pl.ds(pl.multiple_of(j * BK, BK), BK)
            s = jnp.dot(kaug[rows, :], q_a, preferred_element_type=f32)
            dp = jnp.dot(vnat[rows, :], do_a, preferred_element_type=f32)
            p = jnp.exp(s)
            ds = (p * dp).astype(jnp.bfloat16)
            dv[j] += lax.dot_general(do_b, p.astype(jnp.bfloat16), nt, preferred_element_type=f32)
            dk[j] += lax.dot_general(q_b, ds, nt, preferred_element_type=f32)
            return dq + jnp.dot(kT_s[j], ds, preferred_element_type=f32)

        dq = lax.fori_loop(low, high, body, dq0[:, cols])
        out_ref[step, :DH, cols] = (dq * 0.125).astype(jnp.bfloat16)

    @pl.when(step == sources - 1)
    def _():
        def finish(s, c):
            for t in range(per):
                cols = slice(t * BK, (t + 1) * BK)
                out_ref[s, DH : 2 * DH, cols] = dk[s * per + t].astype(jnp.bfloat16)
                out_ref[s, 2 * DH :, cols] = dv[s * per + t].astype(jnp.bfloat16)
            return c

        lax.fori_loop(0, sources, finish, 0)


def attend_back(lengths, qkv, ok, out, grad, lse):
    sources, _, frames = qkv.shape
    total = sources * frames
    utts = lengths.shape[0]
    whole = lambda shape: pl.BlockSpec(shape, lambda i, *_: (0,) * len(shape))
    return pl.pallas_call(
        functools.partial(bwd_kernel, utts),
        out_shape=jax.ShapeDtypeStruct(qkv.shape, jnp.bfloat16),
        grid_spec=pltpu.PrefetchScalarGridSpec(
            num_scalar_prefetch=1,
            grid=(sources,),
            in_specs=[whole(a.shape) for a in (qkv, ok, out, grad, lse)],
            out_specs=whole(qkv.shape),
            scratch_shapes=[
                pltpu.VMEM((total, 128), jnp.bfloat16),
                pltpu.VMEM((total, 128), jnp.bfloat16),
                pltpu.VMEM((total // BK, DH, BK), jnp.bfloat16),
                pltpu.VMEM((total // BK, DH, BK), jnp.float32),
                pltpu.VMEM((total // BK, DH, BK), jnp.float32),
            ],
        ),
        cost_estimate=cost(320),
        name="attend_back",
    )(lengths, qkv, ok, out, grad, lse)


FF_TILE = 512
EPS = 1e-06


def dot(left, right):
    return jnp.dot(left, right, preferred_element_type=jnp.float32)


def dot_nt(left, right):
    return lax.dot_general(left, right, (((1,), (1,)), ((), ())), preferred_element_type=jnp.float32)


def norm_stats(x):
    mean = jnp.mean(x, axis=1, keepdims=True)
    centred = x - mean
    rstd = lax.rsqrt(jnp.mean(centred * centred, axis=1, keepdims=True) + EPS)
    return centred * rstd, rstd


def norm_back(grad, normed, rstd):
    first = jnp.mean(grad, axis=1, keepdims=True)
    second = jnp.mean(grad * normed, axis=1, keepdims=True)
    return rstd * (grad - first - normed * second)


def mods_operand(mods_ref):
    rows = mods_ref[...]
    return pad_rows(list(split3(rows)), 128)


def table_rows(utts):
    return -(-utts // 8) * 8


def sum_rows(hot, utts_pad, frames):
    idx = lax.broadcasted_iota(jnp.int32, (16, frames), 0)
    ones = jnp.where(idx == 0, 1.0, 0.0).astype(jnp.bfloat16)
    return jnp.concatenate([hot.astype(jnp.bfloat16), ones], axis=0)


def mid_kernel(
    dims,
    lengths_ref,
    ids_ref,
    *refs,
):
    seq_ways, heads_local, utts, ff = dims
    att_refs = refs[:heads_local]
    (
        hidden_ref,
        mods_ref,
        cot_ref,
        loss_ref,
        w_out_ref,
        b_out_ref,
        w_up_ref,
        b_up_ref,
        w_down_ref,
        b_down_ref,
    ) = refs[heads_local : heads_local + 10]
    outs = refs[heads_local + 10 :]
    output_ref, after_grad_ref, small_ref = outs[:3]
    gatt_refs = outs[3 : 3 + heads_local]
    refs_out = outs[3 + heads_local : 5 + heads_local]
    (
        attT,
        attn_proj,
        after,
        nf,
        nfT,
        gff,
        ff_acc,
        gnf_acc,
        sums,
        cols,
        madd,
        grads,
        sems,
    ) = outs[5 + heads_local :]
    f32, bf16 = jnp.float32, jnp.bfloat16
    step = pl.program_id(0)
    steps = pl.num_programs(0)
    core = ids_ref[0]
    rank = ids_ref[1]
    frames, width = hidden_ref.shape
    up_rows = width // seq_ways
    down_rows = FF_TILE
    z_ways = seq_ways // 2
    parts = grads.shape[1]
    pad_u = table_rows(utts)
    ff_total = ff
    up_part = ff_total // width * up_rows // parts
    down_block = ff_total // seq_ways
    down_part = down_block // parts
    out_part = up_rows // parts

    def mod(index):
        return dot(cols[...], madd[:, index * width : (index + 1) * width])

    def grad_out():
        loss = cols[:, 48:49].astype(f32)
        return cot_ref[...].astype(f32) * loss

    @pl.when(step == 0)
    def _():
        hot = onehot_rows(lengths_ref, utts, 16, rank * frames, frames)
        hotb = hot.astype(bf16)
        idx = lax.broadcasted_iota(jnp.int32, (16, frames), 0)
        loss = jnp.where(idx == 0, loss_ref[...].astype(f32), 0.0).astype(bf16)
        cols[...] = pad_rows([hotb, hotb, hotb, loss], 128).T
        sums[...] = sum_rows(hot, 16, frames)
        madd[...] = mods_operand(mods_ref)
        for c in range(heads_local):
            for s in range(seq_ways):
                attT[(c * seq_ways + s) * DH : (c * seq_ways + s + 1) * DH, :] = att_refs[c][s]
        proj = dot(attT[...].T, w_out_ref[...]) + b_out_ref[...].astype(f32)
        attn_proj[...] = proj
        mixed = hidden_ref[...] + mod(0) * proj
        after[...] = mixed
        normed, _ = norm_stats(mixed)
        value = (normed * (1.0 + mod(2)) + mod(1)).astype(bf16)
        nf[...] = value
        nfT[...] = value.T
        gff[...] = (grad_out() * mod(3)).astype(bf16)
        small_ref[4 * pad_u :, :] = jnp.zeros((8, width), f32)

    up = dot(nf[...], w_up_ref[...]) + b_up_ref[...].astype(f32)
    inner = 0.7978845608028654 * (up + 0.044715 * (up * up * up))
    tanh = jnp.tanh(inner)
    cdf = 0.5 * (1.0 + tanh)
    act = (up * cdf).astype(bf16)
    slope = cdf + 0.5 * up * (1.0 - tanh * tanh) * (
        0.7978845608028654 * (1.0 + (3 * 0.044715) * (up * up))
    )
    ff_part = dot(act, w_down_ref[...])
    gup = (dot_nt(gff[...], w_down_ref[...]) * slope).astype(bf16)
    gnf_part = dot_nt(gup, w_up_ref[...])

    @pl.when(step == 0)
    def _():
        ff_acc[...] = ff_part
        gnf_acc[...] = gnf_part

    @pl.when(step > 0)
    def _():
        ff_acc[...] += ff_part
        gnf_acc[...] += gnf_part

    halves = width // FF_TILE
    chunk = step // halves
    half = step % halves
    col = pl.ds(pl.multiple_of(half * FF_TILE, FF_TILE), FF_TILE)
    per_chunk = up_rows // up_part
    small_ref[pl.ds(4 * pad_u + 2 + chunk, 1), col] = dot(sums[16:32, :], gup)[:1]
    grad_w_up = dot(nfT[...], gup).astype(bf16)
    for s in range(seq_ways):
        side = jnp.where(core == s % 2, 0, 1)
        for h in range(per_chunk):
            lo = s * up_rows + h * up_part
            grads[side, chunk * per_chunk + h, s // 2, 0:up_part, col] = grad_w_up[lo : lo + up_part]
    grad_w_down = dot(act.T, gff[...]).astype(bf16)
    blocks = FF_TILE // down_block
    copies = []
    for b in range(blocks):
        s = step * blocks + b
        side = jnp.where(core == s % 2, 0, 1)
        for k in range(parts):
            lo = b * down_block + k * down_part
            grads[side, k, s // 2, up_part : up_part + down_part, :] = grad_w_down[lo : lo + down_part]

    def region_copy(side, where, index):
        return pltpu.make_async_copy(
            grads.at[side].at[where], refs_out[side].at[where], sems.at[side, index]
        )

    def up_copy(side, j):
        where = (
            pl.ds((j // halves) * per_chunk, per_chunk),
            slice(None),
            pl.ds(0, up_part),
            pl.ds(pl.multiple_of((j % halves) * FF_TILE, FF_TILE), FF_TILE),
        )
        return region_copy(side, where, j)

    def down_copy(side, z, index):
        return region_copy(side, (slice(None), pl.ds(z, 1), pl.ds(up_part, down_part)), index)

    def out_copy(side):
        where = (slice(None), slice(None), pl.ds(up_part + down_part, out_part))
        return region_copy(side, where, ff_total // FF_TILE + z_ways)

    base = ff_total // FF_TILE
    for side in range(2):
        up_copy(side, step).start()
    for b in range(blocks):
        s = step * blocks + b
        for side in range(2):

            @pl.when(lax.rem(s + core, 2) == side)
            def _():
                down_copy(side, s // 2, base + s // 2).start()

    @pl.when(step == steps - 1)
    def _():
        ff_out = ff_acc[...] + b_down_ref[...].astype(f32)
        mixed = after[...]
        go = grad_out()
        output_ref[...] = (mixed + mod(3) * ff_out).astype(bf16)
        rows = sums[...]
        small_ref[3 * pad_u : 4 * pad_u, :] = dot(rows, (go * ff_out).astype(bf16))[:pad_u]
        normed, rstd = norm_stats(mixed)
        gnf = gnf_acc[...]
        small_ref[pad_u : 2 * pad_u, :] = dot(rows, gnf.astype(bf16))[:pad_u]
        small_ref[2 * pad_u : 3 * pad_u, :] = dot(rows, (gnf * normed).astype(bf16))[:pad_u]
        g_after = go + norm_back(gnf * (1.0 + mod(2)), normed, rstd)
        after_grad_ref[...] = g_after
        small_ref[0:pad_u, :] = dot(rows, (g_after * attn_proj[...]).astype(bf16))[:pad_u]
        gattn = (g_after * mod(0)).astype(bf16)
        small_ref[4 * pad_u : 4 * pad_u + 1, :] = dot(rows, gattn)[16:17]
        small_ref[4 * pad_u + 1 : 4 * pad_u + 2, :] = dot(rows, gff[...])[16:17]
        gattT = dot_nt(w_out_ref[...], gattn).astype(bf16)
        for c in range(heads_local):
            for s in range(seq_ways):
                lo = (c * seq_ways + s) * DH
                gatt_refs[c][s] = gattT[lo : lo + DH]
        grad_w_out = dot(attT[...], gattn).astype(bf16)
        for s in range(seq_ways):
            side = jnp.where(core == s % 2, 0, 1)
            for k in range(parts):
                lo = s * up_rows + k * out_part
                grads[side, k, s // 2, up_part + down_part : up_part + down_part + out_part, :] = grad_w_out[
                    lo : lo + out_part
                ]
        for side in range(2):
            out_copy(side).start()
        for side in range(2):
            for j in range(ff_total // FF_TILE):
                up_copy(side, j).wait()
            for z in range(z_ways):
                down_copy(side, z, base + z).wait()
            out_copy(side).wait()


def mid_block(
    lengths, ids, att, hidden, mods, cot, loss, w_out, b_out, w_up, b_up, w_down, b_down, parts
):
    frames, width = hidden.shape
    heads_local = len(att)
    seq_ways = att[0].shape[0]
    ff = w_up.shape[1]
    up_rows = width // seq_ways
    rows = (ff // width * up_rows + ff // seq_ways + up_rows) // parts
    utts = lengths.shape[0]
    f32, bf16 = jnp.float32, jnp.bfloat16
    steps = ff // FF_TILE

    def whole(shape):
        return pl.BlockSpec(shape, lambda j, *_: (0,) * len(shape), pipeline_mode=pl.Buffered(1))

    hbm = pl.BlockSpec(memory_space=pl.ANY)
    gshape = (parts, seq_ways // 2, rows, width)
    out_shape = [
        jax.ShapeDtypeStruct((frames, width), bf16),
        jax.ShapeDtypeStruct((frames, width), f32),
        jax.ShapeDtypeStruct((4 * table_rows(utts) + 8, width), f32),
    ]
    out_shape += [jax.ShapeDtypeStruct(a.shape, bf16) for a in att]
    out_specs = [whole(o.shape) for o in out_shape] + [hbm] * 2
    out_shape += [jax.ShapeDtypeStruct(gshape, bf16)] * 2
    ins = list(att) + [hidden, mods, cot, loss, w_out, b_out]
    return pl.pallas_call(
        functools.partial(mid_kernel, (seq_ways, heads_local, utts, ff)),
        out_shape=out_shape,
        grid_spec=pltpu.PrefetchScalarGridSpec(
            num_scalar_prefetch=2,
            grid=(steps,),
            in_specs=[whole(a.shape) for a in ins]
            + [
                pl.BlockSpec((width, FF_TILE), lambda j, *_: (0, j)),
                pl.BlockSpec((1, FF_TILE), lambda j, *_: (0, j)),
                pl.BlockSpec((FF_TILE, width), lambda j, *_: (j, 0)),
                whole((1, width)),
            ],
            out_specs=out_specs,
            scratch_shapes=[
                pltpu.VMEM((width, frames), bf16),
                pltpu.VMEM((frames, width), f32),
                pltpu.VMEM((frames, width), f32),
                pltpu.VMEM((frames, width), bf16),
                pltpu.VMEM((width, frames), bf16),
                pltpu.VMEM((frames, width), bf16),
                pltpu.VMEM((frames, width), f32),
                pltpu.VMEM((frames, width), f32),
                pltpu.VMEM((32, frames), bf16),
                pltpu.VMEM((frames, 128), bf16),
                pltpu.VMEM((128, 4 * width), bf16),
                pltpu.VMEM((2,) + gshape, bf16),
                pltpu.SemaphoreType.DMA((2, steps + seq_ways // 2 + 1)),
            ],
        ),
        compiler_params=pltpu.CompilerParams(vmem_limit_bytes=63 << 20),
        cost_estimate=cost(500),
        name="mid_block",
    )(lengths, ids, *ins, w_up, b_up, w_down, b_down)


def whole_block(shape):
    return pl.BlockSpec(shape, lambda *_: (0,) * len(shape), pipeline_mode=pl.Buffered(1))


def segment_rows(lengths_ref, drop_ref, utts, base, width):
    col = base + lax.broadcasted_iota(jnp.int32, (1, width), 1)
    start = jnp.int32(0)
    kept = jnp.zeros((1, width), jnp.float32)
    place = jnp.zeros((1, width), jnp.int32)
    for u in range(utts):
        end = start + lengths_ref[u]
        inside = (col >= start) & (col < end)
        kept = jnp.where(inside, (1 - drop_ref[u]).astype(jnp.float32), kept)
        place = jnp.where(inside, col - start, place)
        start = end
    return kept, place.astype(jnp.float32)


def rotary_rows(place, half):
    index = lax.broadcasted_iota(jnp.int32, (half, 1), 0).astype(jnp.float32)
    inverse = jnp.exp(index * (-9.210340371976184 / half))
    angles = inverse * place
    return jnp.cos(angles), jnp.sin(angles)


def frame_columns(hot, extra):
    hotb = hot.astype(jnp.bfloat16)
    idx = lax.broadcasted_iota(jnp.int32, hot.shape, 0)
    last = jnp.where(idx == 0, extra, 0.0).astype(jnp.bfloat16)
    return pad_rows([hotb, hotb, hotb, last], 128).T


def head_kernel(
    utts,
    lengths_ref,
    ids_ref,
    drop_ref,
    tokens_ref,
    skip_ref,
    cond_ref,
    mods_ref,
    w_skip_ref,
    b_skip_ref,
    hidden_ref,
    joinedT_ref,
    naT_ref,
    na_ref,
    cols,
):
    f32, bf16 = jnp.float32, jnp.bfloat16
    step = pl.program_id(0)
    frames, width = tokens_ref.shape
    rank = ids_ref[1]

    @pl.when(step == 0)
    def _():
        hot = onehot_rows(lengths_ref, utts, 16, rank * frames, frames)
        kept, _ = segment_rows(lengths_ref, drop_ref, utts, rank * frames, frames)
        cols[...] = frame_columns(hot, kept)
        keep = cols[:, 48:49].astype(f32)
        mixed = (tokens_ref[...].astype(f32) + keep * cond_ref[...].astype(f32)).astype(bf16)
        joinedT_ref[0:width, :] = mixed.T
        hidden_ref[...] = dot(mixed, w_skip_ref[...]) + b_skip_ref[...].astype(f32)

    @pl.when(step == 1)
    def _():
        skip = skip_ref[...]
        joinedT_ref[width : 2 * width, :] = skip.T
        hidden = hidden_ref[...] + dot(skip, w_skip_ref[...])
        hidden_ref[...] = hidden
        madd = mods_operand(mods_ref)
        shift = dot(cols[...], madd[:, :width])
        scale = dot(cols[...], madd[:, width:])
        normed, _ = norm_stats(hidden)
        value = (normed * (1.0 + scale) + shift).astype(bf16)
        na_ref[...] = value
        naT_ref[...] = value.T


def head_block(lengths, ids, drop, tokens, skip, cond, mods, w_skip, b_skip):
    frames, width = tokens.shape
    utts = lengths.shape[0]
    f32, bf16 = jnp.float32, jnp.bfloat16

    def whole(shape):
        return pl.BlockSpec(shape, lambda j, *_: (0,) * len(shape), pipeline_mode=pl.Buffered(1))

    out_shape = [
        jax.ShapeDtypeStruct((frames, width), f32),
        jax.ShapeDtypeStruct((2 * width, frames), bf16),
        jax.ShapeDtypeStruct((width, frames), bf16),
        jax.ShapeDtypeStruct((frames, width), bf16),
    ]
    return pl.pallas_call(
        functools.partial(head_kernel, utts),
        out_shape=out_shape,
        grid_spec=pltpu.PrefetchScalarGridSpec(
            num_scalar_prefetch=3,
            grid=(2,),
            in_specs=[whole(a.shape) for a in (tokens, skip, cond, mods)]
            + [pl.BlockSpec((width, width), lambda j, *_: (j, 0)), whole((1, width))],
            out_specs=[whole(o.shape) for o in out_shape],
            scratch_shapes=[pltpu.VMEM((frames, 128), bf16)],
        ),
        compiler_params=pltpu.CompilerParams(vmem_limit_bytes=48 << 20),
        cost_estimate=cost(100),
        name="head_block",
    )(lengths, ids, drop, tokens, skip, cond, mods, w_skip, b_skip)


def turn_heads(tensor, cosine, sine):
    half = DH // 2
    first, second = tensor[:, :half], tensor[:, half:]
    return jnp.concatenate([first * cosine - second * sine, second * cosine + first * sine], axis=1)


def qkv_kernel(utts, seq_ways, lengths_ref, ids_ref, drop_ref, na_ref, w_ref, b_ref, out_ref, trig):
    f32, bf16 = jnp.float32, jnp.bfloat16
    part = pl.program_id(0)
    frames = na_ref.shape[0]

    @pl.when(part == 0)
    def _():
        _, place = segment_rows(lengths_ref, drop_ref, utts, ids_ref[1] * frames, frames)
        cosine, sine = rotary_rows(place, DH // 2)
        trig[0] = cosine
        trig[1] = sine

    raw = dot(na_ref[...], w_ref[...]) + b_ref[...].astype(f32)
    rawT = raw.T.reshape(seq_ways, DH, frames)
    turned = part < 2
    cosine = jnp.where(turned, trig[0], 1.0)[None]
    sine = jnp.where(turned, trig[1], 0.0)[None]
    out_ref[:, pl.ds(pl.multiple_of(part * DH, DH), DH), :] = turn_heads(rawT, cosine, sine).astype(bf16)


def qkv_block(lengths, ids, drop, na, w_qkv, b_qkv, chunk, seq_ways):
    frames, width = na.shape
    cols = seq_ways * DH
    chunks = width // cols
    utts = lengths.shape[0]

    def whole(shape):
        return pl.BlockSpec(shape, lambda j, *_: (0,) * len(shape), pipeline_mode=pl.Buffered(1))

    shape = (seq_ways, 3 * DH, frames)
    return pl.pallas_call(
        functools.partial(qkv_kernel, utts, seq_ways),
        out_shape=jax.ShapeDtypeStruct(shape, jnp.bfloat16),
        grid_spec=pltpu.PrefetchScalarGridSpec(
            num_scalar_prefetch=3,
            grid=(3,),
            in_specs=[
                whole(na.shape),
                pl.BlockSpec((width, cols), lambda j, *_: (0, j * chunks + chunk)),
                pl.BlockSpec((1, cols), lambda j, *_: (0, j * chunks + chunk)),
            ],
            out_specs=whole(shape),
            scratch_shapes=[pltpu.VMEM((2, DH // 2, frames), jnp.float32)],
        ),
        cost_estimate=cost(75),
        name="qkv_block",
    )(lengths, ids, drop, na, w_qkv, b_qkv)


def back_kernel(utts, seq_ways, chunk, lengths_ref, ids_ref, drop_ref, grad_ref, naT_ref, w_ref, *refs):
    first = chunk == 0
    acc_in = None if first else refs[0]
    acc_ref, bias_ref, keep_ref, send_ref, trig, grads, sems = refs[0 if first else 3 :]
    f32, bf16 = jnp.float32, jnp.bfloat16
    part = pl.program_id(0)
    width, frames = naT_ref.shape
    core = ids_ref[0]
    parts = keep_ref.shape[0]
    own = width // seq_ways
    rows = own // parts

    @pl.when(part == 0)
    def _():
        _, place = segment_rows(lengths_ref, drop_ref, utts, ids_ref[1] * frames, frames)
        cosine, sine = rotary_rows(place, DH // 2)
        trig[0] = cosine
        trig[1] = sine

    turned = part < 2
    cosine = jnp.where(turned, trig[0], 1.0)[None]
    sine = jnp.where(turned, trig[1], 0.0)[None]
    raw = grad_ref[:, pl.ds(pl.multiple_of(part * DH, DH), DH), :].astype(f32)
    gpT = turn_heads(raw, cosine, -sine).astype(bf16).reshape(seq_ways * DH, frames)
    gna = dot(w_ref[...], gpT)

    @pl.when(part == 0)
    def _():
        acc_ref[...] = gna if first else acc_in[...] + gna

    @pl.when(part > 0)
    def _():
        acc_ref[...] += gna

    ones = jnp.ones((8, frames), bf16)
    bias_ref[0] = dot_nt(ones, gpT)
    grad_w = dot_nt(naT_ref[...], gpT).astype(bf16)
    cols = seq_ways * DH
    at = pl.ds(pl.multiple_of(part * rows, rows), rows)
    for s in range(seq_ways):
        side = jnp.where(core == s % 2, 0, 1)
        for k in range(parts):
            lo = s * own + k * rows
            grads[side, k, s // 2, at, :] = grad_w[lo : lo + rows]

    def copy(side, p):
        where = (slice(None), slice(None), pl.ds(pl.multiple_of(p * rows, rows), rows))
        return pltpu.make_async_copy(
            grads.at[side].at[where],
            (keep_ref, send_ref)[side].at[(*where, pl.ds(chunk * cols, cols))],
            sems.at[side, p],
        )

    for side in (1, 0):
        copy(side, part).start()

    @pl.when(part == 2)
    def _():
        for side in (1, 0):
            for p in range(3):
                copy(side, p).wait()


def back_block(lengths, ids, drop, grad, naT, w_qkv, before, chunk, parts):
    seq_ways, _, frames = grad.shape
    width = naT.shape[0]
    cols = seq_ways * DH
    chunks = width // cols
    utts = lengths.shape[0]
    f32, bf16 = jnp.float32, jnp.bfloat16
    rows = width // seq_ways // parts

    def whole(shape):
        return pl.BlockSpec(shape, lambda j, *_: (0,) * len(shape), pipeline_mode=pl.Buffered(1))

    gspec = pl.BlockSpec(memory_space=pl.ANY)
    gshape = jax.ShapeDtypeStruct((parts, seq_ways // 2, 3 * rows, width), bf16)
    ins = [grad, naT, w_qkv, *before]
    in_specs = [whole(grad.shape), whole(naT.shape)]
    in_specs += [pl.BlockSpec((width, cols), lambda j, *_: (0, j * chunks + chunk))]
    aliases = {}
    if before:
        in_specs += [whole(before[0].shape), gspec, gspec]
        aliases = {7: 2, 8: 3}
    return pl.pallas_call(
        functools.partial(back_kernel, utts, seq_ways, chunk),
        out_shape=[
            jax.ShapeDtypeStruct((width, frames), f32),
            jax.ShapeDtypeStruct((3, 8, cols), f32),
            gshape,
            gshape,
        ],
        grid_spec=pltpu.PrefetchScalarGridSpec(
            num_scalar_prefetch=3,
            grid=(3,),
            in_specs=in_specs,
            out_specs=[
                whole((width, frames)),
                pl.BlockSpec((1, 8, cols), lambda j, *_: (j, 0, 0)),
                gspec,
                gspec,
            ],
            scratch_shapes=[
                pltpu.VMEM((2, DH // 2, frames), f32),
                pltpu.VMEM((2, parts, seq_ways // 2, 3 * rows, cols), bf16),
                pltpu.SemaphoreType.DMA((2, 3)),
            ],
        ),
        compiler_params=pltpu.CompilerParams(vmem_limit_bytes=48 << 20),
        cost_estimate=cost(100),
        input_output_aliases=aliases,
        name="back_block",
    )(lengths, ids, drop, *ins)


def norm_kernel(
    utts, heads_local, lengths_ref, ids_ref, acc_ref, hidden_ref, after_ref, mods_ref, loss_ref, mid_ref, *refs
):
    f32, bf16 = jnp.float32, jnp.bfloat16
    bias_refs, (gh_ref, small_ref) = refs[:heads_local], refs[heads_local:]
    frames, width = hidden_ref.shape
    pad_u = table_rows(utts)
    base = 6 * pad_u
    hot = onehot_rows(lengths_ref, utts, 16, ids_ref[1] * frames, frames)
    cols = frame_columns(hot, jnp.zeros((1, frames), f32))
    madd = mods_operand(mods_ref)
    scale = dot(cols, madd[:, width:])
    gna = acc_ref[...].T
    normed, rstd = norm_stats(hidden_ref[...])
    sums = sum_rows(hot, 16, frames)
    small_ref[0:pad_u, :] = dot(sums, gna.astype(bf16))[:pad_u]
    small_ref[pad_u : 2 * pad_u, :] = dot(sums, (gna * normed).astype(bf16))[:pad_u]
    gh = (after_ref[...] + norm_back(gna * (1.0 + scale), normed, rstd)).astype(bf16)
    gh_ref[...] = gh
    small_ref[2 * pad_u : base, :] = mid_ref[0 : 4 * pad_u, :]
    cols_local = width // heads_local
    for c in range(heads_local):
        for p in range(3):
            small_ref[base + p : base + p + 1, c * cols_local : (c + 1) * cols_local] = bias_refs[c][p, 0:1, :]
    small_ref[base + 3 : base + 4, :] = dot(sums, gh)[16:17]
    small_ref[base + 4 : base + 12, :] = mid_ref[4 * pad_u : 4 * pad_u + 8, :]
    count = jnp.sum(loss_ref[...].astype(f32), axis=1, keepdims=True)
    small_ref[base + 12 : base + 16, :] = jnp.broadcast_to(count, (4, width))


def norm_block(lengths, ids, acc, hidden, after, mods, loss, mid_small, biases):
    frames, width = hidden.shape
    utts = lengths.shape[0]
    out_shape = [
        jax.ShapeDtypeStruct((frames, width), jnp.bfloat16),
        jax.ShapeDtypeStruct((6 * table_rows(utts) + 16, width), jnp.float32),
    ]
    return pl.pallas_call(
        functools.partial(norm_kernel, utts, len(biases)),
        out_shape=out_shape,
        grid_spec=pltpu.PrefetchScalarGridSpec(
            num_scalar_prefetch=2,
            grid=(1,),
            in_specs=[whole_block(a.shape) for a in (acc, hidden, after, mods, loss, mid_small, *biases)],
            out_specs=[whole_block(o.shape) for o in out_shape],
        ),
        compiler_params=pltpu.CompilerParams(vmem_limit_bytes=48 << 20),
        cost_estimate=cost(50),
        name="norm_block",
    )(lengths, ids, acc, hidden, after, mods, loss, mid_small, *biases)


def skip_kernel(seq_ways, ids_ref, joinedT_ref, gh_ref, keep_ref, send_ref, grads, sems):
    step = pl.program_id(0)
    core = ids_ref[0]
    parts = keep_ref.shape[0]
    width = joinedT_ref.shape[0]
    block = 2 * width // seq_ways
    rows = block // parts
    z_step = seq_ways // 4
    grad_w = dot(joinedT_ref[...], gh_ref[...]).astype(jnp.bfloat16)
    for b in range(width // block):
        side = jnp.where(core == b % 2, 0, 1)
        for k in range(parts):
            lo = b * block + k * rows
            grads[side, k, step * z_step + b // 2] = grad_w[lo : lo + rows]

    def copy(side, at):
        where = (slice(None), pl.ds(at * z_step, z_step))
        return pltpu.make_async_copy(
            grads.at[side].at[where], (keep_ref, send_ref)[side].at[where], sems.at[side, at]
        )

    for side in (1, 0):
        copy(side, step).start()

    @pl.when(step == 1)
    def _():
        for side in (1, 0):
            for at in range(2):
                copy(side, at).wait()


def skip_block(ids, joinedT, gh, seq_ways, parts):
    frames, width = gh.shape
    rows = 2 * width // seq_ways // parts
    gshape = (parts, seq_ways // 2, rows, width)
    return pl.pallas_call(
        functools.partial(skip_kernel, seq_ways),
        out_shape=[jax.ShapeDtypeStruct(gshape, jnp.bfloat16)] * 2,
        grid_spec=pltpu.PrefetchScalarGridSpec(
            num_scalar_prefetch=1,
            grid=(2,),
            in_specs=[pl.BlockSpec((width, frames), lambda j, *_: (j, 0)), whole_block(gh.shape)],
            out_specs=[pl.BlockSpec(memory_space=pl.ANY)] * 2,
            scratch_shapes=[pltpu.VMEM((2,) + gshape, jnp.bfloat16), pltpu.SemaphoreType.DMA((2, 2))],
        ),
        compiler_params=pltpu.CompilerParams(vmem_limit_bytes=32 << 20),
        cost_estimate=cost(50),
        name="skip_block",
    )(ids, joinedT, gh)


def joined_kernel(gh_ref, w_ref, scale_ref, first_ref, second_ref):
    step = pl.program_id(0)
    value = dot_nt(gh_ref[...], w_ref[...]) * scale_ref[0:1, 0:1]

    @pl.when(step == 0)
    def _():
        first_ref[...] = value

    @pl.when(step == 1)
    def _():
        second_ref[...] = value


def joined_block(gh, w_skip, scale):
    frames, width = gh.shape
    out = jax.ShapeDtypeStruct((frames, width), jnp.float32)
    return pl.pallas_call(
        joined_kernel,
        out_shape=[out, out],
        grid_spec=pltpu.PrefetchScalarGridSpec(
            num_scalar_prefetch=0,
            grid=(2,),
            in_specs=[
                whole_block(gh.shape),
                pl.BlockSpec((width, width), lambda j: (j, 0)),
                whole_block(scale.shape),
            ],
            out_specs=[whole_block(out.shape)] * 2,
        ),
        compiler_params=pltpu.CompilerParams(vmem_limit_bytes=32 << 20),
        cost_estimate=cost(50),
        name="joined_block",
    )(gh, w_skip, scale)


def add_bf16(left, right):
    return (left.astype(jnp.float32) + right.astype(jnp.float32)).astype(jnp.bfloat16)


def first_kernel(pairs, splits, ids_ref, *refs):
    ins, outs = refs[: 8 * pairs], list(refs[8 * pairs :])
    for i in range(4):
        own = [outs.pop(0) for _ in range(splits if i < 2 else 1)]
        at = 0
        for p in range(pairs):
            left, right = ins[2 * (i * pairs + p)], ins[2 * (i * pairs + p) + 1]
            rows = left.shape[-2]
            value = add_bf16(left[0, 0, 0], right[0, 0, 0])
            if len(own) == 1:
                own[0][0, :, at : at + rows, :] = value
            else:
                for out in own:
                    out[0] = value[:, at : at + out.shape[2], :]
                    at += out.shape[2]
            at += rows


def first_sum(ids, pairs, splits):
    _, _, _, z_ways, _, width = pairs[0][0].shape
    total = sum(k.shape[4] for k, _ in pairs)
    step = 1 if total > 100 else z_ways

    def source(half, axis, mine, rows):
        def at(g, z, ids):
            bit = ids[axis]
            return half, bit if mine else 1 - bit, g, z, 0, 0

        return pl.BlockSpec((1, 1, 1, step, rows, width), at)

    order = [(0, 2, False), (1, 3, False), (0, 2, True), (1, 3, True)]
    sizes = [*splits, *splits, total, total]
    return pl.pallas_call(
        functools.partial(first_kernel, len(pairs), len(splits)),
        out_shape=[jax.ShapeDtypeStruct((2, z_ways, n, width), jnp.bfloat16) for n in sizes],
        grid_spec=pltpu.PrefetchScalarGridSpec(
            num_scalar_prefetch=1,
            grid=(2, z_ways // step),
            in_specs=[source(*o, a.shape[4]) for o in order for pair in pairs for a in pair],
            out_specs=[pl.BlockSpec((1, step, n, width), lambda g, z, ids: (g, z, 0, 0)) for n in sizes],
        ),
        compiler_params=pltpu.CompilerParams(vmem_limit_bytes=48 << 20),
        cost_estimate=cost(60),
        name="first_sum",
    )(ids, *([a for pair in pairs for a in pair] * 4))


def second_kernel(pieces, ids_ref, *refs):
    for i in range(4):
        keep, *got = refs[(pieces + 1) * i : (pieces + 1) * (i + 1)]
        out = refs[4 * (pieces + 1) + i]
        at = 0
        for g in got:
            rows = g.shape[2]
            out[:, at : at + rows, :] = add_bf16(keep[0, :, at : at + rows, :], g[0])
            at += rows


def second_sum(ids, keep_a, got_a, keep_b, got_b):
    _, z_ways, rows, width = keep_a.shape
    step = z_ways // 2 if rows > 100 else z_ways

    def source(axis, mine, value):
        def at(z, ids):
            bit = ids[axis]
            return bit if mine else 1 - bit, z, 0, 0

        return pl.BlockSpec((1, step, *value.shape[2:]), at)

    order = [(3, False), (2, False), (3, True), (2, True)]
    sides = [[keep_a, *got_a], [keep_b, *got_b]]
    out = jax.ShapeDtypeStruct((z_ways, rows, width), jnp.bfloat16)
    return pl.pallas_call(
        functools.partial(second_kernel, len(got_a)),
        out_shape=[out] * 4,
        grid_spec=pltpu.PrefetchScalarGridSpec(
            num_scalar_prefetch=1,
            grid=(z_ways // step,),
            in_specs=[source(*o, v) for i, o in enumerate(order) for v in sides[i % 2]],
            out_specs=[pl.BlockSpec((step, rows, width), lambda z, ids: (z, 0, 0))] * 4,
        ),
        compiler_params=pltpu.CompilerParams(vmem_limit_bytes=48 << 20),
        cost_estimate=cost(30),
        name="second_sum",
    )(ids, *((sides[0] + sides[1]) * 2))


def third_kernel(ids_ref, keep_a, got_a, keep_b, got_b, *outs):
    for j, out in enumerate(outs):
        at = ids_ref[4] ^ j
        out[0] = add_bf16(keep_a[at], got_a[at])
        out[1] = add_bf16(keep_b[at], got_b[at])


def third_sum(ids, keep_a, got_a, keep_b, got_b):
    z_ways, rows, width = keep_a.shape
    out = jax.ShapeDtypeStruct((2, rows, width), jnp.bfloat16)
    return pl.pallas_call(
        third_kernel,
        out_shape=[out] * z_ways,
        grid_spec=pltpu.PrefetchScalarGridSpec(
            num_scalar_prefetch=1,
            grid=(1,),
            in_specs=[whole_block(keep_a.shape)] * 4,
            out_specs=[whole_block(out.shape)] * z_ways,
        ),
        cost_estimate=cost(10),
        name="third_sum",
    )(ids, keep_a, got_a, keep_b, got_b)


def fourth_kernel(*refs):
    total = refs[0][...].astype(jnp.float32)
    for r in refs[1:-1]:
        total = total + r[...].astype(jnp.float32)
    refs[-1][...] = total.astype(jnp.bfloat16)


def fourth_sum(terms):
    shape = terms[0].shape
    return pl.pallas_call(
        fourth_kernel,
        out_shape=jax.ShapeDtypeStruct(shape, jnp.bfloat16),
        grid=(1,),
        in_specs=[whole_block(shape)] * len(terms),
        out_specs=whole_block(shape),
        cost_estimate=cost(10),
        name="fourth_sum",
    )(*terms)


def place_kernel(streams, plan, ids_ref, scale_ref, *refs):
    blocks, outs = refs[: 4 * streams], refs[4 * streams :]
    x, y = ids_ref[2], ids_ref[3]
    scale = scale_ref[0:1, 0:1]
    for stream, row, rows, lane, lanes, out, row_of, lane_of in plan:
        for d in range(4):
            own_x, own_y = x ^ (d & 1), y ^ (d >> 1)
            for half in range(2):
                k = own_x * 2 + own_y if half == 0 else 4 + own_y * 2 + own_x
                tile = blocks[4 * stream + d][half, row : row + rows, lane : lane + lanes]
                outs[out][row_of(k), lane_of(k)] = tile.astype(jnp.float32) * scale


def place_blocks(ids, scale, streams, plan, shapes):
    blocks = [b for s in streams for b in s]
    outs = [jax.ShapeDtypeStruct(s, jnp.float32) for s in shapes]
    return pl.pallas_call(
        functools.partial(place_kernel, len(streams), plan),
        out_shape=outs,
        grid_spec=pltpu.PrefetchScalarGridSpec(
            num_scalar_prefetch=1,
            grid=(1,),
            in_specs=[whole_block(a.shape) for a in (scale, *blocks)],
            out_specs=[whole_block(o.shape) for o in outs],
        ),
        compiler_params=pltpu.CompilerParams(vmem_limit_bytes=32 << 20),
        cost_estimate=cost(20),
        name="place_blocks",
    )(ids, scale, *blocks)


def span(start, size):
    return pl.ds(pl.multiple_of(start, size), size)


def ada_kernel(groups, pad_u, numerator, time_ref, *refs):
    f32 = jnp.float32
    parts, (weight_ref, vector_ref, scale_ref) = refs[:groups], refs[groups:]
    table = pl.program_id(0)
    base = 6 * pad_u
    count = parts[0][base + 12 : base + 13, 0:1]
    for p in parts[1:]:
        count = count + p[base + 12 : base + 13, 0:1]
    scale = numerator / count
    rows = jnp.concatenate([p[pl.ds(pl.multiple_of(table * pad_u, 8), pad_u), :] for p in parts], axis=0) * scale
    vector_ref[pl.ds(table, 1), :] = jnp.sum(rows, axis=0, keepdims=True)
    operand = jnp.concatenate(list(split3(rows)), axis=0)
    weight_ref[...] = dot(time_ref[...], operand)

    @pl.when(table == 0)
    def _():
        total = parts[0][base : base + 16, :]
        for p in parts[1:]:
            total = total + p[base : base + 16, :]
        vector_ref[8:24, :] = total * scale
        scale_ref[...] = jnp.broadcast_to(scale, scale_ref.shape)


def ada_block(time3, parts, utts, numerator):
    pad_u = table_rows(utts)
    width = parts[0].shape[1]
    own = time3.shape[0]
    f32 = jnp.float32
    return pl.pallas_call(
        functools.partial(ada_kernel, len(parts), pad_u, numerator),
        out_shape=[
            jax.ShapeDtypeStruct((own, 6 * width), f32),
            jax.ShapeDtypeStruct((24, width), f32),
            jax.ShapeDtypeStruct((8, 128), f32),
        ],
        grid=(6,),
        in_specs=[whole_block(time3.shape)] + [whole_block(p.shape) for p in parts],
        out_specs=[
            pl.BlockSpec((own, width), lambda j: (0, j)),
            whole_block((24, width)),
            whole_block((8, 128)),
        ],
        cost_estimate=cost(50),
        name="ada_block",
    )(time3, *parts)


def sum_exchange(value, axis, bit):
    ways = lax.axis_size(axis)
    return lax.ppermute(value, axis, [(i, i ^ bit) for i in range(ways)])


def axis_bits(ways):
    return [1 << i for i in range(ways.bit_length() - 1)]


def reduce_stages(ids, blocks, splits):
    batch_ways = lax.axis_size("batch")
    x_bit, y_bit = 1, 1 << ((batch_ways.bit_length() - 1) // 2)
    pairs = []
    for keep, send in blocks:
        shape = (2, 2, 2) + keep.shape[1:]
        pairs.append((keep.reshape(shape), sum_exchange(send, "seq", 1).reshape(shape)))
    *sends, keep_a, keep_b = first_sum(ids, pairs, splits)
    sends = follow(sends, (yield sends))
    got, token = [[], []], None
    for i in range(len(splits)):
        pieces = follow([sends[i], sends[len(splits) + i]], token)
        for side, bit in enumerate((x_bit, y_bit)):
            got[side].append(sum_exchange(pieces[side], "batch", bit))
        token = yield [got[0][i], got[1][i]]
    got_a, got_b = (follow(g, token) for g in got)
    send_a, send_b, keep_a, keep_b = second_sum(ids, keep_a, got_a, keep_b, got_b)
    send_a, send_b = follow([send_a, send_b], (yield [send_a, send_b]))
    got = [sum_exchange(send_a, "batch", y_bit), sum_exchange(send_b, "batch", x_bit)]
    got_a, got_b = follow(got, (yield got))
    own, *away = third_sum(ids, keep_a, got_a, keep_b, got_b)
    away = follow(away, (yield away))
    got = [sum_exchange(a, "seq", 2 * (j + 1)) for j, a in enumerate(away)]
    got = follow(got, (yield got))
    block = fourth_sum([own] + got)
    for bit in axis_bits(batch_ways):
        if bit not in (x_bit, y_bit):
            block = add_bf16(block, sum_exchange(block, "batch", bit))
    (block,) = follow([block], (yield [block]))
    yield [block] + [sum_exchange(block, "batch", bit) for bit in (x_bit, y_bit, x_bit | y_bit)]


def advance(stages, steps, token=None):
    value = stages.send(token)
    for _ in range(steps - 1):
        value = next(stages)
    return value


def last_stage(stages, token=None):
    value = stages.send(token)
    for value in stages:
        pass
    return value


def follow(values, token):
    return values if token is None else [after(v, token) for v in values]


def after(value, *others):
    return lax.optimization_barrier((value,) + others)[0]


def gather_groups(value):
    return [value] + [sum_exchange(value, "batch", i) for i in range(1, lax.axis_size("batch"))]


def sum_seq(value):
    for bit in axis_bits(lax.axis_size("seq")):
        value = value + sum_exchange(value, "seq", bit)
    return value


def shards(
    tokens_in,
    skip_in,
    condition,
    cotangent,
    time_embed,
    lengths,
    key_mask,
    drop_mask,
    loss_mask,
    w_skip,
    b_skip,
    w_ada,
    b_ada,
    w_qkv,
    b_qkv,
    w_out,
    b_out,
    w_up,
    b_up,
    w_down,
    b_down,
):
    f32, bf16 = jnp.float32, jnp.bfloat16
    seq_ways, batch_ways = lax.axis_size("seq"), lax.axis_size("batch")
    seq_rank = lax.axis_index("seq")
    frames, width = tokens_in.shape[1:]
    group_frames = frames * seq_ways
    heads_local = HEADS // seq_ways
    utts = lengths.shape[1]
    lengths_row, drop = lengths[0], drop_mask[0]
    batch_rank = lax.axis_index("batch")
    side = 1 << ((batch_ways.bit_length() - 1) // 2)
    ids = [lax.rem(seq_rank, 2), seq_rank, lax.rem(batch_rank, 2), lax.rem(batch_rank // side, 2), seq_rank // 2]
    ids = jnp.stack(ids).astype(jnp.int32)
    ok = key_mask.reshape(seq_ways, 1, frames)
    exchange = functools.partial(lax.all_to_all, axis_name="seq", split_axis=0, concat_axis=0, tiled=True)

    time_act = jax.nn.silu(time_embed[0]).astype(bf16)
    time_rows = jnp.pad(time_act, ((0, 16 - utts), (0, 0)))

    def modulation(first, last):
        return jnp.dot(time_rows, w_ada[:, first:last], preferred_element_type=f32) + b_ada[
            first:last
        ].astype(f32)

    mods_a = modulation(0, 2 * width)
    hidden, joinedT, naT, na = head_block(
        lengths_row, ids, drop, tokens_in[0], skip_in[0], condition[0], mods_a, w_skip, b_skip[None]
    )
    received = []
    for c in range(heads_local):
        packed = qkv_block(lengths_row, ids, drop, na, w_qkv, b_qkv[None], c, seq_ways)
        received.append(exchange(packed))

    mods_rest = modulation(2 * width, 6 * width)
    own = width // seq_ways
    pad_u = table_rows(utts)
    time_own = lax.dynamic_slice_in_dim(jnp.concatenate(gather_groups(time_rows[:pad_u])), seq_rank * own, own, axis=1)
    time3 = jnp.tile(time_own.T, (1, 3))

    received[0] = after(received[0], mods_rest)
    head_out, log_totals, returned = [], [], []
    for c in range(heads_local):
        out, log_total = attend(lengths_row, received[c], ok)
        head_out.append(out)
        log_totals.append(log_total)
        returned.append(exchange(after(out, *returned)))
        if c < heads_local - 1:
            received[c + 1] = after(received[c + 1], out, time3)
    mid = mid_block(
        lengths_row,
        ids,
        returned,
        hidden,
        mods_rest,
        cotangent[0],
        loss_mask,
        w_out,
        b_out[None],
        w_up,
        b_up[None],
        w_down,
        b_down[None],
        PARTS,
    )
    output, after_grad, mid_small = mid[:3]
    grad_att = mid[3 : 3 + heads_local]
    grad_heads = [exchange(g) for g in grad_att]
    keep = mid[3 + heads_local]
    front = keep.shape[2] * 4 // 9 // 16 * 16
    feed = reduce_stages(ids, [mid[3 + heads_local :]], [front, keep.shape[2] - front])

    ahead = next(feed)
    grad_local = []
    for c in range(heads_local):
        operand = after(grad_heads[c], *ahead)
        moving = feed.send(grad if c else None) if c < 2 else []
        grad = attend_back(lengths_row, received[c], ok, head_out[c], operand, log_totals[c])
        grad_local.append(exchange(after(grad, *moving, *grad_heads[c + 1 :])))
        ahead = [grad]
    if heads_local == 1:
        next(feed)
    ahead = ahead + advance(feed, 1, ahead[0])
    before, biases = (), []
    for c in range(heads_local):
        acc, bias, keep, send = back_block(
            lengths_row, ids, drop, after(grad_local[c], *ahead), naT, w_qkv, before, c, PARTS
        )
        before = (acc, keep, send)
        biases.append(bias)
        ahead = next(feed) and advance(feed, 1, acc) if c == 0 else []
    moving = next(feed)
    acc = after(acc, moving[0])
    gh, small = norm_block(lengths_row, ids, acc, hidden, after_grad, mods_a, loss_mask, mid_small, biases)
    rest = reduce_stages(ids, [skip_block(ids, joinedT, gh, seq_ways, PARTS), (keep, send)], [5 * own // PARTS])
    next(rest)
    next(rest)
    token = advance(rest, 1)[0]
    groups = gather_groups(sum_seq(small))
    numerator = float(group_frames * batch_ways)
    grad_w_ada, vectors, scale = ada_block(time3, groups, utts, numerator)
    grad_tokens, grad_skip = joined_block(gh, w_skip, scale)
    next(feed)
    feed = last_stage(feed, token)
    rest = last_stage(rest)

    ff = w_up.shape[1]
    chunks = ff // width
    up_part = chunks * own // PARTS
    down_part = ff // seq_ways // PARTS
    out_part = own // PARTS
    per_chunk = own // up_part
    whole_lanes = lambda k: span(0, width)
    grad_w_up, grad_w_down, grad_w_out = place_blocks(
        ids,
        scale,
        [feed],
        [
            (
                *(0, 0, up_part, 0, width, 0),
                lambda k: span(lax.rem(k, per_chunk) * up_part, up_part),
                lambda k: span(k // per_chunk * width, width),
            ),
            (0, up_part, down_part, 0, width, 1, lambda k: span(k * down_part, down_part), whole_lanes),
            (0, up_part + down_part, out_part, 0, width, 2, lambda k: span(k * out_part, out_part), whole_lanes),
        ],
        [(own, ff), (ff // seq_ways, width), (own, width)],
    )
    skip_part = 2 * own // PARTS
    grad_w_skip, grad_w_qkv = place_blocks(
        ids,
        scale,
        [rest],
        [(0, 0, skip_part, 0, width, 0, lambda k: span(k * skip_part, skip_part), whole_lanes)]
        + [
            (
                *(0, skip_part + p * out_part, out_part, 0, width, 1),
                lambda k: span(k * out_part, out_part),
                lambda k, at=p * width: span(at, width),
            )
            for p in range(3)
        ],
        [(2 * own, width), (own, 3 * width)],
    )

    def own_slice(vector):
        vector = vector.reshape(-1)
        size = vector.shape[0] // seq_ways
        return lax.dynamic_slice_in_dim(vector, seq_rank * size, size)

    grad_b_ada = own_slice(vectors[:6])
    grad_b_qkv = own_slice(vectors[8:11])
    grad_b_skip = own_slice(vectors[11])
    grad_b_out = own_slice(vectors[12])
    grad_b_down = own_slice(vectors[13])
    grad_b_up = own_slice(vectors[14 : 14 + chunks])
    return (
        output[None],
        grad_tokens[None],
        grad_skip[None],
        grad_w_skip,
        grad_b_skip,
        grad_w_ada,
        grad_b_ada,
        grad_w_qkv,
        grad_b_qkv,
        grad_w_out,
        grad_b_out,
        grad_w_up,
        grad_b_up,
        grad_w_down,
        grad_b_down,
    )


def solution(mesh):
    in_specs = (
        P("batch", "seq", None),
        P("batch", "seq", None),
        P("batch", "seq", None),
        P("batch", "seq", None),
        P("batch", None, None),
        P("batch", None),
        P("batch", None),
        P("batch", None),
        P("batch", "seq"),
        P(),
        P(),
        P(),
        P(),
        P(),
        P(),
        P(),
        P(),
        P(),
        P(),
        P(),
        P(),
    )
    out_specs = (
        P("batch", "seq", None),
        P("batch", "seq", None),
        P("batch", "seq", None),
        P("seq", None),
        P("seq"),
        P("seq", None),
        P("seq"),
        P("seq", None),
        P("seq"),
        P("seq", None),
        P("seq"),
        P("seq", None),
        P("seq"),
        P("seq", None),
        P("seq"),
    )
    return jax.shard_map(shards, mesh=mesh, in_specs=in_specs, out_specs=out_specs, check_vma=False)
```

```python
import functools

import jax
import jax.numpy as jnp
from jax import lax
from jax.experimental import pallas as pl
from jax.experimental.pallas import tpu as pltpu
from jax.sharding import PartitionSpec as P

HEADS = 16
HEAD_DIM = 64
PARTS = 8
BIG = 1e30
DH = 64
BQ = 512
BK = 512


def cost(weight):
    return pl.CostEstimate(flops=weight * 100000000, bytes_accessed=weight * 100000, transcendentals=0)


def onehot_rows(lengths_ref, utts, rows, base, width):
    row = lax.broadcasted_iota(jnp.int32, (rows, width), 0)
    col = base + lax.broadcasted_iota(jnp.int32, (rows, width), 1)
    start = jnp.int32(0)
    hot = jnp.zeros((rows, width), jnp.float32)
    for u in range(utts):
        end = start + lengths_ref[u]
        hot = jnp.where((row == u) & (col >= start) & (col < end), 1.0, hot)
        start = end
    return hot


def key_range(lengths_ref, utts, first, last):
    start = jnp.int32(0)
    low, high = jnp.int32(0), jnp.int32(0)
    for u in range(utts):
        end = start + lengths_ref[u]
        low = jnp.where((start <= first) & (first < end), start, low)
        high = jnp.where((start <= last) & (last < end), end, high)
        start = end
    return low // BK, (high + BK - 1) // BK


def aug_rows(utts):
    return -(-utts // 16) * 16


def split3(row):
    a = row.astype(jnp.bfloat16)
    rest = row - a.astype(jnp.float32)
    b = rest.astype(jnp.bfloat16)
    c = (rest - b.astype(jnp.float32)).astype(jnp.bfloat16)
    return a, b, c


def pad_rows(parts, total):
    have = sum(p.shape[0] for p in parts)
    if have < total:
        parts = parts + [jnp.zeros((total - have, parts[0].shape[1]), parts[0].dtype)]
    return jnp.concatenate(parts, axis=0)


def rows16(rows, width):
    idx = lax.broadcasted_iota(jnp.int32, (16, width), 0)
    out = jnp.zeros((16, width), jnp.float32)
    for i, r in enumerate(rows):
        out = jnp.where(idx == i, r, out)
    return out.astype(jnp.bfloat16)


def fwd_kernel(utts, lengths_ref, qkv_ref, ok_ref, out_ref, lse_ref, kaug, vaug):
    sources, _, frames = qkv_ref.shape
    per = frames // BQ
    pad_u = aug_rows(utts)
    step = pl.program_id(0)

    @pl.when(step == 0)
    def _():
        def build(s, c):
            hot = onehot_rows(lengths_ref, utts, pad_u, s * frames, frames)
            ok = ok_ref[s].astype(jnp.float32)
            block = qkv_ref[s]
            one = jnp.ones((1, frames), jnp.float32)
            kT = pad_rows(
                [block[DH : 2 * DH], (1.0 - hot).astype(jnp.bfloat16), rows16([1.0 - ok], frames)], 128
            )
            kaug[pl.ds(pl.multiple_of(s * frames, frames), frames), :] = kT.T
            vT = jnp.concatenate([block[2 * DH :], rows16([one], frames)], axis=0)
            for t in range(frames // BK):
                vaug[s * (frames // BK) + t] = vT[:, t * BK : (t + 1) * BK]
            return c

        lax.fori_loop(0, sources, build, 0)

    block = qkv_ref[step]
    hot_q = onehot_rows(lengths_ref, utts, pad_u, step * frames, frames)
    qT = (block[:DH].astype(jnp.float32) * 0.125)
    one = jnp.ones((1, frames), jnp.float32)
    qaug = pad_rows(
        [qT.astype(jnp.bfloat16), (hot_q * -BIG).astype(jnp.bfloat16), rows16([one * -BIG], frames)], 128
    )
    kT = block[DH : 2 * DH].astype(jnp.float32)
    vT = block[2 * DH :].astype(jnp.float32)
    ok = ok_ref[step] > 0
    s_self = jnp.sum(qT * kT, axis=0, keepdims=True)
    m0 = jnp.where(ok, -3e38, s_self)
    acc0 = jnp.concatenate([jnp.where(ok, 0.0, vT), jnp.where(ok, 0.0, jnp.ones((16, frames), jnp.float32))], axis=0)
    for t in range(per):
        cols = slice(t * BQ, (t + 1) * BQ)
        low, high = key_range(lengths_ref, utts, step * frames + t * BQ, step * frames + (t + 1) * BQ - 1)
        q_b = qaug[:, cols]

        def body(j, carry):
            m, acc = carry
            s = jnp.dot(kaug[pl.ds(pl.multiple_of(j * BK, BK), BK), :], q_b, preferred_element_type=jnp.float32)
            m_new = jnp.maximum(m, jnp.max(s, axis=0, keepdims=True))
            p = jnp.exp(s - m_new).astype(jnp.bfloat16)
            alpha = jnp.exp(m - m_new)
            acc = acc * alpha + jnp.dot(vaug[j], p, preferred_element_type=jnp.float32)
            return m_new, acc

        m, acc = lax.fori_loop(low, high, body, (m0[:, cols], acc0[:, cols]))
        total = acc[DH : DH + 1]
        out_ref[0, :, cols] = (acc[:DH] / total).astype(jnp.bfloat16)
        lse_ref[0, :, cols] = m + jnp.log(total)


def attend(lengths, qkv, ok):
    sources, _, frames = qkv.shape
    total = sources * frames
    utts = lengths.shape[0]
    whole = lambda shape: pl.BlockSpec(shape, lambda i, *_: (0,) * len(shape))
    return pl.pallas_call(
        functools.partial(fwd_kernel, utts),
        out_shape=(
            jax.ShapeDtypeStruct((sources, DH, frames), jnp.bfloat16),
            jax.ShapeDtypeStruct((sources, 1, frames), jnp.float32),
        ),
        grid_spec=pltpu.PrefetchScalarGridSpec(
            num_scalar_prefetch=1,
            grid=(sources,),
            in_specs=[whole(qkv.shape), whole(ok.shape)],
            out_specs=(
                pl.BlockSpec((1, DH, frames), lambda i, *_: (i, 0, 0)),
                pl.BlockSpec((1, 1, frames), lambda i, *_: (i, 0, 0)),
            ),
            scratch_shapes=[
                pltpu.VMEM((total, 128), jnp.bfloat16),
                pltpu.VMEM((total // BK, DH + 16, BK), jnp.bfloat16),
            ],
        ),
        cost_estimate=cost(250),
        name="attend",
    )(lengths, qkv, ok)


def bwd_kernel(utts, chunk, lengths_ref, qkv_ref, ok_ref, o_ref, do_ref, lse_ref, out_ref, kaug, vnat, kT_s, dk, dv):
    sources, _, frames = qkv_ref.shape
    per = frames // BK
    pad_u = aug_rows(utts)
    step = pl.program_id(0)
    f32 = jnp.float32

    @pl.when(step == 0)
    def _():
        def build(s, c):
            hot = onehot_rows(lengths_ref, utts, pad_u, s * frames, frames)
            ok = ok_ref[s]
            block = qkv_ref[s]
            one = jnp.ones((1, frames), f32)
            kT = block[DH : 2 * DH]
            vT = block[2 * DH :]
            kA = pad_rows(
                [kT, (1.0 - hot).astype(jnp.bfloat16), rows16([1.0 - ok.astype(f32), one, one, one], frames)], 128
            )
            rows = pl.ds(pl.multiple_of(s * frames, frames), frames)
            kaug[rows, :] = kA.T
            vnat[rows, :] = pad_rows([vT, rows16([one, one, one], frames)], 128).T
            qT = block[:DH].astype(f32) * 0.125
            do = do_ref[s, chunk * DH : (chunk + 1) * DH, :].astype(f32)
            s_self = jnp.sum(qT * kT.astype(f32), axis=0, keepdims=True)
            delta = jnp.sum(do * o_ref[s].astype(f32), axis=0, keepdims=True)
            p_self = jnp.where(ok > 0, 0.0, jnp.exp(s_self - lse_ref[s]))
            ds_self = p_self * (jnp.sum(do * vT.astype(f32), axis=0, keepdims=True) - delta)
            dk0 = ds_self * qT
            dv0 = p_self * do
            for t in range(per):
                cols = slice(t * BK, (t + 1) * BK)
                kT_s[s * per + t] = kT[:, cols]
                dk[s * per + t] = dk0[:, cols]
                dv[s * per + t] = dv0[:, cols]
            return c

        lax.fori_loop(0, sources, build, 0)

    block = qkv_ref[step]
    one = jnp.ones((1, frames), f32)
    hot_q = onehot_rows(lengths_ref, utts, pad_u, step * frames, frames)
    qT = block[:DH].astype(f32) * 0.125
    qTb = qT.astype(jnp.bfloat16)
    kT = block[DH : 2 * DH].astype(f32)
    vT = block[2 * DH :].astype(f32)
    ok = ok_ref[step]
    dob = do_ref[step, chunk * DH : (chunk + 1) * DH, :]
    do = dob.astype(f32)
    lse = lse_ref[step]
    delta = jnp.sum(do * o_ref[step].astype(f32), axis=0, keepdims=True)
    l3 = [-r.astype(f32) for r in split3(lse)]
    d3 = [-r.astype(f32) for r in split3(delta)]
    qaug = pad_rows([qTb, (hot_q * -BIG).astype(jnp.bfloat16), rows16([one * -BIG] + l3, frames)], 128)
    doaug = pad_rows([dob, rows16(d3, frames)], 128)
    s_self = jnp.sum(qT * kT, axis=0, keepdims=True)
    p_self = jnp.where(ok > 0, 0.0, jnp.exp(s_self - lse))
    ds_self = p_self * (jnp.sum(do * vT, axis=0, keepdims=True) - delta)
    dq0 = ds_self * kT
    nt = (((1,), (1,)), ((), ()))
    for t in range(frames // BQ):
        cols = slice(t * BQ, (t + 1) * BQ)
        low, high = key_range(lengths_ref, utts, step * frames + t * BQ, step * frames + (t + 1) * BQ - 1)
        q_a = qaug[:, cols]
        q_b = qTb[:, cols]
        do_a = doaug[:, cols]
        do_b = dob[:, cols]

        def body(j, dq):
            rows = pl.ds(pl.multiple_of(j * BK, BK), BK)
            s = jnp.dot(kaug[rows, :], q_a, preferred_element_type=f32)
            dp = jnp.dot(vnat[rows, :], do_a, preferred_element_type=f32)
            p = jnp.exp(s)
            ds = (p * dp).astype(jnp.bfloat16)
            dv[j] += lax.dot_general(do_b, p.astype(jnp.bfloat16), nt, preferred_element_type=f32)
            dk[j] += lax.dot_general(q_b, ds, nt, preferred_element_type=f32)
            return dq + jnp.dot(kT_s[j], ds, preferred_element_type=f32)

        dq = lax.fori_loop(low, high, body, dq0[:, cols])
        out_ref[step, :DH, cols] = (dq * 0.125).astype(jnp.bfloat16)

    @pl.when(step == sources - 1)
    def _():
        def finish(s, c):
            for t in range(per):
                cols = slice(t * BK, (t + 1) * BK)
                out_ref[s, DH : 2 * DH, cols] = dk[s * per + t].astype(jnp.bfloat16)
                out_ref[s, 2 * DH :, cols] = dv[s * per + t].astype(jnp.bfloat16)
            return c

        lax.fori_loop(0, sources, finish, 0)


def attend_back(lengths, qkv, ok, out, grad, lse, chunk):
    sources, _, frames = qkv.shape
    total = sources * frames
    utts = lengths.shape[0]
    whole = lambda shape: pl.BlockSpec(shape, lambda i, *_: (0,) * len(shape))
    return pl.pallas_call(
        functools.partial(bwd_kernel, utts, chunk),
        out_shape=jax.ShapeDtypeStruct(qkv.shape, jnp.bfloat16),
        grid_spec=pltpu.PrefetchScalarGridSpec(
            num_scalar_prefetch=1,
            grid=(sources,),
            in_specs=[whole(a.shape) for a in (qkv, ok, out, grad, lse)],
            out_specs=whole(qkv.shape),
            scratch_shapes=[
                pltpu.VMEM((total, 128), jnp.bfloat16),
                pltpu.VMEM((total, 128), jnp.bfloat16),
                pltpu.VMEM((total // BK, DH, BK), jnp.bfloat16),
                pltpu.VMEM((total // BK, DH, BK), jnp.float32),
                pltpu.VMEM((total // BK, DH, BK), jnp.float32),
            ],
        ),
        cost_estimate=cost(320),
        name="attend_back",
    )(lengths, qkv, ok, out, grad, lse)


FF_TILE = 512
EPS = 1e-06


def dot(left, right):
    return jnp.dot(left, right, preferred_element_type=jnp.float32)


def dot_nt(left, right):
    return lax.dot_general(left, right, (((1,), (1,)), ((), ())), preferred_element_type=jnp.float32)


def norm_stats(x):
    mean = jnp.mean(x, axis=1, keepdims=True)
    centred = x - mean
    rstd = lax.rsqrt(jnp.mean(centred * centred, axis=1, keepdims=True) + EPS)
    return centred * rstd, rstd


def norm_back(grad, normed, rstd):
    first = jnp.mean(grad, axis=1, keepdims=True)
    second = jnp.mean(grad * normed, axis=1, keepdims=True)
    return rstd * (grad - first - normed * second)


def mods_operand(mods_ref):
    rows = mods_ref[...]
    return pad_rows(list(split3(rows)), 128)


def table_rows(utts):
    return -(-utts // 8) * 8


def sum_rows(hot, utts_pad, frames):
    idx = lax.broadcasted_iota(jnp.int32, (16, frames), 0)
    ones = jnp.where(idx == 0, 1.0, 0.0).astype(jnp.bfloat16)
    return jnp.concatenate([hot.astype(jnp.bfloat16), ones], axis=0)


def mid_kernel(
    dims,
    lengths_ref,
    ids_ref,
    *refs,
):
    seq_ways, heads_local, utts, ff = dims
    att_refs = refs[:heads_local]
    (
        hidden_ref,
        mods_ref,
        cot_ref,
        loss_ref,
        w_out_ref,
        b_out_ref,
        w_up_ref,
        b_up_ref,
        w_down_ref,
        b_down_ref,
    ) = refs[heads_local : heads_local + 10]
    outs = refs[heads_local + 10 :]
    output_ref, after_grad_ref, small_ref, gatt_ref = outs[:4]
    refs_out = outs[4:6]
    (
        attT,
        attn_proj,
        after,
        nf,
        nfT,
        gff,
        ff_acc,
        gnf_acc,
        sums,
        cols,
        madd,
        grads,
        sems,
    ) = outs[6:]
    f32, bf16 = jnp.float32, jnp.bfloat16
    step = pl.program_id(0)
    steps = pl.num_programs(0)
    core = ids_ref[0]
    rank = ids_ref[1]
    frames, width = hidden_ref.shape
    up_rows = width // seq_ways
    down_rows = FF_TILE
    z_ways = seq_ways // 2
    parts = grads.shape[1]
    pad_u = table_rows(utts)
    ff_total = ff
    up_part = ff_total // width * up_rows // parts
    down_block = ff_total // seq_ways
    down_part = down_block // parts
    out_part = up_rows // parts

    def mod(index):
        return dot(cols[...], madd[:, index * width : (index + 1) * width])

    def grad_out():
        loss = cols[:, 48:49].astype(f32)
        return cot_ref[...].astype(f32) * loss

    @pl.when(step == 0)
    def _():
        hot = onehot_rows(lengths_ref, utts, 16, rank * frames, frames)
        hotb = hot.astype(bf16)
        idx = lax.broadcasted_iota(jnp.int32, (16, frames), 0)
        loss = jnp.where(idx == 0, loss_ref[...].astype(f32), 0.0).astype(bf16)
        cols[...] = pad_rows([hotb, hotb, hotb, loss], 128).T
        sums[...] = sum_rows(hot, 16, frames)
        madd[...] = mods_operand(mods_ref)
        for c in range(heads_local):
            for s in range(seq_ways):
                attT[(c * seq_ways + s) * DH : (c * seq_ways + s + 1) * DH, :] = att_refs[c][s]
        proj = dot(attT[...].T, w_out_ref[...]) + b_out_ref[...].astype(f32)
        attn_proj[...] = proj
        mixed = hidden_ref[...] + mod(0) * proj
        after[...] = mixed
        normed, _ = norm_stats(mixed)
        value = (normed * (1.0 + mod(2)) + mod(1)).astype(bf16)
        nf[...] = value
        nfT[...] = value.T
        gff[...] = (grad_out() * mod(3)).astype(bf16)
        small_ref[4 * pad_u :, :] = jnp.zeros((8, width), f32)

    up = dot(nf[...], w_up_ref[...]) + b_up_ref[...].astype(f32)
    inner = 0.7978845608028654 * (up + 0.044715 * (up * up * up))
    tanh = jnp.tanh(inner)
    cdf = 0.5 * (1.0 + tanh)
    act = (up * cdf).astype(bf16)
    slope = cdf + 0.5 * up * (1.0 - tanh * tanh) * (
        0.7978845608028654 * (1.0 + (3 * 0.044715) * (up * up))
    )
    ff_part = dot(act, w_down_ref[...])
    gup = (dot_nt(gff[...], w_down_ref[...]) * slope).astype(bf16)
    gnf_part = dot_nt(gup, w_up_ref[...])

    @pl.when(step == 0)
    def _():
        ff_acc[...] = ff_part
        gnf_acc[...] = gnf_part

    @pl.when(step > 0)
    def _():
        ff_acc[...] += ff_part
        gnf_acc[...] += gnf_part

    halves = width // FF_TILE
    chunk = step // halves
    half = step % halves
    col = pl.ds(pl.multiple_of(half * FF_TILE, FF_TILE), FF_TILE)
    per_chunk = up_rows // up_part
    small_ref[pl.ds(4 * pad_u + 2 + chunk, 1), col] = dot(sums[16:32, :], gup)[:1]
    grad_w_up = dot(nfT[...], gup).astype(bf16)
    for s in range(seq_ways):
        side = jnp.where(core == s % 2, 0, 1)
        for h in range(per_chunk):
            lo = s * up_rows + h * up_part
            grads[side, chunk * per_chunk + h, s // 2, 0:up_part, col] = grad_w_up[lo : lo + up_part]
    grad_w_down = dot(act.T, gff[...]).astype(bf16)
    blocks = FF_TILE // down_block
    copies = []
    for b in range(blocks):
        s = step * blocks + b
        side = jnp.where(core == s % 2, 0, 1)
        for k in range(parts):
            lo = b * down_block + k * down_part
            grads[side, k, s // 2, up_part : up_part + down_part, :] = grad_w_down[lo : lo + down_part]

    def region_copy(side, where, index):
        return pltpu.make_async_copy(
            grads.at[side].at[where], refs_out[side].at[where], sems.at[side, index]
        )

    def up_copy(side, j):
        where = (
            pl.ds((j // halves) * per_chunk, per_chunk),
            slice(None),
            pl.ds(0, up_part),
            pl.ds(pl.multiple_of((j % halves) * FF_TILE, FF_TILE), FF_TILE),
        )
        return region_copy(side, where, j)

    def down_copy(side, z, index):
        return region_copy(side, (slice(None), pl.ds(z, 1), pl.ds(up_part, down_part)), index)

    def out_copy(side):
        where = (slice(None), slice(None), pl.ds(up_part + down_part, out_part))
        return region_copy(side, where, ff_total // FF_TILE + z_ways)

    base = ff_total // FF_TILE
    for side in range(2):
        up_copy(side, step).start()
    for b in range(blocks):
        s = step * blocks + b
        for side in range(2):

            @pl.when(lax.rem(s + core, 2) == side)
            def _():
                down_copy(side, s // 2, base + s // 2).start()

    @pl.when(step == steps - 1)
    def _():
        ff_out = ff_acc[...] + b_down_ref[...].astype(f32)
        mixed = after[...]
        go = grad_out()
        output_ref[...] = (mixed + mod(3) * ff_out).astype(bf16)
        rows = sums[...]
        small_ref[3 * pad_u : 4 * pad_u, :] = dot(rows, (go * ff_out).astype(bf16))[:pad_u]
        normed, rstd = norm_stats(mixed)
        gnf = gnf_acc[...]
        small_ref[pad_u : 2 * pad_u, :] = dot(rows, gnf.astype(bf16))[:pad_u]
        small_ref[2 * pad_u : 3 * pad_u, :] = dot(rows, (gnf * normed).astype(bf16))[:pad_u]
        g_after = go + norm_back(gnf * (1.0 + mod(2)), normed, rstd)
        after_grad_ref[...] = g_after
        small_ref[0:pad_u, :] = dot(rows, (g_after * attn_proj[...]).astype(bf16))[:pad_u]
        gattn = (g_after * mod(0)).astype(bf16)
        small_ref[4 * pad_u : 4 * pad_u + 1, :] = dot(rows, gattn)[16:17]
        small_ref[4 * pad_u + 1 : 4 * pad_u + 2, :] = dot(rows, gff[...])[16:17]
        gattT = dot_nt(w_out_ref[...], gattn).astype(bf16)
        for c in range(heads_local):
            for s in range(seq_ways):
                lo = (c * seq_ways + s) * DH
                gatt_ref[s, c * DH : (c + 1) * DH, :] = gattT[lo : lo + DH]
        grad_w_out = dot(attT[...], gattn).astype(bf16)
        for s in range(seq_ways):
            side = jnp.where(core == s % 2, 0, 1)
            for k in range(parts):
                lo = s * up_rows + k * out_part
                grads[side, k, s // 2, up_part + down_part : up_part + down_part + out_part, :] = grad_w_out[
                    lo : lo + out_part
                ]
        for side in range(2):
            out_copy(side).start()
        for side in range(2):
            for j in range(ff_total // FF_TILE):
                up_copy(side, j).wait()
            for z in range(z_ways):
                down_copy(side, z, base + z).wait()
            out_copy(side).wait()


def mid_block(
    lengths, ids, att, hidden, mods, cot, loss, w_out, b_out, w_up, b_up, w_down, b_down, parts
):
    frames, width = hidden.shape
    heads_local = len(att)
    seq_ways = att[0].shape[0]
    ff = w_up.shape[1]
    up_rows = width // seq_ways
    rows = (ff // width * up_rows + ff // seq_ways + up_rows) // parts
    utts = lengths.shape[0]
    f32, bf16 = jnp.float32, jnp.bfloat16
    steps = ff // FF_TILE

    def whole(shape):
        return pl.BlockSpec(shape, lambda j, *_: (0,) * len(shape), pipeline_mode=pl.Buffered(1))

    hbm = pl.BlockSpec(memory_space=pl.ANY)
    gshape = (parts, seq_ways // 2, rows, width)
    out_shape = [
        jax.ShapeDtypeStruct((frames, width), bf16),
        jax.ShapeDtypeStruct((frames, width), f32),
        jax.ShapeDtypeStruct((4 * table_rows(utts) + 8, width), f32),
    ]
    out_shape += [jax.ShapeDtypeStruct((seq_ways, heads_local * DH, frames), bf16)]
    out_specs = [whole(o.shape) for o in out_shape] + [hbm] * 2
    out_shape += [jax.ShapeDtypeStruct(gshape, bf16)] * 2
    ins = list(att) + [hidden, mods, cot, loss, w_out, b_out]
    return pl.pallas_call(
        functools.partial(mid_kernel, (seq_ways, heads_local, utts, ff)),
        out_shape=out_shape,
        grid_spec=pltpu.PrefetchScalarGridSpec(
            num_scalar_prefetch=2,
            grid=(steps,),
            in_specs=[whole(a.shape) for a in ins]
            + [
                pl.BlockSpec((width, FF_TILE), lambda j, *_: (0, j)),
                pl.BlockSpec((1, FF_TILE), lambda j, *_: (0, j)),
                pl.BlockSpec((FF_TILE, width), lambda j, *_: (j, 0)),
                whole((1, width)),
            ],
            out_specs=out_specs,
            scratch_shapes=[
                pltpu.VMEM((width, frames), bf16),
                pltpu.VMEM((frames, width), f32),
                pltpu.VMEM((frames, width), f32),
                pltpu.VMEM((frames, width), bf16),
                pltpu.VMEM((width, frames), bf16),
                pltpu.VMEM((frames, width), bf16),
                pltpu.VMEM((frames, width), f32),
                pltpu.VMEM((frames, width), f32),
                pltpu.VMEM((32, frames), bf16),
                pltpu.VMEM((frames, 128), bf16),
                pltpu.VMEM((128, 4 * width), bf16),
                pltpu.VMEM((2,) + gshape, bf16),
                pltpu.SemaphoreType.DMA((2, steps + seq_ways // 2 + 1)),
            ],
        ),
        compiler_params=pltpu.CompilerParams(vmem_limit_bytes=63 << 20),
        cost_estimate=cost(500),
        name="mid_block",
    )(lengths, ids, *ins, w_up, b_up, w_down, b_down)


def whole_block(shape):
    return pl.BlockSpec(shape, lambda *_: (0,) * len(shape), pipeline_mode=pl.Buffered(1))


def segment_rows(lengths_ref, drop_ref, utts, base, width):
    col = base + lax.broadcasted_iota(jnp.int32, (1, width), 1)
    start = jnp.int32(0)
    kept = jnp.zeros((1, width), jnp.float32)
    place = jnp.zeros((1, width), jnp.int32)
    for u in range(utts):
        end = start + lengths_ref[u]
        inside = (col >= start) & (col < end)
        kept = jnp.where(inside, (1 - drop_ref[u]).astype(jnp.float32), kept)
        place = jnp.where(inside, col - start, place)
        start = end
    return kept, place.astype(jnp.float32)


def rotary_rows(place, half):
    index = lax.broadcasted_iota(jnp.int32, (half, 1), 0).astype(jnp.float32)
    inverse = jnp.exp(index * (-9.210340371976184 / half))
    angles = inverse * place
    return jnp.cos(angles), jnp.sin(angles)


def frame_columns(hot, extra):
    hotb = hot.astype(jnp.bfloat16)
    idx = lax.broadcasted_iota(jnp.int32, hot.shape, 0)
    last = jnp.where(idx == 0, extra, 0.0).astype(jnp.bfloat16)
    return pad_rows([hotb, hotb, hotb, last], 128).T


def head_kernel(
    utts,
    lengths_ref,
    ids_ref,
    drop_ref,
    tokens_ref,
    skip_ref,
    cond_ref,
    mods_ref,
    w_skip_ref,
    b_skip_ref,
    hidden_ref,
    joinedT_ref,
    naT_ref,
    na_ref,
    cols,
):
    f32, bf16 = jnp.float32, jnp.bfloat16
    step = pl.program_id(0)
    frames, width = tokens_ref.shape
    rank = ids_ref[1]

    @pl.when(step == 0)
    def _():
        hot = onehot_rows(lengths_ref, utts, 16, rank * frames, frames)
        kept, _ = segment_rows(lengths_ref, drop_ref, utts, rank * frames, frames)
        cols[...] = frame_columns(hot, kept)
        keep = cols[:, 48:49].astype(f32)
        mixed = (tokens_ref[...].astype(f32) + keep * cond_ref[...].astype(f32)).astype(bf16)
        joinedT_ref[0:width, :] = mixed.T
        hidden_ref[...] = dot(mixed, w_skip_ref[...]) + b_skip_ref[...].astype(f32)

    @pl.when(step == 1)
    def _():
        skip = skip_ref[...]
        joinedT_ref[width : 2 * width, :] = skip.T
        hidden = hidden_ref[...] + dot(skip, w_skip_ref[...])
        hidden_ref[...] = hidden
        madd = mods_operand(mods_ref)
        shift = dot(cols[...], madd[:, :width])
        scale = dot(cols[...], madd[:, width:])
        normed, _ = norm_stats(hidden)
        value = (normed * (1.0 + scale) + shift).astype(bf16)
        na_ref[...] = value
        naT_ref[...] = value.T


def head_block(lengths, ids, drop, tokens, skip, cond, mods, w_skip, b_skip):
    frames, width = tokens.shape
    utts = lengths.shape[0]
    f32, bf16 = jnp.float32, jnp.bfloat16

    def whole(shape):
        return pl.BlockSpec(shape, lambda j, *_: (0,) * len(shape), pipeline_mode=pl.Buffered(1))

    out_shape = [
        jax.ShapeDtypeStruct((frames, width), f32),
        jax.ShapeDtypeStruct((2 * width, frames), bf16),
        jax.ShapeDtypeStruct((width, frames), bf16),
        jax.ShapeDtypeStruct((frames, width), bf16),
    ]
    return pl.pallas_call(
        functools.partial(head_kernel, utts),
        out_shape=out_shape,
        grid_spec=pltpu.PrefetchScalarGridSpec(
            num_scalar_prefetch=3,
            grid=(2,),
            in_specs=[whole(a.shape) for a in (tokens, skip, cond, mods)]
            + [pl.BlockSpec((width, width), lambda j, *_: (j, 0)), whole((1, width))],
            out_specs=[whole(o.shape) for o in out_shape],
            scratch_shapes=[pltpu.VMEM((frames, 128), bf16)],
        ),
        compiler_params=pltpu.CompilerParams(vmem_limit_bytes=48 << 20),
        cost_estimate=cost(100),
        name="head_block",
    )(lengths, ids, drop, tokens, skip, cond, mods, w_skip, b_skip)


def turn_heads(tensor, cosine, sine):
    half = DH // 2
    first, second = tensor[:, :half], tensor[:, half:]
    return jnp.concatenate([first * cosine - second * sine, second * cosine + first * sine], axis=1)


def qkv_kernel(utts, seq_ways, lengths_ref, ids_ref, drop_ref, na_ref, w_ref, b_ref, out_ref, trig):
    f32, bf16 = jnp.float32, jnp.bfloat16
    part = pl.program_id(0)
    frames = na_ref.shape[0]

    @pl.when(part == 0)
    def _():
        _, place = segment_rows(lengths_ref, drop_ref, utts, ids_ref[1] * frames, frames)
        cosine, sine = rotary_rows(place, DH // 2)
        trig[0] = cosine
        trig[1] = sine

    raw = dot(na_ref[...], w_ref[...]) + b_ref[...].astype(f32)
    rawT = raw.T.reshape(seq_ways, DH, frames)
    turned = part < 2
    cosine = jnp.where(turned, trig[0], 1.0)[None]
    sine = jnp.where(turned, trig[1], 0.0)[None]
    out_ref[:, pl.ds(pl.multiple_of(part * DH, DH), DH), :] = turn_heads(rawT, cosine, sine).astype(bf16)


def qkv_block(lengths, ids, drop, na, w_qkv, b_qkv, chunk, seq_ways):
    frames, width = na.shape
    cols = seq_ways * DH
    chunks = width // cols
    utts = lengths.shape[0]

    def whole(shape):
        return pl.BlockSpec(shape, lambda j, *_: (0,) * len(shape), pipeline_mode=pl.Buffered(1))

    shape = (seq_ways, 3 * DH, frames)
    return pl.pallas_call(
        functools.partial(qkv_kernel, utts, seq_ways),
        out_shape=jax.ShapeDtypeStruct(shape, jnp.bfloat16),
        grid_spec=pltpu.PrefetchScalarGridSpec(
            num_scalar_prefetch=3,
            grid=(3,),
            in_specs=[
                whole(na.shape),
                pl.BlockSpec((width, cols), lambda j, *_: (0, j * chunks + chunk)),
                pl.BlockSpec((1, cols), lambda j, *_: (0, j * chunks + chunk)),
            ],
            out_specs=whole(shape),
            scratch_shapes=[pltpu.VMEM((2, DH // 2, frames), jnp.float32)],
        ),
        cost_estimate=cost(75),
        name="qkv_block",
    )(lengths, ids, drop, na, w_qkv, b_qkv)


def back_kernel(utts, seq_ways, chunk, lengths_ref, ids_ref, drop_ref, grad_ref, naT_ref, w_ref, *refs):
    first = chunk == 0
    acc_in = None if first else refs[0]
    acc_ref, bias_ref, keep_ref, send_ref, trig, grads, sems = refs[0 if first else 3 :]
    f32, bf16 = jnp.float32, jnp.bfloat16
    part = pl.program_id(0)
    width, frames = naT_ref.shape
    core = ids_ref[0]
    parts = keep_ref.shape[0]
    own = width // seq_ways
    rows = own // parts

    @pl.when(part == 0)
    def _():
        _, place = segment_rows(lengths_ref, drop_ref, utts, ids_ref[1] * frames, frames)
        cosine, sine = rotary_rows(place, DH // 2)
        trig[0] = cosine
        trig[1] = sine

    turned = part < 2
    cosine = jnp.where(turned, trig[0], 1.0)[None]
    sine = jnp.where(turned, trig[1], 0.0)[None]
    raw = grad_ref[:, pl.ds(pl.multiple_of(part * DH, DH), DH), :].astype(f32)
    gpT = turn_heads(raw, cosine, -sine).astype(bf16).reshape(seq_ways * DH, frames)
    gna = dot(w_ref[...], gpT)

    @pl.when(part == 0)
    def _():
        acc_ref[...] = gna if first else acc_in[...] + gna

    @pl.when(part > 0)
    def _():
        acc_ref[...] += gna

    ones = jnp.ones((8, frames), bf16)
    bias_ref[0] = dot_nt(ones, gpT)
    grad_w = dot_nt(naT_ref[...], gpT).astype(bf16)
    cols = seq_ways * DH
    at = pl.ds(pl.multiple_of(part * rows, rows), rows)
    for s in range(seq_ways):
        side = jnp.where(core == s % 2, 0, 1)
        for k in range(parts):
            lo = s * own + k * rows
            grads[side, k, s // 2, at, :] = grad_w[lo : lo + rows]

    def copy(side, p):
        where = (slice(None), slice(None), pl.ds(pl.multiple_of(p * rows, rows), rows))
        return pltpu.make_async_copy(
            grads.at[side].at[where],
            (keep_ref, send_ref)[side].at[(*where, pl.ds(chunk * cols, cols))],
            sems.at[side, p],
        )

    for side in (1, 0):
        copy(side, part).start()

    @pl.when(part == 2)
    def _():
        for side in (1, 0):
            for p in range(3):
                copy(side, p).wait()


def back_block(lengths, ids, drop, grad, naT, w_qkv, before, chunk, parts):
    seq_ways, _, frames = grad.shape
    width = naT.shape[0]
    cols = seq_ways * DH
    chunks = width // cols
    utts = lengths.shape[0]
    f32, bf16 = jnp.float32, jnp.bfloat16
    rows = width // seq_ways // parts

    def whole(shape):
        return pl.BlockSpec(shape, lambda j, *_: (0,) * len(shape), pipeline_mode=pl.Buffered(1))

    gspec = pl.BlockSpec(memory_space=pl.ANY)
    gshape = jax.ShapeDtypeStruct((parts, seq_ways // 2, 3 * rows, width), bf16)
    ins = [grad, naT, w_qkv, *before]
    in_specs = [whole(grad.shape), whole(naT.shape)]
    in_specs += [pl.BlockSpec((width, cols), lambda j, *_: (0, j * chunks + chunk))]
    aliases = {}
    if before:
        in_specs += [whole(before[0].shape), gspec, gspec]
        aliases = {7: 2, 8: 3}
    return pl.pallas_call(
        functools.partial(back_kernel, utts, seq_ways, chunk),
        out_shape=[
            jax.ShapeDtypeStruct((width, frames), f32),
            jax.ShapeDtypeStruct((3, 8, cols), f32),
            gshape,
            gshape,
        ],
        grid_spec=pltpu.PrefetchScalarGridSpec(
            num_scalar_prefetch=3,
            grid=(3,),
            in_specs=in_specs,
            out_specs=[
                whole((width, frames)),
                pl.BlockSpec((1, 8, cols), lambda j, *_: (j, 0, 0)),
                gspec,
                gspec,
            ],
            scratch_shapes=[
                pltpu.VMEM((2, DH // 2, frames), f32),
                pltpu.VMEM((2, parts, seq_ways // 2, 3 * rows, cols), bf16),
                pltpu.SemaphoreType.DMA((2, 3)),
            ],
        ),
        compiler_params=pltpu.CompilerParams(vmem_limit_bytes=48 << 20),
        cost_estimate=cost(100),
        input_output_aliases=aliases,
        name="back_block",
    )(lengths, ids, drop, *ins)


def norm_kernel(
    utts, heads_local, lengths_ref, ids_ref, acc_ref, hidden_ref, after_ref, mods_ref, loss_ref, mid_ref, *refs
):
    f32, bf16 = jnp.float32, jnp.bfloat16
    bias_refs, (gh_ref, small_ref) = refs[:heads_local], refs[heads_local:]
    frames, width = hidden_ref.shape
    pad_u = table_rows(utts)
    base = 6 * pad_u
    hot = onehot_rows(lengths_ref, utts, 16, ids_ref[1] * frames, frames)
    cols = frame_columns(hot, jnp.zeros((1, frames), f32))
    madd = mods_operand(mods_ref)
    scale = dot(cols, madd[:, width:])
    gna = acc_ref[...].T
    normed, rstd = norm_stats(hidden_ref[...])
    sums = sum_rows(hot, 16, frames)
    small_ref[0:pad_u, :] = dot(sums, gna.astype(bf16))[:pad_u]
    small_ref[pad_u : 2 * pad_u, :] = dot(sums, (gna * normed).astype(bf16))[:pad_u]
    gh = (after_ref[...] + norm_back(gna * (1.0 + scale), normed, rstd)).astype(bf16)
    gh_ref[...] = gh
    small_ref[2 * pad_u : base, :] = mid_ref[0 : 4 * pad_u, :]
    cols_local = width // heads_local
    for c in range(heads_local):
        for p in range(3):
            small_ref[base + p : base + p + 1, c * cols_local : (c + 1) * cols_local] = bias_refs[c][p, 0:1, :]
    small_ref[base + 3 : base + 4, :] = dot(sums, gh)[16:17]
    small_ref[base + 4 : base + 12, :] = mid_ref[4 * pad_u : 4 * pad_u + 8, :]
    count = jnp.sum(loss_ref[...].astype(f32), axis=1, keepdims=True)
    small_ref[base + 12 : base + 16, :] = jnp.broadcast_to(count, (4, width))


def norm_block(lengths, ids, acc, hidden, after, mods, loss, mid_small, biases):
    frames, width = hidden.shape
    utts = lengths.shape[0]
    out_shape = [
        jax.ShapeDtypeStruct((frames, width), jnp.bfloat16),
        jax.ShapeDtypeStruct((6 * table_rows(utts) + 16, width), jnp.float32),
    ]
    return pl.pallas_call(
        functools.partial(norm_kernel, utts, len(biases)),
        out_shape=out_shape,
        grid_spec=pltpu.PrefetchScalarGridSpec(
            num_scalar_prefetch=2,
            grid=(1,),
            in_specs=[whole_block(a.shape) for a in (acc, hidden, after, mods, loss, mid_small, *biases)],
            out_specs=[whole_block(o.shape) for o in out_shape],
        ),
        compiler_params=pltpu.CompilerParams(vmem_limit_bytes=48 << 20),
        cost_estimate=cost(50),
        name="norm_block",
    )(lengths, ids, acc, hidden, after, mods, loss, mid_small, *biases)


def skip_kernel(seq_ways, ids_ref, joinedT_ref, gh_ref, keep_ref, send_ref, grads, sems):
    step = pl.program_id(0)
    core = ids_ref[0]
    parts = keep_ref.shape[0]
    width = joinedT_ref.shape[0]
    block = 2 * width // seq_ways
    rows = block // parts
    z_step = seq_ways // 4
    grad_w = dot(joinedT_ref[...], gh_ref[...]).astype(jnp.bfloat16)
    for b in range(width // block):
        side = jnp.where(core == b % 2, 0, 1)
        for k in range(parts):
            lo = b * block + k * rows
            grads[side, k, step * z_step + b // 2] = grad_w[lo : lo + rows]

    def copy(side, at):
        where = (slice(None), pl.ds(at * z_step, z_step))
        return pltpu.make_async_copy(
            grads.at[side].at[where], (keep_ref, send_ref)[side].at[where], sems.at[side, at]
        )

    for side in (1, 0):
        copy(side, step).start()

    @pl.when(step == 1)
    def _():
        for side in (1, 0):
            for at in range(2):
                copy(side, at).wait()


def skip_block(ids, joinedT, gh, seq_ways, parts):
    frames, width = gh.shape
    rows = 2 * width // seq_ways // parts
    gshape = (parts, seq_ways // 2, rows, width)
    return pl.pallas_call(
        functools.partial(skip_kernel, seq_ways),
        out_shape=[jax.ShapeDtypeStruct(gshape, jnp.bfloat16)] * 2,
        grid_spec=pltpu.PrefetchScalarGridSpec(
            num_scalar_prefetch=1,
            grid=(2,),
            in_specs=[pl.BlockSpec((width, frames), lambda j, *_: (j, 0)), whole_block(gh.shape)],
            out_specs=[pl.BlockSpec(memory_space=pl.ANY)] * 2,
            scratch_shapes=[pltpu.VMEM((2,) + gshape, jnp.bfloat16), pltpu.SemaphoreType.DMA((2, 2))],
        ),
        compiler_params=pltpu.CompilerParams(vmem_limit_bytes=32 << 20),
        cost_estimate=cost(50),
        name="skip_block",
    )(ids, joinedT, gh)


def joined_kernel(gh_ref, w_ref, scale_ref, first_ref, second_ref):
    step = pl.program_id(0)
    value = dot_nt(gh_ref[...], w_ref[...]) * scale_ref[0:1, 0:1]

    @pl.when(step == 0)
    def _():
        first_ref[...] = value

    @pl.when(step == 1)
    def _():
        second_ref[...] = value


def joined_block(gh, w_skip, scale):
    frames, width = gh.shape
    out = jax.ShapeDtypeStruct((frames, width), jnp.float32)
    return pl.pallas_call(
        joined_kernel,
        out_shape=[out, out],
        grid_spec=pltpu.PrefetchScalarGridSpec(
            num_scalar_prefetch=0,
            grid=(2,),
            in_specs=[
                whole_block(gh.shape),
                pl.BlockSpec((width, width), lambda j: (j, 0)),
                whole_block(scale.shape),
            ],
            out_specs=[whole_block(out.shape)] * 2,
        ),
        compiler_params=pltpu.CompilerParams(vmem_limit_bytes=32 << 20),
        cost_estimate=cost(50),
        name="joined_block",
    )(gh, w_skip, scale)


def add_bf16(left, right):
    return (left.astype(jnp.float32) + right.astype(jnp.float32)).astype(jnp.bfloat16)


def first_kernel(pairs, splits, ids_ref, *refs):
    ins, outs = refs[: 8 * pairs], list(refs[8 * pairs :])
    for i in range(4):
        own = [outs.pop(0) for _ in range(splits if i < 2 else 1)]
        at = 0
        for p in range(pairs):
            left, right = ins[2 * (i * pairs + p)], ins[2 * (i * pairs + p) + 1]
            rows = left.shape[-2]
            value = add_bf16(left[0, 0, 0], right[0, 0, 0])
            if len(own) == 1:
                own[0][0, :, at : at + rows, :] = value
            else:
                for out in own:
                    out[0] = value[:, at : at + out.shape[2], :]
                    at += out.shape[2]
            at += rows


def first_sum(ids, pairs, splits):
    _, _, _, z_ways, _, width = pairs[0][0].shape
    total = sum(k.shape[4] for k, _ in pairs)
    step = 1 if total > 100 else z_ways

    def source(half, axis, mine, rows):
        def at(g, z, ids):
            bit = ids[axis]
            return half, bit if mine else 1 - bit, g, z, 0, 0

        return pl.BlockSpec((1, 1, 1, step, rows, width), at)

    order = [(0, 2, False), (1, 3, False), (0, 2, True), (1, 3, True)]
    sizes = [*splits, *splits, total, total]
    return pl.pallas_call(
        functools.partial(first_kernel, len(pairs), len(splits)),
        out_shape=[jax.ShapeDtypeStruct((2, z_ways, n, width), jnp.bfloat16) for n in sizes],
        grid_spec=pltpu.PrefetchScalarGridSpec(
            num_scalar_prefetch=1,
            grid=(2, z_ways // step),
            in_specs=[source(*o, a.shape[4]) for o in order for pair in pairs for a in pair],
            out_specs=[pl.BlockSpec((1, step, n, width), lambda g, z, ids: (g, z, 0, 0)) for n in sizes],
        ),
        compiler_params=pltpu.CompilerParams(vmem_limit_bytes=48 << 20),
        cost_estimate=cost(60),
        name="first_sum",
    )(ids, *([a for pair in pairs for a in pair] * 4))


def second_kernel(pieces, ids_ref, *refs):
    for i in range(4):
        keep, *got = refs[(pieces + 1) * i : (pieces + 1) * (i + 1)]
        out = refs[4 * (pieces + 1) + i]
        at = 0
        for g in got:
            rows = g.shape[2]
            out[:, at : at + rows, :] = add_bf16(keep[0, :, at : at + rows, :], g[0])
            at += rows


def second_sum(ids, keep_a, got_a, keep_b, got_b):
    _, z_ways, rows, width = keep_a.shape
    step = z_ways // 2 if rows > 100 else z_ways

    def source(axis, mine, value):
        def at(z, ids):
            bit = ids[axis]
            return bit if mine else 1 - bit, z, 0, 0

        return pl.BlockSpec((1, step, *value.shape[2:]), at)

    order = [(3, False), (2, False), (3, True), (2, True)]
    sides = [[keep_a, *got_a], [keep_b, *got_b]]
    out = jax.ShapeDtypeStruct((z_ways, rows, width), jnp.bfloat16)
    return pl.pallas_call(
        functools.partial(second_kernel, len(got_a)),
        out_shape=[out] * 4,
        grid_spec=pltpu.PrefetchScalarGridSpec(
            num_scalar_prefetch=1,
            grid=(z_ways // step,),
            in_specs=[source(*o, v) for i, o in enumerate(order) for v in sides[i % 2]],
            out_specs=[pl.BlockSpec((step, rows, width), lambda z, ids: (z, 0, 0))] * 4,
        ),
        compiler_params=pltpu.CompilerParams(vmem_limit_bytes=48 << 20),
        cost_estimate=cost(30),
        name="second_sum",
    )(ids, *((sides[0] + sides[1]) * 2))


def third_kernel(ids_ref, keep_a, got_a, keep_b, got_b, *outs):
    for j, out in enumerate(outs):
        at = ids_ref[4] ^ j
        out[0] = add_bf16(keep_a[at], got_a[at])
        out[1] = add_bf16(keep_b[at], got_b[at])


def third_sum(ids, keep_a, got_a, keep_b, got_b):
    z_ways, rows, width = keep_a.shape
    out = jax.ShapeDtypeStruct((2, rows, width), jnp.bfloat16)
    return pl.pallas_call(
        third_kernel,
        out_shape=[out] * z_ways,
        grid_spec=pltpu.PrefetchScalarGridSpec(
            num_scalar_prefetch=1,
            grid=(1,),
            in_specs=[whole_block(keep_a.shape)] * 4,
            out_specs=[whole_block(out.shape)] * z_ways,
        ),
        cost_estimate=cost(10),
        name="third_sum",
    )(ids, keep_a, got_a, keep_b, got_b)


def third_all_kernel(ids_ref, keep_a, got_a, keep_b, got_b, out):
    for z in range(keep_a.shape[0]):
        out[z, 0] = add_bf16(keep_a[z], got_a[z])
        out[z, 1] = add_bf16(keep_b[z], got_b[z])


def third_sum_all(ids, keep_a, got_a, keep_b, got_b):
    z_ways, rows, width = keep_a.shape
    out = jax.ShapeDtypeStruct((z_ways, 2, rows, width), jnp.bfloat16)
    step = max(1, z_ways // 2)
    return pl.pallas_call(
        third_all_kernel,
        out_shape=out,
        grid_spec=pltpu.PrefetchScalarGridSpec(
            num_scalar_prefetch=1,
            grid=(z_ways // step,),
            in_specs=[pl.BlockSpec((step, rows, width), lambda i, *_: (i, 0, 0))] * 4,
            out_specs=pl.BlockSpec((step, 2, rows, width), lambda i, *_: (i, 0, 0, 0)),
        ),
        cost_estimate=cost(10),
        name="third_sum_all",
    )(ids, keep_a, got_a, keep_b, got_b)


def fourth_all_kernel(x, out):
    total = x[0].astype(jnp.float32)
    for z in range(1, x.shape[0]):
        total = total + x[z].astype(jnp.float32)
    out[...] = total.astype(jnp.bfloat16)


def fourth_sum_all(terms):
    return pl.pallas_call(
        fourth_all_kernel,
        out_shape=jax.ShapeDtypeStruct(terms.shape[1:], jnp.bfloat16),
        grid=(1,),
        in_specs=[whole_block(terms.shape)],
        out_specs=whole_block(terms.shape[1:]),
        cost_estimate=cost(10),
        name="fourth_sum_all",
    )(terms)


def fourth_kernel(*refs):
    total = refs[0][...].astype(jnp.float32)
    for r in refs[1:-1]:
        total = total + r[...].astype(jnp.float32)
    refs[-1][...] = total.astype(jnp.bfloat16)


def fourth_sum(terms):
    shape = terms[0].shape
    return pl.pallas_call(
        fourth_kernel,
        out_shape=jax.ShapeDtypeStruct(shape, jnp.bfloat16),
        grid=(1,),
        in_specs=[whole_block(shape)] * len(terms),
        out_specs=whole_block(shape),
        cost_estimate=cost(10),
        name="fourth_sum",
    )(*terms)


def place_kernel(streams, plan, ids_ref, scale_ref, *refs):
    blocks, outs = refs[: 4 * streams], refs[4 * streams :]
    x, y = ids_ref[2], ids_ref[3]
    scale = scale_ref[0:1, 0:1]
    for stream, row, rows, lane, lanes, out, row_of, lane_of in plan:
        for d in range(4):
            own_x, own_y = x ^ (d & 1), y ^ (d >> 1)
            for half in range(2):
                k = own_x * 2 + own_y if half == 0 else 4 + own_y * 2 + own_x
                tile = blocks[4 * stream + d][half, row : row + rows, lane : lane + lanes]
                outs[out][row_of(k), lane_of(k)] = tile.astype(jnp.float32) * scale


def place_blocks(ids, scale, streams, plan, shapes):
    blocks = [b for s in streams for b in s]
    outs = [jax.ShapeDtypeStruct(s, jnp.float32) for s in shapes]
    return pl.pallas_call(
        functools.partial(place_kernel, len(streams), plan),
        out_shape=outs,
        grid_spec=pltpu.PrefetchScalarGridSpec(
            num_scalar_prefetch=1,
            grid=(1,),
            in_specs=[whole_block(a.shape) for a in (scale, *blocks)],
            out_specs=[whole_block(o.shape) for o in outs],
        ),
        compiler_params=pltpu.CompilerParams(vmem_limit_bytes=32 << 20),
        cost_estimate=cost(20),
        name="place_blocks",
    )(ids, scale, *blocks)


def span(start, size):
    return pl.ds(pl.multiple_of(start, size), size)


def ada_kernel(groups, pad_u, numerator, time_ref, *refs):
    f32 = jnp.float32
    parts, (weight_ref, vector_ref, scale_ref) = refs[:groups], refs[groups:]
    table = pl.program_id(0)
    base = 6 * pad_u
    count = parts[0][base + 12 : base + 13, 0:1]
    for p in parts[1:]:
        count = count + p[base + 12 : base + 13, 0:1]
    scale = numerator / count
    rows = jnp.concatenate([p[pl.ds(pl.multiple_of(table * pad_u, 8), pad_u), :] for p in parts], axis=0) * scale
    vector_ref[pl.ds(table, 1), :] = jnp.sum(rows, axis=0, keepdims=True)
    operand = jnp.concatenate(list(split3(rows)), axis=0)
    weight_ref[...] = dot(time_ref[...], operand)

    @pl.when(table == 0)
    def _():
        total = parts[0][base : base + 16, :]
        for p in parts[1:]:
            total = total + p[base : base + 16, :]
        vector_ref[8:24, :] = total * scale
        scale_ref[...] = jnp.broadcast_to(scale, scale_ref.shape)


def ada_block(time3, parts, utts, numerator):
    pad_u = table_rows(utts)
    width = parts[0].shape[1]
    own = time3.shape[0]
    f32 = jnp.float32
    return pl.pallas_call(
        functools.partial(ada_kernel, len(parts), pad_u, numerator),
        out_shape=[
            jax.ShapeDtypeStruct((own, 6 * width), f32),
            jax.ShapeDtypeStruct((24, width), f32),
            jax.ShapeDtypeStruct((8, 128), f32),
        ],
        grid=(6,),
        in_specs=[whole_block(time3.shape)] + [whole_block(p.shape) for p in parts],
        out_specs=[
            pl.BlockSpec((own, width), lambda j: (0, j)),
            whole_block((24, width)),
            whole_block((8, 128)),
        ],
        cost_estimate=cost(50),
        name="ada_block",
    )(time3, *parts)


def sum_exchange(value, axis, bit):
    ways = lax.axis_size(axis)
    return lax.ppermute(value, axis, [(i, i ^ bit) for i in range(ways)])


def axis_bits(ways):
    return [1 << i for i in range(ways.bit_length() - 1)]


def reduce_stages(ids, blocks, splits, whole_z):
    batch_ways = lax.axis_size("batch")
    x_bit, y_bit = 1, 1 << ((batch_ways.bit_length() - 1) // 2)
    pairs = []
    for keep, send in blocks:
        shape = (2, 2, 2) + keep.shape[1:]
        pairs.append((keep.reshape(shape), sum_exchange(send, "seq", 1).reshape(shape)))
    *sends, keep_a, keep_b = first_sum(ids, pairs, splits)
    sends = follow(sends, (yield sends))
    got, token = [[], []], None
    for i in range(len(splits)):
        pieces = follow([sends[i], sends[len(splits) + i]], token)
        for side, bit in enumerate((x_bit, y_bit)):
            got[side].append(sum_exchange(pieces[side], "batch", bit))
        token = yield [got[0][i], got[1][i]]
    got_a, got_b = (follow(g, token) for g in got)
    send_a, send_b, keep_a, keep_b = second_sum(ids, keep_a, got_a, keep_b, got_b)
    send_a, send_b = follow([send_a, send_b], (yield [send_a, send_b]))
    got = [sum_exchange(send_a, "batch", y_bit), sum_exchange(send_b, "batch", x_bit)]
    got_a, got_b = follow(got, (yield got))
    if whole_z:
        ways = lax.axis_size("seq")
        groups = [list(range(c, ways, 2)) for c in range(2)]
        away = [third_sum_all(ids, keep_a, got_a, keep_b, got_b)]
        away = follow(away, (yield away))
        got = [lax.all_to_all(away[0], "seq", 0, 0, axis_index_groups=groups, tiled=True)]
        got = follow(got, (yield got))
        block = fourth_sum_all(got[0])
    else:
        own, *away = third_sum(ids, keep_a, got_a, keep_b, got_b)
        away = follow(away, (yield away))
        got = [sum_exchange(a, "seq", 2 * (j + 1)) for j, a in enumerate(away)]
        got = follow(got, (yield got))
        block = fourth_sum([own] + got)
    for bit in axis_bits(batch_ways):
        if bit not in (x_bit, y_bit):
            block = add_bf16(block, sum_exchange(block, "batch", bit))
    (block,) = follow([block], (yield [block]))
    yield [block] + [sum_exchange(block, "batch", bit) for bit in (x_bit, y_bit, x_bit | y_bit)]


def advance(stages, steps, token=None):
    value = next(stages) if token is None else stages.send(token)
    for _ in range(steps - 1):
        value = next(stages)
    return value


def last_stage(stages, token=None):
    value = stages.send(token)
    for value in stages:
        pass
    return value


def follow(values, token):
    return values if token is None else [after(v, token) for v in values]


def after(value, *others):
    return lax.optimization_barrier((value,) + others)[0]


def gather_groups(value):
    return [value] + [sum_exchange(value, "batch", i) for i in range(1, lax.axis_size("batch"))]


def sum_seq(value):
    for bit in axis_bits(lax.axis_size("seq")):
        value = value + sum_exchange(value, "seq", bit)
    return value


def shards(
    tokens_in,
    skip_in,
    condition,
    cotangent,
    time_embed,
    lengths,
    key_mask,
    drop_mask,
    loss_mask,
    w_skip,
    b_skip,
    w_ada,
    b_ada,
    w_qkv,
    b_qkv,
    w_out,
    b_out,
    w_up,
    b_up,
    w_down,
    b_down,
):
    f32, bf16 = jnp.float32, jnp.bfloat16
    seq_ways, batch_ways = lax.axis_size("seq"), lax.axis_size("batch")
    seq_rank = lax.axis_index("seq")
    frames, width = tokens_in.shape[1:]
    group_frames = frames * seq_ways
    heads_local = HEADS // seq_ways
    utts = lengths.shape[1]
    lengths_row, drop = lengths[0], drop_mask[0]
    batch_rank = lax.axis_index("batch")
    side = 1 << ((batch_ways.bit_length() - 1) // 2)
    ids = [lax.rem(seq_rank, 2), seq_rank, lax.rem(batch_rank, 2), lax.rem(batch_rank // side, 2), seq_rank // 2]
    ids = jnp.stack(ids).astype(jnp.int32)
    ok = key_mask.reshape(seq_ways, 1, frames)
    exchange = functools.partial(lax.all_to_all, axis_name="seq", split_axis=0, concat_axis=0, tiled=True)

    time_act = jax.nn.silu(time_embed[0]).astype(bf16)
    time_rows = jnp.pad(time_act, ((0, 16 - utts), (0, 0)))

    def modulation(first, last):
        return jnp.dot(time_rows, w_ada[:, first:last], preferred_element_type=f32) + b_ada[
            first:last
        ].astype(f32)

    mods_a = modulation(0, 2 * width)
    hidden, joinedT, naT, na = head_block(
        lengths_row, ids, drop, tokens_in[0], skip_in[0], condition[0], mods_a, w_skip, b_skip[None]
    )
    mods_rest = modulation(2 * width, 6 * width)
    received = []
    for c in range(heads_local):
        packed = qkv_block(lengths_row, ids, drop, na, w_qkv, b_qkv[None], c, seq_ways)
        if c == 0:
            na = after(na, mods_rest)
        received.append(exchange(packed))

    own = width // seq_ways
    pad_u = table_rows(utts)
    time_own = lax.dynamic_slice_in_dim(jnp.concatenate(gather_groups(time_rows[:pad_u])), seq_rank * own, own, axis=1)
    time3 = jnp.tile(time_own.T, (1, 3))

    received[0] = after(received[0], mods_rest)
    head_out, log_totals, returned = [], [], []
    for c in range(heads_local):
        out, log_total = attend(lengths_row, received[c], ok)
        head_out.append(out)
        log_totals.append(log_total)
        returned.append(exchange(after(out, *returned)))
        if c < heads_local - 1:
            received[c + 1] = after(received[c + 1], out, time3)
    mid = mid_block(
        lengths_row,
        ids,
        returned,
        hidden,
        mods_rest,
        cotangent[0],
        loss_mask,
        w_out,
        b_out[None],
        w_up,
        b_up[None],
        w_down,
        b_down[None],
        PARTS,
    )
    output, after_grad, mid_small, grad_att, keep, send = mid
    grad_heads = exchange(grad_att)
    front = keep.shape[2] * 4 // 9 // 16 * 16
    feed = reduce_stages(ids, [(keep, send)], [front, keep.shape[2] - front], True)

    ahead = next(feed)
    grad_local = []
    for c in range(heads_local):
        operand = after(grad_heads, *ahead)
        moving = feed.send(grad if c else None) if c < 2 else []
        grad = attend_back(lengths_row, received[c], ok, head_out[c], operand, log_totals[c], c)
        grad_local.append(exchange(after(grad, *moving)))
        ahead = [grad]
    if heads_local == 1:
        next(feed)
    ahead = ahead + advance(feed, 1, ahead[0])
    before, biases = (), []
    for c in range(heads_local):
        acc, bias, keep, send = back_block(
            lengths_row, ids, drop, after(grad_local[c], *ahead), naT, w_qkv, before, c, PARTS
        )
        before = (acc, keep, send)
        biases.append(bias)
        ahead = next(feed) and advance(feed, 1, acc) if c == 0 else []
    moving = next(feed)
    gh, small = norm_block(lengths_row, ids, acc, hidden, after_grad, mods_a, loss_mask, mid_small, biases)
    rest = reduce_stages(ids, [skip_block(ids, joinedT, gh, seq_ways, PARTS), (keep, send)], [5 * own // PARTS], False)
    small = after(small, *moving, *advance(rest, 3))
    token = advance(rest, 2)[0]
    groups = gather_groups(sum_seq(small))
    numerator = float(group_frames * batch_ways)
    grad_w_ada, vectors, scale = ada_block(time3, groups, utts, numerator)
    grad_tokens, grad_skip = joined_block(gh, w_skip, scale)
    next(feed)
    feed = last_stage(feed, token)
    rest = last_stage(rest)

    ff = w_up.shape[1]
    chunks = ff // width
    up_part = chunks * own // PARTS
    down_part = ff // seq_ways // PARTS
    out_part = own // PARTS
    per_chunk = own // up_part
    whole_lanes = lambda k: span(0, width)
    grad_w_up, grad_w_down, grad_w_out = place_blocks(
        ids,
        scale,
        [feed],
        [
            (
                *(0, 0, up_part, 0, width, 0),
                lambda k: span(lax.rem(k, per_chunk) * up_part, up_part),
                lambda k: span(k // per_chunk * width, width),
            ),
            (0, up_part, down_part, 0, width, 1, lambda k: span(k * down_part, down_part), whole_lanes),
            (0, up_part + down_part, out_part, 0, width, 2, lambda k: span(k * out_part, out_part), whole_lanes),
        ],
        [(own, ff), (ff // seq_ways, width), (own, width)],
    )
    skip_part = 2 * own // PARTS
    grad_w_skip, grad_w_qkv = place_blocks(
        ids,
        scale,
        [rest],
        [(0, 0, skip_part, 0, width, 0, lambda k: span(k * skip_part, skip_part), whole_lanes)]
        + [
            (
                *(0, skip_part + p * out_part, out_part, 0, width, 1),
                lambda k: span(k * out_part, out_part),
                lambda k, at=p * width: span(at, width),
            )
            for p in range(3)
        ],
        [(2 * own, width), (own, 3 * width)],
    )

    def own_slice(vector):
        vector = vector.reshape(-1)
        size = vector.shape[0] // seq_ways
        return lax.dynamic_slice_in_dim(vector, seq_rank * size, size)

    grad_b_ada = own_slice(vectors[:6])
    grad_b_qkv = own_slice(vectors[8:11])
    grad_b_skip = own_slice(vectors[11])
    grad_b_out = own_slice(vectors[12])
    grad_b_down = own_slice(vectors[13])
    grad_b_up = own_slice(vectors[14 : 14 + chunks])
    return (
        output[None],
        grad_tokens[None],
        grad_skip[None],
        grad_w_skip,
        grad_b_skip,
        grad_w_ada,
        grad_b_ada,
        grad_w_qkv,
        grad_b_qkv,
        grad_w_out,
        grad_b_out,
        grad_w_up,
        grad_b_up,
        grad_w_down,
        grad_b_down,
    )


def solution(mesh):
    in_specs = (
        P("batch", "seq", None),
        P("batch", "seq", None),
        P("batch", "seq", None),
        P("batch", "seq", None),
        P("batch", None, None),
        P("batch", None),
        P("batch", None),
        P("batch", None),
        P("batch", "seq"),
        P(),
        P(),
        P(),
        P(),
        P(),
        P(),
        P(),
        P(),
        P(),
        P(),
        P(),
        P(),
    )
    out_specs = (
        P("batch", "seq", None),
        P("batch", "seq", None),
        P("batch", "seq", None),
        P("seq", None),
        P("seq"),
        P("seq", None),
        P("seq"),
        P("seq", None),
        P("seq"),
        P("seq", None),
        P("seq"),
        P("seq", None),
        P("seq"),
        P("seq", None),
        P("seq"),
    )
    return jax.shard_map(shards, mesh=mesh, in_specs=in_specs, out_specs=out_specs, check_vma=False)
```

```python
import functools

import jax
import jax.numpy as jnp
from jax import lax
from jax.experimental import pallas as pl
from jax.experimental.pallas import tpu as pltpu
from jax.sharding import PartitionSpec as P

HEADS = 16
HEAD_DIM = 64
PARTS = 8
BIG = 1e30
DH = 64
BQ = 512
BK = 512


def cost(weight):
    return pl.CostEstimate(flops=weight * 100000000, bytes_accessed=weight * 100000, transcendentals=0)


def onehot_rows(lengths_ref, utts, rows, base, width):
    row = lax.broadcasted_iota(jnp.int32, (rows, width), 0)
    col = base + lax.broadcasted_iota(jnp.int32, (rows, width), 1)
    start = jnp.int32(0)
    hot = jnp.zeros((rows, width), jnp.float32)
    for u in range(utts):
        end = start + lengths_ref[u]
        hot = jnp.where((row == u) & (col >= start) & (col < end), 1.0, hot)
        start = end
    return hot


def key_range(lengths_ref, utts, first, last):
    start = jnp.int32(0)
    low, high = jnp.int32(0), jnp.int32(0)
    for u in range(utts):
        end = start + lengths_ref[u]
        low = jnp.where((start <= first) & (first < end), start, low)
        high = jnp.where((start <= last) & (last < end), end, high)
        start = end
    return low // BK, (high + BK - 1) // BK


def aug_rows(utts):
    return -(-utts // 16) * 16


def split3(row):
    a = row.astype(jnp.bfloat16)
    rest = row - a.astype(jnp.float32)
    b = rest.astype(jnp.bfloat16)
    c = (rest - b.astype(jnp.float32)).astype(jnp.bfloat16)
    return a, b, c


def pad_rows(parts, total):
    have = sum(p.shape[0] for p in parts)
    if have < total:
        parts = parts + [jnp.zeros((total - have, parts[0].shape[1]), parts[0].dtype)]
    return jnp.concatenate(parts, axis=0)


def rows16(rows, width):
    idx = lax.broadcasted_iota(jnp.int32, (16, width), 0)
    out = jnp.zeros((16, width), jnp.float32)
    for i, r in enumerate(rows):
        out = jnp.where(idx == i, r, out)
    return out.astype(jnp.bfloat16)


def fwd_kernel(utts, lengths_ref, qkv_ref, ok_ref, out_ref, lse_ref, kaug, vaug):
    sources, _, frames = qkv_ref.shape
    per = frames // BQ
    pad_u = aug_rows(utts)
    step = pl.program_id(0)

    @pl.when(step == 0)
    def _():
        def build(s, c):
            hot = onehot_rows(lengths_ref, utts, pad_u, s * frames, frames)
            ok = ok_ref[s].astype(jnp.float32)
            block = qkv_ref[s]
            one = jnp.ones((1, frames), jnp.float32)
            kT = pad_rows(
                [block[DH : 2 * DH], (1.0 - hot).astype(jnp.bfloat16), rows16([1.0 - ok], frames)], 128
            )
            kaug[pl.ds(pl.multiple_of(s * frames, frames), frames), :] = kT.T
            vT = jnp.concatenate([block[2 * DH :], rows16([one], frames)], axis=0)
            for t in range(frames // BK):
                vaug[s * (frames // BK) + t] = vT[:, t * BK : (t + 1) * BK]
            return c

        lax.fori_loop(0, sources, build, 0)

    block = qkv_ref[step]
    hot_q = onehot_rows(lengths_ref, utts, pad_u, step * frames, frames)
    qT = (block[:DH].astype(jnp.float32) * 0.125)
    one = jnp.ones((1, frames), jnp.float32)
    qaug = pad_rows(
        [qT.astype(jnp.bfloat16), (hot_q * -BIG).astype(jnp.bfloat16), rows16([one * -BIG], frames)], 128
    )
    kT = block[DH : 2 * DH].astype(jnp.float32)
    vT = block[2 * DH :].astype(jnp.float32)
    ok = ok_ref[step] > 0
    s_self = jnp.sum(qT * kT, axis=0, keepdims=True)
    m0 = jnp.where(ok, -3e38, s_self)
    acc0 = jnp.concatenate([jnp.where(ok, 0.0, vT), jnp.where(ok, 0.0, jnp.ones((16, frames), jnp.float32))], axis=0)
    for t in range(per):
        cols = slice(t * BQ, (t + 1) * BQ)
        low, high = key_range(lengths_ref, utts, step * frames + t * BQ, step * frames + (t + 1) * BQ - 1)
        q_b = qaug[:, cols]

        def body(j, carry):
            m, acc = carry
            s = jnp.dot(kaug[pl.ds(pl.multiple_of(j * BK, BK), BK), :], q_b, preferred_element_type=jnp.float32)
            m_new = jnp.maximum(m, jnp.max(s, axis=0, keepdims=True))
            p = jnp.exp(s - m_new).astype(jnp.bfloat16)
            alpha = jnp.exp(m - m_new)
            acc = acc * alpha + jnp.dot(vaug[j], p, preferred_element_type=jnp.float32)
            return m_new, acc

        m, acc = lax.fori_loop(low, high, body, (m0[:, cols], acc0[:, cols]))
        total = acc[DH : DH + 1]
        out_ref[0, :, cols] = (acc[:DH] / total).astype(jnp.bfloat16)
        lse_ref[0, :, cols] = m + jnp.log(total)


def attend(lengths, qkv, ok):
    sources, _, frames = qkv.shape
    total = sources * frames
    utts = lengths.shape[0]
    whole = lambda shape: pl.BlockSpec(shape, lambda i, *_: (0,) * len(shape))
    return pl.pallas_call(
        functools.partial(fwd_kernel, utts),
        out_shape=(
            jax.ShapeDtypeStruct((sources, DH, frames), jnp.bfloat16),
            jax.ShapeDtypeStruct((sources, 1, frames), jnp.float32),
        ),
        grid_spec=pltpu.PrefetchScalarGridSpec(
            num_scalar_prefetch=1,
            grid=(sources,),
            in_specs=[whole(qkv.shape), whole(ok.shape)],
            out_specs=(
                pl.BlockSpec((1, DH, frames), lambda i, *_: (i, 0, 0)),
                pl.BlockSpec((1, 1, frames), lambda i, *_: (i, 0, 0)),
            ),
            scratch_shapes=[
                pltpu.VMEM((total, 128), jnp.bfloat16),
                pltpu.VMEM((total // BK, DH + 16, BK), jnp.bfloat16),
            ],
        ),
        cost_estimate=cost(250),
        name="attend",
    )(lengths, qkv, ok)


def bwd_kernel(utts, chunk, lengths_ref, qkv_ref, ok_ref, o_ref, do_ref, lse_ref, out_ref, kaug, vnat, kT_s, dk, dv):
    sources, _, frames = qkv_ref.shape
    per = frames // BK
    pad_u = aug_rows(utts)
    step = pl.program_id(0)
    f32 = jnp.float32

    @pl.when(step == 0)
    def _():
        def build(s, c):
            hot = onehot_rows(lengths_ref, utts, pad_u, s * frames, frames)
            ok = ok_ref[s]
            block = qkv_ref[s]
            one = jnp.ones((1, frames), f32)
            kT = block[DH : 2 * DH]
            vT = block[2 * DH :]
            kA = pad_rows(
                [kT, (1.0 - hot).astype(jnp.bfloat16), rows16([1.0 - ok.astype(f32), one, one, one], frames)], 128
            )
            rows = pl.ds(pl.multiple_of(s * frames, frames), frames)
            kaug[rows, :] = kA.T
            vnat[rows, :] = pad_rows([vT, rows16([one, one, one], frames)], 128).T
            qT = block[:DH].astype(f32) * 0.125
            do = do_ref[s, chunk * DH : (chunk + 1) * DH, :].astype(f32)
            s_self = jnp.sum(qT * kT.astype(f32), axis=0, keepdims=True)
            delta = jnp.sum(do * o_ref[s].astype(f32), axis=0, keepdims=True)
            p_self = jnp.where(ok > 0, 0.0, jnp.exp(s_self - lse_ref[s]))
            ds_self = p_self * (jnp.sum(do * vT.astype(f32), axis=0, keepdims=True) - delta)
            dk0 = ds_self * qT
            dv0 = p_self * do
            for t in range(per):
                cols = slice(t * BK, (t + 1) * BK)
                kT_s[s * per + t] = kT[:, cols]
                dk[s * per + t] = dk0[:, cols]
                dv[s * per + t] = dv0[:, cols]
            return c

        lax.fori_loop(0, sources, build, 0)

    block = qkv_ref[step]
    one = jnp.ones((1, frames), f32)
    hot_q = onehot_rows(lengths_ref, utts, pad_u, step * frames, frames)
    qT = block[:DH].astype(f32) * 0.125
    qTb = qT.astype(jnp.bfloat16)
    kT = block[DH : 2 * DH].astype(f32)
    vT = block[2 * DH :].astype(f32)
    ok = ok_ref[step]
    dob = do_ref[step, chunk * DH : (chunk + 1) * DH, :]
    do = dob.astype(f32)
    lse = lse_ref[step]
    delta = jnp.sum(do * o_ref[step].astype(f32), axis=0, keepdims=True)
    l3 = [-r.astype(f32) for r in split3(lse)]
    d3 = [-r.astype(f32) for r in split3(delta)]
    qaug = pad_rows([qTb, (hot_q * -BIG).astype(jnp.bfloat16), rows16([one * -BIG] + l3, frames)], 128)
    doaug = pad_rows([dob, rows16(d3, frames)], 128)
    s_self = jnp.sum(qT * kT, axis=0, keepdims=True)
    p_self = jnp.where(ok > 0, 0.0, jnp.exp(s_self - lse))
    ds_self = p_self * (jnp.sum(do * vT, axis=0, keepdims=True) - delta)
    dq0 = ds_self * kT
    nt = (((1,), (1,)), ((), ()))
    for t in range(frames // BQ):
        cols = slice(t * BQ, (t + 1) * BQ)
        low, high = key_range(lengths_ref, utts, step * frames + t * BQ, step * frames + (t + 1) * BQ - 1)
        q_a = qaug[:, cols]
        q_b = qTb[:, cols]
        do_a = doaug[:, cols]
        do_b = dob[:, cols]

        def body(j, dq):
            rows = pl.ds(pl.multiple_of(j * BK, BK), BK)
            s = jnp.dot(kaug[rows, :], q_a, preferred_element_type=f32)
            dp = jnp.dot(vnat[rows, :], do_a, preferred_element_type=f32)
            p = jnp.exp(s)
            ds = (p * dp).astype(jnp.bfloat16)
            dv[j] += lax.dot_general(do_b, p.astype(jnp.bfloat16), nt, preferred_element_type=f32)
            dk[j] += lax.dot_general(q_b, ds, nt, preferred_element_type=f32)
            return dq + jnp.dot(kT_s[j], ds, preferred_element_type=f32)

        dq = lax.fori_loop(low, high, body, dq0[:, cols])
        out_ref[step, :DH, cols] = (dq * 0.125).astype(jnp.bfloat16)

    @pl.when(step == sources - 1)
    def _():
        def finish(s, c):
            for t in range(per):
                cols = slice(t * BK, (t + 1) * BK)
                out_ref[s, DH : 2 * DH, cols] = dk[s * per + t].astype(jnp.bfloat16)
                out_ref[s, 2 * DH :, cols] = dv[s * per + t].astype(jnp.bfloat16)
            return c

        lax.fori_loop(0, sources, finish, 0)


def attend_back(lengths, qkv, ok, out, grad, lse, chunk):
    sources, _, frames = qkv.shape
    total = sources * frames
    utts = lengths.shape[0]
    whole = lambda shape: pl.BlockSpec(shape, lambda i, *_: (0,) * len(shape))
    return pl.pallas_call(
        functools.partial(bwd_kernel, utts, chunk),
        out_shape=jax.ShapeDtypeStruct(qkv.shape, jnp.bfloat16),
        grid_spec=pltpu.PrefetchScalarGridSpec(
            num_scalar_prefetch=1,
            grid=(sources,),
            in_specs=[whole(a.shape) for a in (qkv, ok, out, grad, lse)],
            out_specs=whole(qkv.shape),
            scratch_shapes=[
                pltpu.VMEM((total, 128), jnp.bfloat16),
                pltpu.VMEM((total, 128), jnp.bfloat16),
                pltpu.VMEM((total // BK, DH, BK), jnp.bfloat16),
                pltpu.VMEM((total // BK, DH, BK), jnp.float32),
                pltpu.VMEM((total // BK, DH, BK), jnp.float32),
            ],
        ),
        cost_estimate=cost(320),
        name="attend_back",
    )(lengths, qkv, ok, out, grad, lse)


FF_TILE = 512
EPS = 1e-06


def dot(left, right):
    return jnp.dot(left, right, preferred_element_type=jnp.float32)


def dot_nt(left, right):
    return lax.dot_general(left, right, (((1,), (1,)), ((), ())), preferred_element_type=jnp.float32)


def norm_stats(x):
    mean = jnp.mean(x, axis=1, keepdims=True)
    centred = x - mean
    rstd = lax.rsqrt(jnp.mean(centred * centred, axis=1, keepdims=True) + EPS)
    return centred * rstd, rstd


def norm_back(grad, normed, rstd):
    first = jnp.mean(grad, axis=1, keepdims=True)
    second = jnp.mean(grad * normed, axis=1, keepdims=True)
    return rstd * (grad - first - normed * second)


def mods_operand(mods_ref):
    rows = mods_ref[...]
    return pad_rows(list(split3(rows)), 128)


def table_rows(utts):
    return -(-utts // 8) * 8


def sum_rows(hot, utts_pad, frames):
    idx = lax.broadcasted_iota(jnp.int32, (16, frames), 0)
    ones = jnp.where(idx == 0, 1.0, 0.0).astype(jnp.bfloat16)
    return jnp.concatenate([hot.astype(jnp.bfloat16), ones], axis=0)


def mid_kernel(
    dims,
    lengths_ref,
    ids_ref,
    *refs,
):
    seq_ways, heads_local, utts, ff = dims
    att_refs = refs[:heads_local]
    (
        hidden_ref,
        mods_ref,
        cot_ref,
        loss_ref,
        w_out_ref,
        b_out_ref,
        w_up_ref,
        b_up_ref,
        w_down_ref,
        b_down_ref,
    ) = refs[heads_local : heads_local + 10]
    outs = refs[heads_local + 10 :]
    output_ref, after_grad_ref, small_ref, gatt_ref = outs[:4]
    refs_out = outs[4:6]
    (
        attT,
        attn_proj,
        after,
        nf,
        nfT,
        gff,
        ff_acc,
        gnf_acc,
        sums,
        cols,
        madd,
        grads,
        sems,
    ) = outs[6:]
    f32, bf16 = jnp.float32, jnp.bfloat16
    step = pl.program_id(0)
    steps = pl.num_programs(0)
    core = ids_ref[0]
    rank = ids_ref[1]
    frames, width = hidden_ref.shape
    up_rows = width // seq_ways
    down_rows = FF_TILE
    z_ways = seq_ways // 2
    parts = grads.shape[1]
    pad_u = table_rows(utts)
    ff_total = ff
    up_part = ff_total // width * up_rows // parts
    down_block = ff_total // seq_ways
    down_part = down_block // parts
    out_part = up_rows // parts

    def mod(index):
        return dot(cols[...], madd[:, index * width : (index + 1) * width])

    def grad_out():
        loss = cols[:, 48:49].astype(f32)
        return cot_ref[...].astype(f32) * loss

    @pl.when(step == 0)
    def _():
        hot = onehot_rows(lengths_ref, utts, 16, rank * frames, frames)
        hotb = hot.astype(bf16)
        idx = lax.broadcasted_iota(jnp.int32, (16, frames), 0)
        loss = jnp.where(idx == 0, loss_ref[...].astype(f32), 0.0).astype(bf16)
        cols[...] = pad_rows([hotb, hotb, hotb, loss], 128).T
        sums[...] = sum_rows(hot, 16, frames)
        madd[...] = mods_operand(mods_ref)
        for c in range(heads_local):
            for s in range(seq_ways):
                attT[(c * seq_ways + s) * DH : (c * seq_ways + s + 1) * DH, :] = att_refs[c][s]
        proj = dot(attT[...].T, w_out_ref[...]) + b_out_ref[...].astype(f32)
        attn_proj[...] = proj
        mixed = hidden_ref[...] + mod(0) * proj
        after[...] = mixed
        normed, _ = norm_stats(mixed)
        value = (normed * (1.0 + mod(2)) + mod(1)).astype(bf16)
        nf[...] = value
        nfT[...] = value.T
        gff[...] = (grad_out() * mod(3)).astype(bf16)
        small_ref[4 * pad_u :, :] = jnp.zeros((8, width), f32)

    up = dot(nf[...], w_up_ref[...]) + b_up_ref[...].astype(f32)
    inner = 0.7978845608028654 * (up + 0.044715 * (up * up * up))
    tanh = jnp.tanh(inner)
    cdf = 0.5 * (1.0 + tanh)
    act = (up * cdf).astype(bf16)
    slope = cdf + 0.5 * up * (1.0 - tanh * tanh) * (
        0.7978845608028654 * (1.0 + (3 * 0.044715) * (up * up))
    )
    ff_part = dot(act, w_down_ref[...])
    gup = (dot_nt(gff[...], w_down_ref[...]) * slope).astype(bf16)
    gnf_part = dot_nt(gup, w_up_ref[...])

    @pl.when(step == 0)
    def _():
        ff_acc[...] = ff_part
        gnf_acc[...] = gnf_part

    @pl.when(step > 0)
    def _():
        ff_acc[...] += ff_part
        gnf_acc[...] += gnf_part

    halves = width // FF_TILE
    chunk = step // halves
    half = step % halves
    col = pl.ds(pl.multiple_of(half * FF_TILE, FF_TILE), FF_TILE)
    per_chunk = up_rows // up_part
    small_ref[pl.ds(4 * pad_u + 2 + chunk, 1), col] = dot(sums[16:32, :], gup)[:1]
    grad_w_up = dot(nfT[...], gup).astype(bf16)
    for s in range(seq_ways):
        side = jnp.where(core == s % 2, 0, 1)
        for h in range(per_chunk):
            lo = s * up_rows + h * up_part
            grads[side, chunk * per_chunk + h, s // 2, 0:up_part, col] = grad_w_up[lo : lo + up_part]
    grad_w_down = dot(act.T, gff[...]).astype(bf16)
    blocks = FF_TILE // down_block
    copies = []
    for b in range(blocks):
        s = step * blocks + b
        side = jnp.where(core == s % 2, 0, 1)
        for k in range(parts):
            lo = b * down_block + k * down_part
            grads[side, k, s // 2, up_part : up_part + down_part, :] = grad_w_down[lo : lo + down_part]

    def region_copy(side, where, index):
        return pltpu.make_async_copy(
            grads.at[side].at[where], refs_out[side].at[where], sems.at[side, index]
        )

    def up_copy(side, j):
        where = (
            pl.ds((j // halves) * per_chunk, per_chunk),
            slice(None),
            pl.ds(0, up_part),
            pl.ds(pl.multiple_of((j % halves) * FF_TILE, FF_TILE), FF_TILE),
        )
        return region_copy(side, where, j)

    def down_copy(side, z, index):
        return region_copy(side, (slice(None), pl.ds(z, 1), pl.ds(up_part, down_part)), index)

    def out_copy(side):
        where = (slice(None), slice(None), pl.ds(up_part + down_part, out_part))
        return region_copy(side, where, ff_total // FF_TILE + z_ways)

    base = ff_total // FF_TILE
    for side in range(2):
        up_copy(side, step).start()
    for b in range(blocks):
        s = step * blocks + b
        for side in range(2):

            @pl.when(lax.rem(s + core, 2) == side)
            def _():
                down_copy(side, s // 2, base + s // 2).start()

    @pl.when(step == steps - 1)
    def _():
        ff_out = ff_acc[...] + b_down_ref[...].astype(f32)
        mixed = after[...]
        go = grad_out()
        output_ref[...] = (mixed + mod(3) * ff_out).astype(bf16)
        rows = sums[...]
        small_ref[3 * pad_u : 4 * pad_u, :] = dot(rows, (go * ff_out).astype(bf16))[:pad_u]
        normed, rstd = norm_stats(mixed)
        gnf = gnf_acc[...]
        small_ref[pad_u : 2 * pad_u, :] = dot(rows, gnf.astype(bf16))[:pad_u]
        small_ref[2 * pad_u : 3 * pad_u, :] = dot(rows, (gnf * normed).astype(bf16))[:pad_u]
        g_after = go + norm_back(gnf * (1.0 + mod(2)), normed, rstd)
        after_grad_ref[...] = g_after
        small_ref[0:pad_u, :] = dot(rows, (g_after * attn_proj[...]).astype(bf16))[:pad_u]
        gattn = (g_after * mod(0)).astype(bf16)
        small_ref[4 * pad_u : 4 * pad_u + 1, :] = dot(rows, gattn)[16:17]
        small_ref[4 * pad_u + 1 : 4 * pad_u + 2, :] = dot(rows, gff[...])[16:17]
        gattT = dot_nt(w_out_ref[...], gattn).astype(bf16)
        for c in range(heads_local):
            for s in range(seq_ways):
                lo = (c * seq_ways + s) * DH
                gatt_ref[s, c * DH : (c + 1) * DH, :] = gattT[lo : lo + DH]
        grad_w_out = dot(attT[...], gattn).astype(bf16)
        for s in range(seq_ways):
            side = jnp.where(core == s % 2, 0, 1)
            for k in range(parts):
                lo = s * up_rows + k * out_part
                grads[side, k, s // 2, up_part + down_part : up_part + down_part + out_part, :] = grad_w_out[
                    lo : lo + out_part
                ]
        for side in range(2):
            out_copy(side).start()
        for side in range(2):
            for j in range(ff_total // FF_TILE):
                up_copy(side, j).wait()
            for z in range(z_ways):
                down_copy(side, z, base + z).wait()
            out_copy(side).wait()


def mid_block(
    lengths, ids, att, hidden, mods, cot, loss, w_out, b_out, w_up, b_up, w_down, b_down, parts
):
    frames, width = hidden.shape
    heads_local = len(att)
    seq_ways = att[0].shape[0]
    ff = w_up.shape[1]
    up_rows = width // seq_ways
    rows = (ff // width * up_rows + ff // seq_ways + up_rows) // parts
    utts = lengths.shape[0]
    f32, bf16 = jnp.float32, jnp.bfloat16
    steps = ff // FF_TILE

    def whole(shape):
        return pl.BlockSpec(shape, lambda j, *_: (0,) * len(shape), pipeline_mode=pl.Buffered(1))

    hbm = pl.BlockSpec(memory_space=pl.ANY)
    gshape = (parts, seq_ways // 2, rows, width)
    out_shape = [
        jax.ShapeDtypeStruct((frames, width), bf16),
        jax.ShapeDtypeStruct((frames, width), f32),
        jax.ShapeDtypeStruct((4 * table_rows(utts) + 8, width), f32),
    ]
    out_shape += [jax.ShapeDtypeStruct((seq_ways, heads_local * DH, frames), bf16)]
    out_specs = [whole(o.shape) for o in out_shape] + [hbm] * 2
    out_shape += [jax.ShapeDtypeStruct(gshape, bf16)] * 2
    ins = list(att) + [hidden, mods, cot, loss, w_out, b_out]
    return pl.pallas_call(
        functools.partial(mid_kernel, (seq_ways, heads_local, utts, ff)),
        out_shape=out_shape,
        grid_spec=pltpu.PrefetchScalarGridSpec(
            num_scalar_prefetch=2,
            grid=(steps,),
            in_specs=[whole(a.shape) for a in ins]
            + [
                pl.BlockSpec((width, FF_TILE), lambda j, *_: (0, j)),
                pl.BlockSpec((1, FF_TILE), lambda j, *_: (0, j)),
                pl.BlockSpec((FF_TILE, width), lambda j, *_: (j, 0)),
                whole((1, width)),
            ],
            out_specs=out_specs,
            scratch_shapes=[
                pltpu.VMEM((width, frames), bf16),
                pltpu.VMEM((frames, width), f32),
                pltpu.VMEM((frames, width), f32),
                pltpu.VMEM((frames, width), bf16),
                pltpu.VMEM((width, frames), bf16),
                pltpu.VMEM((frames, width), bf16),
                pltpu.VMEM((frames, width), f32),
                pltpu.VMEM((frames, width), f32),
                pltpu.VMEM((32, frames), bf16),
                pltpu.VMEM((frames, 128), bf16),
                pltpu.VMEM((128, 4 * width), bf16),
                pltpu.VMEM((2,) + gshape, bf16),
                pltpu.SemaphoreType.DMA((2, steps + seq_ways // 2 + 1)),
            ],
        ),
        compiler_params=pltpu.CompilerParams(vmem_limit_bytes=63 << 20),
        cost_estimate=cost(500),
        name="mid_block",
    )(lengths, ids, *ins, w_up, b_up, w_down, b_down)


def whole_block(shape):
    return pl.BlockSpec(shape, lambda *_: (0,) * len(shape), pipeline_mode=pl.Buffered(1))


def segment_rows(lengths_ref, drop_ref, utts, base, width):
    col = base + lax.broadcasted_iota(jnp.int32, (1, width), 1)
    start = jnp.int32(0)
    kept = jnp.zeros((1, width), jnp.float32)
    place = jnp.zeros((1, width), jnp.int32)
    for u in range(utts):
        end = start + lengths_ref[u]
        inside = (col >= start) & (col < end)
        kept = jnp.where(inside, (1 - drop_ref[u]).astype(jnp.float32), kept)
        place = jnp.where(inside, col - start, place)
        start = end
    return kept, place.astype(jnp.float32)


def rotary_rows(place, half):
    index = lax.broadcasted_iota(jnp.int32, (half, 1), 0).astype(jnp.float32)
    inverse = jnp.exp(index * (-9.210340371976184 / half))
    angles = inverse * place
    return jnp.cos(angles), jnp.sin(angles)


def frame_columns(hot, extra):
    hotb = hot.astype(jnp.bfloat16)
    idx = lax.broadcasted_iota(jnp.int32, hot.shape, 0)
    last = jnp.where(idx == 0, extra, 0.0).astype(jnp.bfloat16)
    return pad_rows([hotb, hotb, hotb, last], 128).T


def head_kernel(
    utts,
    lengths_ref,
    ids_ref,
    drop_ref,
    tokens_ref,
    skip_ref,
    cond_ref,
    mods_ref,
    w_skip_ref,
    b_skip_ref,
    hidden_ref,
    joinedT_ref,
    naT_ref,
    na_ref,
    cols,
):
    f32, bf16 = jnp.float32, jnp.bfloat16
    step = pl.program_id(0)
    frames, width = tokens_ref.shape
    rank = ids_ref[1]

    @pl.when(step == 0)
    def _():
        hot = onehot_rows(lengths_ref, utts, 16, rank * frames, frames)
        kept, _ = segment_rows(lengths_ref, drop_ref, utts, rank * frames, frames)
        cols[...] = frame_columns(hot, kept)
        keep = cols[:, 48:49].astype(f32)
        mixed = (tokens_ref[...].astype(f32) + keep * cond_ref[...].astype(f32)).astype(bf16)
        joinedT_ref[0:width, :] = mixed.T
        hidden_ref[...] = dot(mixed, w_skip_ref[...]) + b_skip_ref[...].astype(f32)

    @pl.when(step == 1)
    def _():
        skip = skip_ref[...]
        joinedT_ref[width : 2 * width, :] = skip.T
        hidden = hidden_ref[...] + dot(skip, w_skip_ref[...])
        hidden_ref[...] = hidden
        madd = mods_operand(mods_ref)
        shift = dot(cols[...], madd[:, :width])
        scale = dot(cols[...], madd[:, width:])
        normed, _ = norm_stats(hidden)
        value = (normed * (1.0 + scale) + shift).astype(bf16)
        na_ref[...] = value
        naT_ref[...] = value.T


def head_block(lengths, ids, drop, tokens, skip, cond, mods, w_skip, b_skip):
    frames, width = tokens.shape
    utts = lengths.shape[0]
    f32, bf16 = jnp.float32, jnp.bfloat16

    def whole(shape):
        return pl.BlockSpec(shape, lambda j, *_: (0,) * len(shape), pipeline_mode=pl.Buffered(1))

    out_shape = [
        jax.ShapeDtypeStruct((frames, width), f32),
        jax.ShapeDtypeStruct((2 * width, frames), bf16),
        jax.ShapeDtypeStruct((width, frames), bf16),
        jax.ShapeDtypeStruct((frames, width), bf16),
    ]
    return pl.pallas_call(
        functools.partial(head_kernel, utts),
        out_shape=out_shape,
        grid_spec=pltpu.PrefetchScalarGridSpec(
            num_scalar_prefetch=3,
            grid=(2,),
            in_specs=[whole(a.shape) for a in (tokens, skip, cond, mods)]
            + [pl.BlockSpec((width, width), lambda j, *_: (j, 0)), whole((1, width))],
            out_specs=[whole(o.shape) for o in out_shape],
            scratch_shapes=[pltpu.VMEM((frames, 128), bf16)],
        ),
        compiler_params=pltpu.CompilerParams(vmem_limit_bytes=48 << 20),
        cost_estimate=cost(100),
        name="head_block",
    )(lengths, ids, drop, tokens, skip, cond, mods, w_skip, b_skip)


def turn_heads(tensor, cosine, sine):
    half = DH // 2
    first, second = tensor[:, :half], tensor[:, half:]
    return jnp.concatenate([first * cosine - second * sine, second * cosine + first * sine], axis=1)


def qkv_kernel(utts, seq_ways, lengths_ref, ids_ref, drop_ref, na_ref, w_ref, b_ref, out_ref, trig):
    f32, bf16 = jnp.float32, jnp.bfloat16
    part = pl.program_id(0)
    frames = na_ref.shape[0]

    @pl.when(part == 0)
    def _():
        _, place = segment_rows(lengths_ref, drop_ref, utts, ids_ref[1] * frames, frames)
        cosine, sine = rotary_rows(place, DH // 2)
        trig[0] = cosine
        trig[1] = sine

    raw = dot(na_ref[...], w_ref[...]) + b_ref[...].astype(f32)
    rawT = raw.T.reshape(seq_ways, DH, frames)
    turned = part < 2
    cosine = jnp.where(turned, trig[0], 1.0)[None]
    sine = jnp.where(turned, trig[1], 0.0)[None]
    out_ref[:, pl.ds(pl.multiple_of(part * DH, DH), DH), :] = turn_heads(rawT, cosine, sine).astype(bf16)


def qkv_block(lengths, ids, drop, na, w_qkv, b_qkv, chunk, seq_ways):
    frames, width = na.shape
    cols = seq_ways * DH
    chunks = width // cols
    utts = lengths.shape[0]

    def whole(shape):
        return pl.BlockSpec(shape, lambda j, *_: (0,) * len(shape), pipeline_mode=pl.Buffered(1))

    shape = (seq_ways, 3 * DH, frames)
    return pl.pallas_call(
        functools.partial(qkv_kernel, utts, seq_ways),
        out_shape=jax.ShapeDtypeStruct(shape, jnp.bfloat16),
        grid_spec=pltpu.PrefetchScalarGridSpec(
            num_scalar_prefetch=3,
            grid=(3,),
            in_specs=[
                whole(na.shape),
                pl.BlockSpec((width, cols), lambda j, *_: (0, j * chunks + chunk)),
                pl.BlockSpec((1, cols), lambda j, *_: (0, j * chunks + chunk)),
            ],
            out_specs=whole(shape),
            scratch_shapes=[pltpu.VMEM((2, DH // 2, frames), jnp.float32)],
        ),
        cost_estimate=cost(75),
        name="qkv_block",
    )(lengths, ids, drop, na, w_qkv, b_qkv)


def back_kernel(utts, seq_ways, chunk, lengths_ref, ids_ref, drop_ref, grad_ref, naT_ref, w_ref, *refs):
    first = chunk == 0
    acc_in = None if first else refs[0]
    acc_ref, bias_ref, keep_ref, send_ref, trig, grads, sems = refs[0 if first else 3 :]
    f32, bf16 = jnp.float32, jnp.bfloat16
    part = pl.program_id(0)
    width, frames = naT_ref.shape
    core = ids_ref[0]
    parts = keep_ref.shape[0]
    own = width // seq_ways
    rows = own // parts

    @pl.when(part == 0)
    def _():
        _, place = segment_rows(lengths_ref, drop_ref, utts, ids_ref[1] * frames, frames)
        cosine, sine = rotary_rows(place, DH // 2)
        trig[0] = cosine
        trig[1] = sine

    turned = part < 2
    cosine = jnp.where(turned, trig[0], 1.0)[None]
    sine = jnp.where(turned, trig[1], 0.0)[None]
    raw = grad_ref[:, pl.ds(pl.multiple_of(part * DH, DH), DH), :].astype(f32)
    gpT = turn_heads(raw, cosine, -sine).astype(bf16).reshape(seq_ways * DH, frames)
    gna = dot(w_ref[...], gpT)

    @pl.when(part == 0)
    def _():
        acc_ref[...] = gna if first else acc_in[...] + gna

    @pl.when(part > 0)
    def _():
        acc_ref[...] += gna

    ones = jnp.ones((8, frames), bf16)
    bias_ref[0] = dot_nt(ones, gpT)
    grad_w = dot_nt(naT_ref[...], gpT).astype(bf16)
    cols = seq_ways * DH
    at = pl.ds(pl.multiple_of(part * rows, rows), rows)
    for s in range(seq_ways):
        side = jnp.where(core == s % 2, 0, 1)
        for k in range(parts):
            lo = s * own + k * rows
            grads[side, k, s // 2, at, :] = grad_w[lo : lo + rows]

    def copy(side, p):
        where = (slice(None), slice(None), pl.ds(pl.multiple_of(p * rows, rows), rows))
        return pltpu.make_async_copy(
            grads.at[side].at[where],
            (keep_ref, send_ref)[side].at[(*where, pl.ds(chunk * cols, cols))],
            sems.at[side, p],
        )

    for side in (1, 0):
        copy(side, part).start()

    @pl.when(part == 2)
    def _():
        for side in (1, 0):
            for p in range(3):
                copy(side, p).wait()


def back_block(lengths, ids, drop, grad, naT, w_qkv, before, chunk, parts):
    seq_ways, _, frames = grad.shape
    width = naT.shape[0]
    cols = seq_ways * DH
    chunks = width // cols
    utts = lengths.shape[0]
    f32, bf16 = jnp.float32, jnp.bfloat16
    rows = width // seq_ways // parts

    def whole(shape):
        return pl.BlockSpec(shape, lambda j, *_: (0,) * len(shape), pipeline_mode=pl.Buffered(1))

    gspec = pl.BlockSpec(memory_space=pl.ANY)
    gshape = jax.ShapeDtypeStruct((parts, seq_ways // 2, 3 * rows, width), bf16)
    ins = [grad, naT, w_qkv, *before]
    in_specs = [whole(grad.shape), whole(naT.shape)]
    in_specs += [pl.BlockSpec((width, cols), lambda j, *_: (0, j * chunks + chunk))]
    aliases = {}
    if before:
        in_specs += [whole(before[0].shape), gspec, gspec]
        aliases = {7: 2, 8: 3}
    return pl.pallas_call(
        functools.partial(back_kernel, utts, seq_ways, chunk),
        out_shape=[
            jax.ShapeDtypeStruct((width, frames), f32),
            jax.ShapeDtypeStruct((3, 8, cols), f32),
            gshape,
            gshape,
        ],
        grid_spec=pltpu.PrefetchScalarGridSpec(
            num_scalar_prefetch=3,
            grid=(3,),
            in_specs=in_specs,
            out_specs=[
                whole((width, frames)),
                pl.BlockSpec((1, 8, cols), lambda j, *_: (j, 0, 0)),
                gspec,
                gspec,
            ],
            scratch_shapes=[
                pltpu.VMEM((2, DH // 2, frames), f32),
                pltpu.VMEM((2, parts, seq_ways // 2, 3 * rows, cols), bf16),
                pltpu.SemaphoreType.DMA((2, 3)),
            ],
        ),
        compiler_params=pltpu.CompilerParams(vmem_limit_bytes=48 << 20),
        cost_estimate=cost(100),
        input_output_aliases=aliases,
        name="back_block",
    )(lengths, ids, drop, *ins)


def norm_kernel(
    utts, heads_local, lengths_ref, ids_ref, acc_ref, hidden_ref, after_ref, mods_ref, loss_ref, mid_ref, *refs
):
    f32, bf16 = jnp.float32, jnp.bfloat16
    bias_refs, (gh_ref, small_ref) = refs[:heads_local], refs[heads_local:]
    frames, width = hidden_ref.shape
    pad_u = table_rows(utts)
    base = 6 * pad_u
    hot = onehot_rows(lengths_ref, utts, 16, ids_ref[1] * frames, frames)
    cols = frame_columns(hot, jnp.zeros((1, frames), f32))
    madd = mods_operand(mods_ref)
    scale = dot(cols, madd[:, width:])
    gna = acc_ref[...].T
    normed, rstd = norm_stats(hidden_ref[...])
    sums = sum_rows(hot, 16, frames)
    small_ref[0:pad_u, :] = dot(sums, gna.astype(bf16))[:pad_u]
    small_ref[pad_u : 2 * pad_u, :] = dot(sums, (gna * normed).astype(bf16))[:pad_u]
    gh = (after_ref[...] + norm_back(gna * (1.0 + scale), normed, rstd)).astype(bf16)
    gh_ref[...] = gh
    small_ref[2 * pad_u : base, :] = mid_ref[0 : 4 * pad_u, :]
    cols_local = width // heads_local
    for c in range(heads_local):
        for p in range(3):
            small_ref[base + p : base + p + 1, c * cols_local : (c + 1) * cols_local] = bias_refs[c][p, 0:1, :]
    small_ref[base + 3 : base + 4, :] = dot(sums, gh)[16:17]
    small_ref[base + 4 : base + 12, :] = mid_ref[4 * pad_u : 4 * pad_u + 8, :]
    count = jnp.sum(loss_ref[...].astype(f32), axis=1, keepdims=True)
    small_ref[base + 12 : base + 16, :] = jnp.broadcast_to(count, (4, width))


def norm_block(lengths, ids, acc, hidden, after, mods, loss, mid_small, biases):
    frames, width = hidden.shape
    utts = lengths.shape[0]
    out_shape = [
        jax.ShapeDtypeStruct((frames, width), jnp.bfloat16),
        jax.ShapeDtypeStruct((6 * table_rows(utts) + 16, width), jnp.float32),
    ]
    return pl.pallas_call(
        functools.partial(norm_kernel, utts, len(biases)),
        out_shape=out_shape,
        grid_spec=pltpu.PrefetchScalarGridSpec(
            num_scalar_prefetch=2,
            grid=(1,),
            in_specs=[whole_block(a.shape) for a in (acc, hidden, after, mods, loss, mid_small, *biases)],
            out_specs=[whole_block(o.shape) for o in out_shape],
        ),
        compiler_params=pltpu.CompilerParams(vmem_limit_bytes=48 << 20),
        cost_estimate=cost(50),
        name="norm_block",
    )(lengths, ids, acc, hidden, after, mods, loss, mid_small, *biases)


def skip_kernel(seq_ways, ids_ref, joinedT_ref, gh_ref, keep_ref, send_ref, grads, sems):
    step = pl.program_id(0)
    core = ids_ref[0]
    parts = keep_ref.shape[0]
    width = joinedT_ref.shape[0]
    block = 2 * width // seq_ways
    rows = block // parts
    z_step = seq_ways // 4
    grad_w = dot(joinedT_ref[...], gh_ref[...]).astype(jnp.bfloat16)
    for b in range(width // block):
        side = jnp.where(core == b % 2, 0, 1)
        for k in range(parts):
            lo = b * block + k * rows
            grads[side, k, step * z_step + b // 2] = grad_w[lo : lo + rows]

    def copy(side, at):
        where = (slice(None), pl.ds(at * z_step, z_step))
        return pltpu.make_async_copy(
            grads.at[side].at[where], (keep_ref, send_ref)[side].at[where], sems.at[side, at]
        )

    for side in (1, 0):
        copy(side, step).start()

    @pl.when(step == 1)
    def _():
        for side in (1, 0):
            for at in range(2):
                copy(side, at).wait()


def skip_block(ids, joinedT, gh, seq_ways, parts):
    frames, width = gh.shape
    rows = 2 * width // seq_ways // parts
    gshape = (parts, seq_ways // 2, rows, width)
    return pl.pallas_call(
        functools.partial(skip_kernel, seq_ways),
        out_shape=[jax.ShapeDtypeStruct(gshape, jnp.bfloat16)] * 2,
        grid_spec=pltpu.PrefetchScalarGridSpec(
            num_scalar_prefetch=1,
            grid=(2,),
            in_specs=[pl.BlockSpec((width, frames), lambda j, *_: (j, 0)), whole_block(gh.shape)],
            out_specs=[pl.BlockSpec(memory_space=pl.ANY)] * 2,
            scratch_shapes=[pltpu.VMEM((2,) + gshape, jnp.bfloat16), pltpu.SemaphoreType.DMA((2, 2))],
        ),
        compiler_params=pltpu.CompilerParams(vmem_limit_bytes=32 << 20),
        cost_estimate=cost(50),
        name="skip_block",
    )(ids, joinedT, gh)


def joined_kernel(gh_ref, w_ref, scale_ref, first_ref, second_ref):
    step = pl.program_id(0)
    value = dot_nt(gh_ref[...], w_ref[...]) * scale_ref[0:1, 0:1]

    @pl.when(step == 0)
    def _():
        first_ref[...] = value

    @pl.when(step == 1)
    def _():
        second_ref[...] = value


def joined_block(gh, w_skip, scale):
    frames, width = gh.shape
    out = jax.ShapeDtypeStruct((frames, width), jnp.float32)
    return pl.pallas_call(
        joined_kernel,
        out_shape=[out, out],
        grid_spec=pltpu.PrefetchScalarGridSpec(
            num_scalar_prefetch=0,
            grid=(2,),
            in_specs=[
                whole_block(gh.shape),
                pl.BlockSpec((width, width), lambda j: (j, 0)),
                whole_block(scale.shape),
            ],
            out_specs=[whole_block(out.shape)] * 2,
        ),
        compiler_params=pltpu.CompilerParams(vmem_limit_bytes=32 << 20),
        cost_estimate=cost(50),
        name="joined_block",
    )(gh, w_skip, scale)


def add_bf16(left, right):
    return (left.astype(jnp.float32) + right.astype(jnp.float32)).astype(jnp.bfloat16)


def first_kernel(pairs, splits, ids_ref, *refs):
    ins, outs = refs[: 8 * pairs], list(refs[8 * pairs :])
    for i in range(4):
        own = [outs.pop(0) for _ in range(splits if i < 2 else 1)]
        at = 0
        for p in range(pairs):
            left, right = ins[2 * (i * pairs + p)], ins[2 * (i * pairs + p) + 1]
            rows = left.shape[-2]
            value = add_bf16(left[0, 0, 0], right[0, 0, 0])
            if len(own) == 1:
                own[0][0, :, at : at + rows, :] = value
            else:
                for out in own:
                    out[0] = value[:, at : at + out.shape[2], :]
                    at += out.shape[2]
            at += rows


def first_sum(ids, pairs, splits):
    _, _, _, z_ways, _, width = pairs[0][0].shape
    total = sum(k.shape[4] for k, _ in pairs)
    step = 1 if total > 100 else z_ways

    def source(half, axis, mine, rows):
        def at(g, z, ids):
            bit = ids[axis]
            return half, bit if mine else 1 - bit, g, z, 0, 0

        return pl.BlockSpec((1, 1, 1, step, rows, width), at)

    order = [(0, 2, False), (1, 3, False), (0, 2, True), (1, 3, True)]
    sizes = [*splits, *splits, total, total]
    return pl.pallas_call(
        functools.partial(first_kernel, len(pairs), len(splits)),
        out_shape=[jax.ShapeDtypeStruct((2, z_ways, n, width), jnp.bfloat16) for n in sizes],
        grid_spec=pltpu.PrefetchScalarGridSpec(
            num_scalar_prefetch=1,
            grid=(2, z_ways // step),
            in_specs=[source(*o, a.shape[4]) for o in order for pair in pairs for a in pair],
            out_specs=[pl.BlockSpec((1, step, n, width), lambda g, z, ids: (g, z, 0, 0)) for n in sizes],
        ),
        compiler_params=pltpu.CompilerParams(vmem_limit_bytes=48 << 20),
        cost_estimate=cost(60),
        name="first_sum",
    )(ids, *([a for pair in pairs for a in pair] * 4))


def second_kernel(pieces, ids_ref, *refs):
    for i in range(4):
        keep, *got = refs[(pieces + 1) * i : (pieces + 1) * (i + 1)]
        out = refs[4 * (pieces + 1) + i]
        at = 0
        for g in got:
            rows = g.shape[2]
            out[:, at : at + rows, :] = add_bf16(keep[0, :, at : at + rows, :], g[0])
            at += rows


def second_sum(ids, keep_a, got_a, keep_b, got_b):
    _, z_ways, rows, width = keep_a.shape
    step = z_ways // 2 if rows > 100 else z_ways

    def source(axis, mine, value):
        def at(z, ids):
            bit = ids[axis]
            return bit if mine else 1 - bit, z, 0, 0

        return pl.BlockSpec((1, step, *value.shape[2:]), at)

    order = [(3, False), (2, False), (3, True), (2, True)]
    sides = [[keep_a, *got_a], [keep_b, *got_b]]
    out = jax.ShapeDtypeStruct((z_ways, rows, width), jnp.bfloat16)
    return pl.pallas_call(
        functools.partial(second_kernel, len(got_a)),
        out_shape=[out] * 4,
        grid_spec=pltpu.PrefetchScalarGridSpec(
            num_scalar_prefetch=1,
            grid=(z_ways // step,),
            in_specs=[source(*o, v) for i, o in enumerate(order) for v in sides[i % 2]],
            out_specs=[pl.BlockSpec((step, rows, width), lambda z, ids: (z, 0, 0))] * 4,
        ),
        compiler_params=pltpu.CompilerParams(vmem_limit_bytes=48 << 20),
        cost_estimate=cost(30),
        name="second_sum",
    )(ids, *((sides[0] + sides[1]) * 2))


def third_kernel(ids_ref, keep_a, got_a, keep_b, got_b, *outs):
    for j, out in enumerate(outs):
        at = ids_ref[4] ^ j
        out[0] = add_bf16(keep_a[at], got_a[at])
        out[1] = add_bf16(keep_b[at], got_b[at])


def third_sum(ids, keep_a, got_a, keep_b, got_b):
    z_ways, rows, width = keep_a.shape
    out = jax.ShapeDtypeStruct((2, rows, width), jnp.bfloat16)
    return pl.pallas_call(
        third_kernel,
        out_shape=[out] * z_ways,
        grid_spec=pltpu.PrefetchScalarGridSpec(
            num_scalar_prefetch=1,
            grid=(1,),
            in_specs=[whole_block(keep_a.shape)] * 4,
            out_specs=[whole_block(out.shape)] * z_ways,
        ),
        cost_estimate=cost(10),
        name="third_sum",
    )(ids, keep_a, got_a, keep_b, got_b)


def third_all_kernel(ids_ref, keep_a, got_a, keep_b, got_b, out):
    for z in range(keep_a.shape[0]):
        out[z, 0] = add_bf16(keep_a[z], got_a[z])
        out[z, 1] = add_bf16(keep_b[z], got_b[z])


def third_sum_all(ids, keep_a, got_a, keep_b, got_b):
    z_ways, rows, width = keep_a.shape
    out = jax.ShapeDtypeStruct((z_ways, 2, rows, width), jnp.bfloat16)
    step = max(1, z_ways // 2)
    return pl.pallas_call(
        third_all_kernel,
        out_shape=out,
        grid_spec=pltpu.PrefetchScalarGridSpec(
            num_scalar_prefetch=1,
            grid=(z_ways // step,),
            in_specs=[pl.BlockSpec((step, rows, width), lambda i, *_: (i, 0, 0))] * 4,
            out_specs=pl.BlockSpec((step, 2, rows, width), lambda i, *_: (i, 0, 0, 0)),
        ),
        cost_estimate=cost(10),
        name="third_sum_all",
    )(ids, keep_a, got_a, keep_b, got_b)


def fourth_all_kernel(x, out):
    total = x[0].astype(jnp.float32)
    for z in range(1, x.shape[0]):
        total = total + x[z].astype(jnp.float32)
    out[...] = total.astype(jnp.bfloat16)


def fourth_sum_all(terms):
    return pl.pallas_call(
        fourth_all_kernel,
        out_shape=jax.ShapeDtypeStruct(terms.shape[1:], jnp.bfloat16),
        grid=(1,),
        in_specs=[whole_block(terms.shape)],
        out_specs=whole_block(terms.shape[1:]),
        cost_estimate=cost(10),
        name="fourth_sum_all",
    )(terms)


def fourth_kernel(*refs):
    total = refs[0][...].astype(jnp.float32)
    for r in refs[1:-1]:
        total = total + r[...].astype(jnp.float32)
    refs[-1][...] = total.astype(jnp.bfloat16)


def fourth_sum(terms):
    shape = terms[0].shape
    return pl.pallas_call(
        fourth_kernel,
        out_shape=jax.ShapeDtypeStruct(shape, jnp.bfloat16),
        grid=(1,),
        in_specs=[whole_block(shape)] * len(terms),
        out_specs=whole_block(shape),
        cost_estimate=cost(10),
        name="fourth_sum",
    )(*terms)


def place_kernel(streams, plan, ids_ref, scale_ref, *refs):
    blocks, outs = refs[: 4 * streams], refs[4 * streams :]
    x, y = ids_ref[2], ids_ref[3]
    scale = scale_ref[0:1, 0:1]
    for stream, row, rows, lane, lanes, out, row_of, lane_of in plan:
        for d in range(4):
            own_x, own_y = x ^ (d & 1), y ^ (d >> 1)
            for half in range(2):
                k = own_x * 2 + own_y if half == 0 else 4 + own_y * 2 + own_x
                tile = blocks[4 * stream + d][half, row : row + rows, lane : lane + lanes]
                outs[out][row_of(k), lane_of(k)] = tile.astype(jnp.float32) * scale


def place_blocks(ids, scale, streams, plan, shapes):
    blocks = [b for s in streams for b in s]
    outs = [jax.ShapeDtypeStruct(s, jnp.float32) for s in shapes]
    return pl.pallas_call(
        functools.partial(place_kernel, len(streams), plan),
        out_shape=outs,
        grid_spec=pltpu.PrefetchScalarGridSpec(
            num_scalar_prefetch=1,
            grid=(1,),
            in_specs=[whole_block(a.shape) for a in (scale, *blocks)],
            out_specs=[whole_block(o.shape) for o in outs],
        ),
        compiler_params=pltpu.CompilerParams(vmem_limit_bytes=32 << 20),
        cost_estimate=cost(20),
        name="place_blocks",
    )(ids, scale, *blocks)


def span(start, size):
    return pl.ds(pl.multiple_of(start, size), size)


def ada_kernel(groups, pad_u, numerator, time_ref, *refs):
    f32 = jnp.float32
    parts, (weight_ref, vector_ref, scale_ref) = refs[:groups], refs[groups:]
    table = pl.program_id(0)
    base = 6 * pad_u
    count = parts[0][base + 12 : base + 13, 0:1]
    for p in parts[1:]:
        count = count + p[base + 12 : base + 13, 0:1]
    scale = numerator / count
    rows = jnp.concatenate([p[pl.ds(pl.multiple_of(table * pad_u, 8), pad_u), :] for p in parts], axis=0) * scale
    vector_ref[pl.ds(table, 1), :] = jnp.sum(rows, axis=0, keepdims=True)
    operand = jnp.concatenate(list(split3(rows)), axis=0)
    weight_ref[...] = dot(time_ref[...], operand)

    @pl.when(table == 0)
    def _():
        total = parts[0][base : base + 16, :]
        for p in parts[1:]:
            total = total + p[base : base + 16, :]
        vector_ref[8:24, :] = total * scale
        scale_ref[...] = jnp.broadcast_to(scale, scale_ref.shape)


def ada_block(time3, parts, utts, numerator):
    pad_u = table_rows(utts)
    width = parts[0].shape[1]
    own = time3.shape[0]
    f32 = jnp.float32
    return pl.pallas_call(
        functools.partial(ada_kernel, len(parts), pad_u, numerator),
        out_shape=[
            jax.ShapeDtypeStruct((own, 6 * width), f32),
            jax.ShapeDtypeStruct((24, width), f32),
            jax.ShapeDtypeStruct((8, 128), f32),
        ],
        grid=(6,),
        in_specs=[whole_block(time3.shape)] + [whole_block(p.shape) for p in parts],
        out_specs=[
            pl.BlockSpec((own, width), lambda j: (0, j)),
            whole_block((24, width)),
            whole_block((8, 128)),
        ],
        cost_estimate=cost(50),
        name="ada_block",
    )(time3, *parts)


def sum_exchange(value, axis, bit):
    ways = lax.axis_size(axis)
    return lax.ppermute(value, axis, [(i, i ^ bit) for i in range(ways)])


def axis_bits(ways):
    return [1 << i for i in range(ways.bit_length() - 1)]


def reduce_stages(ids, blocks, splits, whole_z):
    batch_ways = lax.axis_size("batch")
    x_bit, y_bit = 1, 1 << ((batch_ways.bit_length() - 1) // 2)
    pairs = []
    for keep, send in blocks:
        shape = (2, 2, 2) + keep.shape[1:]
        pairs.append((keep.reshape(shape), sum_exchange(send, "seq", 1).reshape(shape)))
    *sends, keep_a, keep_b = first_sum(ids, pairs, splits)
    sends = follow(sends, (yield sends))
    got, token = [[], []], None
    for i in range(len(splits)):
        pieces = follow([sends[i], sends[len(splits) + i]], token)
        for side, bit in enumerate((x_bit, y_bit)):
            got[side].append(sum_exchange(pieces[side], "batch", bit))
        token = yield [got[0][i], got[1][i]]
    got_a, got_b = (follow(g, token) for g in got)
    send_a, send_b, keep_a, keep_b = second_sum(ids, keep_a, got_a, keep_b, got_b)
    send_a, send_b = follow([send_a, send_b], (yield [send_a, send_b]))
    got = [sum_exchange(send_a, "batch", y_bit), sum_exchange(send_b, "batch", x_bit)]
    got_a, got_b = follow(got, (yield got))
    if whole_z:
        ways = lax.axis_size("seq")
        groups = [list(range(c, ways, 2)) for c in range(2)]
        away = [third_sum_all(ids, keep_a, got_a, keep_b, got_b)]
        away = follow(away, (yield away))
        got = [lax.all_to_all(away[0], "seq", 0, 0, axis_index_groups=groups, tiled=True)]
        got = follow(got, (yield got))
        block = fourth_sum_all(got[0])
    else:
        own, *away = third_sum(ids, keep_a, got_a, keep_b, got_b)
        away = follow(away, (yield away))
        got = [sum_exchange(a, "seq", 2 * (j + 1)) for j, a in enumerate(away)]
        got = follow(got, (yield got))
        block = fourth_sum([own] + got)
    for bit in axis_bits(batch_ways):
        if bit not in (x_bit, y_bit):
            block = add_bf16(block, sum_exchange(block, "batch", bit))
    (block,) = follow([block], (yield [block]))
    yield [block] + [sum_exchange(block, "batch", bit) for bit in (x_bit, y_bit, x_bit | y_bit)]


def advance(stages, steps, token=None):
    value = next(stages) if token is None else stages.send(token)
    for _ in range(steps - 1):
        value = next(stages)
    return value


def last_stage(stages, token=None):
    value = stages.send(token)
    for value in stages:
        pass
    return value


def follow(values, token):
    return values if token is None else [after(v, token) for v in values]


def after(value, *others):
    return lax.optimization_barrier((value,) + others)[0]


def gather_groups(value):
    return [value] + [sum_exchange(value, "batch", i) for i in range(1, lax.axis_size("batch"))]


def sum_seq(value, token):
    value = value + sum_exchange(value, "seq", 1)
    away = after(value, *token)
    for j in range(1, lax.axis_size("seq") // 2):
        value = value + sum_exchange(away, "seq", 2 * j)
    return value


def shards(
    tokens_in,
    skip_in,
    condition,
    cotangent,
    time_embed,
    lengths,
    key_mask,
    drop_mask,
    loss_mask,
    w_skip,
    b_skip,
    w_ada,
    b_ada,
    w_qkv,
    b_qkv,
    w_out,
    b_out,
    w_up,
    b_up,
    w_down,
    b_down,
):
    f32, bf16 = jnp.float32, jnp.bfloat16
    seq_ways, batch_ways = lax.axis_size("seq"), lax.axis_size("batch")
    seq_rank = lax.axis_index("seq")
    frames, width = tokens_in.shape[1:]
    group_frames = frames * seq_ways
    heads_local = HEADS // seq_ways
    utts = lengths.shape[1]
    lengths_row, drop = lengths[0], drop_mask[0]
    batch_rank = lax.axis_index("batch")
    side = 1 << ((batch_ways.bit_length() - 1) // 2)
    ids = [lax.rem(seq_rank, 2), seq_rank, lax.rem(batch_rank, 2), lax.rem(batch_rank // side, 2), seq_rank // 2]
    ids = jnp.stack(ids).astype(jnp.int32)
    ok = key_mask.reshape(seq_ways, 1, frames)
    exchange = functools.partial(lax.all_to_all, axis_name="seq", split_axis=0, concat_axis=0, tiled=True)

    time_act = jax.nn.silu(time_embed[0]).astype(bf16)
    time_rows = jnp.pad(time_act, ((0, 16 - utts), (0, 0)))

    def modulation(first, last):
        return jnp.dot(time_rows, w_ada[:, first:last], preferred_element_type=f32) + b_ada[
            first:last
        ].astype(f32)

    mods_a = modulation(0, 2 * width)
    hidden, joinedT, naT, na = head_block(
        lengths_row, ids, drop, tokens_in[0], skip_in[0], condition[0], mods_a, w_skip, b_skip[None]
    )
    mods_rest = modulation(2 * width, 6 * width)
    received = []
    for c in range(heads_local):
        packed = qkv_block(lengths_row, ids, drop, na, w_qkv, b_qkv[None], c, seq_ways)
        if c == 0:
            na = after(na, mods_rest)
        received.append(exchange(packed))

    own = width // seq_ways
    pad_u = table_rows(utts)
    time_own = lax.dynamic_slice_in_dim(jnp.concatenate(gather_groups(time_rows[:pad_u])), seq_rank * own, own, axis=1)
    time3 = jnp.tile(time_own.T, (1, 3))

    received[0] = after(received[0], mods_rest)
    head_out, log_totals, returned = [], [], []
    for c in range(heads_local):
        out, log_total = attend(lengths_row, received[c], ok)
        head_out.append(out)
        log_totals.append(log_total)
        returned.append(exchange(after(out, *returned)))
        if c < heads_local - 1:
            received[c + 1] = after(received[c + 1], out, time3)
    mid = mid_block(
        lengths_row,
        ids,
        returned,
        hidden,
        mods_rest,
        cotangent[0],
        loss_mask,
        w_out,
        b_out[None],
        w_up,
        b_up[None],
        w_down,
        b_down[None],
        PARTS,
    )
    output, after_grad, mid_small, grad_att, keep, send = mid
    grad_heads = exchange(grad_att)
    front = keep.shape[2] * 4 // 9 // 16 * 16
    feed = reduce_stages(ids, [(keep, send)], [front, keep.shape[2] - front], True)

    ahead = next(feed)
    grad_local = []
    for c in range(heads_local):
        operand = after(grad_heads, *ahead)
        moving = feed.send(grad if c else None) if c < 2 else []
        grad = attend_back(lengths_row, received[c], ok, head_out[c], operand, log_totals[c], c)
        grad_local.append(exchange(after(grad, *moving)))
        ahead = [grad]
    if heads_local == 1:
        next(feed)
    ahead = ahead + advance(feed, 1, ahead[0])
    before, biases = (), []
    for c in range(heads_local):
        acc, bias, keep, send = back_block(
            lengths_row, ids, drop, after(grad_local[c], *ahead), naT, w_qkv, before, c, PARTS
        )
        before = (acc, keep, send)
        biases.append(bias)
        ahead = next(feed) and advance(feed, 1, acc) if c == 0 else []
    moving = next(feed)
    gh, small = norm_block(lengths_row, ids, acc, hidden, after_grad, mods_a, loss_mask, mid_small, biases)
    rest = reduce_stages(ids, [skip_block(ids, joinedT, gh, seq_ways, PARTS), (keep, send)], [5 * own // PARTS], False)
    small = sum_seq(small, [*moving, *advance(rest, 3)])
    next(rest)
    groups = gather_groups(after(small, *next(rest)))
    numerator = float(group_frames * batch_ways)
    grad_w_ada, vectors, scale = ada_block(time3, groups, utts, numerator)
    grad_tokens, grad_skip = joined_block(gh, w_skip, scale)
    next(feed)
    feed = last_stage(feed, groups[-1])
    rest = last_stage(rest, small)

    ff = w_up.shape[1]
    chunks = ff // width
    up_part = chunks * own // PARTS
    down_part = ff // seq_ways // PARTS
    out_part = own // PARTS
    per_chunk = own // up_part
    whole_lanes = lambda k: span(0, width)
    grad_w_up, grad_w_down, grad_w_out = place_blocks(
        ids,
        scale,
        [feed],
        [
            (
                *(0, 0, up_part, 0, width, 0),
                lambda k: span(lax.rem(k, per_chunk) * up_part, up_part),
                lambda k: span(k // per_chunk * width, width),
            ),
            (0, up_part, down_part, 0, width, 1, lambda k: span(k * down_part, down_part), whole_lanes),
            (0, up_part + down_part, out_part, 0, width, 2, lambda k: span(k * out_part, out_part), whole_lanes),
        ],
        [(own, ff), (ff // seq_ways, width), (own, width)],
    )
    skip_part = 2 * own // PARTS
    grad_w_skip, grad_w_qkv = place_blocks(
        ids,
        scale,
        [rest],
        [(0, 0, skip_part, 0, width, 0, lambda k: span(k * skip_part, skip_part), whole_lanes)]
        + [
            (
                *(0, skip_part + p * out_part, out_part, 0, width, 1),
                lambda k: span(k * out_part, out_part),
                lambda k, at=p * width: span(at, width),
            )
            for p in range(3)
        ],
        [(2 * own, width), (own, 3 * width)],
    )

    def own_slice(vector):
        vector = vector.reshape(-1)
        size = vector.shape[0] // seq_ways
        return lax.dynamic_slice_in_dim(vector, seq_rank * size, size)

    grad_b_ada = own_slice(vectors[:6])
    grad_b_qkv = own_slice(vectors[8:11])
    grad_b_skip = own_slice(vectors[11])
    grad_b_out = own_slice(vectors[12])
    grad_b_down = own_slice(vectors[13])
    grad_b_up = own_slice(vectors[14 : 14 + chunks])
    return (
        output[None],
        grad_tokens[None],
        grad_skip[None],
        grad_w_skip,
        grad_b_skip,
        grad_w_ada,
        grad_b_ada,
        grad_w_qkv,
        grad_b_qkv,
        grad_w_out,
        grad_b_out,
        grad_w_up,
        grad_b_up,
        grad_w_down,
        grad_b_down,
    )


def solution(mesh):
    in_specs = (
        P("batch", "seq", None),
        P("batch", "seq", None),
        P("batch", "seq", None),
        P("batch", "seq", None),
        P("batch", None, None),
        P("batch", None),
        P("batch", None),
        P("batch", None),
        P("batch", "seq"),
        P(),
        P(),
        P(),
        P(),
        P(),
        P(),
        P(),
        P(),
        P(),
        P(),
        P(),
        P(),
    )
    out_specs = (
        P("batch", "seq", None),
        P("batch", "seq", None),
        P("batch", "seq", None),
        P("seq", None),
        P("seq"),
        P("seq", None),
        P("seq"),
        P("seq", None),
        P("seq"),
        P("seq", None),
        P("seq"),
        P("seq", None),
        P("seq"),
        P("seq", None),
        P("seq"),
    )
    return jax.shard_map(shards, mesh=mesh, in_specs=in_specs, out_specs=out_specs, check_vma=False)
```

```python
import functools

import jax
import jax.numpy as jnp
from jax import lax
from jax.experimental import pallas as pl
from jax.experimental.pallas import tpu as pltpu
from jax.sharding import PartitionSpec as P

HEADS = 16
HEAD_DIM = 64
PARTS = 8
BIG = 1e30
DH = 64
BQ = 512
BK = 512


def cost(weight):
    return pl.CostEstimate(flops=weight * 100000000, bytes_accessed=weight * 100000, transcendentals=0)


def onehot_rows(lengths_ref, utts, rows, base, width):
    row = lax.broadcasted_iota(jnp.int32, (rows, width), 0)
    col = base + lax.broadcasted_iota(jnp.int32, (rows, width), 1)
    start = jnp.int32(0)
    hot = jnp.zeros((rows, width), jnp.float32)
    for u in range(utts):
        end = start + lengths_ref[u]
        hot = jnp.where((row == u) & (col >= start) & (col < end), 1.0, hot)
        start = end
    return hot


def key_range(lengths_ref, utts, first, last):
    start = jnp.int32(0)
    low, high = jnp.int32(0), jnp.int32(0)
    for u in range(utts):
        end = start + lengths_ref[u]
        low = jnp.where((start <= first) & (first < end), start, low)
        high = jnp.where((start <= last) & (last < end), end, high)
        start = end
    return low // BK, (high + BK - 1) // BK


def aug_rows(utts):
    return -(-utts // 16) * 16


def split3(row):
    a = row.astype(jnp.bfloat16)
    rest = row - a.astype(jnp.float32)
    b = rest.astype(jnp.bfloat16)
    c = (rest - b.astype(jnp.float32)).astype(jnp.bfloat16)
    return a, b, c


def pad_rows(parts, total):
    have = sum(p.shape[0] for p in parts)
    if have < total:
        parts = parts + [jnp.zeros((total - have, parts[0].shape[1]), parts[0].dtype)]
    return jnp.concatenate(parts, axis=0)


def rows16(rows, width):
    idx = lax.broadcasted_iota(jnp.int32, (16, width), 0)
    out = jnp.zeros((16, width), jnp.float32)
    for i, r in enumerate(rows):
        out = jnp.where(idx == i, r, out)
    return out.astype(jnp.bfloat16)


def fwd_kernel(utts, lengths_ref, qkv_ref, ok_ref, out_ref, lse_ref, kaug, vaug):
    sources, _, frames = qkv_ref.shape
    per = frames // BQ
    pad_u = aug_rows(utts)
    step = pl.program_id(0)

    @pl.when(step == 0)
    def _():
        def build(s, c):
            hot = onehot_rows(lengths_ref, utts, pad_u, s * frames, frames)
            ok = ok_ref[s].astype(jnp.float32)
            block = qkv_ref[s]
            one = jnp.ones((1, frames), jnp.float32)
            kT = pad_rows(
                [block[DH : 2 * DH], (1.0 - hot).astype(jnp.bfloat16), rows16([1.0 - ok], frames)], 128
            )
            kaug[pl.ds(pl.multiple_of(s * frames, frames), frames), :] = kT.T
            vT = jnp.concatenate([block[2 * DH :], rows16([one], frames)], axis=0)
            for t in range(frames // BK):
                vaug[s * (frames // BK) + t] = vT[:, t * BK : (t + 1) * BK]
            return c

        lax.fori_loop(0, sources, build, 0)

    block = qkv_ref[step]
    hot_q = onehot_rows(lengths_ref, utts, pad_u, step * frames, frames)
    qT = (block[:DH].astype(jnp.float32) * 0.125)
    one = jnp.ones((1, frames), jnp.float32)
    qaug = pad_rows(
        [qT.astype(jnp.bfloat16), (hot_q * -BIG).astype(jnp.bfloat16), rows16([one * -BIG], frames)], 128
    )
    kT = block[DH : 2 * DH].astype(jnp.float32)
    vT = block[2 * DH :].astype(jnp.float32)
    ok = ok_ref[step] > 0
    s_self = jnp.sum(qT * kT, axis=0, keepdims=True)
    m0 = jnp.where(ok, -3e38, s_self)
    acc0 = jnp.concatenate([jnp.where(ok, 0.0, vT), jnp.where(ok, 0.0, jnp.ones((16, frames), jnp.float32))], axis=0)
    for t in range(per):
        cols = slice(t * BQ, (t + 1) * BQ)
        low, high = key_range(lengths_ref, utts, step * frames + t * BQ, step * frames + (t + 1) * BQ - 1)
        q_b = qaug[:, cols]

        def body(j, carry):
            m, acc = carry
            s = jnp.dot(kaug[pl.ds(pl.multiple_of(j * BK, BK), BK), :], q_b, preferred_element_type=jnp.float32)
            m_new = jnp.maximum(m, jnp.max(s, axis=0, keepdims=True))
            p = jnp.exp(s - m_new).astype(jnp.bfloat16)
            alpha = jnp.exp(m - m_new)
            acc = acc * alpha + jnp.dot(vaug[j], p, preferred_element_type=jnp.float32)
            return m_new, acc

        m, acc = lax.fori_loop(low, high, body, (m0[:, cols], acc0[:, cols]))
        total = acc[DH : DH + 1]
        out_ref[0, :, cols] = (acc[:DH] / total).astype(jnp.bfloat16)
        lse_ref[0, :, cols] = m + jnp.log(total)


def attend(lengths, qkv, ok):
    sources, _, frames = qkv.shape
    total = sources * frames
    utts = lengths.shape[0]
    whole = lambda shape: pl.BlockSpec(shape, lambda i, *_: (0,) * len(shape))
    return pl.pallas_call(
        functools.partial(fwd_kernel, utts),
        out_shape=(
            jax.ShapeDtypeStruct((sources, DH, frames), jnp.bfloat16),
            jax.ShapeDtypeStruct((sources, 1, frames), jnp.float32),
        ),
        grid_spec=pltpu.PrefetchScalarGridSpec(
            num_scalar_prefetch=1,
            grid=(sources,),
            in_specs=[whole(qkv.shape), whole(ok.shape)],
            out_specs=(
                pl.BlockSpec((1, DH, frames), lambda i, *_: (i, 0, 0)),
                pl.BlockSpec((1, 1, frames), lambda i, *_: (i, 0, 0)),
            ),
            scratch_shapes=[
                pltpu.VMEM((total, 128), jnp.bfloat16),
                pltpu.VMEM((total // BK, DH + 16, BK), jnp.bfloat16),
            ],
        ),
        cost_estimate=cost(250),
        name="attend",
    )(lengths, qkv, ok)


def bwd_kernel(utts, chunk, lengths_ref, qkv_ref, ok_ref, o_ref, do_ref, lse_ref, out_ref, kaug, vnat, kT_s, dk, dv):
    sources, _, frames = qkv_ref.shape
    per = frames // BK
    pad_u = aug_rows(utts)
    step = pl.program_id(0)
    f32 = jnp.float32

    @pl.when(step == 0)
    def _():
        def build(s, c):
            hot = onehot_rows(lengths_ref, utts, pad_u, s * frames, frames)
            ok = ok_ref[s]
            block = qkv_ref[s]
            one = jnp.ones((1, frames), f32)
            kT = block[DH : 2 * DH]
            vT = block[2 * DH :]
            kA = pad_rows(
                [kT, (1.0 - hot).astype(jnp.bfloat16), rows16([1.0 - ok.astype(f32), one, one, one], frames)], 128
            )
            rows = pl.ds(pl.multiple_of(s * frames, frames), frames)
            kaug[rows, :] = kA.T
            vnat[rows, :] = pad_rows([vT, rows16([one, one, one], frames)], 128).T
            qT = block[:DH].astype(f32) * 0.125
            do = do_ref[s, chunk * DH : (chunk + 1) * DH, :].astype(f32)
            s_self = jnp.sum(qT * kT.astype(f32), axis=0, keepdims=True)
            delta = jnp.sum(do * o_ref[s].astype(f32), axis=0, keepdims=True)
            p_self = jnp.where(ok > 0, 0.0, jnp.exp(s_self - lse_ref[s]))
            ds_self = p_self * (jnp.sum(do * vT.astype(f32), axis=0, keepdims=True) - delta)
            dk0 = ds_self * qT
            dv0 = p_self * do
            for t in range(per):
                cols = slice(t * BK, (t + 1) * BK)
                kT_s[s * per + t] = kT[:, cols]
                dk[s * per + t] = dk0[:, cols]
                dv[s * per + t] = dv0[:, cols]
            return c

        lax.fori_loop(0, sources, build, 0)

    block = qkv_ref[step]
    one = jnp.ones((1, frames), f32)
    hot_q = onehot_rows(lengths_ref, utts, pad_u, step * frames, frames)
    qT = block[:DH].astype(f32) * 0.125
    qTb = qT.astype(jnp.bfloat16)
    kT = block[DH : 2 * DH].astype(f32)
    vT = block[2 * DH :].astype(f32)
    ok = ok_ref[step]
    dob = do_ref[step, chunk * DH : (chunk + 1) * DH, :]
    do = dob.astype(f32)
    lse = lse_ref[step]
    delta = jnp.sum(do * o_ref[step].astype(f32), axis=0, keepdims=True)
    l3 = [-r.astype(f32) for r in split3(lse)]
    d3 = [-r.astype(f32) for r in split3(delta)]
    qaug = pad_rows([qTb, (hot_q * -BIG).astype(jnp.bfloat16), rows16([one * -BIG] + l3, frames)], 128)
    doaug = pad_rows([dob, rows16(d3, frames)], 128)
    s_self = jnp.sum(qT * kT, axis=0, keepdims=True)
    p_self = jnp.where(ok > 0, 0.0, jnp.exp(s_self - lse))
    ds_self = p_self * (jnp.sum(do * vT, axis=0, keepdims=True) - delta)
    dq0 = ds_self * kT
    nt = (((1,), (1,)), ((), ()))
    for t in range(frames // BQ):
        cols = slice(t * BQ, (t + 1) * BQ)
        low, high = key_range(lengths_ref, utts, step * frames + t * BQ, step * frames + (t + 1) * BQ - 1)
        q_a = qaug[:, cols]
        q_b = qTb[:, cols]
        do_a = doaug[:, cols]
        do_b = dob[:, cols]

        def body(j, dq):
            rows = pl.ds(pl.multiple_of(j * BK, BK), BK)
            s = jnp.dot(kaug[rows, :], q_a, preferred_element_type=f32)
            dp = jnp.dot(vnat[rows, :], do_a, preferred_element_type=f32)
            p = jnp.exp(s)
            ds = (p * dp).astype(jnp.bfloat16)
            dv[j] += lax.dot_general(do_b, p.astype(jnp.bfloat16), nt, preferred_element_type=f32)
            dk[j] += lax.dot_general(q_b, ds, nt, preferred_element_type=f32)
            return dq + jnp.dot(kT_s[j], ds, preferred_element_type=f32)

        dq = lax.fori_loop(low, high, body, dq0[:, cols])
        out_ref[step, :DH, cols] = (dq * 0.125).astype(jnp.bfloat16)

    @pl.when(step == sources - 1)
    def _():
        def finish(s, c):
            for t in range(per):
                cols = slice(t * BK, (t + 1) * BK)
                out_ref[s, DH : 2 * DH, cols] = dk[s * per + t].astype(jnp.bfloat16)
                out_ref[s, 2 * DH :, cols] = dv[s * per + t].astype(jnp.bfloat16)
            return c

        lax.fori_loop(0, sources, finish, 0)


def attend_back(lengths, qkv, ok, out, grad, lse, chunk):
    sources, _, frames = qkv.shape
    total = sources * frames
    utts = lengths.shape[0]
    whole = lambda shape: pl.BlockSpec(shape, lambda i, *_: (0,) * len(shape))
    return pl.pallas_call(
        functools.partial(bwd_kernel, utts, chunk),
        out_shape=jax.ShapeDtypeStruct(qkv.shape, jnp.bfloat16),
        grid_spec=pltpu.PrefetchScalarGridSpec(
            num_scalar_prefetch=1,
            grid=(sources,),
            in_specs=[whole(a.shape) for a in (qkv, ok, out, grad, lse)],
            out_specs=whole(qkv.shape),
            scratch_shapes=[
                pltpu.VMEM((total, 128), jnp.bfloat16),
                pltpu.VMEM((total, 128), jnp.bfloat16),
                pltpu.VMEM((total // BK, DH, BK), jnp.bfloat16),
                pltpu.VMEM((total // BK, DH, BK), jnp.float32),
                pltpu.VMEM((total // BK, DH, BK), jnp.float32),
            ],
        ),
        cost_estimate=cost(320),
        name="attend_back",
    )(lengths, qkv, ok, out, grad, lse)


FF_TILE = 512
EPS = 1e-06


def dot(left, right):
    return jnp.dot(left, right, preferred_element_type=jnp.float32)


def dot_nt(left, right):
    return lax.dot_general(left, right, (((1,), (1,)), ((), ())), preferred_element_type=jnp.float32)


def norm_stats(x):
    mean = jnp.mean(x, axis=1, keepdims=True)
    centred = x - mean
    rstd = lax.rsqrt(jnp.mean(centred * centred, axis=1, keepdims=True) + EPS)
    return centred * rstd, rstd


def norm_back(grad, normed, rstd):
    first = jnp.mean(grad, axis=1, keepdims=True)
    second = jnp.mean(grad * normed, axis=1, keepdims=True)
    return rstd * (grad - first - normed * second)


def mods_operand(mods_ref):
    rows = mods_ref[...]
    return pad_rows(list(split3(rows)), 128)


def table_rows(utts):
    return -(-utts // 8) * 8


def sum_rows(hot, utts_pad, frames):
    idx = lax.broadcasted_iota(jnp.int32, (16, frames), 0)
    ones = jnp.where(idx == 0, 1.0, 0.0).astype(jnp.bfloat16)
    return jnp.concatenate([hot.astype(jnp.bfloat16), ones], axis=0)


def mid_kernel(
    dims,
    lengths_ref,
    ids_ref,
    *refs,
):
    seq_ways, heads_local, utts, ff = dims
    att_refs = refs[:heads_local]
    (
        hidden_ref,
        mods_ref,
        cot_ref,
        loss_ref,
        w_out_ref,
        b_out_ref,
        w_up_ref,
        b_up_ref,
        w_down_ref,
        b_down_ref,
    ) = refs[heads_local : heads_local + 10]
    outs = refs[heads_local + 10 :]
    output_ref, after_grad_ref, small_ref, gatt_ref = outs[:4]
    refs_out = outs[4:6]
    (
        attT,
        attn_proj,
        after,
        nf,
        nfT,
        gff,
        ff_acc,
        gnf_acc,
        sums,
        cols,
        madd,
        grads,
        sems,
    ) = outs[6:]
    f32, bf16 = jnp.float32, jnp.bfloat16
    step = pl.program_id(0)
    steps = pl.num_programs(0)
    core = ids_ref[0]
    rank = ids_ref[1]
    frames, width = hidden_ref.shape
    up_rows = width // seq_ways
    down_rows = FF_TILE
    z_ways = seq_ways // 2
    parts = grads.shape[1]
    pad_u = table_rows(utts)
    ff_total = ff
    up_part = ff_total // width * up_rows // parts
    down_block = ff_total // seq_ways
    down_part = down_block // parts
    out_part = up_rows // parts

    def mod(index):
        return dot(cols[...], madd[:, index * width : (index + 1) * width])

    def grad_out():
        loss = cols[:, 48:49].astype(f32)
        return cot_ref[...].astype(f32) * loss

    @pl.when(step == 0)
    def _():
        hot = onehot_rows(lengths_ref, utts, 16, rank * frames, frames)
        hotb = hot.astype(bf16)
        idx = lax.broadcasted_iota(jnp.int32, (16, frames), 0)
        loss = jnp.where(idx == 0, loss_ref[...].astype(f32), 0.0).astype(bf16)
        cols[...] = pad_rows([hotb, hotb, hotb, loss], 128).T
        sums[...] = sum_rows(hot, 16, frames)
        madd[...] = mods_operand(mods_ref)
        for c in range(heads_local):
            for s in range(seq_ways):
                attT[(c * seq_ways + s) * DH : (c * seq_ways + s + 1) * DH, :] = att_refs[c][s]
        proj = dot(attT[...].T, w_out_ref[...]) + b_out_ref[...].astype(f32)
        attn_proj[...] = proj
        mixed = hidden_ref[...] + mod(0) * proj
        after[...] = mixed
        normed, _ = norm_stats(mixed)
        value = (normed * (1.0 + mod(2)) + mod(1)).astype(bf16)
        nf[...] = value
        nfT[...] = value.T
        gff[...] = (grad_out() * mod(3)).astype(bf16)
        small_ref[4 * pad_u :, :] = jnp.zeros((8, width), f32)

    up = dot(nf[...], w_up_ref[...]) + b_up_ref[...].astype(f32)
    inner = 0.7978845608028654 * (up + 0.044715 * (up * up * up))
    tanh = jnp.tanh(inner)
    cdf = 0.5 * (1.0 + tanh)
    act = (up * cdf).astype(bf16)
    slope = cdf + 0.5 * up * (1.0 - tanh * tanh) * (
        0.7978845608028654 * (1.0 + (3 * 0.044715) * (up * up))
    )
    ff_part = dot(act, w_down_ref[...])
    gup = (dot_nt(gff[...], w_down_ref[...]) * slope).astype(bf16)
    gnf_part = dot_nt(gup, w_up_ref[...])

    @pl.when(step == 0)
    def _():
        ff_acc[...] = ff_part
        gnf_acc[...] = gnf_part

    @pl.when(step > 0)
    def _():
        ff_acc[...] += ff_part
        gnf_acc[...] += gnf_part

    halves = width // FF_TILE
    chunk = step // halves
    half = step % halves
    col = pl.ds(pl.multiple_of(half * FF_TILE, FF_TILE), FF_TILE)
    per_chunk = up_rows // up_part
    small_ref[pl.ds(4 * pad_u + 2 + chunk, 1), col] = dot(sums[16:32, :], gup)[:1]
    grad_w_up = dot(nfT[...], gup).astype(bf16)
    for s in range(seq_ways):
        side = jnp.where(core == s % 2, 0, 1)
        for h in range(per_chunk):
            lo = s * up_rows + h * up_part
            grads[side, chunk * per_chunk + h, s // 2, 0:up_part, col] = grad_w_up[lo : lo + up_part]
    grad_w_down = dot(act.T, gff[...]).astype(bf16)
    blocks = FF_TILE // down_block
    copies = []
    for b in range(blocks):
        s = step * blocks + b
        side = jnp.where(core == s % 2, 0, 1)
        for k in range(parts):
            lo = b * down_block + k * down_part
            grads[side, k, s // 2, up_part : up_part + down_part, :] = grad_w_down[lo : lo + down_part]

    def region_copy(side, where, index):
        return pltpu.make_async_copy(
            grads.at[side].at[where], refs_out[side].at[where], sems.at[side, index]
        )

    def up_copy(side, j):
        where = (
            pl.ds((j // halves) * per_chunk, per_chunk),
            slice(None),
            pl.ds(0, up_part),
            pl.ds(pl.multiple_of((j % halves) * FF_TILE, FF_TILE), FF_TILE),
        )
        return region_copy(side, where, j)

    def down_copy(side, z, index):
        return region_copy(side, (slice(None), pl.ds(z, 1), pl.ds(up_part, down_part)), index)

    def out_copy(side):
        where = (slice(None), slice(None), pl.ds(up_part + down_part, out_part))
        return region_copy(side, where, ff_total // FF_TILE + z_ways)

    base = ff_total // FF_TILE
    for side in range(2):
        up_copy(side, step).start()
    for b in range(blocks):
        s = step * blocks + b
        for side in range(2):

            @pl.when(lax.rem(s + core, 2) == side)
            def _():
                down_copy(side, s // 2, base + s // 2).start()

    @pl.when(step == steps - 1)
    def _():
        ff_out = ff_acc[...] + b_down_ref[...].astype(f32)
        mixed = after[...]
        go = grad_out()
        output_ref[...] = (mixed + mod(3) * ff_out).astype(bf16)
        rows = sums[...]
        small_ref[3 * pad_u : 4 * pad_u, :] = dot(rows, (go * ff_out).astype(bf16))[:pad_u]
        normed, rstd = norm_stats(mixed)
        gnf = gnf_acc[...]
        small_ref[pad_u : 2 * pad_u, :] = dot(rows, gnf.astype(bf16))[:pad_u]
        small_ref[2 * pad_u : 3 * pad_u, :] = dot(rows, (gnf * normed).astype(bf16))[:pad_u]
        g_after = go + norm_back(gnf * (1.0 + mod(2)), normed, rstd)
        after_grad_ref[...] = g_after
        small_ref[0:pad_u, :] = dot(rows, (g_after * attn_proj[...]).astype(bf16))[:pad_u]
        gattn = (g_after * mod(0)).astype(bf16)
        small_ref[4 * pad_u : 4 * pad_u + 1, :] = dot(rows, gattn)[16:17]
        small_ref[4 * pad_u + 1 : 4 * pad_u + 2, :] = dot(rows, gff[...])[16:17]
        gattT = dot_nt(w_out_ref[...], gattn).astype(bf16)
        for c in range(heads_local):
            for s in range(seq_ways):
                lo = (c * seq_ways + s) * DH
                gatt_ref[s, c * DH : (c + 1) * DH, :] = gattT[lo : lo + DH]
        grad_w_out = dot(attT[...], gattn).astype(bf16)
        for s in range(seq_ways):
            side = jnp.where(core == s % 2, 0, 1)
            for k in range(parts):
                lo = s * up_rows + k * out_part
                grads[side, k, s // 2, up_part + down_part : up_part + down_part + out_part, :] = grad_w_out[
                    lo : lo + out_part
                ]
        for side in range(2):
            out_copy(side).start()
        for side in range(2):
            for j in range(ff_total // FF_TILE):
                up_copy(side, j).wait()
            for z in range(z_ways):
                down_copy(side, z, base + z).wait()
            out_copy(side).wait()


def mid_block(
    lengths, ids, att, hidden, mods, cot, loss, w_out, b_out, w_up, b_up, w_down, b_down, parts
):
    frames, width = hidden.shape
    heads_local = len(att)
    seq_ways = att[0].shape[0]
    ff = w_up.shape[1]
    up_rows = width // seq_ways
    rows = (ff // width * up_rows + ff // seq_ways + up_rows) // parts
    utts = lengths.shape[0]
    f32, bf16 = jnp.float32, jnp.bfloat16
    steps = ff // FF_TILE

    def whole(shape):
        return pl.BlockSpec(shape, lambda j, *_: (0,) * len(shape), pipeline_mode=pl.Buffered(1))

    hbm = pl.BlockSpec(memory_space=pl.ANY)
    gshape = (parts, seq_ways // 2, rows, width)
    out_shape = [
        jax.ShapeDtypeStruct((frames, width), bf16),
        jax.ShapeDtypeStruct((frames, width), f32),
        jax.ShapeDtypeStruct((4 * table_rows(utts) + 8, width), f32),
    ]
    out_shape += [jax.ShapeDtypeStruct((seq_ways, heads_local * DH, frames), bf16)]
    out_specs = [whole(o.shape) for o in out_shape] + [hbm] * 2
    out_shape += [jax.ShapeDtypeStruct(gshape, bf16)] * 2
    ins = list(att) + [hidden, mods, cot, loss, w_out, b_out]
    return pl.pallas_call(
        functools.partial(mid_kernel, (seq_ways, heads_local, utts, ff)),
        out_shape=out_shape,
        grid_spec=pltpu.PrefetchScalarGridSpec(
            num_scalar_prefetch=2,
            grid=(steps,),
            in_specs=[whole(a.shape) for a in ins]
            + [
                pl.BlockSpec((width, FF_TILE), lambda j, *_: (0, j)),
                pl.BlockSpec((1, FF_TILE), lambda j, *_: (0, j)),
                pl.BlockSpec((FF_TILE, width), lambda j, *_: (j, 0)),
                whole((1, width)),
            ],
            out_specs=out_specs,
            scratch_shapes=[
                pltpu.VMEM((width, frames), bf16),
                pltpu.VMEM((frames, width), f32),
                pltpu.VMEM((frames, width), f32),
                pltpu.VMEM((frames, width), bf16),
                pltpu.VMEM((width, frames), bf16),
                pltpu.VMEM((frames, width), bf16),
                pltpu.VMEM((frames, width), f32),
                pltpu.VMEM((frames, width), f32),
                pltpu.VMEM((32, frames), bf16),
                pltpu.VMEM((frames, 128), bf16),
                pltpu.VMEM((128, 4 * width), bf16),
                pltpu.VMEM((2,) + gshape, bf16),
                pltpu.SemaphoreType.DMA((2, steps + seq_ways // 2 + 1)),
            ],
        ),
        compiler_params=pltpu.CompilerParams(vmem_limit_bytes=63 << 20),
        cost_estimate=cost(500),
        name="mid_block",
    )(lengths, ids, *ins, w_up, b_up, w_down, b_down)


def whole_block(shape):
    return pl.BlockSpec(shape, lambda *_: (0,) * len(shape), pipeline_mode=pl.Buffered(1))


def segment_rows(lengths_ref, drop_ref, utts, base, width):
    col = base + lax.broadcasted_iota(jnp.int32, (1, width), 1)
    start = jnp.int32(0)
    kept = jnp.zeros((1, width), jnp.float32)
    place = jnp.zeros((1, width), jnp.int32)
    for u in range(utts):
        end = start + lengths_ref[u]
        inside = (col >= start) & (col < end)
        kept = jnp.where(inside, (1 - drop_ref[u]).astype(jnp.float32), kept)
        place = jnp.where(inside, col - start, place)
        start = end
    return kept, place.astype(jnp.float32)


def rotary_rows(place, half):
    index = lax.broadcasted_iota(jnp.int32, (half, 1), 0).astype(jnp.float32)
    inverse = jnp.exp(index * (-9.210340371976184 / half))
    angles = inverse * place
    return jnp.cos(angles), jnp.sin(angles)


def frame_columns(hot, extra):
    hotb = hot.astype(jnp.bfloat16)
    idx = lax.broadcasted_iota(jnp.int32, hot.shape, 0)
    last = jnp.where(idx == 0, extra, 0.0).astype(jnp.bfloat16)
    return pad_rows([hotb, hotb, hotb, last], 128).T


def head_kernel(
    utts,
    lengths_ref,
    ids_ref,
    drop_ref,
    tokens_ref,
    skip_ref,
    cond_ref,
    mods_ref,
    w_skip_ref,
    b_skip_ref,
    hidden_ref,
    joinedT_ref,
    naT_ref,
    na_ref,
    cols,
):
    f32, bf16 = jnp.float32, jnp.bfloat16
    step = pl.program_id(0)
    frames, width = tokens_ref.shape
    rank = ids_ref[1]

    @pl.when(step == 0)
    def _():
        hot = onehot_rows(lengths_ref, utts, 16, rank * frames, frames)
        kept, _ = segment_rows(lengths_ref, drop_ref, utts, rank * frames, frames)
        cols[...] = frame_columns(hot, kept)
        keep = cols[:, 48:49].astype(f32)
        mixed = (tokens_ref[...].astype(f32) + keep * cond_ref[...].astype(f32)).astype(bf16)
        joinedT_ref[0:width, :] = mixed.T
        hidden_ref[...] = dot(mixed, w_skip_ref[...]) + b_skip_ref[...].astype(f32)

    @pl.when(step == 1)
    def _():
        skip = skip_ref[...]
        joinedT_ref[width : 2 * width, :] = skip.T
        hidden = hidden_ref[...] + dot(skip, w_skip_ref[...])
        hidden_ref[...] = hidden
        madd = mods_operand(mods_ref)
        shift = dot(cols[...], madd[:, :width])
        scale = dot(cols[...], madd[:, width:])
        normed, _ = norm_stats(hidden)
        value = (normed * (1.0 + scale) + shift).astype(bf16)
        na_ref[...] = value
        naT_ref[...] = value.T


def head_block(lengths, ids, drop, tokens, skip, cond, mods, w_skip, b_skip):
    frames, width = tokens.shape
    utts = lengths.shape[0]
    f32, bf16 = jnp.float32, jnp.bfloat16

    def whole(shape):
        return pl.BlockSpec(shape, lambda j, *_: (0,) * len(shape), pipeline_mode=pl.Buffered(1))

    out_shape = [
        jax.ShapeDtypeStruct((frames, width), f32),
        jax.ShapeDtypeStruct((2 * width, frames), bf16),
        jax.ShapeDtypeStruct((width, frames), bf16),
        jax.ShapeDtypeStruct((frames, width), bf16),
    ]
    return pl.pallas_call(
        functools.partial(head_kernel, utts),
        out_shape=out_shape,
        grid_spec=pltpu.PrefetchScalarGridSpec(
            num_scalar_prefetch=3,
            grid=(2,),
            in_specs=[whole(a.shape) for a in (tokens, skip, cond, mods)]
            + [pl.BlockSpec((width, width), lambda j, *_: (j, 0)), whole((1, width))],
            out_specs=[whole(o.shape) for o in out_shape],
            scratch_shapes=[pltpu.VMEM((frames, 128), bf16)],
        ),
        compiler_params=pltpu.CompilerParams(vmem_limit_bytes=48 << 20),
        cost_estimate=cost(100),
        name="head_block",
    )(lengths, ids, drop, tokens, skip, cond, mods, w_skip, b_skip)


def turn_heads(tensor, cosine, sine):
    half = DH // 2
    first, second = tensor[:, :half], tensor[:, half:]
    return jnp.concatenate([first * cosine - second * sine, second * cosine + first * sine], axis=1)


def qkv_kernel(utts, seq_ways, lengths_ref, ids_ref, drop_ref, na_ref, w_ref, b_ref, out_ref, trig):
    f32, bf16 = jnp.float32, jnp.bfloat16
    part = pl.program_id(0)
    frames = na_ref.shape[0]

    @pl.when(part == 0)
    def _():
        _, place = segment_rows(lengths_ref, drop_ref, utts, ids_ref[1] * frames, frames)
        cosine, sine = rotary_rows(place, DH // 2)
        trig[0] = cosine
        trig[1] = sine

    raw = dot(na_ref[...], w_ref[...]) + b_ref[...].astype(f32)
    rawT = raw.T.reshape(seq_ways, DH, frames)
    turned = part < 2
    cosine = jnp.where(turned, trig[0], 1.0)[None]
    sine = jnp.where(turned, trig[1], 0.0)[None]
    out_ref[:, pl.ds(pl.multiple_of(part * DH, DH), DH), :] = turn_heads(rawT, cosine, sine).astype(bf16)


def qkv_block(lengths, ids, drop, na, w_qkv, b_qkv, chunk, seq_ways):
    frames, width = na.shape
    cols = seq_ways * DH
    chunks = width // cols
    utts = lengths.shape[0]

    def whole(shape):
        return pl.BlockSpec(shape, lambda j, *_: (0,) * len(shape), pipeline_mode=pl.Buffered(1))

    shape = (seq_ways, 3 * DH, frames)
    return pl.pallas_call(
        functools.partial(qkv_kernel, utts, seq_ways),
        out_shape=jax.ShapeDtypeStruct(shape, jnp.bfloat16),
        grid_spec=pltpu.PrefetchScalarGridSpec(
            num_scalar_prefetch=3,
            grid=(3,),
            in_specs=[
                whole(na.shape),
                pl.BlockSpec((width, cols), lambda j, *_: (0, j * chunks + chunk)),
                pl.BlockSpec((1, cols), lambda j, *_: (0, j * chunks + chunk)),
            ],
            out_specs=whole(shape),
            scratch_shapes=[pltpu.VMEM((2, DH // 2, frames), jnp.float32)],
        ),
        cost_estimate=cost(75),
        name="qkv_block",
    )(lengths, ids, drop, na, w_qkv, b_qkv)


def back_kernel(utts, seq_ways, chunk, lengths_ref, ids_ref, drop_ref, grad_ref, naT_ref, w_ref, *refs):
    first = chunk == 0
    acc_in = None if first else refs[0]
    acc_ref, bias_ref, keep_ref, send_ref, trig, grads, sems = refs[0 if first else 3 :]
    f32, bf16 = jnp.float32, jnp.bfloat16
    part = pl.program_id(0)
    width, frames = naT_ref.shape
    core = ids_ref[0]
    parts = keep_ref.shape[0]
    own = width // seq_ways
    rows = own // parts

    @pl.when(part == 0)
    def _():
        _, place = segment_rows(lengths_ref, drop_ref, utts, ids_ref[1] * frames, frames)
        cosine, sine = rotary_rows(place, DH // 2)
        trig[0] = cosine
        trig[1] = sine

    turned = part < 2
    cosine = jnp.where(turned, trig[0], 1.0)[None]
    sine = jnp.where(turned, trig[1], 0.0)[None]
    raw = grad_ref[:, pl.ds(pl.multiple_of(part * DH, DH), DH), :].astype(f32)
    gpT = turn_heads(raw, cosine, -sine).astype(bf16).reshape(seq_ways * DH, frames)
    gna = dot(w_ref[...], gpT)

    @pl.when(part == 0)
    def _():
        acc_ref[...] = gna if first else acc_in[...] + gna

    @pl.when(part > 0)
    def _():
        acc_ref[...] += gna

    ones = jnp.ones((8, frames), bf16)
    bias_ref[0] = dot_nt(ones, gpT)
    grad_w = dot_nt(naT_ref[...], gpT).astype(bf16)
    cols = seq_ways * DH
    at = pl.ds(pl.multiple_of(part * rows, rows), rows)
    for s in range(seq_ways):
        side = jnp.where(core == s % 2, 0, 1)
        for k in range(parts):
            lo = s * own + k * rows
            grads[side, k, s // 2, at, :] = grad_w[lo : lo + rows]

    def copy(side, p):
        where = (slice(None), slice(None), pl.ds(pl.multiple_of(p * rows, rows), rows))
        return pltpu.make_async_copy(
            grads.at[side].at[where],
            (keep_ref, send_ref)[side].at[(*where, pl.ds(chunk * cols, cols))],
            sems.at[side, p],
        )

    for side in (1, 0):
        copy(side, part).start()

    @pl.when(part == 2)
    def _():
        for side in (1, 0):
            for p in range(3):
                copy(side, p).wait()


def back_block(lengths, ids, drop, grad, naT, w_qkv, before, chunk, parts):
    seq_ways, _, frames = grad.shape
    width = naT.shape[0]
    cols = seq_ways * DH
    chunks = width // cols
    utts = lengths.shape[0]
    f32, bf16 = jnp.float32, jnp.bfloat16
    rows = width // seq_ways // parts

    def whole(shape):
        return pl.BlockSpec(shape, lambda j, *_: (0,) * len(shape), pipeline_mode=pl.Buffered(1))

    gspec = pl.BlockSpec(memory_space=pl.ANY)
    gshape = jax.ShapeDtypeStruct((parts, seq_ways // 2, 3 * rows, width), bf16)
    ins = [grad, naT, w_qkv, *before]
    in_specs = [whole(grad.shape), whole(naT.shape)]
    in_specs += [pl.BlockSpec((width, cols), lambda j, *_: (0, j * chunks + chunk))]
    aliases = {}
    if before:
        in_specs += [whole(before[0].shape), gspec, gspec]
        aliases = {7: 2, 8: 3}
    return pl.pallas_call(
        functools.partial(back_kernel, utts, seq_ways, chunk),
        out_shape=[
            jax.ShapeDtypeStruct((width, frames), f32),
            jax.ShapeDtypeStruct((3, 8, cols), f32),
            gshape,
            gshape,
        ],
        grid_spec=pltpu.PrefetchScalarGridSpec(
            num_scalar_prefetch=3,
            grid=(3,),
            in_specs=in_specs,
            out_specs=[
                whole((width, frames)),
                pl.BlockSpec((1, 8, cols), lambda j, *_: (j, 0, 0)),
                gspec,
                gspec,
            ],
            scratch_shapes=[
                pltpu.VMEM((2, DH // 2, frames), f32),
                pltpu.VMEM((2, parts, seq_ways // 2, 3 * rows, cols), bf16),
                pltpu.SemaphoreType.DMA((2, 3)),
            ],
        ),
        compiler_params=pltpu.CompilerParams(vmem_limit_bytes=48 << 20),
        cost_estimate=cost(100),
        input_output_aliases=aliases,
        name="back_block",
    )(lengths, ids, drop, *ins)


def norm_kernel(
    utts, heads_local, lengths_ref, ids_ref, acc_ref, hidden_ref, after_ref, mods_ref, loss_ref, mid_ref, *refs
):
    f32, bf16 = jnp.float32, jnp.bfloat16
    bias_refs, (gh_ref, small_ref) = refs[:heads_local], refs[heads_local:]
    frames, width = hidden_ref.shape
    pad_u = table_rows(utts)
    base = 6 * pad_u
    hot = onehot_rows(lengths_ref, utts, 16, ids_ref[1] * frames, frames)
    cols = frame_columns(hot, jnp.zeros((1, frames), f32))
    madd = mods_operand(mods_ref)
    scale = dot(cols, madd[:, width:])
    gna = acc_ref[...].T
    normed, rstd = norm_stats(hidden_ref[...])
    sums = sum_rows(hot, 16, frames)
    small_ref[0:pad_u, :] = dot(sums, gna.astype(bf16))[:pad_u]
    small_ref[pad_u : 2 * pad_u, :] = dot(sums, (gna * normed).astype(bf16))[:pad_u]
    gh = (after_ref[...] + norm_back(gna * (1.0 + scale), normed, rstd)).astype(bf16)
    gh_ref[...] = gh
    small_ref[2 * pad_u : base, :] = mid_ref[0 : 4 * pad_u, :]
    cols_local = width // heads_local
    for c in range(heads_local):
        for p in range(3):
            small_ref[base + p : base + p + 1, c * cols_local : (c + 1) * cols_local] = bias_refs[c][p, 0:1, :]
    small_ref[base + 3 : base + 4, :] = dot(sums, gh)[16:17]
    small_ref[base + 4 : base + 12, :] = mid_ref[4 * pad_u : 4 * pad_u + 8, :]
    count = jnp.sum(loss_ref[...].astype(f32), axis=1, keepdims=True)
    high = jnp.floor(count / 32.0) * 32.0
    small_ref[base + 12 : base + 13, :] = jnp.broadcast_to(high, (1, width))
    small_ref[base + 13 : base + 16, :] = jnp.broadcast_to(count - high, (3, width))


def norm_block(lengths, ids, acc, hidden, after, mods, loss, mid_small, biases):
    frames, width = hidden.shape
    utts = lengths.shape[0]
    out_shape = [
        jax.ShapeDtypeStruct((frames, width), jnp.bfloat16),
        jax.ShapeDtypeStruct((6 * table_rows(utts) + 16, width), jnp.float32),
    ]
    return pl.pallas_call(
        functools.partial(norm_kernel, utts, len(biases)),
        out_shape=out_shape,
        grid_spec=pltpu.PrefetchScalarGridSpec(
            num_scalar_prefetch=2,
            grid=(1,),
            in_specs=[whole_block(a.shape) for a in (acc, hidden, after, mods, loss, mid_small, *biases)],
            out_specs=[whole_block(o.shape) for o in out_shape],
        ),
        compiler_params=pltpu.CompilerParams(vmem_limit_bytes=48 << 20),
        cost_estimate=cost(50),
        name="norm_block",
    )(lengths, ids, acc, hidden, after, mods, loss, mid_small, *biases)


def skip_kernel(seq_ways, ids_ref, joinedT_ref, gh_ref, keep_ref, send_ref, grads, sems):
    step = pl.program_id(0)
    core = ids_ref[0]
    parts = keep_ref.shape[0]
    width = joinedT_ref.shape[0]
    block = 2 * width // seq_ways
    rows = block // parts
    z_step = seq_ways // 4
    grad_w = dot(joinedT_ref[...], gh_ref[...]).astype(jnp.bfloat16)
    for b in range(width // block):
        side = jnp.where(core == b % 2, 0, 1)
        for k in range(parts):
            lo = b * block + k * rows
            grads[side, k, step * z_step + b // 2] = grad_w[lo : lo + rows]

    def copy(side, at):
        where = (slice(None), pl.ds(at * z_step, z_step))
        return pltpu.make_async_copy(
            grads.at[side].at[where], (keep_ref, send_ref)[side].at[where], sems.at[side, at]
        )

    for side in (1, 0):
        copy(side, step).start()

    @pl.when(step == 1)
    def _():
        for side in (1, 0):
            for at in range(2):
                copy(side, at).wait()


def skip_block(ids, joinedT, gh, seq_ways, parts):
    frames, width = gh.shape
    rows = 2 * width // seq_ways // parts
    gshape = (parts, seq_ways // 2, rows, width)
    return pl.pallas_call(
        functools.partial(skip_kernel, seq_ways),
        out_shape=[jax.ShapeDtypeStruct(gshape, jnp.bfloat16)] * 2,
        grid_spec=pltpu.PrefetchScalarGridSpec(
            num_scalar_prefetch=1,
            grid=(2,),
            in_specs=[pl.BlockSpec((width, frames), lambda j, *_: (j, 0)), whole_block(gh.shape)],
            out_specs=[pl.BlockSpec(memory_space=pl.ANY)] * 2,
            scratch_shapes=[pltpu.VMEM((2,) + gshape, jnp.bfloat16), pltpu.SemaphoreType.DMA((2, 2))],
        ),
        compiler_params=pltpu.CompilerParams(vmem_limit_bytes=32 << 20),
        cost_estimate=cost(50),
        name="skip_block",
    )(ids, joinedT, gh)


def joined_kernel(gh_ref, w_ref, scale_ref, first_ref, second_ref):
    step = pl.program_id(0)
    value = dot_nt(gh_ref[...], w_ref[...]) * scale_ref[0:1, 0:1]

    @pl.when(step == 0)
    def _():
        first_ref[...] = value

    @pl.when(step == 1)
    def _():
        second_ref[...] = value


def joined_block(gh, w_skip, scale):
    frames, width = gh.shape
    out = jax.ShapeDtypeStruct((frames, width), jnp.float32)
    return pl.pallas_call(
        joined_kernel,
        out_shape=[out, out],
        grid_spec=pltpu.PrefetchScalarGridSpec(
            num_scalar_prefetch=0,
            grid=(2,),
            in_specs=[
                whole_block(gh.shape),
                pl.BlockSpec((width, width), lambda j: (j, 0)),
                whole_block(scale.shape),
            ],
            out_specs=[whole_block(out.shape)] * 2,
        ),
        compiler_params=pltpu.CompilerParams(vmem_limit_bytes=32 << 20),
        cost_estimate=cost(50),
        name="joined_block",
    )(gh, w_skip, scale)


def add_bf16(left, right):
    return (left.astype(jnp.float32) + right.astype(jnp.float32)).astype(jnp.bfloat16)


def first_kernel(pairs, splits, ids_ref, *refs):
    ins, outs = refs[: 8 * pairs], list(refs[8 * pairs :])
    for i in range(4):
        own = [outs.pop(0) for _ in range(splits if i < 2 else 1)]
        at = 0
        for p in range(pairs):
            left, right = ins[2 * (i * pairs + p)], ins[2 * (i * pairs + p) + 1]
            rows = left.shape[-2]
            value = add_bf16(left[0, 0, 0], right[0, 0, 0])
            if len(own) == 1:
                own[0][0, :, at : at + rows, :] = value
            else:
                for out in own:
                    out[0] = value[:, at : at + out.shape[2], :]
                    at += out.shape[2]
            at += rows


def first_sum(ids, pairs, splits):
    _, _, _, z_ways, _, width = pairs[0][0].shape
    total = sum(k.shape[4] for k, _ in pairs)
    step = 1 if total > 100 else z_ways

    def source(half, axis, mine, rows):
        def at(g, z, ids):
            bit = ids[axis]
            return half, bit if mine else 1 - bit, g, z, 0, 0

        return pl.BlockSpec((1, 1, 1, step, rows, width), at)

    order = [(0, 2, False), (1, 3, False), (0, 2, True), (1, 3, True)]
    sizes = [*splits, *splits, total, total]
    return pl.pallas_call(
        functools.partial(first_kernel, len(pairs), len(splits)),
        out_shape=[jax.ShapeDtypeStruct((2, z_ways, n, width), jnp.bfloat16) for n in sizes],
        grid_spec=pltpu.PrefetchScalarGridSpec(
            num_scalar_prefetch=1,
            grid=(2, z_ways // step),
            in_specs=[source(*o, a.shape[4]) for o in order for pair in pairs for a in pair],
            out_specs=[pl.BlockSpec((1, step, n, width), lambda g, z, ids: (g, z, 0, 0)) for n in sizes],
        ),
        compiler_params=pltpu.CompilerParams(vmem_limit_bytes=48 << 20),
        cost_estimate=cost(60),
        name="first_sum",
    )(ids, *([a for pair in pairs for a in pair] * 4))


def second_kernel(pieces, ids_ref, *refs):
    for i in range(4):
        keep, *got = refs[(pieces + 1) * i : (pieces + 1) * (i + 1)]
        out = refs[4 * (pieces + 1) + i]
        at = 0
        for g in got:
            rows = g.shape[2]
            out[:, at : at + rows, :] = add_bf16(keep[0, :, at : at + rows, :], g[0])
            at += rows


def second_sum(ids, keep_a, got_a, keep_b, got_b):
    _, z_ways, rows, width = keep_a.shape
    step = z_ways // 2 if rows > 100 else z_ways

    def source(axis, mine, value):
        def at(z, ids):
            bit = ids[axis]
            return bit if mine else 1 - bit, z, 0, 0

        return pl.BlockSpec((1, step, *value.shape[2:]), at)

    order = [(3, False), (2, False), (3, True), (2, True)]
    sides = [[keep_a, *got_a], [keep_b, *got_b]]
    out = jax.ShapeDtypeStruct((z_ways, rows, width), jnp.bfloat16)
    return pl.pallas_call(
        functools.partial(second_kernel, len(got_a)),
        out_shape=[out] * 4,
        grid_spec=pltpu.PrefetchScalarGridSpec(
            num_scalar_prefetch=1,
            grid=(z_ways // step,),
            in_specs=[source(*o, v) for i, o in enumerate(order) for v in sides[i % 2]],
            out_specs=[pl.BlockSpec((step, rows, width), lambda z, ids: (z, 0, 0))] * 4,
        ),
        compiler_params=pltpu.CompilerParams(vmem_limit_bytes=48 << 20),
        cost_estimate=cost(30),
        name="second_sum",
    )(ids, *((sides[0] + sides[1]) * 2))


def third_kernel(ids_ref, keep_a, got_a, keep_b, got_b, *outs):
    for j, out in enumerate(outs):
        at = ids_ref[4] ^ j
        out[0] = add_bf16(keep_a[at], got_a[at])
        out[1] = add_bf16(keep_b[at], got_b[at])


def third_sum(ids, keep_a, got_a, keep_b, got_b):
    z_ways, rows, width = keep_a.shape
    out = jax.ShapeDtypeStruct((2, rows, width), jnp.bfloat16)
    return pl.pallas_call(
        third_kernel,
        out_shape=[out] * z_ways,
        grid_spec=pltpu.PrefetchScalarGridSpec(
            num_scalar_prefetch=1,
            grid=(1,),
            in_specs=[whole_block(keep_a.shape)] * 4,
            out_specs=[whole_block(out.shape)] * z_ways,
        ),
        cost_estimate=cost(10),
        name="third_sum",
    )(ids, keep_a, got_a, keep_b, got_b)


def third_all_kernel(ids_ref, keep_a, got_a, keep_b, got_b, out):
    for z in range(keep_a.shape[0]):
        out[z, 0] = add_bf16(keep_a[z], got_a[z])
        out[z, 1] = add_bf16(keep_b[z], got_b[z])


def third_sum_all(ids, keep_a, got_a, keep_b, got_b):
    z_ways, rows, width = keep_a.shape
    out = jax.ShapeDtypeStruct((z_ways, 2, rows, width), jnp.bfloat16)
    step = max(1, z_ways // 2)
    return pl.pallas_call(
        third_all_kernel,
        out_shape=out,
        grid_spec=pltpu.PrefetchScalarGridSpec(
            num_scalar_prefetch=1,
            grid=(z_ways // step,),
            in_specs=[pl.BlockSpec((step, rows, width), lambda i, *_: (i, 0, 0))] * 4,
            out_specs=pl.BlockSpec((step, 2, rows, width), lambda i, *_: (i, 0, 0, 0)),
        ),
        cost_estimate=cost(10),
        name="third_sum_all",
    )(ids, keep_a, got_a, keep_b, got_b)


def fourth_all_kernel(x, out):
    total = x[0].astype(jnp.float32)
    for z in range(1, x.shape[0]):
        total = total + x[z].astype(jnp.float32)
    out[...] = total.astype(jnp.bfloat16)


def fourth_sum_all(terms):
    return pl.pallas_call(
        fourth_all_kernel,
        out_shape=jax.ShapeDtypeStruct(terms.shape[1:], jnp.bfloat16),
        grid=(1,),
        in_specs=[whole_block(terms.shape)],
        out_specs=whole_block(terms.shape[1:]),
        cost_estimate=cost(10),
        name="fourth_sum_all",
    )(terms)


def fourth_kernel(*refs):
    total = refs[0][...].astype(jnp.float32)
    for r in refs[1:-1]:
        total = total + r[...].astype(jnp.float32)
    refs[-1][...] = total.astype(jnp.bfloat16)


def fourth_sum(terms):
    shape = terms[0].shape
    return pl.pallas_call(
        fourth_kernel,
        out_shape=jax.ShapeDtypeStruct(shape, jnp.bfloat16),
        grid=(1,),
        in_specs=[whole_block(shape)] * len(terms),
        out_specs=whole_block(shape),
        cost_estimate=cost(10),
        name="fourth_sum",
    )(*terms)


def place_kernel(streams, plan, ids_ref, scale_ref, *refs):
    blocks, outs = refs[: 4 * streams], refs[4 * streams :]
    x, y = ids_ref[2], ids_ref[3]
    scale = scale_ref[0:1, 0:1]
    for stream, row, rows, lane, lanes, out, row_of, lane_of in plan:
        for d in range(4):
            own_x, own_y = x ^ (d & 1), y ^ (d >> 1)
            for half in range(2):
                k = own_x * 2 + own_y if half == 0 else 4 + own_y * 2 + own_x
                tile = blocks[4 * stream + d][half, row : row + rows, lane : lane + lanes]
                outs[out][row_of(k), lane_of(k)] = tile.astype(jnp.float32) * scale


def place_blocks(ids, scale, streams, plan, shapes):
    blocks = [b for s in streams for b in s]
    outs = [jax.ShapeDtypeStruct(s, jnp.float32) for s in shapes]
    return pl.pallas_call(
        functools.partial(place_kernel, len(streams), plan),
        out_shape=outs,
        grid_spec=pltpu.PrefetchScalarGridSpec(
            num_scalar_prefetch=1,
            grid=(1,),
            in_specs=[whole_block(a.shape) for a in (scale, *blocks)],
            out_specs=[whole_block(o.shape) for o in outs],
        ),
        compiler_params=pltpu.CompilerParams(vmem_limit_bytes=32 << 20),
        cost_estimate=cost(20),
        name="place_blocks",
    )(ids, scale, *blocks)


def span(start, size):
    return pl.ds(pl.multiple_of(start, size), size)


def ada_kernel(groups, pad_u, numerator, time_ref, *refs):
    f32 = jnp.float32
    parts, (weight_ref, vector_ref, scale_ref) = refs[:groups], refs[groups:]
    table = pl.program_id(0)
    base = 6 * pad_u
    count = parts[0][base + 12 : base + 13, 0:1] + parts[0][base + 13 : base + 14, 0:1]
    for p in parts[1:]:
        count = count + p[base + 12 : base + 13, 0:1] + p[base + 13 : base + 14, 0:1]
    scale = numerator / count
    rows = jnp.concatenate([p[pl.ds(pl.multiple_of(table * pad_u, 8), pad_u), :] for p in parts], axis=0) * scale
    vector_ref[pl.ds(table, 1), :] = jnp.sum(rows, axis=0, keepdims=True)
    operand = jnp.concatenate(list(split3(rows)), axis=0)
    weight_ref[...] = dot(time_ref[...], operand)

    @pl.when(table == 0)
    def _():
        total = parts[0][base : base + 16, :]
        for p in parts[1:]:
            total = total + p[base : base + 16, :]
        vector_ref[8:24, :] = total * scale
        scale_ref[...] = jnp.broadcast_to(scale, scale_ref.shape)


def ada_block(time3, parts, utts, numerator):
    pad_u = table_rows(utts)
    width = parts[0].shape[1]
    own = time3.shape[0]
    f32 = jnp.float32
    return pl.pallas_call(
        functools.partial(ada_kernel, len(parts), pad_u, numerator),
        out_shape=[
            jax.ShapeDtypeStruct((own, 6 * width), f32),
            jax.ShapeDtypeStruct((24, width), f32),
            jax.ShapeDtypeStruct((8, 128), f32),
        ],
        grid=(6,),
        in_specs=[whole_block(time3.shape)] + [whole_block(p.shape) for p in parts],
        out_specs=[
            pl.BlockSpec((own, width), lambda j: (0, j)),
            whole_block((24, width)),
            whole_block((8, 128)),
        ],
        cost_estimate=cost(50),
        name="ada_block",
    )(time3, *parts)


def sum_exchange(value, axis, bit):
    ways = lax.axis_size(axis)
    return lax.ppermute(value, axis, [(i, i ^ bit) for i in range(ways)])


def axis_bits(ways):
    return [1 << i for i in range(ways.bit_length() - 1)]


def reduce_stages(ids, blocks, splits, whole_z):
    batch_ways = lax.axis_size("batch")
    x_bit, y_bit = 1, 1 << ((batch_ways.bit_length() - 1) // 2)
    pairs = []
    for keep, send in blocks:
        shape = (2, 2, 2) + keep.shape[1:]
        pairs.append((keep.reshape(shape), sum_exchange(send, "seq", 1).reshape(shape)))
    *sends, keep_a, keep_b = first_sum(ids, pairs, splits)
    sends = follow(sends, (yield sends))
    got, token = [[], []], None
    for i in range(len(splits)):
        pieces = follow([sends[i], sends[len(splits) + i]], token)
        for side, bit in enumerate((x_bit, y_bit)):
            got[side].append(sum_exchange(pieces[side], "batch", bit))
        token = yield [got[0][i], got[1][i]]
    got_a, got_b = (follow(g, token) for g in got)
    send_a, send_b, keep_a, keep_b = second_sum(ids, keep_a, got_a, keep_b, got_b)
    send_a, send_b = follow([send_a, send_b], (yield [send_a, send_b]))
    got = [sum_exchange(send_a, "batch", y_bit), sum_exchange(send_b, "batch", x_bit)]
    got_a, got_b = follow(got, (yield got))
    if whole_z:
        ways = lax.axis_size("seq")
        groups = [list(range(c, ways, 2)) for c in range(2)]
        away = [third_sum_all(ids, keep_a, got_a, keep_b, got_b)]
        away = follow(away, (yield away))
        got = [lax.all_to_all(away[0], "seq", 0, 0, axis_index_groups=groups, tiled=True)]
        got = follow(got, (yield got))
        block = fourth_sum_all(got[0])
    else:
        own, *away = third_sum(ids, keep_a, got_a, keep_b, got_b)
        away = follow(away, (yield away))
        got = [sum_exchange(a, "seq", 2 * (j + 1)) for j, a in enumerate(away)]
        got = follow(got, (yield got))
        block = fourth_sum([own] + got)
    for bit in axis_bits(batch_ways):
        if bit not in (x_bit, y_bit):
            block = add_bf16(block, sum_exchange(block, "batch", bit))
    (block,) = follow([block], (yield [block]))
    yield [block] + [sum_exchange(block, "batch", bit) for bit in (x_bit, y_bit, x_bit | y_bit)]


def advance(stages, steps, token=None):
    value = next(stages) if token is None else stages.send(token)
    for _ in range(steps - 1):
        value = next(stages)
    return value


def last_stage(stages, token=None):
    value = stages.send(token)
    for value in stages:
        pass
    return value


def follow(values, token):
    return values if token is None else [after(v, token) for v in values]


def after(value, *others):
    return lax.optimization_barrier((value,) + others)[0]


def gather_groups(value):
    return [value] + [sum_exchange(value, "batch", i) for i in range(1, lax.axis_size("batch"))]


def sum_z(value):
    away = value.astype(jnp.bfloat16)
    for j in range(1, lax.axis_size("seq") // 2):
        value = value + sum_exchange(away, "seq", 2 * j).astype(jnp.float32)
    return value


def shards(
    tokens_in,
    skip_in,
    condition,
    cotangent,
    time_embed,
    lengths,
    key_mask,
    drop_mask,
    loss_mask,
    w_skip,
    b_skip,
    w_ada,
    b_ada,
    w_qkv,
    b_qkv,
    w_out,
    b_out,
    w_up,
    b_up,
    w_down,
    b_down,
):
    f32, bf16 = jnp.float32, jnp.bfloat16
    seq_ways, batch_ways = lax.axis_size("seq"), lax.axis_size("batch")
    seq_rank = lax.axis_index("seq")
    frames, width = tokens_in.shape[1:]
    group_frames = frames * seq_ways
    heads_local = HEADS // seq_ways
    utts = lengths.shape[1]
    lengths_row, drop = lengths[0], drop_mask[0]
    batch_rank = lax.axis_index("batch")
    side = 1 << ((batch_ways.bit_length() - 1) // 2)
    ids = [lax.rem(seq_rank, 2), seq_rank, lax.rem(batch_rank, 2), lax.rem(batch_rank // side, 2), seq_rank // 2]
    ids = jnp.stack(ids).astype(jnp.int32)
    ok = key_mask.reshape(seq_ways, 1, frames)
    exchange = functools.partial(lax.all_to_all, axis_name="seq", split_axis=0, concat_axis=0, tiled=True)

    time_act = jax.nn.silu(time_embed[0]).astype(bf16)
    time_rows = jnp.pad(time_act, ((0, 16 - utts), (0, 0)))

    def modulation(first, last):
        return jnp.dot(time_rows, w_ada[:, first:last], preferred_element_type=f32) + b_ada[
            first:last
        ].astype(f32)

    mods_a = modulation(0, 2 * width)
    hidden, joinedT, naT, na = head_block(
        lengths_row, ids, drop, tokens_in[0], skip_in[0], condition[0], mods_a, w_skip, b_skip[None]
    )
    mods_rest = modulation(2 * width, 6 * width)
    received = []
    for c in range(heads_local):
        packed = qkv_block(lengths_row, ids, drop, na, w_qkv, b_qkv[None], c, seq_ways)
        if c == 0:
            na = after(na, mods_rest)
        received.append(exchange(packed))

    own = width // seq_ways
    pad_u = table_rows(utts)
    time_own = lax.dynamic_slice_in_dim(jnp.concatenate(gather_groups(time_rows[:pad_u])), seq_rank * own, own, axis=1)
    time3 = jnp.tile(time_own.T, (1, 3))

    received[0] = after(received[0], mods_rest)
    head_out, log_totals, returned = [], [], []
    for c in range(heads_local):
        out, log_total = attend(lengths_row, received[c], ok)
        head_out.append(out)
        log_totals.append(log_total)
        returned.append(exchange(after(out, *returned)))
        if c < heads_local - 1:
            received[c + 1] = after(received[c + 1], out, time3)
    mid = mid_block(
        lengths_row,
        ids,
        returned,
        hidden,
        mods_rest,
        cotangent[0],
        loss_mask,
        w_out,
        b_out[None],
        w_up,
        b_up[None],
        w_down,
        b_down[None],
        PARTS,
    )
    output, after_grad, mid_small, grad_att, keep, send = mid
    grad_heads = exchange(grad_att)
    front = keep.shape[2] * 4 // 9 // 16 * 16
    feed = reduce_stages(ids, [(keep, send)], [front, keep.shape[2] - front], True)

    ahead = next(feed)
    grad_local = []
    for c in range(heads_local):
        operand = after(grad_heads, *ahead)
        moving = feed.send(grad if c else None) if c < 2 else []
        grad = attend_back(lengths_row, received[c], ok, head_out[c], operand, log_totals[c], c)
        grad_local.append(exchange(after(grad, *moving)))
        ahead = [grad]
    if heads_local == 1:
        next(feed)
    ahead = ahead + advance(feed, 1, ahead[0])
    before, biases = (), []
    for c in range(heads_local):
        acc, bias, keep, send = back_block(
            lengths_row, ids, drop, after(grad_local[c], *ahead), naT, w_qkv, before, c, PARTS
        )
        before = (acc, keep, send)
        biases.append(bias)
        ahead = next(feed) and advance(feed, 1, acc) if c == 0 else []
    gh, small = norm_block(lengths_row, ids, acc, hidden, after_grad, mods_a, loss_mask, mid_small, biases)
    small = small + sum_exchange(small, "seq", 1)
    small = sum_z(small)
    moving = feed.send(small)
    skip_keep, skip_send = skip_block(ids, joinedT, gh, seq_ways, PARTS)
    blocks = [(after(skip_keep, small), skip_send), (keep, send)]
    rest = reduce_stages(ids, blocks, [5 * own // PARTS], False)
    advance(rest, 4)
    groups = gather_groups(after(small, *rest.send(moving[0])))
    numerator = float(group_frames * batch_ways)
    grad_w_ada, vectors, scale = ada_block(time3, groups, utts, numerator)
    grad_tokens, grad_skip = joined_block(gh, w_skip, scale)
    next(feed)
    feed = last_stage(feed, groups[-1])
    rest = last_stage(rest)

    ff = w_up.shape[1]
    chunks = ff // width
    up_part = chunks * own // PARTS
    down_part = ff // seq_ways // PARTS
    out_part = own // PARTS
    per_chunk = own // up_part
    whole_lanes = lambda k: span(0, width)
    grad_w_up, grad_w_down, grad_w_out = place_blocks(
        ids,
        scale,
        [feed],
        [
            (
                *(0, 0, up_part, 0, width, 0),
                lambda k: span(lax.rem(k, per_chunk) * up_part, up_part),
                lambda k: span(k // per_chunk * width, width),
            ),
            (0, up_part, down_part, 0, width, 1, lambda k: span(k * down_part, down_part), whole_lanes),
            (0, up_part + down_part, out_part, 0, width, 2, lambda k: span(k * out_part, out_part), whole_lanes),
        ],
        [(own, ff), (ff // seq_ways, width), (own, width)],
    )
    skip_part = 2 * own // PARTS
    grad_w_skip, grad_w_qkv = place_blocks(
        ids,
        scale,
        [rest],
        [(0, 0, skip_part, 0, width, 0, lambda k: span(k * skip_part, skip_part), whole_lanes)]
        + [
            (
                *(0, skip_part + p * out_part, out_part, 0, width, 1),
                lambda k: span(k * out_part, out_part),
                lambda k, at=p * width: span(at, width),
            )
            for p in range(3)
        ],
        [(2 * own, width), (own, 3 * width)],
    )

    def own_slice(vector):
        vector = vector.reshape(-1)
        size = vector.shape[0] // seq_ways
        return lax.dynamic_slice_in_dim(vector, seq_rank * size, size)

    grad_b_ada = own_slice(vectors[:6])
    grad_b_qkv = own_slice(vectors[8:11])
    grad_b_skip = own_slice(vectors[11])
    grad_b_out = own_slice(vectors[12])
    grad_b_down = own_slice(vectors[13])
    grad_b_up = own_slice(vectors[14 : 14 + chunks])
    return (
        output[None],
        grad_tokens[None],
        grad_skip[None],
        grad_w_skip,
        grad_b_skip,
        grad_w_ada,
        grad_b_ada,
        grad_w_qkv,
        grad_b_qkv,
        grad_w_out,
        grad_b_out,
        grad_w_up,
        grad_b_up,
        grad_w_down,
        grad_b_down,
    )


def solution(mesh):
    in_specs = (
        P("batch", "seq", None),
        P("batch", "seq", None),
        P("batch", "seq", None),
        P("batch", "seq", None),
        P("batch", None, None),
        P("batch", None),
        P("batch", None),
        P("batch", None),
        P("batch", "seq"),
        P(),
        P(),
        P(),
        P(),
        P(),
        P(),
        P(),
        P(),
        P(),
        P(),
        P(),
        P(),
    )
    out_specs = (
        P("batch", "seq", None),
        P("batch", "seq", None),
        P("batch", "seq", None),
        P("seq", None),
        P("seq"),
        P("seq", None),
        P("seq"),
        P("seq", None),
        P("seq"),
        P("seq", None),
        P("seq"),
        P("seq", None),
        P("seq"),
        P("seq", None),
        P("seq"),
    )
    return jax.shard_map(shards, mesh=mesh, in_specs=in_specs, out_specs=out_specs, check_vma=False)
```

```python
import functools

import jax
import jax.numpy as jnp
from jax import lax
from jax.experimental import pallas as pl
from jax.experimental.pallas import tpu as pltpu
from jax.sharding import PartitionSpec as P

HEADS = 16
HEAD_DIM = 64
PARTS = 8
BIG = 1e30
DH = 64
BQ = 512
BK = 512


def cost(weight):
    return pl.CostEstimate(flops=weight * 100000000, bytes_accessed=weight * 100000, transcendentals=0)


def onehot_rows(lengths_ref, utts, rows, base, width):
    row = lax.broadcasted_iota(jnp.int32, (rows, width), 0)
    col = base + lax.broadcasted_iota(jnp.int32, (rows, width), 1)
    start = jnp.int32(0)
    hot = jnp.zeros((rows, width), jnp.float32)
    for u in range(utts):
        end = start + lengths_ref[u]
        hot = jnp.where((row == u) & (col >= start) & (col < end), 1.0, hot)
        start = end
    return hot


def key_range(lengths_ref, utts, first, last):
    start = jnp.int32(0)
    low, high = jnp.int32(0), jnp.int32(0)
    for u in range(utts):
        end = start + lengths_ref[u]
        low = jnp.where((start <= first) & (first < end), start, low)
        high = jnp.where((start <= last) & (last < end), end, high)
        start = end
    return low // BK, (high + BK - 1) // BK


def aug_rows(utts):
    return -(-utts // 16) * 16


def split3(row):
    a = row.astype(jnp.bfloat16)
    rest = row - a.astype(jnp.float32)
    b = rest.astype(jnp.bfloat16)
    c = (rest - b.astype(jnp.float32)).astype(jnp.bfloat16)
    return a, b, c


def pad_rows(parts, total):
    have = sum(p.shape[0] for p in parts)
    if have < total:
        parts = parts + [jnp.zeros((total - have, parts[0].shape[1]), parts[0].dtype)]
    return jnp.concatenate(parts, axis=0)


def rows16(rows, width):
    idx = lax.broadcasted_iota(jnp.int32, (16, width), 0)
    out = jnp.zeros((16, width), jnp.float32)
    for i, r in enumerate(rows):
        out = jnp.where(idx == i, r, out)
    return out.astype(jnp.bfloat16)


def fwd_kernel(utts, lengths_ref, qkv_ref, ok_ref, out_ref, lse_ref, kaug, vaug):
    sources, _, frames = qkv_ref.shape
    per = frames // BQ
    pad_u = aug_rows(utts)
    step = pl.program_id(0)

    @pl.when(step == 0)
    def _():
        def build(s, c):
            hot = onehot_rows(lengths_ref, utts, pad_u, s * frames, frames)
            ok = ok_ref[s].astype(jnp.float32)
            block = qkv_ref[s]
            one = jnp.ones((1, frames), jnp.float32)
            kT = pad_rows(
                [block[DH : 2 * DH], (1.0 - hot).astype(jnp.bfloat16), rows16([1.0 - ok], frames)], 128
            )
            kaug[pl.ds(pl.multiple_of(s * frames, frames), frames), :] = kT.T
            vT = jnp.concatenate([block[2 * DH :], rows16([one], frames)], axis=0)
            for t in range(frames // BK):
                vaug[s * (frames // BK) + t] = vT[:, t * BK : (t + 1) * BK]
            return c

        lax.fori_loop(0, sources, build, 0)

    block = qkv_ref[step]
    hot_q = onehot_rows(lengths_ref, utts, pad_u, step * frames, frames)
    qT = (block[:DH].astype(jnp.float32) * 0.125)
    one = jnp.ones((1, frames), jnp.float32)
    qaug = pad_rows(
        [qT.astype(jnp.bfloat16), (hot_q * -BIG).astype(jnp.bfloat16), rows16([one * -BIG], frames)], 128
    )
    kT = block[DH : 2 * DH].astype(jnp.float32)
    vT = block[2 * DH :].astype(jnp.float32)
    ok = ok_ref[step] > 0
    s_self = jnp.sum(qT * kT, axis=0, keepdims=True)
    m0 = jnp.where(ok, -3e38, s_self)
    acc0 = jnp.concatenate([jnp.where(ok, 0.0, vT), jnp.where(ok, 0.0, jnp.ones((16, frames), jnp.float32))], axis=0)
    for t in range(per):
        cols = slice(t * BQ, (t + 1) * BQ)
        low, high = key_range(lengths_ref, utts, step * frames + t * BQ, step * frames + (t + 1) * BQ - 1)
        q_b = qaug[:, cols]

        def body(j, carry):
            m, acc = carry
            s = jnp.dot(kaug[pl.ds(pl.multiple_of(j * BK, BK), BK), :], q_b, preferred_element_type=jnp.float32)
            m_new = jnp.maximum(m, jnp.max(s, axis=0, keepdims=True))
            p = jnp.exp(s - m_new).astype(jnp.bfloat16)
            alpha = jnp.exp(m - m_new)
            acc = acc * alpha + jnp.dot(vaug[j], p, preferred_element_type=jnp.float32)
            return m_new, acc

        m, acc = lax.fori_loop(low, high, body, (m0[:, cols], acc0[:, cols]))
        total = acc[DH : DH + 1]
        out_ref[0, :, cols] = (acc[:DH] / total).astype(jnp.bfloat16)
        lse_ref[0, :, cols] = m + jnp.log(total)


def attend(lengths, qkv, ok):
    sources, _, frames = qkv.shape
    total = sources * frames
    utts = lengths.shape[0]
    whole = lambda shape: pl.BlockSpec(shape, lambda i, *_: (0,) * len(shape))
    return pl.pallas_call(
        functools.partial(fwd_kernel, utts),
        out_shape=(
            jax.ShapeDtypeStruct((sources, DH, frames), jnp.bfloat16),
            jax.ShapeDtypeStruct((sources, 1, frames), jnp.float32),
        ),
        grid_spec=pltpu.PrefetchScalarGridSpec(
            num_scalar_prefetch=1,
            grid=(sources,),
            in_specs=[whole(qkv.shape), whole(ok.shape)],
            out_specs=(
                pl.BlockSpec((1, DH, frames), lambda i, *_: (i, 0, 0)),
                pl.BlockSpec((1, 1, frames), lambda i, *_: (i, 0, 0)),
            ),
            scratch_shapes=[
                pltpu.VMEM((total, 128), jnp.bfloat16),
                pltpu.VMEM((total // BK, DH + 16, BK), jnp.bfloat16),
            ],
        ),
        cost_estimate=cost(250),
        name="attend",
    )(lengths, qkv, ok)


def bwd_kernel(utts, chunk, lengths_ref, qkv_ref, ok_ref, o_ref, do_ref, lse_ref, out_ref, kaug, vnat, kT_s, dk, dv):
    sources, _, frames = qkv_ref.shape
    per = frames // BK
    pad_u = aug_rows(utts)
    step = pl.program_id(0)
    f32 = jnp.float32

    @pl.when(step == 0)
    def _():
        def build(s, c):
            hot = onehot_rows(lengths_ref, utts, pad_u, s * frames, frames)
            ok = ok_ref[s]
            block = qkv_ref[s]
            one = jnp.ones((1, frames), f32)
            kT = block[DH : 2 * DH]
            vT = block[2 * DH :]
            kA = pad_rows(
                [kT, (1.0 - hot).astype(jnp.bfloat16), rows16([1.0 - ok.astype(f32), one, one, one], frames)], 128
            )
            rows = pl.ds(pl.multiple_of(s * frames, frames), frames)
            kaug[rows, :] = kA.T
            vnat[rows, :] = pad_rows([vT, rows16([one, one, one], frames)], 128).T
            qT = block[:DH].astype(f32) * 0.125
            do = do_ref[s, chunk * DH : (chunk + 1) * DH, :].astype(f32)
            s_self = jnp.sum(qT * kT.astype(f32), axis=0, keepdims=True)
            delta = jnp.sum(do * o_ref[s].astype(f32), axis=0, keepdims=True)
            p_self = jnp.where(ok > 0, 0.0, jnp.exp(s_self - lse_ref[s]))
            ds_self = p_self * (jnp.sum(do * vT.astype(f32), axis=0, keepdims=True) - delta)
            dk0 = ds_self * qT
            dv0 = p_self * do
            for t in range(per):
                cols = slice(t * BK, (t + 1) * BK)
                kT_s[s * per + t] = kT[:, cols]
                dk[s * per + t] = dk0[:, cols]
                dv[s * per + t] = dv0[:, cols]
            return c

        lax.fori_loop(0, sources, build, 0)

    block = qkv_ref[step]
    one = jnp.ones((1, frames), f32)
    hot_q = onehot_rows(lengths_ref, utts, pad_u, step * frames, frames)
    qT = block[:DH].astype(f32) * 0.125
    qTb = qT.astype(jnp.bfloat16)
    kT = block[DH : 2 * DH].astype(f32)
    vT = block[2 * DH :].astype(f32)
    ok = ok_ref[step]
    dob = do_ref[step, chunk * DH : (chunk + 1) * DH, :]
    do = dob.astype(f32)
    lse = lse_ref[step]
    delta = jnp.sum(do * o_ref[step].astype(f32), axis=0, keepdims=True)
    l3 = [-r.astype(f32) for r in split3(lse)]
    d3 = [-r.astype(f32) for r in split3(delta)]
    qaug = pad_rows([qTb, (hot_q * -BIG).astype(jnp.bfloat16), rows16([one * -BIG] + l3, frames)], 128)
    doaug = pad_rows([dob, rows16(d3, frames)], 128)
    s_self = jnp.sum(qT * kT, axis=0, keepdims=True)
    p_self = jnp.where(ok > 0, 0.0, jnp.exp(s_self - lse))
    ds_self = p_self * (jnp.sum(do * vT, axis=0, keepdims=True) - delta)
    dq0 = ds_self * kT
    nt = (((1,), (1,)), ((), ()))
    for t in range(frames // BQ):
        cols = slice(t * BQ, (t + 1) * BQ)
        low, high = key_range(lengths_ref, utts, step * frames + t * BQ, step * frames + (t + 1) * BQ - 1)
        q_a = qaug[:, cols]
        q_b = qTb[:, cols]
        do_a = doaug[:, cols]
        do_b = dob[:, cols]

        def body(j, dq):
            rows = pl.ds(pl.multiple_of(j * BK, BK), BK)
            s = jnp.dot(kaug[rows, :], q_a, preferred_element_type=f32)
            dp = jnp.dot(vnat[rows, :], do_a, preferred_element_type=f32)
            p = jnp.exp(s)
            ds = (p * dp).astype(jnp.bfloat16)
            dv[j] += lax.dot_general(do_b, p.astype(jnp.bfloat16), nt, preferred_element_type=f32)
            dk[j] += lax.dot_general(q_b, ds, nt, preferred_element_type=f32)
            return dq + jnp.dot(kT_s[j], ds, preferred_element_type=f32)

        dq = lax.fori_loop(low, high, body, dq0[:, cols])
        out_ref[step, :DH, cols] = (dq * 0.125).astype(jnp.bfloat16)

    @pl.when(step == sources - 1)
    def _():
        def finish(s, c):
            for t in range(per):
                cols = slice(t * BK, (t + 1) * BK)
                out_ref[s, DH : 2 * DH, cols] = dk[s * per + t].astype(jnp.bfloat16)
                out_ref[s, 2 * DH :, cols] = dv[s * per + t].astype(jnp.bfloat16)
            return c

        lax.fori_loop(0, sources, finish, 0)


def attend_back(lengths, qkv, ok, out, grad, lse, chunk):
    sources, _, frames = qkv.shape
    total = sources * frames
    utts = lengths.shape[0]
    whole = lambda shape: pl.BlockSpec(shape, lambda i, *_: (0,) * len(shape))
    return pl.pallas_call(
        functools.partial(bwd_kernel, utts, chunk),
        out_shape=jax.ShapeDtypeStruct(qkv.shape, jnp.bfloat16),
        grid_spec=pltpu.PrefetchScalarGridSpec(
            num_scalar_prefetch=1,
            grid=(sources,),
            in_specs=[whole(a.shape) for a in (qkv, ok, out, grad, lse)],
            out_specs=whole(qkv.shape),
            scratch_shapes=[
                pltpu.VMEM((total, 128), jnp.bfloat16),
                pltpu.VMEM((total, 128), jnp.bfloat16),
                pltpu.VMEM((total // BK, DH, BK), jnp.bfloat16),
                pltpu.VMEM((total // BK, DH, BK), jnp.float32),
                pltpu.VMEM((total // BK, DH, BK), jnp.float32),
            ],
        ),
        cost_estimate=cost(320),
        name="attend_back",
    )(lengths, qkv, ok, out, grad, lse)


FF_TILE = 512
EPS = 1e-06


def dot(left, right):
    return jnp.dot(left, right, preferred_element_type=jnp.float32)


def dot_nt(left, right):
    return lax.dot_general(left, right, (((1,), (1,)), ((), ())), preferred_element_type=jnp.float32)


def norm_stats(x):
    mean = jnp.mean(x, axis=1, keepdims=True)
    centred = x - mean
    rstd = lax.rsqrt(jnp.mean(centred * centred, axis=1, keepdims=True) + EPS)
    return centred * rstd, rstd


def norm_back(grad, normed, rstd):
    first = jnp.mean(grad, axis=1, keepdims=True)
    second = jnp.mean(grad * normed, axis=1, keepdims=True)
    return rstd * (grad - first - normed * second)


def mods_operand(mods_ref):
    rows = mods_ref[...]
    return pad_rows(list(split3(rows)), 128)


def table_rows(utts):
    return -(-utts // 8) * 8


def sum_rows(hot, utts_pad, frames):
    idx = lax.broadcasted_iota(jnp.int32, (16, frames), 0)
    ones = jnp.where(idx == 0, 1.0, 0.0).astype(jnp.bfloat16)
    return jnp.concatenate([hot.astype(jnp.bfloat16), ones], axis=0)


def mid_kernel(
    dims,
    lengths_ref,
    ids_ref,
    *refs,
):
    seq_ways, heads_local, utts, ff = dims
    att_refs = refs[:heads_local]
    (
        hidden_ref,
        mods_ref,
        cot_ref,
        loss_ref,
        w_out_ref,
        b_out_ref,
        w_up_ref,
        b_up_ref,
        w_down_ref,
        b_down_ref,
    ) = refs[heads_local : heads_local + 10]
    outs = refs[heads_local + 10 :]
    output_ref, after_grad_ref, small_ref, gatt_ref = outs[:4]
    refs_out = outs[4:6]
    (
        attT,
        attn_proj,
        after,
        nf,
        nfT,
        gff,
        ff_acc,
        gnf_acc,
        sums,
        cols,
        madd,
        grads,
        sems,
    ) = outs[6:]
    f32, bf16 = jnp.float32, jnp.bfloat16
    step = pl.program_id(0)
    steps = pl.num_programs(0)
    core = ids_ref[0]
    rank = ids_ref[1]
    frames, width = hidden_ref.shape
    up_rows = width // seq_ways
    down_rows = FF_TILE
    z_ways = seq_ways // 2
    parts = grads.shape[1]
    pad_u = table_rows(utts)
    ff_total = ff
    up_part = ff_total // width * up_rows // parts
    down_block = ff_total // seq_ways
    down_part = down_block // parts
    out_part = up_rows // parts

    def mod(index):
        return dot(cols[...], madd[:, index * width : (index + 1) * width])

    def grad_out():
        loss = cols[:, 48:49].astype(f32)
        return cot_ref[...].astype(f32) * loss

    @pl.when(step == 0)
    def _():
        hot = onehot_rows(lengths_ref, utts, 16, rank * frames, frames)
        hotb = hot.astype(bf16)
        idx = lax.broadcasted_iota(jnp.int32, (16, frames), 0)
        loss = jnp.where(idx == 0, loss_ref[...].astype(f32), 0.0).astype(bf16)
        cols[...] = pad_rows([hotb, hotb, hotb, loss], 128).T
        sums[...] = sum_rows(hot, 16, frames)
        madd[...] = mods_operand(mods_ref)
        for c in range(heads_local):
            for s in range(seq_ways):
                attT[(c * seq_ways + s) * DH : (c * seq_ways + s + 1) * DH, :] = att_refs[c][s]
        proj = dot(attT[...].T, w_out_ref[...]) + b_out_ref[...].astype(f32)
        attn_proj[...] = proj
        mixed = hidden_ref[...] + mod(0) * proj
        after[...] = mixed
        normed, _ = norm_stats(mixed)
        value = (normed * (1.0 + mod(2)) + mod(1)).astype(bf16)
        nf[...] = value
        nfT[...] = value.T
        gff[...] = (grad_out() * mod(3)).astype(bf16)
        small_ref[4 * pad_u :, :] = jnp.zeros((8, width), f32)

    up = dot(nf[...], w_up_ref[...]) + b_up_ref[...].astype(f32)
    inner = 0.7978845608028654 * (up + 0.044715 * (up * up * up))
    tanh = jnp.tanh(inner)
    cdf = 0.5 * (1.0 + tanh)
    act = (up * cdf).astype(bf16)
    slope = cdf + 0.5 * up * (1.0 - tanh * tanh) * (
        0.7978845608028654 * (1.0 + (3 * 0.044715) * (up * up))
    )
    ff_part = dot(act, w_down_ref[...])
    gup = (dot_nt(gff[...], w_down_ref[...]) * slope).astype(bf16)
    gnf_part = dot_nt(gup, w_up_ref[...])

    @pl.when(step == 0)
    def _():
        ff_acc[...] = ff_part
        gnf_acc[...] = gnf_part

    @pl.when(step > 0)
    def _():
        ff_acc[...] += ff_part
        gnf_acc[...] += gnf_part

    halves = width // FF_TILE
    chunk = step // halves
    half = step % halves
    col = pl.ds(pl.multiple_of(half * FF_TILE, FF_TILE), FF_TILE)
    per_chunk = up_rows // up_part
    small_ref[pl.ds(4 * pad_u + 2 + chunk, 1), col] = dot(sums[16:32, :], gup)[:1]
    grad_w_up = dot(nfT[...], gup).astype(bf16)
    for s in range(seq_ways):
        side = jnp.where(core == s % 2, 0, 1)
        for h in range(per_chunk):
            lo = s * up_rows + h * up_part
            grads[side, chunk * per_chunk + h, s // 2, 0:up_part, col] = grad_w_up[lo : lo + up_part]
    grad_w_down = dot(act.T, gff[...]).astype(bf16)
    blocks = FF_TILE // down_block
    copies = []
    for b in range(blocks):
        s = step * blocks + b
        side = jnp.where(core == s % 2, 0, 1)
        for k in range(parts):
            lo = b * down_block + k * down_part
            grads[side, k, s // 2, up_part : up_part + down_part, :] = grad_w_down[lo : lo + down_part]

    def region_copy(side, where, index):
        return pltpu.make_async_copy(
            grads.at[side].at[where], refs_out[side].at[where], sems.at[side, index]
        )

    def up_copy(side, j):
        where = (
            pl.ds((j // halves) * per_chunk, per_chunk),
            slice(None),
            pl.ds(0, up_part),
            pl.ds(pl.multiple_of((j % halves) * FF_TILE, FF_TILE), FF_TILE),
        )
        return region_copy(side, where, j)

    def down_copy(side, z, index):
        return region_copy(side, (slice(None), pl.ds(z, 1), pl.ds(up_part, down_part)), index)

    def out_copy(side):
        where = (slice(None), slice(None), pl.ds(up_part + down_part, out_part))
        return region_copy(side, where, ff_total // FF_TILE + z_ways)

    base = ff_total // FF_TILE
    for side in range(2):
        up_copy(side, step).start()
    for b in range(blocks):
        s = step * blocks + b
        for side in range(2):

            @pl.when(lax.rem(s + core, 2) == side)
            def _():
                down_copy(side, s // 2, base + s // 2).start()

    @pl.when(step == steps - 1)
    def _():
        ff_out = ff_acc[...] + b_down_ref[...].astype(f32)
        mixed = after[...]
        go = grad_out()
        output_ref[...] = (mixed + mod(3) * ff_out).astype(bf16)
        rows = sums[...]
        small_ref[3 * pad_u : 4 * pad_u, :] = dot(rows, (go * ff_out).astype(bf16))[:pad_u]
        normed, rstd = norm_stats(mixed)
        gnf = gnf_acc[...]
        small_ref[pad_u : 2 * pad_u, :] = dot(rows, gnf.astype(bf16))[:pad_u]
        small_ref[2 * pad_u : 3 * pad_u, :] = dot(rows, (gnf * normed).astype(bf16))[:pad_u]
        g_after = go + norm_back(gnf * (1.0 + mod(2)), normed, rstd)
        after_grad_ref[...] = g_after
        small_ref[0:pad_u, :] = dot(rows, (g_after * attn_proj[...]).astype(bf16))[:pad_u]
        gattn = (g_after * mod(0)).astype(bf16)
        small_ref[4 * pad_u : 4 * pad_u + 1, :] = dot(rows, gattn)[16:17]
        small_ref[4 * pad_u + 1 : 4 * pad_u + 2, :] = dot(rows, gff[...])[16:17]
        gattT = dot_nt(w_out_ref[...], gattn).astype(bf16)
        for c in range(heads_local):
            for s in range(seq_ways):
                lo = (c * seq_ways + s) * DH
                gatt_ref[s, c * DH : (c + 1) * DH, :] = gattT[lo : lo + DH]
        grad_w_out = dot(attT[...], gattn).astype(bf16)
        for s in range(seq_ways):
            side = jnp.where(core == s % 2, 0, 1)
            for k in range(parts):
                lo = s * up_rows + k * out_part
                grads[side, k, s // 2, up_part + down_part : up_part + down_part + out_part, :] = grad_w_out[
                    lo : lo + out_part
                ]
        for side in range(2):
            out_copy(side).start()
        for side in range(2):
            for j in range(ff_total // FF_TILE):
                up_copy(side, j).wait()
            for z in range(z_ways):
                down_copy(side, z, base + z).wait()
            out_copy(side).wait()


def mid_block(
    lengths, ids, att, hidden, mods, cot, loss, w_out, b_out, w_up, b_up, w_down, b_down, parts
):
    frames, width = hidden.shape
    heads_local = len(att)
    seq_ways = att[0].shape[0]
    ff = w_up.shape[1]
    up_rows = width // seq_ways
    rows = (ff // width * up_rows + ff // seq_ways + up_rows) // parts
    utts = lengths.shape[0]
    f32, bf16 = jnp.float32, jnp.bfloat16
    steps = ff // FF_TILE

    def whole(shape):
        return pl.BlockSpec(shape, lambda j, *_: (0,) * len(shape), pipeline_mode=pl.Buffered(1))

    hbm = pl.BlockSpec(memory_space=pl.ANY)
    gshape = (parts, seq_ways // 2, rows, width)
    out_shape = [
        jax.ShapeDtypeStruct((frames, width), bf16),
        jax.ShapeDtypeStruct((frames, width), f32),
        jax.ShapeDtypeStruct((4 * table_rows(utts) + 8, width), f32),
    ]
    out_shape += [jax.ShapeDtypeStruct((seq_ways, heads_local * DH, frames), bf16)]
    out_specs = [whole(o.shape) for o in out_shape] + [hbm] * 2
    out_shape += [jax.ShapeDtypeStruct(gshape, bf16)] * 2
    ins = list(att) + [hidden, mods, cot, loss, w_out, b_out]
    return pl.pallas_call(
        functools.partial(mid_kernel, (seq_ways, heads_local, utts, ff)),
        out_shape=out_shape,
        grid_spec=pltpu.PrefetchScalarGridSpec(
            num_scalar_prefetch=2,
            grid=(steps,),
            in_specs=[whole(a.shape) for a in ins]
            + [
                pl.BlockSpec((width, FF_TILE), lambda j, *_: (0, j)),
                pl.BlockSpec((1, FF_TILE), lambda j, *_: (0, j)),
                pl.BlockSpec((FF_TILE, width), lambda j, *_: (j, 0)),
                whole((1, width)),
            ],
            out_specs=out_specs,
            scratch_shapes=[
                pltpu.VMEM((width, frames), bf16),
                pltpu.VMEM((frames, width), f32),
                pltpu.VMEM((frames, width), f32),
                pltpu.VMEM((frames, width), bf16),
                pltpu.VMEM((width, frames), bf16),
                pltpu.VMEM((frames, width), bf16),
                pltpu.VMEM((frames, width), f32),
                pltpu.VMEM((frames, width), f32),
                pltpu.VMEM((32, frames), bf16),
                pltpu.VMEM((frames, 128), bf16),
                pltpu.VMEM((128, 4 * width), bf16),
                pltpu.VMEM((2,) + gshape, bf16),
                pltpu.SemaphoreType.DMA((2, steps + seq_ways // 2 + 1)),
            ],
        ),
        compiler_params=pltpu.CompilerParams(vmem_limit_bytes=63 << 20),
        cost_estimate=cost(500),
        name="mid_block",
    )(lengths, ids, *ins, w_up, b_up, w_down, b_down)


def whole_block(shape):
    return pl.BlockSpec(shape, lambda *_: (0,) * len(shape), pipeline_mode=pl.Buffered(1))


def segment_rows(lengths_ref, drop_ref, utts, base, width):
    col = base + lax.broadcasted_iota(jnp.int32, (1, width), 1)
    start = jnp.int32(0)
    kept = jnp.zeros((1, width), jnp.float32)
    place = jnp.zeros((1, width), jnp.int32)
    for u in range(utts):
        end = start + lengths_ref[u]
        inside = (col >= start) & (col < end)
        kept = jnp.where(inside, (1 - drop_ref[u]).astype(jnp.float32), kept)
        place = jnp.where(inside, col - start, place)
        start = end
    return kept, place.astype(jnp.float32)


def rotary_rows(place, half):
    index = lax.broadcasted_iota(jnp.int32, (half, 1), 0).astype(jnp.float32)
    inverse = jnp.exp(index * (-9.210340371976184 / half))
    angles = inverse * place
    return jnp.cos(angles), jnp.sin(angles)


def frame_columns(hot, extra):
    hotb = hot.astype(jnp.bfloat16)
    idx = lax.broadcasted_iota(jnp.int32, hot.shape, 0)
    last = jnp.where(idx == 0, extra, 0.0).astype(jnp.bfloat16)
    return pad_rows([hotb, hotb, hotb, last], 128).T


def head_kernel(
    utts,
    lengths_ref,
    ids_ref,
    drop_ref,
    tokens_ref,
    skip_ref,
    cond_ref,
    mods_ref,
    w_skip_ref,
    b_skip_ref,
    hidden_ref,
    joinedT_ref,
    naT_ref,
    na_ref,
    cols,
):
    f32, bf16 = jnp.float32, jnp.bfloat16
    step = pl.program_id(0)
    frames, width = tokens_ref.shape
    rank = ids_ref[1]

    @pl.when(step == 0)
    def _():
        hot = onehot_rows(lengths_ref, utts, 16, rank * frames, frames)
        kept, _ = segment_rows(lengths_ref, drop_ref, utts, rank * frames, frames)
        cols[...] = frame_columns(hot, kept)
        keep = cols[:, 48:49].astype(f32)
        mixed = (tokens_ref[...].astype(f32) + keep * cond_ref[...].astype(f32)).astype(bf16)
        joinedT_ref[0:width, :] = mixed.T
        hidden_ref[...] = dot(mixed, w_skip_ref[...]) + b_skip_ref[...].astype(f32)

    @pl.when(step == 1)
    def _():
        skip = skip_ref[...]
        joinedT_ref[width : 2 * width, :] = skip.T
        hidden = hidden_ref[...] + dot(skip, w_skip_ref[...])
        hidden_ref[...] = hidden
        madd = mods_operand(mods_ref)
        shift = dot(cols[...], madd[:, :width])
        scale = dot(cols[...], madd[:, width:])
        normed, _ = norm_stats(hidden)
        value = (normed * (1.0 + scale) + shift).astype(bf16)
        na_ref[...] = value
        naT_ref[...] = value.T


def head_block(lengths, ids, drop, tokens, skip, cond, mods, w_skip, b_skip):
    frames, width = tokens.shape
    utts = lengths.shape[0]
    f32, bf16 = jnp.float32, jnp.bfloat16

    def whole(shape):
        return pl.BlockSpec(shape, lambda j, *_: (0,) * len(shape), pipeline_mode=pl.Buffered(1))

    out_shape = [
        jax.ShapeDtypeStruct((frames, width), f32),
        jax.ShapeDtypeStruct((2 * width, frames), bf16),
        jax.ShapeDtypeStruct((width, frames), bf16),
        jax.ShapeDtypeStruct((frames, width), bf16),
    ]
    return pl.pallas_call(
        functools.partial(head_kernel, utts),
        out_shape=out_shape,
        grid_spec=pltpu.PrefetchScalarGridSpec(
            num_scalar_prefetch=3,
            grid=(2,),
            in_specs=[whole(a.shape) for a in (tokens, skip, cond, mods)]
            + [pl.BlockSpec((width, width), lambda j, *_: (j, 0)), whole((1, width))],
            out_specs=[whole(o.shape) for o in out_shape],
            scratch_shapes=[pltpu.VMEM((frames, 128), bf16)],
        ),
        compiler_params=pltpu.CompilerParams(vmem_limit_bytes=48 << 20),
        cost_estimate=cost(100),
        name="head_block",
    )(lengths, ids, drop, tokens, skip, cond, mods, w_skip, b_skip)


def turn_heads(tensor, cosine, sine):
    half = DH // 2
    first, second = tensor[:, :half], tensor[:, half:]
    return jnp.concatenate([first * cosine - second * sine, second * cosine + first * sine], axis=1)


def qkv_kernel(utts, seq_ways, lengths_ref, ids_ref, drop_ref, na_ref, w_ref, b_ref, out_ref, trig):
    f32, bf16 = jnp.float32, jnp.bfloat16
    part = pl.program_id(0)
    frames = na_ref.shape[0]

    @pl.when(part == 0)
    def _():
        _, place = segment_rows(lengths_ref, drop_ref, utts, ids_ref[1] * frames, frames)
        cosine, sine = rotary_rows(place, DH // 2)
        trig[0] = cosine
        trig[1] = sine

    raw = dot(na_ref[...], w_ref[...]) + b_ref[...].astype(f32)
    rawT = raw.T.reshape(seq_ways, DH, frames)
    turned = part < 2
    cosine = jnp.where(turned, trig[0], 1.0)[None]
    sine = jnp.where(turned, trig[1], 0.0)[None]
    out_ref[:, pl.ds(pl.multiple_of(part * DH, DH), DH), :] = turn_heads(rawT, cosine, sine).astype(bf16)


def qkv_block(lengths, ids, drop, na, w_qkv, b_qkv, chunk, seq_ways):
    frames, width = na.shape
    cols = seq_ways * DH
    chunks = width // cols
    utts = lengths.shape[0]

    def whole(shape):
        return pl.BlockSpec(shape, lambda j, *_: (0,) * len(shape), pipeline_mode=pl.Buffered(1))

    shape = (seq_ways, 3 * DH, frames)
    return pl.pallas_call(
        functools.partial(qkv_kernel, utts, seq_ways),
        out_shape=jax.ShapeDtypeStruct(shape, jnp.bfloat16),
        grid_spec=pltpu.PrefetchScalarGridSpec(
            num_scalar_prefetch=3,
            grid=(3,),
            in_specs=[
                whole(na.shape),
                pl.BlockSpec((width, cols), lambda j, *_: (0, j * chunks + chunk)),
                pl.BlockSpec((1, cols), lambda j, *_: (0, j * chunks + chunk)),
            ],
            out_specs=whole(shape),
            scratch_shapes=[pltpu.VMEM((2, DH // 2, frames), jnp.float32)],
        ),
        cost_estimate=cost(75),
        name="qkv_block",
    )(lengths, ids, drop, na, w_qkv, b_qkv)


def back_kernel(utts, seq_ways, chunk, lengths_ref, ids_ref, drop_ref, grad_ref, naT_ref, w_ref, *refs):
    first = chunk == 0
    acc_in = None if first else refs[0]
    acc_ref, bias_ref, keep_ref, send_ref, trig, grads, sems = refs[0 if first else 3 :]
    f32, bf16 = jnp.float32, jnp.bfloat16
    part = pl.program_id(0)
    width, frames = naT_ref.shape
    core = ids_ref[0]
    parts = keep_ref.shape[0]
    own = width // seq_ways
    rows = own // parts

    @pl.when(part == 0)
    def _():
        _, place = segment_rows(lengths_ref, drop_ref, utts, ids_ref[1] * frames, frames)
        cosine, sine = rotary_rows(place, DH // 2)
        trig[0] = cosine
        trig[1] = sine

    turned = part < 2
    cosine = jnp.where(turned, trig[0], 1.0)[None]
    sine = jnp.where(turned, trig[1], 0.0)[None]
    raw = grad_ref[:, pl.ds(pl.multiple_of(part * DH, DH), DH), :].astype(f32)
    gpT = turn_heads(raw, cosine, -sine).astype(bf16).reshape(seq_ways * DH, frames)
    gna = dot(w_ref[...], gpT)

    @pl.when(part == 0)
    def _():
        acc_ref[...] = gna if first else acc_in[...] + gna

    @pl.when(part > 0)
    def _():
        acc_ref[...] += gna

    ones = jnp.ones((8, frames), bf16)
    bias_ref[0] = dot_nt(ones, gpT)
    grad_w = dot_nt(naT_ref[...], gpT).astype(bf16)
    cols = seq_ways * DH
    at = pl.ds(pl.multiple_of(part * rows, rows), rows)
    for s in range(seq_ways):
        side = jnp.where(core == s % 2, 0, 1)
        for k in range(parts):
            lo = s * own + k * rows
            grads[side, k, s // 2, at, :] = grad_w[lo : lo + rows]

    def copy(side, p):
        where = (slice(None), slice(None), pl.ds(pl.multiple_of(p * rows, rows), rows))
        return pltpu.make_async_copy(
            grads.at[side].at[where],
            (keep_ref, send_ref)[side].at[(*where, pl.ds(chunk * cols, cols))],
            sems.at[side, p],
        )

    for side in (1, 0):
        copy(side, part).start()

    @pl.when(part == 2)
    def _():
        for side in (1, 0):
            for p in range(3):
                copy(side, p).wait()


def back_block(lengths, ids, drop, grad, naT, w_qkv, before, chunk, parts):
    seq_ways, _, frames = grad.shape
    width = naT.shape[0]
    cols = seq_ways * DH
    chunks = width // cols
    utts = lengths.shape[0]
    f32, bf16 = jnp.float32, jnp.bfloat16
    rows = width // seq_ways // parts

    def whole(shape):
        return pl.BlockSpec(shape, lambda j, *_: (0,) * len(shape), pipeline_mode=pl.Buffered(1))

    gspec = pl.BlockSpec(memory_space=pl.ANY)
    gshape = jax.ShapeDtypeStruct((parts, seq_ways // 2, 3 * rows, width), bf16)
    ins = [grad, naT, w_qkv, *before]
    in_specs = [whole(grad.shape), whole(naT.shape)]
    in_specs += [pl.BlockSpec((width, cols), lambda j, *_: (0, j * chunks + chunk))]
    aliases = {}
    if before:
        in_specs += [whole(before[0].shape), gspec, gspec]
        aliases = {7: 2, 8: 3}
    return pl.pallas_call(
        functools.partial(back_kernel, utts, seq_ways, chunk),
        out_shape=[
            jax.ShapeDtypeStruct((width, frames), f32),
            jax.ShapeDtypeStruct((3, 8, cols), f32),
            gshape,
            gshape,
        ],
        grid_spec=pltpu.PrefetchScalarGridSpec(
            num_scalar_prefetch=3,
            grid=(3,),
            in_specs=in_specs,
            out_specs=[
                whole((width, frames)),
                pl.BlockSpec((1, 8, cols), lambda j, *_: (j, 0, 0)),
                gspec,
                gspec,
            ],
            scratch_shapes=[
                pltpu.VMEM((2, DH // 2, frames), f32),
                pltpu.VMEM((2, parts, seq_ways // 2, 3 * rows, cols), bf16),
                pltpu.SemaphoreType.DMA((2, 3)),
            ],
        ),
        compiler_params=pltpu.CompilerParams(vmem_limit_bytes=48 << 20),
        cost_estimate=cost(100),
        input_output_aliases=aliases,
        name="back_block",
    )(lengths, ids, drop, *ins)


def norm_kernel(
    utts, heads_local, lengths_ref, ids_ref, acc_ref, hidden_ref, after_ref, mods_ref, loss_ref, mid_ref, *refs
):
    f32, bf16 = jnp.float32, jnp.bfloat16
    bias_refs, (gh_ref, small_ref) = refs[:heads_local], refs[heads_local:]
    frames, width = hidden_ref.shape
    pad_u = table_rows(utts)
    base = 6 * pad_u
    hot = onehot_rows(lengths_ref, utts, 16, ids_ref[1] * frames, frames)
    cols = frame_columns(hot, jnp.zeros((1, frames), f32))
    madd = mods_operand(mods_ref)
    scale = dot(cols, madd[:, width:])
    gna = acc_ref[...].T
    normed, rstd = norm_stats(hidden_ref[...])
    sums = sum_rows(hot, 16, frames)
    small_ref[0:pad_u, :] = dot(sums, gna.astype(bf16))[:pad_u]
    small_ref[pad_u : 2 * pad_u, :] = dot(sums, (gna * normed).astype(bf16))[:pad_u]
    gh = (after_ref[...] + norm_back(gna * (1.0 + scale), normed, rstd)).astype(bf16)
    gh_ref[...] = gh
    small_ref[2 * pad_u : base, :] = mid_ref[0 : 4 * pad_u, :]
    cols_local = width // heads_local
    for c in range(heads_local):
        for p in range(3):
            small_ref[base + p : base + p + 1, c * cols_local : (c + 1) * cols_local] = bias_refs[c][p, 0:1, :]
    small_ref[base + 3 : base + 4, :] = dot(sums, gh)[16:17]
    small_ref[base + 4 : base + 12, :] = mid_ref[4 * pad_u : 4 * pad_u + 8, :]
    count = jnp.sum(loss_ref[...].astype(f32), axis=1, keepdims=True)
    high = jnp.floor(count / 32.0) * 32.0
    small_ref[base + 12 : base + 13, :] = jnp.broadcast_to(high, (1, width))
    small_ref[base + 13 : base + 16, :] = jnp.broadcast_to(count - high, (3, width))


def norm_block(lengths, ids, acc, hidden, after, mods, loss, mid_small, biases):
    frames, width = hidden.shape
    utts = lengths.shape[0]
    out_shape = [
        jax.ShapeDtypeStruct((frames, width), jnp.bfloat16),
        jax.ShapeDtypeStruct((6 * table_rows(utts) + 16, width), jnp.float32),
    ]
    return pl.pallas_call(
        functools.partial(norm_kernel, utts, len(biases)),
        out_shape=out_shape,
        grid_spec=pltpu.PrefetchScalarGridSpec(
            num_scalar_prefetch=2,
            grid=(1,),
            in_specs=[whole_block(a.shape) for a in (acc, hidden, after, mods, loss, mid_small, *biases)],
            out_specs=[whole_block(o.shape) for o in out_shape],
        ),
        compiler_params=pltpu.CompilerParams(vmem_limit_bytes=48 << 20),
        cost_estimate=cost(50),
        name="norm_block",
    )(lengths, ids, acc, hidden, after, mods, loss, mid_small, *biases)


def skip_kernel(seq_ways, ids_ref, joinedT_ref, gh_ref, keep_ref, send_ref, grads, sems):
    step = pl.program_id(0)
    core = ids_ref[0]
    parts = keep_ref.shape[0]
    width = joinedT_ref.shape[0]
    block = 2 * width // seq_ways
    rows = block // parts
    z_step = seq_ways // 4
    grad_w = dot(joinedT_ref[...], gh_ref[...]).astype(jnp.bfloat16)
    for b in range(width // block):
        side = jnp.where(core == b % 2, 0, 1)
        for k in range(parts):
            lo = b * block + k * rows
            grads[side, k, step * z_step + b // 2] = grad_w[lo : lo + rows]

    def copy(side, at):
        where = (slice(None), pl.ds(at * z_step, z_step))
        return pltpu.make_async_copy(
            grads.at[side].at[where], (keep_ref, send_ref)[side].at[where], sems.at[side, at]
        )

    for side in (1, 0):
        copy(side, step).start()

    @pl.when(step == 1)
    def _():
        for side in (1, 0):
            for at in range(2):
                copy(side, at).wait()


def skip_block(ids, joinedT, gh, seq_ways, parts):
    frames, width = gh.shape
    rows = 2 * width // seq_ways // parts
    gshape = (parts, seq_ways // 2, rows, width)
    return pl.pallas_call(
        functools.partial(skip_kernel, seq_ways),
        out_shape=[jax.ShapeDtypeStruct(gshape, jnp.bfloat16)] * 2,
        grid_spec=pltpu.PrefetchScalarGridSpec(
            num_scalar_prefetch=1,
            grid=(2,),
            in_specs=[pl.BlockSpec((width, frames), lambda j, *_: (j, 0)), whole_block(gh.shape)],
            out_specs=[pl.BlockSpec(memory_space=pl.ANY)] * 2,
            scratch_shapes=[pltpu.VMEM((2,) + gshape, jnp.bfloat16), pltpu.SemaphoreType.DMA((2, 2))],
        ),
        compiler_params=pltpu.CompilerParams(vmem_limit_bytes=32 << 20),
        cost_estimate=cost(50),
        name="skip_block",
    )(ids, joinedT, gh)


def joined_kernel(gh_ref, w_ref, scale_ref, first_ref, second_ref):
    step = pl.program_id(0)
    value = dot_nt(gh_ref[...], w_ref[...]) * scale_ref[0:1, 0:1]

    @pl.when(step == 0)
    def _():
        first_ref[...] = value

    @pl.when(step == 1)
    def _():
        second_ref[...] = value


def joined_block(gh, w_skip, scale):
    frames, width = gh.shape
    out = jax.ShapeDtypeStruct((frames, width), jnp.float32)
    return pl.pallas_call(
        joined_kernel,
        out_shape=[out, out],
        grid_spec=pltpu.PrefetchScalarGridSpec(
            num_scalar_prefetch=0,
            grid=(2,),
            in_specs=[
                whole_block(gh.shape),
                pl.BlockSpec((width, width), lambda j: (j, 0)),
                whole_block(scale.shape),
            ],
            out_specs=[whole_block(out.shape)] * 2,
        ),
        compiler_params=pltpu.CompilerParams(vmem_limit_bytes=32 << 20),
        cost_estimate=cost(50),
        name="joined_block",
    )(gh, w_skip, scale)


def add_bf16(left, right):
    return (left.astype(jnp.float32) + right.astype(jnp.float32)).astype(jnp.bfloat16)


def first_kernel(pairs, splits, ids_ref, *refs):
    ins, outs = refs[: 8 * pairs], list(refs[8 * pairs :])
    for i in range(4):
        own = [outs.pop(0) for _ in range(splits if i < 2 else 1)]
        at = 0
        for p in range(pairs):
            left, right = ins[2 * (i * pairs + p)], ins[2 * (i * pairs + p) + 1]
            rows = left.shape[-2]
            value = add_bf16(left[0, 0, 0], right[0, 0, 0])
            if len(own) == 1:
                own[0][0, :, at : at + rows, :] = value
            else:
                for out in own:
                    out[0] = value[:, at : at + out.shape[2], :]
                    at += out.shape[2]
            at += rows


def first_sum(ids, pairs, splits):
    _, _, _, z_ways, _, width = pairs[0][0].shape
    total = sum(k.shape[4] for k, _ in pairs)
    step = 1 if total > 100 else z_ways

    def source(half, axis, mine, rows):
        def at(g, z, ids):
            bit = ids[axis]
            return half, bit if mine else 1 - bit, g, z, 0, 0

        return pl.BlockSpec((1, 1, 1, step, rows, width), at)

    order = [(0, 2, False), (1, 3, False), (0, 2, True), (1, 3, True)]
    sizes = [*splits, *splits, total, total]
    return pl.pallas_call(
        functools.partial(first_kernel, len(pairs), len(splits)),
        out_shape=[jax.ShapeDtypeStruct((2, z_ways, n, width), jnp.bfloat16) for n in sizes],
        grid_spec=pltpu.PrefetchScalarGridSpec(
            num_scalar_prefetch=1,
            grid=(2, z_ways // step),
            in_specs=[source(*o, a.shape[4]) for o in order for pair in pairs for a in pair],
            out_specs=[pl.BlockSpec((1, step, n, width), lambda g, z, ids: (g, z, 0, 0)) for n in sizes],
        ),
        compiler_params=pltpu.CompilerParams(vmem_limit_bytes=48 << 20),
        cost_estimate=cost(60),
        name="first_sum",
    )(ids, *([a for pair in pairs for a in pair] * 4))


def second_kernel(pieces, ids_ref, *refs):
    for i in range(4):
        keep, *got = refs[(pieces + 1) * i : (pieces + 1) * (i + 1)]
        out = refs[4 * (pieces + 1) + i]
        at = 0
        for g in got:
            rows = g.shape[2]
            out[:, at : at + rows, :] = add_bf16(keep[0, :, at : at + rows, :], g[0])
            at += rows


def second_sum(ids, keep_a, got_a, keep_b, got_b):
    _, z_ways, rows, width = keep_a.shape
    step = z_ways // 2 if rows > 100 else z_ways

    def source(axis, mine, value):
        def at(z, ids):
            bit = ids[axis]
            return bit if mine else 1 - bit, z, 0, 0

        return pl.BlockSpec((1, step, *value.shape[2:]), at)

    order = [(3, False), (2, False), (3, True), (2, True)]
    sides = [[keep_a, *got_a], [keep_b, *got_b]]
    out = jax.ShapeDtypeStruct((z_ways, rows, width), jnp.bfloat16)
    return pl.pallas_call(
        functools.partial(second_kernel, len(got_a)),
        out_shape=[out] * 4,
        grid_spec=pltpu.PrefetchScalarGridSpec(
            num_scalar_prefetch=1,
            grid=(z_ways // step,),
            in_specs=[source(*o, v) for i, o in enumerate(order) for v in sides[i % 2]],
            out_specs=[pl.BlockSpec((step, rows, width), lambda z, ids: (z, 0, 0))] * 4,
        ),
        compiler_params=pltpu.CompilerParams(vmem_limit_bytes=48 << 20),
        cost_estimate=cost(30),
        name="second_sum",
    )(ids, *((sides[0] + sides[1]) * 2))


def third_kernel(ids_ref, keep_a, got_a, keep_b, got_b, *outs):
    for j, out in enumerate(outs):
        at = ids_ref[4] ^ j
        out[0] = add_bf16(keep_a[at], got_a[at])
        out[1] = add_bf16(keep_b[at], got_b[at])


def third_sum(ids, keep_a, got_a, keep_b, got_b):
    z_ways, rows, width = keep_a.shape
    out = jax.ShapeDtypeStruct((2, rows, width), jnp.bfloat16)
    return pl.pallas_call(
        third_kernel,
        out_shape=[out] * z_ways,
        grid_spec=pltpu.PrefetchScalarGridSpec(
            num_scalar_prefetch=1,
            grid=(1,),
            in_specs=[whole_block(keep_a.shape)] * 4,
            out_specs=[whole_block(out.shape)] * z_ways,
        ),
        cost_estimate=cost(10),
        name="third_sum",
    )(ids, keep_a, got_a, keep_b, got_b)


def third_all_kernel(ids_ref, keep_a, got_a, keep_b, got_b, out):
    for z in range(keep_a.shape[0]):
        out[z, 0] = add_bf16(keep_a[z], got_a[z])
        out[z, 1] = add_bf16(keep_b[z], got_b[z])


def third_sum_all(ids, keep_a, got_a, keep_b, got_b):
    z_ways, rows, width = keep_a.shape
    out = jax.ShapeDtypeStruct((z_ways, 2, rows, width), jnp.bfloat16)
    step = max(1, z_ways // 2)
    return pl.pallas_call(
        third_all_kernel,
        out_shape=out,
        grid_spec=pltpu.PrefetchScalarGridSpec(
            num_scalar_prefetch=1,
            grid=(z_ways // step,),
            in_specs=[pl.BlockSpec((step, rows, width), lambda i, *_: (i, 0, 0))] * 4,
            out_specs=pl.BlockSpec((step, 2, rows, width), lambda i, *_: (i, 0, 0, 0)),
        ),
        cost_estimate=cost(10),
        name="third_sum_all",
    )(ids, keep_a, got_a, keep_b, got_b)


def fourth_all_kernel(x, out):
    total = x[0].astype(jnp.float32)
    for z in range(1, x.shape[0]):
        total = total + x[z].astype(jnp.float32)
    out[...] = total.astype(jnp.bfloat16)


def fourth_sum_all(terms):
    return pl.pallas_call(
        fourth_all_kernel,
        out_shape=jax.ShapeDtypeStruct(terms.shape[1:], jnp.bfloat16),
        grid=(1,),
        in_specs=[whole_block(terms.shape)],
        out_specs=whole_block(terms.shape[1:]),
        cost_estimate=cost(10),
        name="fourth_sum_all",
    )(terms)


def fourth_kernel(*refs):
    total = refs[0][...].astype(jnp.float32)
    for r in refs[1:-1]:
        total = total + r[...].astype(jnp.float32)
    refs[-1][...] = total.astype(jnp.bfloat16)


def fourth_sum(terms):
    shape = terms[0].shape
    return pl.pallas_call(
        fourth_kernel,
        out_shape=jax.ShapeDtypeStruct(shape, jnp.bfloat16),
        grid=(1,),
        in_specs=[whole_block(shape)] * len(terms),
        out_specs=whole_block(shape),
        cost_estimate=cost(10),
        name="fourth_sum",
    )(*terms)


def place_kernel(streams, plan, ids_ref, scale_ref, *refs):
    blocks, outs = refs[: 4 * streams], refs[4 * streams :]
    x, y = ids_ref[2], ids_ref[3]
    scale = scale_ref[0:1, 0:1]
    for stream, row, rows, lane, lanes, out, row_of, lane_of in plan:
        for d in range(4):
            own_x, own_y = x ^ (d & 1), y ^ (d >> 1)
            for half in range(2):
                k = own_x * 2 + own_y if half == 0 else 4 + own_y * 2 + own_x
                tile = blocks[4 * stream + d][half, row : row + rows, lane : lane + lanes]
                outs[out][row_of(k), lane_of(k)] = tile.astype(jnp.float32) * scale


def place_blocks(ids, scale, streams, plan, shapes):
    blocks = [b for s in streams for b in s]
    outs = [jax.ShapeDtypeStruct(s, jnp.float32) for s in shapes]
    return pl.pallas_call(
        functools.partial(place_kernel, len(streams), plan),
        out_shape=outs,
        grid_spec=pltpu.PrefetchScalarGridSpec(
            num_scalar_prefetch=1,
            grid=(1,),
            in_specs=[whole_block(a.shape) for a in (scale, *blocks)],
            out_specs=[whole_block(o.shape) for o in outs],
        ),
        compiler_params=pltpu.CompilerParams(vmem_limit_bytes=32 << 20),
        cost_estimate=cost(20),
        name="place_blocks",
    )(ids, scale, *blocks)


def span(start, size):
    return pl.ds(pl.multiple_of(start, size), size)


def ada_kernel(groups, pad_u, numerator, time_ref, *refs):
    f32 = jnp.float32
    parts, (weight_ref, vector_ref, scale_ref) = refs[:groups], refs[groups:]
    table = pl.program_id(0)
    base = 6 * pad_u
    count = parts[0][base + 12 : base + 13, 0:1] + parts[0][base + 13 : base + 14, 0:1]
    for p in parts[1:]:
        count = count + p[base + 12 : base + 13, 0:1] + p[base + 13 : base + 14, 0:1]
    scale = numerator / count
    rows = jnp.concatenate([p[pl.ds(pl.multiple_of(table * pad_u, 8), pad_u), :] for p in parts], axis=0) * scale
    vector_ref[pl.ds(table, 1), :] = jnp.sum(rows, axis=0, keepdims=True)
    operand = jnp.concatenate(list(split3(rows)), axis=0)
    weight_ref[...] = dot(time_ref[...], operand)

    @pl.when(table == 0)
    def _():
        total = parts[0][base : base + 16, :]
        for p in parts[1:]:
            total = total + p[base : base + 16, :]
        vector_ref[8:24, :] = total * scale
        scale_ref[...] = jnp.broadcast_to(scale, scale_ref.shape)


def ada_block(time3, parts, utts, numerator):
    pad_u = table_rows(utts)
    width = parts[0].shape[1]
    own = time3.shape[0]
    f32 = jnp.float32
    return pl.pallas_call(
        functools.partial(ada_kernel, len(parts), pad_u, numerator),
        out_shape=[
            jax.ShapeDtypeStruct((own, 6 * width), f32),
            jax.ShapeDtypeStruct((24, width), f32),
            jax.ShapeDtypeStruct((8, 128), f32),
        ],
        grid=(6,),
        in_specs=[whole_block(time3.shape)] + [whole_block(p.shape) for p in parts],
        out_specs=[
            pl.BlockSpec((own, width), lambda j: (0, j)),
            whole_block((24, width)),
            whole_block((8, 128)),
        ],
        cost_estimate=cost(50),
        name="ada_block",
    )(time3, *parts)


def sum_exchange(value, axis, bit):
    ways = lax.axis_size(axis)
    return lax.ppermute(value, axis, [(i, i ^ bit) for i in range(ways)])


def axis_bits(ways):
    return [1 << i for i in range(ways.bit_length() - 1)]


def reduce_stages(ids, blocks, splits, whole_z):
    batch_ways = lax.axis_size("batch")
    x_bit, y_bit = 1, 1 << ((batch_ways.bit_length() - 1) // 2)
    pairs = []
    for keep, send in blocks:
        shape = (2, 2, 2) + keep.shape[1:]
        pairs.append((keep.reshape(shape), sum_exchange(send, "seq", 1).reshape(shape)))
    *sends, keep_a, keep_b = first_sum(ids, pairs, splits)
    sends = follow(sends, (yield sends))
    got, token = [[], []], None
    for i in range(len(splits)):
        pieces = follow([sends[i], sends[len(splits) + i]], token)
        for side, bit in enumerate((x_bit, y_bit)):
            got[side].append(sum_exchange(pieces[side], "batch", bit))
        token = yield [got[0][i], got[1][i]]
    got_a, got_b = (follow(g, token) for g in got)
    send_a, send_b, keep_a, keep_b = second_sum(ids, keep_a, got_a, keep_b, got_b)
    send_a, send_b = follow([send_a, send_b], (yield [send_a, send_b]))
    got = [sum_exchange(send_a, "batch", y_bit), sum_exchange(send_b, "batch", x_bit)]
    got_a, got_b = follow(got, (yield got))
    if whole_z:
        ways = lax.axis_size("seq")
        groups = [list(range(c, ways, 2)) for c in range(2)]
        away = [third_sum_all(ids, keep_a, got_a, keep_b, got_b)]
        away = follow(away, (yield away))
        got = [lax.all_to_all(away[0], "seq", 0, 0, axis_index_groups=groups, tiled=True)]
        got = follow(got, (yield got))
        block = fourth_sum_all(got[0])
    else:
        own, *away = third_sum(ids, keep_a, got_a, keep_b, got_b)
        away = follow(away, (yield away))
        got = [sum_exchange(a, "seq", 2 * (j + 1)) for j, a in enumerate(away)]
        got = follow(got, (yield got))
        block = fourth_sum([own] + got)
    for bit in axis_bits(batch_ways):
        if bit not in (x_bit, y_bit):
            block = add_bf16(block, sum_exchange(block, "batch", bit))
    (block,) = follow([block], (yield [block]))
    yield [block] + [sum_exchange(block, "batch", bit) for bit in (x_bit, y_bit, x_bit | y_bit)]


def advance(stages, steps, token=None):
    value = next(stages) if token is None else stages.send(token)
    for _ in range(steps - 1):
        value = next(stages)
    return value


def last_stage(stages, token=None):
    value = stages.send(token)
    for value in stages:
        pass
    return value


def follow(values, token):
    return values if token is None else [after(v, token) for v in values]


def after(value, *others):
    return lax.optimization_barrier((value,) + others)[0]


def gather_groups(value):
    return [value] + [sum_exchange(value, "batch", i) for i in range(1, lax.axis_size("batch"))]


def sum_z(value, token):
    away = value.astype(jnp.bfloat16)
    for j in range(1, lax.axis_size("seq") // 2):
        value = value + after(sum_exchange(away, "seq", 2 * j), token).astype(jnp.float32)
    return value


def shards(
    tokens_in,
    skip_in,
    condition,
    cotangent,
    time_embed,
    lengths,
    key_mask,
    drop_mask,
    loss_mask,
    w_skip,
    b_skip,
    w_ada,
    b_ada,
    w_qkv,
    b_qkv,
    w_out,
    b_out,
    w_up,
    b_up,
    w_down,
    b_down,
):
    f32, bf16 = jnp.float32, jnp.bfloat16
    seq_ways, batch_ways = lax.axis_size("seq"), lax.axis_size("batch")
    seq_rank = lax.axis_index("seq")
    frames, width = tokens_in.shape[1:]
    group_frames = frames * seq_ways
    heads_local = HEADS // seq_ways
    utts = lengths.shape[1]
    lengths_row, drop = lengths[0], drop_mask[0]
    batch_rank = lax.axis_index("batch")
    side = 1 << ((batch_ways.bit_length() - 1) // 2)
    ids = [lax.rem(seq_rank, 2), seq_rank, lax.rem(batch_rank, 2), lax.rem(batch_rank // side, 2), seq_rank // 2]
    ids = jnp.stack(ids).astype(jnp.int32)
    ok = key_mask.reshape(seq_ways, 1, frames)
    exchange = functools.partial(lax.all_to_all, axis_name="seq", split_axis=0, concat_axis=0, tiled=True)

    time_act = jax.nn.silu(time_embed[0]).astype(bf16)
    time_rows = jnp.pad(time_act, ((0, 16 - utts), (0, 0)))

    def modulation(first, last):
        return jnp.dot(time_rows, w_ada[:, first:last], preferred_element_type=f32) + b_ada[
            first:last
        ].astype(f32)

    mods_a = modulation(0, 2 * width)
    hidden, joinedT, naT, na = head_block(
        lengths_row, ids, drop, tokens_in[0], skip_in[0], condition[0], mods_a, w_skip, b_skip[None]
    )
    mods_rest = modulation(2 * width, 6 * width)
    received = []
    for c in range(heads_local):
        packed = qkv_block(lengths_row, ids, drop, na, w_qkv, b_qkv[None], c, seq_ways)
        if c == 0:
            na = after(na, mods_rest)
        received.append(exchange(packed))

    own = width // seq_ways
    pad_u = table_rows(utts)
    time_own = lax.dynamic_slice_in_dim(jnp.concatenate(gather_groups(time_rows[:pad_u])), seq_rank * own, own, axis=1)
    time3 = jnp.tile(time_own.T, (1, 3))

    received[0] = after(received[0], mods_rest)
    head_out, log_totals, returned = [], [], []
    for c in range(heads_local):
        out, log_total = attend(lengths_row, received[c], ok)
        head_out.append(out)
        log_totals.append(log_total)
        returned.append(exchange(after(out, *returned)))
        if c < heads_local - 1:
            received[c + 1] = after(received[c + 1], out, time3)
    mid = mid_block(
        lengths_row,
        ids,
        returned,
        hidden,
        mods_rest,
        cotangent[0],
        loss_mask,
        w_out,
        b_out[None],
        w_up,
        b_up[None],
        w_down,
        b_down[None],
        PARTS,
    )
    output, after_grad, mid_small, grad_att, keep, send = mid
    grad_heads = exchange(grad_att)
    front = keep.shape[2] * 4 // 9 // 16 * 16
    feed = reduce_stages(ids, [(keep, send)], [front, keep.shape[2] - front], True)

    ahead = next(feed)
    grad_local = []
    for c in range(heads_local):
        operand = after(grad_heads, *ahead)
        moving = feed.send(grad if c else None) if c < 2 else []
        grad = attend_back(lengths_row, received[c], ok, head_out[c], operand, log_totals[c], c)
        grad_local.append(exchange(after(grad, *moving)))
        ahead = [grad]
    if heads_local == 1:
        next(feed)
    ahead = ahead + advance(feed, 1, ahead[0])
    before, biases = (), []
    for c in range(heads_local):
        acc, bias, keep, send = back_block(
            lengths_row, ids, drop, after(grad_local[c], *ahead), naT, w_qkv, before, c, PARTS
        )
        before = (acc, keep, send)
        biases.append(bias)
        ahead = next(feed) and advance(feed, 1, acc) if c == 0 else []
    gh, small = norm_block(lengths_row, ids, acc, hidden, after_grad, mods_a, loss_mask, mid_small, biases)
    small = small + sum_exchange(small, "seq", 1)
    skip_keep, skip_send = skip_block(ids, joinedT, gh, seq_ways, PARTS)
    blocks = [(skip_keep, skip_send), (keep, send)]
    rest = reduce_stages(ids, blocks, [5 * own // PARTS], False)
    small = sum_z(small, next(rest)[0])
    moving = feed.send(small)
    advance(rest, 3)
    groups = gather_groups(after(small, *rest.send(moving[0])))
    numerator = float(group_frames * batch_ways)
    grad_w_ada, vectors, scale = ada_block(time3, groups, utts, numerator)
    grad_tokens, grad_skip = joined_block(gh, w_skip, scale)
    next(feed)
    feed = last_stage(feed, groups[-1])
    next(rest)
    rest.send(grad_tokens)
    rest = last_stage(rest)

    ff = w_up.shape[1]
    chunks = ff // width
    up_part = chunks * own // PARTS
    down_part = ff // seq_ways // PARTS
    out_part = own // PARTS
    per_chunk = own // up_part
    whole_lanes = lambda k: span(0, width)
    grad_w_up, grad_w_down, grad_w_out = place_blocks(
        ids,
        scale,
        [feed],
        [
            (
                *(0, 0, up_part, 0, width, 0),
                lambda k: span(lax.rem(k, per_chunk) * up_part, up_part),
                lambda k: span(k // per_chunk * width, width),
            ),
            (0, up_part, down_part, 0, width, 1, lambda k: span(k * down_part, down_part), whole_lanes),
            (0, up_part + down_part, out_part, 0, width, 2, lambda k: span(k * out_part, out_part), whole_lanes),
        ],
        [(own, ff), (ff // seq_ways, width), (own, width)],
    )
    skip_part = 2 * own // PARTS
    grad_w_skip, grad_w_qkv = place_blocks(
        ids,
        after(scale, grad_w_down),
        [rest],
        [(0, 0, skip_part, 0, width, 0, lambda k: span(k * skip_part, skip_part), whole_lanes)]
        + [
            (
                *(0, skip_part + p * out_part, out_part, 0, width, 1),
                lambda k: span(k * out_part, out_part),
                lambda k, at=p * width: span(at, width),
            )
            for p in range(3)
        ],
        [(2 * own, width), (own, 3 * width)],
    )

    def own_slice(vector):
        vector = vector.reshape(-1)
        size = vector.shape[0] // seq_ways
        return lax.dynamic_slice_in_dim(vector, seq_rank * size, size)

    grad_b_ada = own_slice(vectors[:6])
    grad_b_qkv = own_slice(vectors[8:11])
    grad_b_skip = own_slice(vectors[11])
    grad_b_out = own_slice(vectors[12])
    grad_b_down = own_slice(vectors[13])
    grad_b_up = own_slice(vectors[14 : 14 + chunks])
    return (
        output[None],
        grad_tokens[None],
        grad_skip[None],
        grad_w_skip,
        grad_b_skip,
        grad_w_ada,
        grad_b_ada,
        grad_w_qkv,
        grad_b_qkv,
        grad_w_out,
        grad_b_out,
        grad_w_up,
        grad_b_up,
        grad_w_down,
        grad_b_down,
    )


def solution(mesh):
    in_specs = (
        P("batch", "seq", None),
        P("batch", "seq", None),
        P("batch", "seq", None),
        P("batch", "seq", None),
        P("batch", None, None),
        P("batch", None),
        P("batch", None),
        P("batch", None),
        P("batch", "seq"),
        P(),
        P(),
        P(),
        P(),
        P(),
        P(),
        P(),
        P(),
        P(),
        P(),
        P(),
        P(),
    )
    out_specs = (
        P("batch", "seq", None),
        P("batch", "seq", None),
        P("batch", "seq", None),
        P("seq", None),
        P("seq"),
        P("seq", None),
        P("seq"),
        P("seq", None),
        P("seq"),
        P("seq", None),
        P("seq"),
        P("seq", None),
        P("seq"),
        P("seq", None),
        P("seq"),
    )
    return jax.shard_map(shards, mesh=mesh, in_specs=in_specs, out_specs=out_specs, check_vma=False)
```

```python
import functools

import jax
import jax.numpy as jnp
from jax import lax
from jax.experimental import pallas as pl
from jax.experimental.pallas import tpu as pltpu
from jax.sharding import PartitionSpec as P

HEADS = 16
HEAD_DIM = 64
PARTS = 8
BIG = 1e30
DH = 64
BQ = 512
BK = 512


def cost(weight):
    return pl.CostEstimate(flops=weight * 100000000, bytes_accessed=weight * 100000, transcendentals=0)


def onehot_rows(lengths_ref, utts, rows, base, width):
    row = lax.broadcasted_iota(jnp.int32, (rows, width), 0)
    col = base + lax.broadcasted_iota(jnp.int32, (rows, width), 1)
    start = jnp.int32(0)
    hot = jnp.zeros((rows, width), jnp.float32)
    for u in range(utts):
        end = start + lengths_ref[u]
        hot = jnp.where((row == u) & (col >= start) & (col < end), 1.0, hot)
        start = end
    return hot


def key_range(lengths_ref, utts, first, last):
    start = jnp.int32(0)
    low, high = jnp.int32(0), jnp.int32(0)
    for u in range(utts):
        end = start + lengths_ref[u]
        low = jnp.where((start <= first) & (first < end), start, low)
        high = jnp.where((start <= last) & (last < end), end, high)
        start = end
    return low // BK, (high + BK - 1) // BK


def aug_rows(utts):
    return -(-utts // 16) * 16


def split3(row):
    a = row.astype(jnp.bfloat16)
    rest = row - a.astype(jnp.float32)
    b = rest.astype(jnp.bfloat16)
    c = (rest - b.astype(jnp.float32)).astype(jnp.bfloat16)
    return a, b, c


def pad_rows(parts, total):
    have = sum(p.shape[0] for p in parts)
    if have < total:
        parts = parts + [jnp.zeros((total - have, parts[0].shape[1]), parts[0].dtype)]
    return jnp.concatenate(parts, axis=0)


def rows16(rows, width):
    idx = lax.broadcasted_iota(jnp.int32, (16, width), 0)
    out = jnp.zeros((16, width), jnp.float32)
    for i, r in enumerate(rows):
        out = jnp.where(idx == i, r, out)
    return out.astype(jnp.bfloat16)


def fwd_kernel(utts, lengths_ref, qkv_ref, ok_ref, out_ref, lse_ref, kaug, vaug):
    sources, _, frames = qkv_ref.shape
    per = frames // BQ
    pad_u = aug_rows(utts)
    step = pl.program_id(0)

    @pl.when(step == 0)
    def _():
        def build(s, c):
            hot = onehot_rows(lengths_ref, utts, pad_u, s * frames, frames)
            ok = ok_ref[s].astype(jnp.float32)
            block = qkv_ref[s]
            one = jnp.ones((1, frames), jnp.float32)
            kT = pad_rows(
                [block[DH : 2 * DH], (1.0 - hot).astype(jnp.bfloat16), rows16([1.0 - ok], frames)], 128
            )
            kaug[pl.ds(pl.multiple_of(s * frames, frames), frames), :] = kT.T
            vT = jnp.concatenate([block[2 * DH :], rows16([one], frames)], axis=0)
            for t in range(frames // BK):
                vaug[s * (frames // BK) + t] = vT[:, t * BK : (t + 1) * BK]
            return c

        lax.fori_loop(0, sources, build, 0)

    block = qkv_ref[step]
    hot_q = onehot_rows(lengths_ref, utts, pad_u, step * frames, frames)
    qT = (block[:DH].astype(jnp.float32) * 0.125)
    one = jnp.ones((1, frames), jnp.float32)
    qaug = pad_rows(
        [qT.astype(jnp.bfloat16), (hot_q * -BIG).astype(jnp.bfloat16), rows16([one * -BIG], frames)], 128
    )
    kT = block[DH : 2 * DH].astype(jnp.float32)
    vT = block[2 * DH :].astype(jnp.float32)
    ok = ok_ref[step] > 0
    s_self = jnp.sum(qT * kT, axis=0, keepdims=True)
    m0 = jnp.where(ok, -3e38, s_self)
    acc0 = jnp.concatenate([jnp.where(ok, 0.0, vT), jnp.where(ok, 0.0, jnp.ones((16, frames), jnp.float32))], axis=0)
    for t in range(per):
        cols = slice(t * BQ, (t + 1) * BQ)
        low, high = key_range(lengths_ref, utts, step * frames + t * BQ, step * frames + (t + 1) * BQ - 1)
        q_b = qaug[:, cols]

        def body(j, carry):
            m, acc = carry
            s = jnp.dot(kaug[pl.ds(pl.multiple_of(j * BK, BK), BK), :], q_b, preferred_element_type=jnp.float32)
            m_new = jnp.maximum(m, jnp.max(s, axis=0, keepdims=True))
            p = jnp.exp(s - m_new).astype(jnp.bfloat16)
            alpha = jnp.exp(m - m_new)
            acc = acc * alpha + jnp.dot(vaug[j], p, preferred_element_type=jnp.float32)
            return m_new, acc

        m, acc = lax.fori_loop(low, high, body, (m0[:, cols], acc0[:, cols]))
        total = acc[DH : DH + 1]
        out_ref[0, :, cols] = (acc[:DH] / total).astype(jnp.bfloat16)
        lse_ref[0, :, cols] = m + jnp.log(total)


def attend(lengths, qkv, ok):
    sources, _, frames = qkv.shape
    total = sources * frames
    utts = lengths.shape[0]
    whole = lambda shape: pl.BlockSpec(shape, lambda i, *_: (0,) * len(shape))
    return pl.pallas_call(
        functools.partial(fwd_kernel, utts),
        out_shape=(
            jax.ShapeDtypeStruct((sources, DH, frames), jnp.bfloat16),
            jax.ShapeDtypeStruct((sources, 1, frames), jnp.float32),
        ),
        grid_spec=pltpu.PrefetchScalarGridSpec(
            num_scalar_prefetch=1,
            grid=(sources,),
            in_specs=[whole(qkv.shape), whole(ok.shape)],
            out_specs=(
                pl.BlockSpec((1, DH, frames), lambda i, *_: (i, 0, 0)),
                pl.BlockSpec((1, 1, frames), lambda i, *_: (i, 0, 0)),
            ),
            scratch_shapes=[
                pltpu.VMEM((total, 128), jnp.bfloat16),
                pltpu.VMEM((total // BK, DH + 16, BK), jnp.bfloat16),
            ],
        ),
        cost_estimate=cost(250),
        name="attend",
    )(lengths, qkv, ok)


def bwd_kernel(utts, chunk, lengths_ref, qkv_ref, ok_ref, o_ref, do_ref, lse_ref, out_ref, kaug, vnat, kT_s, dk, dv):
    sources, _, frames = qkv_ref.shape
    per = frames // BK
    pad_u = aug_rows(utts)
    step = pl.program_id(0)
    f32 = jnp.float32

    @pl.when(step == 0)
    def _():
        def build(s, c):
            hot = onehot_rows(lengths_ref, utts, pad_u, s * frames, frames)
            ok = ok_ref[s]
            block = qkv_ref[s]
            one = jnp.ones((1, frames), f32)
            kT = block[DH : 2 * DH]
            vT = block[2 * DH :]
            kA = pad_rows(
                [kT, (1.0 - hot).astype(jnp.bfloat16), rows16([1.0 - ok.astype(f32), one, one, one], frames)], 128
            )
            rows = pl.ds(pl.multiple_of(s * frames, frames), frames)
            kaug[rows, :] = kA.T
            vnat[rows, :] = pad_rows([vT, rows16([one, one, one], frames)], 128).T
            qT = block[:DH].astype(f32) * 0.125
            do = do_ref[s, chunk * DH : (chunk + 1) * DH, :].astype(f32)
            s_self = jnp.sum(qT * kT.astype(f32), axis=0, keepdims=True)
            delta = jnp.sum(do * o_ref[s].astype(f32), axis=0, keepdims=True)
            p_self = jnp.where(ok > 0, 0.0, jnp.exp(s_self - lse_ref[s]))
            ds_self = p_self * (jnp.sum(do * vT.astype(f32), axis=0, keepdims=True) - delta)
            dk0 = ds_self * qT
            dv0 = p_self * do
            for t in range(per):
                cols = slice(t * BK, (t + 1) * BK)
                kT_s[s * per + t] = kT[:, cols]
                dk[s * per + t] = dk0[:, cols]
                dv[s * per + t] = dv0[:, cols]
            return c

        lax.fori_loop(0, sources, build, 0)

    block = qkv_ref[step]
    one = jnp.ones((1, frames), f32)
    hot_q = onehot_rows(lengths_ref, utts, pad_u, step * frames, frames)
    qT = block[:DH].astype(f32) * 0.125
    qTb = qT.astype(jnp.bfloat16)
    kT = block[DH : 2 * DH].astype(f32)
    vT = block[2 * DH :].astype(f32)
    ok = ok_ref[step]
    dob = do_ref[step, chunk * DH : (chunk + 1) * DH, :]
    do = dob.astype(f32)
    lse = lse_ref[step]
    delta = jnp.sum(do * o_ref[step].astype(f32), axis=0, keepdims=True)
    l3 = [-r.astype(f32) for r in split3(lse)]
    d3 = [-r.astype(f32) for r in split3(delta)]
    qaug = pad_rows([qTb, (hot_q * -BIG).astype(jnp.bfloat16), rows16([one * -BIG] + l3, frames)], 128)
    doaug = pad_rows([dob, rows16(d3, frames)], 128)
    s_self = jnp.sum(qT * kT, axis=0, keepdims=True)
    p_self = jnp.where(ok > 0, 0.0, jnp.exp(s_self - lse))
    ds_self = p_self * (jnp.sum(do * vT, axis=0, keepdims=True) - delta)
    dq0 = ds_self * kT
    nt = (((1,), (1,)), ((), ()))
    for t in range(frames // BQ):
        cols = slice(t * BQ, (t + 1) * BQ)
        low, high = key_range(lengths_ref, utts, step * frames + t * BQ, step * frames + (t + 1) * BQ - 1)
        q_a = qaug[:, cols]
        q_b = qTb[:, cols]
        do_a = doaug[:, cols]
        do_b = dob[:, cols]

        def body(j, dq):
            rows = pl.ds(pl.multiple_of(j * BK, BK), BK)
            s = jnp.dot(kaug[rows, :], q_a, preferred_element_type=f32)
            dp = jnp.dot(vnat[rows, :], do_a, preferred_element_type=f32)
            p = jnp.exp(s)
            ds = (p * dp).astype(jnp.bfloat16)
            dv[j] += lax.dot_general(do_b, p.astype(jnp.bfloat16), nt, preferred_element_type=f32)
            dk[j] += lax.dot_general(q_b, ds, nt, preferred_element_type=f32)
            return dq + jnp.dot(kT_s[j], ds, preferred_element_type=f32)

        dq = lax.fori_loop(low, high, body, dq0[:, cols])
        out_ref[step, :DH, cols] = (dq * 0.125).astype(jnp.bfloat16)

    @pl.when(step == sources - 1)
    def _():
        def finish(s, c):
            for t in range(per):
                cols = slice(t * BK, (t + 1) * BK)
                out_ref[s, DH : 2 * DH, cols] = dk[s * per + t].astype(jnp.bfloat16)
                out_ref[s, 2 * DH :, cols] = dv[s * per + t].astype(jnp.bfloat16)
            return c

        lax.fori_loop(0, sources, finish, 0)


def attend_back(lengths, qkv, ok, out, grad, lse, chunk):
    sources, _, frames = qkv.shape
    total = sources * frames
    utts = lengths.shape[0]
    whole = lambda shape: pl.BlockSpec(shape, lambda i, *_: (0,) * len(shape))
    return pl.pallas_call(
        functools.partial(bwd_kernel, utts, chunk),
        out_shape=jax.ShapeDtypeStruct(qkv.shape, jnp.bfloat16),
        grid_spec=pltpu.PrefetchScalarGridSpec(
            num_scalar_prefetch=1,
            grid=(sources,),
            in_specs=[whole(a.shape) for a in (qkv, ok, out, grad, lse)],
            out_specs=whole(qkv.shape),
            scratch_shapes=[
                pltpu.VMEM((total, 128), jnp.bfloat16),
                pltpu.VMEM((total, 128), jnp.bfloat16),
                pltpu.VMEM((total // BK, DH, BK), jnp.bfloat16),
                pltpu.VMEM((total // BK, DH, BK), jnp.float32),
                pltpu.VMEM((total // BK, DH, BK), jnp.float32),
            ],
        ),
        cost_estimate=cost(320),
        name="attend_back",
    )(lengths, qkv, ok, out, grad, lse)


FF_TILE = 512
EPS = 1e-06


def dot(left, right):
    return jnp.dot(left, right, preferred_element_type=jnp.float32)


def dot_nt(left, right):
    return lax.dot_general(left, right, (((1,), (1,)), ((), ())), preferred_element_type=jnp.float32)


def norm_stats(x):
    mean = jnp.mean(x, axis=1, keepdims=True)
    centred = x - mean
    rstd = lax.rsqrt(jnp.mean(centred * centred, axis=1, keepdims=True) + EPS)
    return centred * rstd, rstd


def norm_back(grad, normed, rstd):
    first = jnp.mean(grad, axis=1, keepdims=True)
    second = jnp.mean(grad * normed, axis=1, keepdims=True)
    return rstd * (grad - first - normed * second)


def mods_operand(mods_ref):
    rows = mods_ref[...]
    return pad_rows(list(split3(rows)), 128)


def table_rows(utts):
    return -(-utts // 8) * 8


def sum_rows(hot, utts_pad, frames):
    idx = lax.broadcasted_iota(jnp.int32, (16, frames), 0)
    ones = jnp.where(idx == 0, 1.0, 0.0).astype(jnp.bfloat16)
    return jnp.concatenate([hot.astype(jnp.bfloat16), ones], axis=0)


def mid_kernel(
    dims,
    lengths_ref,
    ids_ref,
    *refs,
):
    seq_ways, heads_local, utts, ff = dims
    att_refs = refs[:heads_local]
    (
        hidden_ref,
        mods_ref,
        cot_ref,
        loss_ref,
        w_out_ref,
        b_out_ref,
        w_up_ref,
        b_up_ref,
        w_down_ref,
        b_down_ref,
    ) = refs[heads_local : heads_local + 10]
    outs = refs[heads_local + 10 :]
    output_ref, after_grad_ref, small_ref, gatt_ref = outs[:4]
    refs_out = outs[4:6]
    (
        attT,
        attn_proj,
        after,
        nf,
        nfT,
        gff,
        ff_acc,
        gnf_acc,
        sums,
        cols,
        madd,
        grads,
        sems,
    ) = outs[6:]
    f32, bf16 = jnp.float32, jnp.bfloat16
    step = pl.program_id(0)
    steps = pl.num_programs(0)
    core = ids_ref[0]
    rank = ids_ref[1]
    frames, width = hidden_ref.shape
    up_rows = width // seq_ways
    down_rows = FF_TILE
    z_ways = seq_ways // 2
    parts = grads.shape[1]
    pad_u = table_rows(utts)
    ff_total = ff
    up_part = ff_total // width * up_rows // parts
    down_block = ff_total // seq_ways
    down_part = down_block // parts
    out_part = up_rows // parts

    def mod(index):
        return dot(cols[...], madd[:, index * width : (index + 1) * width])

    def grad_out():
        loss = cols[:, 48:49].astype(f32)
        return cot_ref[...].astype(f32) * loss

    @pl.when(step == 0)
    def _():
        hot = onehot_rows(lengths_ref, utts, 16, rank * frames, frames)
        hotb = hot.astype(bf16)
        idx = lax.broadcasted_iota(jnp.int32, (16, frames), 0)
        loss = jnp.where(idx == 0, loss_ref[...].astype(f32), 0.0).astype(bf16)
        cols[...] = pad_rows([hotb, hotb, hotb, loss], 128).T
        sums[...] = sum_rows(hot, 16, frames)
        madd[...] = mods_operand(mods_ref)
        for c in range(heads_local):
            for s in range(seq_ways):
                attT[(c * seq_ways + s) * DH : (c * seq_ways + s + 1) * DH, :] = att_refs[c][s]
        proj = dot(attT[...].T, w_out_ref[...]) + b_out_ref[...].astype(f32)
        attn_proj[...] = proj
        mixed = hidden_ref[...] + mod(0) * proj
        after[...] = mixed
        normed, _ = norm_stats(mixed)
        value = (normed * (1.0 + mod(2)) + mod(1)).astype(bf16)
        nf[...] = value
        nfT[...] = value.T
        gff[...] = (grad_out() * mod(3)).astype(bf16)
        small_ref[4 * pad_u :, :] = jnp.zeros((8, width), f32)

    up = dot(nf[...], w_up_ref[...]) + b_up_ref[...].astype(f32)
    inner = 0.7978845608028654 * (up + 0.044715 * (up * up * up))
    tanh = jnp.tanh(inner)
    cdf = 0.5 * (1.0 + tanh)
    act = (up * cdf).astype(bf16)
    slope = cdf + 0.5 * up * (1.0 - tanh * tanh) * (
        0.7978845608028654 * (1.0 + (3 * 0.044715) * (up * up))
    )
    ff_part = dot(act, w_down_ref[...])
    gup = (dot_nt(gff[...], w_down_ref[...]) * slope).astype(bf16)
    gnf_part = dot_nt(gup, w_up_ref[...])

    @pl.when(step == 0)
    def _():
        ff_acc[...] = ff_part
        gnf_acc[...] = gnf_part

    @pl.when(step > 0)
    def _():
        ff_acc[...] += ff_part
        gnf_acc[...] += gnf_part

    halves = width // FF_TILE
    chunk = step // halves
    half = step % halves
    col = pl.ds(pl.multiple_of(half * FF_TILE, FF_TILE), FF_TILE)
    per_chunk = up_rows // up_part
    small_ref[pl.ds(4 * pad_u + 2 + chunk, 1), col] = dot(sums[16:32, :], gup)[:1]
    grad_w_up = dot(nfT[...], gup).astype(bf16)
    for s in range(seq_ways):
        side = jnp.where(core == s % 2, 0, 1)
        for h in range(per_chunk):
            lo = s * up_rows + h * up_part
            grads[side, chunk * per_chunk + h, s // 2, 0:up_part, col] = grad_w_up[lo : lo + up_part]
    grad_w_down = dot(act.T, gff[...]).astype(bf16)
    blocks = FF_TILE // down_block
    copies = []
    for b in range(blocks):
        s = step * blocks + b
        side = jnp.where(core == s % 2, 0, 1)
        for k in range(parts):
            lo = b * down_block + k * down_part
            grads[side, k, s // 2, up_part : up_part + down_part, :] = grad_w_down[lo : lo + down_part]

    def region_copy(side, where, index):
        return pltpu.make_async_copy(
            grads.at[side].at[where], refs_out[side].at[where], sems.at[side, index]
        )

    def up_copy(side, j):
        where = (
            pl.ds((j // halves) * per_chunk, per_chunk),
            slice(None),
            pl.ds(0, up_part),
            pl.ds(pl.multiple_of((j % halves) * FF_TILE, FF_TILE), FF_TILE),
        )
        return region_copy(side, where, j)

    def down_copy(side, z, index):
        return region_copy(side, (slice(None), pl.ds(z, 1), pl.ds(up_part, down_part)), index)

    def out_copy(side):
        where = (slice(None), slice(None), pl.ds(up_part + down_part, out_part))
        return region_copy(side, where, ff_total // FF_TILE + z_ways)

    base = ff_total // FF_TILE
    for side in range(2):
        up_copy(side, step).start()
    for b in range(blocks):
        s = step * blocks + b
        for side in range(2):

            @pl.when(lax.rem(s + core, 2) == side)
            def _():
                down_copy(side, s // 2, base + s // 2).start()

    @pl.when(step == steps - 1)
    def _():
        ff_out = ff_acc[...] + b_down_ref[...].astype(f32)
        mixed = after[...]
        go = grad_out()
        output_ref[...] = (mixed + mod(3) * ff_out).astype(bf16)
        rows = sums[...]
        small_ref[3 * pad_u : 4 * pad_u, :] = dot(rows, (go * ff_out).astype(bf16))[:pad_u]
        normed, rstd = norm_stats(mixed)
        gnf = gnf_acc[...]
        small_ref[pad_u : 2 * pad_u, :] = dot(rows, gnf.astype(bf16))[:pad_u]
        small_ref[2 * pad_u : 3 * pad_u, :] = dot(rows, (gnf * normed).astype(bf16))[:pad_u]
        g_after = go + norm_back(gnf * (1.0 + mod(2)), normed, rstd)
        after_grad_ref[...] = g_after
        small_ref[0:pad_u, :] = dot(rows, (g_after * attn_proj[...]).astype(bf16))[:pad_u]
        gattn = (g_after * mod(0)).astype(bf16)
        small_ref[4 * pad_u : 4 * pad_u + 1, :] = dot(rows, gattn)[16:17]
        small_ref[4 * pad_u + 1 : 4 * pad_u + 2, :] = dot(rows, gff[...])[16:17]
        gattT = dot_nt(w_out_ref[...], gattn).astype(bf16)
        for c in range(heads_local):
            for s in range(seq_ways):
                lo = (c * seq_ways + s) * DH
                gatt_ref[s, c * DH : (c + 1) * DH, :] = gattT[lo : lo + DH]
        grad_w_out = dot(attT[...], gattn).astype(bf16)
        for s in range(seq_ways):
            side = jnp.where(core == s % 2, 0, 1)
            for k in range(parts):
                lo = s * up_rows + k * out_part
                grads[side, k, s // 2, up_part + down_part : up_part + down_part + out_part, :] = grad_w_out[
                    lo : lo + out_part
                ]
        for side in range(2):
            out_copy(side).start()
        for side in range(2):
            for j in range(ff_total // FF_TILE):
                up_copy(side, j).wait()
            for z in range(z_ways):
                down_copy(side, z, base + z).wait()
            out_copy(side).wait()


def mid_block(
    lengths, ids, att, hidden, mods, cot, loss, w_out, b_out, w_up, b_up, w_down, b_down, parts
):
    frames, width = hidden.shape
    heads_local = len(att)
    seq_ways = att[0].shape[0]
    ff = w_up.shape[1]
    up_rows = width // seq_ways
    rows = (ff // width * up_rows + ff // seq_ways + up_rows) // parts
    utts = lengths.shape[0]
    f32, bf16 = jnp.float32, jnp.bfloat16
    steps = ff // FF_TILE

    def whole(shape):
        return pl.BlockSpec(shape, lambda j, *_: (0,) * len(shape), pipeline_mode=pl.Buffered(1))

    hbm = pl.BlockSpec(memory_space=pl.ANY)
    gshape = (parts, seq_ways // 2, rows, width)
    out_shape = [
        jax.ShapeDtypeStruct((frames, width), bf16),
        jax.ShapeDtypeStruct((frames, width), f32),
        jax.ShapeDtypeStruct((4 * table_rows(utts) + 8, width), f32),
    ]
    out_shape += [jax.ShapeDtypeStruct((seq_ways, heads_local * DH, frames), bf16)]
    out_specs = [whole(o.shape) for o in out_shape] + [hbm] * 2
    out_shape += [jax.ShapeDtypeStruct(gshape, bf16)] * 2
    ins = list(att) + [hidden, mods, cot, loss, w_out, b_out]
    return pl.pallas_call(
        functools.partial(mid_kernel, (seq_ways, heads_local, utts, ff)),
        out_shape=out_shape,
        grid_spec=pltpu.PrefetchScalarGridSpec(
            num_scalar_prefetch=2,
            grid=(steps,),
            in_specs=[whole(a.shape) for a in ins]
            + [
                pl.BlockSpec((width, FF_TILE), lambda j, *_: (0, j)),
                pl.BlockSpec((1, FF_TILE), lambda j, *_: (0, j)),
                pl.BlockSpec((FF_TILE, width), lambda j, *_: (j, 0)),
                whole((1, width)),
            ],
            out_specs=out_specs,
            scratch_shapes=[
                pltpu.VMEM((width, frames), bf16),
                pltpu.VMEM((frames, width), f32),
                pltpu.VMEM((frames, width), f32),
                pltpu.VMEM((frames, width), bf16),
                pltpu.VMEM((width, frames), bf16),
                pltpu.VMEM((frames, width), bf16),
                pltpu.VMEM((frames, width), f32),
                pltpu.VMEM((frames, width), f32),
                pltpu.VMEM((32, frames), bf16),
                pltpu.VMEM((frames, 128), bf16),
                pltpu.VMEM((128, 4 * width), bf16),
                pltpu.VMEM((2,) + gshape, bf16),
                pltpu.SemaphoreType.DMA((2, steps + seq_ways // 2 + 1)),
            ],
        ),
        compiler_params=pltpu.CompilerParams(vmem_limit_bytes=63 << 20),
        cost_estimate=cost(500),
        name="mid_block",
    )(lengths, ids, *ins, w_up, b_up, w_down, b_down)


def whole_block(shape):
    return pl.BlockSpec(shape, lambda *_: (0,) * len(shape), pipeline_mode=pl.Buffered(1))


def segment_rows(lengths_ref, drop_ref, utts, base, width):
    col = base + lax.broadcasted_iota(jnp.int32, (1, width), 1)
    start = jnp.int32(0)
    kept = jnp.zeros((1, width), jnp.float32)
    place = jnp.zeros((1, width), jnp.int32)
    for u in range(utts):
        end = start + lengths_ref[u]
        inside = (col >= start) & (col < end)
        kept = jnp.where(inside, (1 - drop_ref[u]).astype(jnp.float32), kept)
        place = jnp.where(inside, col - start, place)
        start = end
    return kept, place.astype(jnp.float32)


def rotary_rows(place, half):
    index = lax.broadcasted_iota(jnp.int32, (half, 1), 0).astype(jnp.float32)
    inverse = jnp.exp(index * (-9.210340371976184 / half))
    angles = inverse * place
    return jnp.cos(angles), jnp.sin(angles)


def frame_columns(hot, extra):
    hotb = hot.astype(jnp.bfloat16)
    idx = lax.broadcasted_iota(jnp.int32, hot.shape, 0)
    last = jnp.where(idx == 0, extra, 0.0).astype(jnp.bfloat16)
    return pad_rows([hotb, hotb, hotb, last], 128).T


def head_kernel(
    utts,
    lengths_ref,
    ids_ref,
    drop_ref,
    tokens_ref,
    skip_ref,
    cond_ref,
    mods_ref,
    w_skip_ref,
    b_skip_ref,
    hidden_ref,
    joinedT_ref,
    naT_ref,
    na_ref,
    cols,
):
    f32, bf16 = jnp.float32, jnp.bfloat16
    step = pl.program_id(0)
    frames, width = tokens_ref.shape
    rank = ids_ref[1]

    @pl.when(step == 0)
    def _():
        hot = onehot_rows(lengths_ref, utts, 16, rank * frames, frames)
        kept, _ = segment_rows(lengths_ref, drop_ref, utts, rank * frames, frames)
        cols[...] = frame_columns(hot, kept)
        keep = cols[:, 48:49].astype(f32)
        mixed = (tokens_ref[...].astype(f32) + keep * cond_ref[...].astype(f32)).astype(bf16)
        joinedT_ref[0:width, :] = mixed.T
        hidden_ref[...] = dot(mixed, w_skip_ref[...]) + b_skip_ref[...].astype(f32)

    @pl.when(step == 1)
    def _():
        skip = skip_ref[...]
        joinedT_ref[width : 2 * width, :] = skip.T
        hidden = hidden_ref[...] + dot(skip, w_skip_ref[...])
        hidden_ref[...] = hidden
        madd = mods_operand(mods_ref)
        shift = dot(cols[...], madd[:, :width])
        scale = dot(cols[...], madd[:, width:])
        normed, _ = norm_stats(hidden)
        value = (normed * (1.0 + scale) + shift).astype(bf16)
        na_ref[...] = value
        naT_ref[...] = value.T


def head_block(lengths, ids, drop, tokens, skip, cond, mods, w_skip, b_skip):
    frames, width = tokens.shape
    utts = lengths.shape[0]
    f32, bf16 = jnp.float32, jnp.bfloat16

    def whole(shape):
        return pl.BlockSpec(shape, lambda j, *_: (0,) * len(shape), pipeline_mode=pl.Buffered(1))

    out_shape = [
        jax.ShapeDtypeStruct((frames, width), f32),
        jax.ShapeDtypeStruct((2 * width, frames), bf16),
        jax.ShapeDtypeStruct((width, frames), bf16),
        jax.ShapeDtypeStruct((frames, width), bf16),
    ]
    return pl.pallas_call(
        functools.partial(head_kernel, utts),
        out_shape=out_shape,
        grid_spec=pltpu.PrefetchScalarGridSpec(
            num_scalar_prefetch=3,
            grid=(2,),
            in_specs=[whole(a.shape) for a in (tokens, skip, cond, mods)]
            + [pl.BlockSpec((width, width), lambda j, *_: (j, 0)), whole((1, width))],
            out_specs=[whole(o.shape) for o in out_shape],
            scratch_shapes=[pltpu.VMEM((frames, 128), bf16)],
        ),
        compiler_params=pltpu.CompilerParams(vmem_limit_bytes=48 << 20),
        cost_estimate=cost(100),
        name="head_block",
    )(lengths, ids, drop, tokens, skip, cond, mods, w_skip, b_skip)


def turn_heads(tensor, cosine, sine):
    half = DH // 2
    first, second = tensor[:, :half], tensor[:, half:]
    return jnp.concatenate([first * cosine - second * sine, second * cosine + first * sine], axis=1)


def qkv_kernel(utts, seq_ways, lengths_ref, ids_ref, drop_ref, na_ref, w_ref, b_ref, out_ref, trig):
    f32, bf16 = jnp.float32, jnp.bfloat16
    part = pl.program_id(0)
    frames = na_ref.shape[0]

    @pl.when(part == 0)
    def _():
        _, place = segment_rows(lengths_ref, drop_ref, utts, ids_ref[1] * frames, frames)
        cosine, sine = rotary_rows(place, DH // 2)
        trig[0] = cosine
        trig[1] = sine

    raw = dot(na_ref[...], w_ref[...]) + b_ref[...].astype(f32)
    rawT = raw.T.reshape(seq_ways, DH, frames)
    turned = part < 2
    cosine = jnp.where(turned, trig[0], 1.0)[None]
    sine = jnp.where(turned, trig[1], 0.0)[None]
    out_ref[:, pl.ds(pl.multiple_of(part * DH, DH), DH), :] = turn_heads(rawT, cosine, sine).astype(bf16)


def qkv_block(lengths, ids, drop, na, w_qkv, b_qkv, chunk, seq_ways):
    frames, width = na.shape
    cols = seq_ways * DH
    chunks = width // cols
    utts = lengths.shape[0]

    def whole(shape):
        return pl.BlockSpec(shape, lambda j, *_: (0,) * len(shape), pipeline_mode=pl.Buffered(1))

    shape = (seq_ways, 3 * DH, frames)
    return pl.pallas_call(
        functools.partial(qkv_kernel, utts, seq_ways),
        out_shape=jax.ShapeDtypeStruct(shape, jnp.bfloat16),
        grid_spec=pltpu.PrefetchScalarGridSpec(
            num_scalar_prefetch=3,
            grid=(3,),
            in_specs=[
                whole(na.shape),
                pl.BlockSpec((width, cols), lambda j, *_: (0, j * chunks + chunk)),
                pl.BlockSpec((1, cols), lambda j, *_: (0, j * chunks + chunk)),
            ],
            out_specs=whole(shape),
            scratch_shapes=[pltpu.VMEM((2, DH // 2, frames), jnp.float32)],
        ),
        cost_estimate=cost(75),
        name="qkv_block",
    )(lengths, ids, drop, na, w_qkv, b_qkv)


def back_kernel(utts, seq_ways, chunk, lengths_ref, ids_ref, drop_ref, grad_ref, naT_ref, w_ref, *refs):
    first = chunk == 0
    acc_in = None if first else refs[0]
    acc_ref, bias_ref, keep_ref, send_ref, trig, grads, sems = refs[0 if first else 3 :]
    f32, bf16 = jnp.float32, jnp.bfloat16
    part = pl.program_id(0)
    width, frames = naT_ref.shape
    core = ids_ref[0]
    parts = keep_ref.shape[0]
    own = width // seq_ways
    rows = own // parts

    @pl.when(part == 0)
    def _():
        _, place = segment_rows(lengths_ref, drop_ref, utts, ids_ref[1] * frames, frames)
        cosine, sine = rotary_rows(place, DH // 2)
        trig[0] = cosine
        trig[1] = sine

    turned = part < 2
    cosine = jnp.where(turned, trig[0], 1.0)[None]
    sine = jnp.where(turned, trig[1], 0.0)[None]
    raw = grad_ref[:, pl.ds(pl.multiple_of(part * DH, DH), DH), :].astype(f32)
    gpT = turn_heads(raw, cosine, -sine).astype(bf16).reshape(seq_ways * DH, frames)
    gna = dot(w_ref[...], gpT)

    @pl.when(part == 0)
    def _():
        acc_ref[...] = gna if first else acc_in[...] + gna

    @pl.when(part > 0)
    def _():
        acc_ref[...] += gna

    ones = jnp.ones((8, frames), bf16)
    bias_ref[0] = dot_nt(ones, gpT)
    grad_w = dot_nt(naT_ref[...], gpT).astype(bf16)
    cols = seq_ways * DH
    at = pl.ds(pl.multiple_of(part * rows, rows), rows)
    for s in range(seq_ways):
        side = jnp.where(core == s % 2, 0, 1)
        for k in range(parts):
            lo = s * own + k * rows
            grads[side, k, s // 2, at, :] = grad_w[lo : lo + rows]

    def copy(side, p):
        where = (slice(None), slice(None), pl.ds(pl.multiple_of(p * rows, rows), rows))
        return pltpu.make_async_copy(
            grads.at[side].at[where],
            (keep_ref, send_ref)[side].at[(*where, pl.ds(chunk * cols, cols))],
            sems.at[side, p],
        )

    for side in (1, 0):
        copy(side, part).start()

    @pl.when(part == 2)
    def _():
        for side in (1, 0):
            for p in range(3):
                copy(side, p).wait()


def back_block(lengths, ids, drop, grad, naT, w_qkv, before, chunk, parts):
    seq_ways, _, frames = grad.shape
    width = naT.shape[0]
    cols = seq_ways * DH
    chunks = width // cols
    utts = lengths.shape[0]
    f32, bf16 = jnp.float32, jnp.bfloat16
    rows = width // seq_ways // parts

    def whole(shape):
        return pl.BlockSpec(shape, lambda j, *_: (0,) * len(shape), pipeline_mode=pl.Buffered(1))

    gspec = pl.BlockSpec(memory_space=pl.ANY)
    gshape = jax.ShapeDtypeStruct((parts, seq_ways // 2, 3 * rows, width), bf16)
    ins = [grad, naT, w_qkv, *before]
    in_specs = [whole(grad.shape), whole(naT.shape)]
    in_specs += [pl.BlockSpec((width, cols), lambda j, *_: (0, j * chunks + chunk))]
    aliases = {}
    if before:
        in_specs += [whole(before[0].shape), gspec, gspec]
        aliases = {7: 2, 8: 3}
    return pl.pallas_call(
        functools.partial(back_kernel, utts, seq_ways, chunk),
        out_shape=[
            jax.ShapeDtypeStruct((width, frames), f32),
            jax.ShapeDtypeStruct((3, 8, cols), f32),
            gshape,
            gshape,
        ],
        grid_spec=pltpu.PrefetchScalarGridSpec(
            num_scalar_prefetch=3,
            grid=(3,),
            in_specs=in_specs,
            out_specs=[
                whole((width, frames)),
                pl.BlockSpec((1, 8, cols), lambda j, *_: (j, 0, 0)),
                gspec,
                gspec,
            ],
            scratch_shapes=[
                pltpu.VMEM((2, DH // 2, frames), f32),
                pltpu.VMEM((2, parts, seq_ways // 2, 3 * rows, cols), bf16),
                pltpu.SemaphoreType.DMA((2, 3)),
            ],
        ),
        compiler_params=pltpu.CompilerParams(vmem_limit_bytes=48 << 20),
        cost_estimate=cost(100),
        input_output_aliases=aliases,
        name="back_block",
    )(lengths, ids, drop, *ins)


def norm_kernel(
    utts, heads_local, lengths_ref, ids_ref, acc_ref, hidden_ref, after_ref, mods_ref, loss_ref, mid_ref, *refs
):
    f32, bf16 = jnp.float32, jnp.bfloat16
    bias_refs, (gh_ref, small_ref) = refs[:heads_local], refs[heads_local:]
    frames, width = hidden_ref.shape
    pad_u = table_rows(utts)
    base = 6 * pad_u
    hot = onehot_rows(lengths_ref, utts, 16, ids_ref[1] * frames, frames)
    cols = frame_columns(hot, jnp.zeros((1, frames), f32))
    madd = mods_operand(mods_ref)
    scale = dot(cols, madd[:, width:])
    gna = acc_ref[...].T
    normed, rstd = norm_stats(hidden_ref[...])
    sums = sum_rows(hot, 16, frames)
    small_ref[0:pad_u, :] = dot(sums, gna.astype(bf16))[:pad_u]
    small_ref[pad_u : 2 * pad_u, :] = dot(sums, (gna * normed).astype(bf16))[:pad_u]
    gh = (after_ref[...] + norm_back(gna * (1.0 + scale), normed, rstd)).astype(bf16)
    gh_ref[...] = gh
    small_ref[2 * pad_u : base, :] = mid_ref[0 : 4 * pad_u, :]
    cols_local = width // heads_local
    for c in range(heads_local):
        for p in range(3):
            small_ref[base + p : base + p + 1, c * cols_local : (c + 1) * cols_local] = bias_refs[c][p, 0:1, :]
    small_ref[base + 3 : base + 4, :] = dot(sums, gh)[16:17]
    small_ref[base + 4 : base + 12, :] = mid_ref[4 * pad_u : 4 * pad_u + 8, :]
    count = jnp.sum(loss_ref[...].astype(f32), axis=1, keepdims=True)
    high = jnp.floor(count / 32.0) * 32.0
    small_ref[base + 12 : base + 13, :] = jnp.broadcast_to(high, (1, width))
    small_ref[base + 13 : base + 16, :] = jnp.broadcast_to(count - high, (3, width))


def norm_block(lengths, ids, acc, hidden, after, mods, loss, mid_small, biases):
    frames, width = hidden.shape
    utts = lengths.shape[0]
    out_shape = [
        jax.ShapeDtypeStruct((frames, width), jnp.bfloat16),
        jax.ShapeDtypeStruct((6 * table_rows(utts) + 16, width), jnp.float32),
    ]
    return pl.pallas_call(
        functools.partial(norm_kernel, utts, len(biases)),
        out_shape=out_shape,
        grid_spec=pltpu.PrefetchScalarGridSpec(
            num_scalar_prefetch=2,
            grid=(1,),
            in_specs=[whole_block(a.shape) for a in (acc, hidden, after, mods, loss, mid_small, *biases)],
            out_specs=[whole_block(o.shape) for o in out_shape],
        ),
        compiler_params=pltpu.CompilerParams(vmem_limit_bytes=48 << 20),
        cost_estimate=cost(50),
        name="norm_block",
    )(lengths, ids, acc, hidden, after, mods, loss, mid_small, *biases)


def skip_kernel(seq_ways, ids_ref, joinedT_ref, gh_ref, keep_ref, send_ref, grads, sems):
    step = pl.program_id(0)
    core = ids_ref[0]
    parts = keep_ref.shape[0]
    width = joinedT_ref.shape[0]
    block = 2 * width // seq_ways
    rows = block // parts
    z_step = seq_ways // 4
    grad_w = dot(joinedT_ref[...], gh_ref[...]).astype(jnp.bfloat16)
    for b in range(width // block):
        side = jnp.where(core == b % 2, 0, 1)
        for k in range(parts):
            lo = b * block + k * rows
            grads[side, k, step * z_step + b // 2] = grad_w[lo : lo + rows]

    def copy(side, at):
        where = (slice(None), pl.ds(at * z_step, z_step))
        return pltpu.make_async_copy(
            grads.at[side].at[where], (keep_ref, send_ref)[side].at[where], sems.at[side, at]
        )

    for side in (1, 0):
        copy(side, step).start()

    @pl.when(step == 1)
    def _():
        for side in (1, 0):
            for at in range(2):
                copy(side, at).wait()


def skip_block(ids, joinedT, gh, seq_ways, parts):
    frames, width = gh.shape
    rows = 2 * width // seq_ways // parts
    gshape = (parts, seq_ways // 2, rows, width)
    return pl.pallas_call(
        functools.partial(skip_kernel, seq_ways),
        out_shape=[jax.ShapeDtypeStruct(gshape, jnp.bfloat16)] * 2,
        grid_spec=pltpu.PrefetchScalarGridSpec(
            num_scalar_prefetch=1,
            grid=(2,),
            in_specs=[pl.BlockSpec((width, frames), lambda j, *_: (j, 0)), whole_block(gh.shape)],
            out_specs=[pl.BlockSpec(memory_space=pl.ANY)] * 2,
            scratch_shapes=[pltpu.VMEM((2,) + gshape, jnp.bfloat16), pltpu.SemaphoreType.DMA((2, 2))],
        ),
        compiler_params=pltpu.CompilerParams(vmem_limit_bytes=32 << 20),
        cost_estimate=cost(50),
        name="skip_block",
    )(ids, joinedT, gh)


def joined_kernel(gh_ref, w_ref, scale_ref, first_ref, second_ref):
    step = pl.program_id(0)
    value = dot_nt(gh_ref[...], w_ref[...]) * scale_ref[0:1, 0:1]

    @pl.when(step == 0)
    def _():
        first_ref[...] = value

    @pl.when(step == 1)
    def _():
        second_ref[...] = value


def joined_block(gh, w_skip, scale):
    frames, width = gh.shape
    out = jax.ShapeDtypeStruct((frames, width), jnp.float32)
    return pl.pallas_call(
        joined_kernel,
        out_shape=[out, out],
        grid_spec=pltpu.PrefetchScalarGridSpec(
            num_scalar_prefetch=0,
            grid=(2,),
            in_specs=[
                whole_block(gh.shape),
                pl.BlockSpec((width, width), lambda j: (j, 0)),
                whole_block(scale.shape),
            ],
            out_specs=[whole_block(out.shape)] * 2,
        ),
        compiler_params=pltpu.CompilerParams(vmem_limit_bytes=32 << 20),
        cost_estimate=cost(50),
        name="joined_block",
    )(gh, w_skip, scale)


def add_bf16(left, right):
    return (left.astype(jnp.float32) + right.astype(jnp.float32)).astype(jnp.bfloat16)


def first_kernel(pairs, splits, ids_ref, *refs):
    ins, outs = refs[: 8 * pairs], list(refs[8 * pairs :])
    for i in range(4):
        own = [outs.pop(0) for _ in range(splits if i < 2 else 1)]
        at = 0
        for p in range(pairs):
            left, right = ins[2 * (i * pairs + p)], ins[2 * (i * pairs + p) + 1]
            rows = left.shape[-2]
            value = add_bf16(left[0, 0, 0], right[0, 0, 0])
            if len(own) == 1:
                own[0][0, :, at : at + rows, :] = value
            else:
                for out in own:
                    out[0] = value[:, at : at + out.shape[2], :]
                    at += out.shape[2]
            at += rows


def first_sum(ids, pairs, splits):
    _, _, _, z_ways, _, width = pairs[0][0].shape
    total = sum(k.shape[4] for k, _ in pairs)
    step = 1 if total > 100 else z_ways

    def source(half, axis, mine, rows):
        def at(g, z, ids):
            bit = ids[axis]
            return half, bit if mine else 1 - bit, g, z, 0, 0

        return pl.BlockSpec((1, 1, 1, step, rows, width), at)

    order = [(0, 2, False), (1, 3, False), (0, 2, True), (1, 3, True)]
    sizes = [*splits, *splits, total, total]
    return pl.pallas_call(
        functools.partial(first_kernel, len(pairs), len(splits)),
        out_shape=[jax.ShapeDtypeStruct((2, z_ways, n, width), jnp.bfloat16) for n in sizes],
        grid_spec=pltpu.PrefetchScalarGridSpec(
            num_scalar_prefetch=1,
            grid=(2, z_ways // step),
            in_specs=[source(*o, a.shape[4]) for o in order for pair in pairs for a in pair],
            out_specs=[pl.BlockSpec((1, step, n, width), lambda g, z, ids: (g, z, 0, 0)) for n in sizes],
        ),
        compiler_params=pltpu.CompilerParams(vmem_limit_bytes=48 << 20),
        cost_estimate=cost(60),
        name="first_sum",
    )(ids, *([a for pair in pairs for a in pair] * 4))


def second_kernel(pieces, ids_ref, *refs):
    for i in range(4):
        keep, *got = refs[(pieces + 1) * i : (pieces + 1) * (i + 1)]
        out = refs[4 * (pieces + 1) + i]
        at = 0
        for g in got:
            rows = g.shape[2]
            out[:, at : at + rows, :] = add_bf16(keep[0, :, at : at + rows, :], g[0])
            at += rows


def second_sum(ids, keep_a, got_a, keep_b, got_b):
    _, z_ways, rows, width = keep_a.shape
    step = z_ways // 2 if rows > 100 else z_ways

    def source(axis, mine, value):
        def at(z, ids):
            bit = ids[axis]
            return bit if mine else 1 - bit, z, 0, 0

        return pl.BlockSpec((1, step, *value.shape[2:]), at)

    order = [(3, False), (2, False), (3, True), (2, True)]
    sides = [[keep_a, *got_a], [keep_b, *got_b]]
    out = jax.ShapeDtypeStruct((z_ways, rows, width), jnp.bfloat16)
    return pl.pallas_call(
        functools.partial(second_kernel, len(got_a)),
        out_shape=[out] * 4,
        grid_spec=pltpu.PrefetchScalarGridSpec(
            num_scalar_prefetch=1,
            grid=(z_ways // step,),
            in_specs=[source(*o, v) for i, o in enumerate(order) for v in sides[i % 2]],
            out_specs=[pl.BlockSpec((step, rows, width), lambda z, ids: (z, 0, 0))] * 4,
        ),
        compiler_params=pltpu.CompilerParams(vmem_limit_bytes=48 << 20),
        cost_estimate=cost(30),
        name="second_sum",
    )(ids, *((sides[0] + sides[1]) * 2))


def third_kernel(ids_ref, keep_a, got_a, keep_b, got_b, *outs):
    for j, out in enumerate(outs):
        at = ids_ref[4] ^ j
        out[0] = add_bf16(keep_a[at], got_a[at])
        out[1] = add_bf16(keep_b[at], got_b[at])


def third_sum(ids, keep_a, got_a, keep_b, got_b):
    z_ways, rows, width = keep_a.shape
    out = jax.ShapeDtypeStruct((2, rows, width), jnp.bfloat16)
    return pl.pallas_call(
        third_kernel,
        out_shape=[out] * z_ways,
        grid_spec=pltpu.PrefetchScalarGridSpec(
            num_scalar_prefetch=1,
            grid=(1,),
            in_specs=[whole_block(keep_a.shape)] * 4,
            out_specs=[whole_block(out.shape)] * z_ways,
        ),
        cost_estimate=cost(10),
        name="third_sum",
    )(ids, keep_a, got_a, keep_b, got_b)


def third_all_kernel(ids_ref, keep_a, got_a, keep_b, got_b, out):
    for z in range(keep_a.shape[0]):
        out[z, 0] = add_bf16(keep_a[z], got_a[z])
        out[z, 1] = add_bf16(keep_b[z], got_b[z])


def third_sum_all(ids, keep_a, got_a, keep_b, got_b):
    z_ways, rows, width = keep_a.shape
    out = jax.ShapeDtypeStruct((z_ways, 2, rows, width), jnp.bfloat16)
    step = max(1, z_ways // 2)
    return pl.pallas_call(
        third_all_kernel,
        out_shape=out,
        grid_spec=pltpu.PrefetchScalarGridSpec(
            num_scalar_prefetch=1,
            grid=(z_ways // step,),
            in_specs=[pl.BlockSpec((step, rows, width), lambda i, *_: (i, 0, 0))] * 4,
            out_specs=pl.BlockSpec((step, 2, rows, width), lambda i, *_: (i, 0, 0, 0)),
        ),
        cost_estimate=cost(10),
        name="third_sum_all",
    )(ids, keep_a, got_a, keep_b, got_b)


def fourth_all_kernel(x, out):
    total = x[0].astype(jnp.float32)
    for z in range(1, x.shape[0]):
        total = total + x[z].astype(jnp.float32)
    out[...] = total.astype(jnp.bfloat16)


def fourth_sum_all(terms):
    return pl.pallas_call(
        fourth_all_kernel,
        out_shape=jax.ShapeDtypeStruct(terms.shape[1:], jnp.bfloat16),
        grid=(1,),
        in_specs=[whole_block(terms.shape)],
        out_specs=whole_block(terms.shape[1:]),
        cost_estimate=cost(10),
        name="fourth_sum_all",
    )(terms)


def fourth_kernel(*refs):
    total = refs[0][...].astype(jnp.float32)
    for r in refs[1:-1]:
        total = total + r[...].astype(jnp.float32)
    refs[-1][...] = total.astype(jnp.bfloat16)


def fourth_sum(terms):
    shape = terms[0].shape
    return pl.pallas_call(
        fourth_kernel,
        out_shape=jax.ShapeDtypeStruct(shape, jnp.bfloat16),
        grid=(1,),
        in_specs=[whole_block(shape)] * len(terms),
        out_specs=whole_block(shape),
        cost_estimate=cost(10),
        name="fourth_sum",
    )(*terms)


def place_kernel(streams, plan, ids_ref, scale_ref, *refs):
    blocks, outs = refs[: 4 * streams], refs[4 * streams :]
    x, y = ids_ref[2], ids_ref[3]
    scale = scale_ref[0:1, 0:1]
    for stream, row, rows, lane, lanes, out, row_of, lane_of in plan:
        for d in range(4):
            own_x, own_y = x ^ (d & 1), y ^ (d >> 1)
            for half in range(2):
                k = own_x * 2 + own_y if half == 0 else 4 + own_y * 2 + own_x
                tile = blocks[4 * stream + d][half, row : row + rows, lane : lane + lanes]
                outs[out][row_of(k), lane_of(k)] = tile.astype(jnp.float32) * scale


def place_blocks(ids, scale, streams, plan, shapes):
    blocks = [b for s in streams for b in s]
    outs = [jax.ShapeDtypeStruct(s, jnp.float32) for s in shapes]
    return pl.pallas_call(
        functools.partial(place_kernel, len(streams), plan),
        out_shape=outs,
        grid_spec=pltpu.PrefetchScalarGridSpec(
            num_scalar_prefetch=1,
            grid=(1,),
            in_specs=[whole_block(a.shape) for a in (scale, *blocks)],
            out_specs=[whole_block(o.shape) for o in outs],
        ),
        compiler_params=pltpu.CompilerParams(vmem_limit_bytes=32 << 20),
        cost_estimate=cost(20),
        name="place_blocks",
    )(ids, scale, *blocks)


def span(start, size):
    return pl.ds(pl.multiple_of(start, size), size)


def ada_kernel(groups, pad_u, numerator, time_ref, *refs):
    f32 = jnp.float32
    parts, (weight_ref, vector_ref, scale_ref) = refs[:groups], refs[groups:]
    table = pl.program_id(0)
    base = 6 * pad_u
    count = parts[0][base + 12 : base + 13, 0:1] + parts[0][base + 13 : base + 14, 0:1]
    for p in parts[1:]:
        count = count + p[base + 12 : base + 13, 0:1] + p[base + 13 : base + 14, 0:1]
    scale = numerator / count
    rows = jnp.concatenate([p[pl.ds(pl.multiple_of(table * pad_u, 8), pad_u), :] for p in parts], axis=0) * scale
    vector_ref[pl.ds(table, 1), :] = jnp.sum(rows, axis=0, keepdims=True)
    operand = jnp.concatenate(list(split3(rows)), axis=0)
    weight_ref[...] = dot(time_ref[...], operand)

    @pl.when(table == 0)
    def _():
        total = parts[0][base : base + 16, :]
        for p in parts[1:]:
            total = total + p[base : base + 16, :]
        vector_ref[8:24, :] = total * scale
        scale_ref[...] = jnp.broadcast_to(scale, scale_ref.shape)


def ada_block(time3, parts, utts, numerator):
    pad_u = table_rows(utts)
    width = parts[0].shape[1]
    own = time3.shape[0]
    f32 = jnp.float32
    return pl.pallas_call(
        functools.partial(ada_kernel, len(parts), pad_u, numerator),
        out_shape=[
            jax.ShapeDtypeStruct((own, 6 * width), f32),
            jax.ShapeDtypeStruct((24, width), f32),
            jax.ShapeDtypeStruct((8, 128), f32),
        ],
        grid=(6,),
        in_specs=[whole_block(time3.shape)] + [whole_block(p.shape) for p in parts],
        out_specs=[
            pl.BlockSpec((own, width), lambda j: (0, j)),
            whole_block((24, width)),
            whole_block((8, 128)),
        ],
        cost_estimate=cost(50),
        name="ada_block",
    )(time3, *parts)


def sum_exchange(value, axis, bit):
    ways = lax.axis_size(axis)
    return lax.ppermute(value, axis, [(i, i ^ bit) for i in range(ways)])


def axis_bits(ways):
    return [1 << i for i in range(ways.bit_length() - 1)]


def reduce_stages(ids, blocks, splits, whole_z):
    batch_ways = lax.axis_size("batch")
    x_bit, y_bit = 1, 1 << ((batch_ways.bit_length() - 1) // 2)
    pairs = []
    for keep, send in blocks:
        shape = (2, 2, 2) + keep.shape[1:]
        pairs.append((keep.reshape(shape), sum_exchange(send, "seq", 1).reshape(shape)))
    *sends, keep_a, keep_b = first_sum(ids, pairs, splits)
    sends = follow(sends, (yield sends))
    got, token = [[], []], None
    for i in range(len(splits)):
        pieces = follow([sends[i], sends[len(splits) + i]], token)
        for side, bit in enumerate((x_bit, y_bit)):
            got[side].append(sum_exchange(pieces[side], "batch", bit))
        token = yield [got[0][i], got[1][i]]
    got_a, got_b = (follow(g, token) for g in got)
    send_a, send_b, keep_a, keep_b = second_sum(ids, keep_a, got_a, keep_b, got_b)
    send_a, send_b = follow([send_a, send_b], (yield [send_a, send_b]))
    got = [sum_exchange(send_a, "batch", y_bit), sum_exchange(send_b, "batch", x_bit)]
    got_a, got_b = follow(got, (yield got))
    if whole_z:
        ways = lax.axis_size("seq")
        groups = [list(range(c, ways, 2)) for c in range(2)]
        away = [third_sum_all(ids, keep_a, got_a, keep_b, got_b)]
        away = follow(away, (yield away))
        got = [lax.all_to_all(away[0], "seq", 0, 0, axis_index_groups=groups, tiled=True)]
        got = follow(got, (yield got))
        block = fourth_sum_all(got[0])
    else:
        own, *away = third_sum(ids, keep_a, got_a, keep_b, got_b)
        away = follow(away, (yield away))
        got = [sum_exchange(a, "seq", 2 * (j + 1)) for j, a in enumerate(away)]
        got = follow(got, (yield got))
        block = fourth_sum([own] + got)
    for bit in axis_bits(batch_ways):
        if bit not in (x_bit, y_bit):
            block = add_bf16(block, sum_exchange(block, "batch", bit))
    (block,) = follow([block], (yield [block]))
    yield [block] + [sum_exchange(block, "batch", bit) for bit in (x_bit, y_bit, x_bit | y_bit)]


def advance(stages, steps, token=None):
    value = next(stages) if token is None else stages.send(token)
    for _ in range(steps - 1):
        value = next(stages)
    return value


def last_stage(stages, token=None):
    value = stages.send(token)
    for value in stages:
        pass
    return value


def follow(values, token):
    return values if token is None else [after(v, token) for v in values]


def after(value, *others):
    return lax.optimization_barrier((value,) + others)[0]


def gather_groups(value):
    away = value.astype(jnp.bfloat16)
    others = [sum_exchange(away, "batch", i) for i in range(1, lax.axis_size("batch"))]
    return [value] + [other.astype(value.dtype) for other in others]


def sum_z(value, tokens):
    away = after(value.astype(jnp.bfloat16), *tokens)
    for j in range(1, lax.axis_size("seq") // 2):
        value = value + sum_exchange(away, "seq", 2 * j).astype(jnp.float32)
    return value


def shards(
    tokens_in,
    skip_in,
    condition,
    cotangent,
    time_embed,
    lengths,
    key_mask,
    drop_mask,
    loss_mask,
    w_skip,
    b_skip,
    w_ada,
    b_ada,
    w_qkv,
    b_qkv,
    w_out,
    b_out,
    w_up,
    b_up,
    w_down,
    b_down,
):
    f32, bf16 = jnp.float32, jnp.bfloat16
    seq_ways, batch_ways = lax.axis_size("seq"), lax.axis_size("batch")
    seq_rank = lax.axis_index("seq")
    frames, width = tokens_in.shape[1:]
    group_frames = frames * seq_ways
    heads_local = HEADS // seq_ways
    utts = lengths.shape[1]
    lengths_row, drop = lengths[0], drop_mask[0]
    batch_rank = lax.axis_index("batch")
    side = 1 << ((batch_ways.bit_length() - 1) // 2)
    ids = [lax.rem(seq_rank, 2), seq_rank, lax.rem(batch_rank, 2), lax.rem(batch_rank // side, 2), seq_rank // 2]
    ids = jnp.stack(ids).astype(jnp.int32)
    ok = key_mask.reshape(seq_ways, 1, frames)
    exchange = functools.partial(lax.all_to_all, axis_name="seq", split_axis=0, concat_axis=0, tiled=True)

    time_act = jax.nn.silu(time_embed[0]).astype(bf16)
    time_rows = jnp.pad(time_act, ((0, 16 - utts), (0, 0)))

    def modulation(first, last):
        return jnp.dot(time_rows, w_ada[:, first:last], preferred_element_type=f32) + b_ada[
            first:last
        ].astype(f32)

    mods_a = modulation(0, 2 * width)
    hidden, joinedT, naT, na = head_block(
        lengths_row, ids, drop, tokens_in[0], skip_in[0], condition[0], mods_a, w_skip, b_skip[None]
    )
    mods_rest = modulation(2 * width, 6 * width)
    received = []
    for c in range(heads_local):
        packed = qkv_block(lengths_row, ids, drop, na, w_qkv, b_qkv[None], c, seq_ways)
        if c == 0:
            na = after(na, mods_rest)
        received.append(exchange(packed))

    own = width // seq_ways
    pad_u = table_rows(utts)
    time_own = lax.dynamic_slice_in_dim(jnp.concatenate(gather_groups(time_rows[:pad_u])), seq_rank * own, own, axis=1)
    time3 = jnp.tile(time_own.T, (1, 3))

    received[0] = after(received[0], mods_rest)
    head_out, log_totals, returned = [], [], []
    for c in range(heads_local):
        out, log_total = attend(lengths_row, received[c], ok)
        head_out.append(out)
        log_totals.append(log_total)
        returned.append(exchange(after(out, *returned)))
        if c < heads_local - 1:
            received[c + 1] = after(received[c + 1], out, time3)
    mid = mid_block(
        lengths_row,
        ids,
        returned,
        hidden,
        mods_rest,
        cotangent[0],
        loss_mask,
        w_out,
        b_out[None],
        w_up,
        b_up[None],
        w_down,
        b_down[None],
        PARTS,
    )
    output, after_grad, mid_small, grad_att, keep, send = mid
    grad_heads = exchange(grad_att)
    front = keep.shape[2] * 4 // 9 // 16 * 16
    feed = reduce_stages(ids, [(keep, send)], [front, keep.shape[2] - front], True)

    ahead = next(feed)
    grad_local = []
    for c in range(heads_local):
        operand = after(grad_heads, *ahead)
        moving = feed.send(grad if c else None) if c < 2 else []
        grad = attend_back(lengths_row, received[c], ok, head_out[c], operand, log_totals[c], c)
        grad_local.append(exchange(after(grad, *moving)))
        ahead = [grad]
    if heads_local == 1:
        next(feed)
    ahead = ahead + advance(feed, 1, ahead[0])
    before, biases = (), []
    for c in range(heads_local):
        acc, bias, keep, send = back_block(
            lengths_row, ids, drop, after(grad_local[c], *ahead), naT, w_qkv, before, c, PARTS
        )
        before = (acc, keep, send)
        biases.append(bias)
        ahead = next(feed) and advance(feed, 1, acc) if c == 0 else []
    gh, small = norm_block(lengths_row, ids, acc, hidden, after_grad, mods_a, loss_mask, mid_small, biases)
    small = small + sum_exchange(small, "seq", 1)
    skip_keep, skip_send = skip_block(ids, joinedT, gh, seq_ways, PARTS)
    blocks = [(skip_keep, skip_send), (keep, send)]
    rest = reduce_stages(ids, blocks, [5 * own // PARTS], False)
    moving = next(feed)
    small = sum_z(small, moving + advance(rest, 3))
    next(rest)
    groups = gather_groups(after(small, *next(rest)))
    numerator = float(group_frames * batch_ways)
    grad_w_ada, vectors, scale = ada_block(time3, groups, utts, numerator)
    grad_tokens, grad_skip = joined_block(gh, w_skip, scale)
    next(feed)
    feed = last_stage(feed, groups[-1])
    next(rest)
    rest.send(grad_tokens)
    rest = last_stage(rest)

    ff = w_up.shape[1]
    chunks = ff // width
    up_part = chunks * own // PARTS
    down_part = ff // seq_ways // PARTS
    out_part = own // PARTS
    per_chunk = own // up_part
    whole_lanes = lambda k: span(0, width)
    grad_w_up, grad_w_down, grad_w_out = place_blocks(
        ids,
        scale,
        [feed],
        [
            (
                *(0, 0, up_part, 0, width, 0),
                lambda k: span(lax.rem(k, per_chunk) * up_part, up_part),
                lambda k: span(k // per_chunk * width, width),
            ),
            (0, up_part, down_part, 0, width, 1, lambda k: span(k * down_part, down_part), whole_lanes),
            (0, up_part + down_part, out_part, 0, width, 2, lambda k: span(k * out_part, out_part), whole_lanes),
        ],
        [(own, ff), (ff // seq_ways, width), (own, width)],
    )
    skip_part = 2 * own // PARTS
    grad_w_skip, grad_w_qkv = place_blocks(
        ids,
        after(scale, grad_w_down),
        [rest],
        [(0, 0, skip_part, 0, width, 0, lambda k: span(k * skip_part, skip_part), whole_lanes)]
        + [
            (
                *(0, skip_part + p * out_part, out_part, 0, width, 1),
                lambda k: span(k * out_part, out_part),
                lambda k, at=p * width: span(at, width),
            )
            for p in range(3)
        ],
        [(2 * own, width), (own, 3 * width)],
    )

    def own_slice(vector):
        vector = vector.reshape(-1)
        size = vector.shape[0] // seq_ways
        return lax.dynamic_slice_in_dim(vector, seq_rank * size, size)

    grad_b_ada = own_slice(vectors[:6])
    grad_b_qkv = own_slice(vectors[8:11])
    grad_b_skip = own_slice(vectors[11])
    grad_b_out = own_slice(vectors[12])
    grad_b_down = own_slice(vectors[13])
    grad_b_up = own_slice(vectors[14 : 14 + chunks])
    return (
        output[None],
        grad_tokens[None],
        grad_skip[None],
        grad_w_skip,
        grad_b_skip,
        grad_w_ada,
        grad_b_ada,
        grad_w_qkv,
        grad_b_qkv,
        grad_w_out,
        grad_b_out,
        grad_w_up,
        grad_b_up,
        grad_w_down,
        grad_b_down,
    )


def solution(mesh):
    in_specs = (
        P("batch", "seq", None),
        P("batch", "seq", None),
        P("batch", "seq", None),
        P("batch", "seq", None),
        P("batch", None, None),
        P("batch", None),
        P("batch", None),
        P("batch", None),
        P("batch", "seq"),
        P(),
        P(),
        P(),
        P(),
        P(),
        P(),
        P(),
        P(),
        P(),
        P(),
        P(),
        P(),
    )
    out_specs = (
        P("batch", "seq", None),
        P("batch", "seq", None),
        P("batch", "seq", None),
        P("seq", None),
        P("seq"),
        P("seq", None),
        P("seq"),
        P("seq", None),
        P("seq"),
        P("seq", None),
        P("seq"),
        P("seq", None),
        P("seq"),
        P("seq", None),
        P("seq"),
    )
    return jax.shard_map(shards, mesh=mesh, in_specs=in_specs, out_specs=out_specs, check_vma=False)
```

```python
import functools

import jax
import jax.numpy as jnp
from jax import lax
from jax.experimental import pallas as pl
from jax.experimental.pallas import tpu as pltpu
from jax.sharding import PartitionSpec as P

HEADS = 16
HEAD_DIM = 64
PARTS = 8
BIG = 1e30
DH = 64
BQ = 512
BK = 512


def cost(weight):
    return pl.CostEstimate(flops=weight * 100000000, bytes_accessed=weight * 100000, transcendentals=0)


def onehot_rows(lengths_ref, utts, rows, base, width):
    row = lax.broadcasted_iota(jnp.int32, (rows, width), 0)
    col = base + lax.broadcasted_iota(jnp.int32, (rows, width), 1)
    start = jnp.int32(0)
    hot = jnp.zeros((rows, width), jnp.float32)
    for u in range(utts):
        end = start + lengths_ref[u]
        hot = jnp.where((row == u) & (col >= start) & (col < end), 1.0, hot)
        start = end
    return hot


def key_range(lengths_ref, utts, first, last):
    start = jnp.int32(0)
    low, high = jnp.int32(0), jnp.int32(0)
    for u in range(utts):
        end = start + lengths_ref[u]
        low = jnp.where((start <= first) & (first < end), start, low)
        high = jnp.where((start <= last) & (last < end), end, high)
        start = end
    return low // BK, (high + BK - 1) // BK


def aug_rows(utts):
    return -(-utts // 16) * 16


def split3(row):
    a = row.astype(jnp.bfloat16)
    rest = row - a.astype(jnp.float32)
    b = rest.astype(jnp.bfloat16)
    c = (rest - b.astype(jnp.float32)).astype(jnp.bfloat16)
    return a, b, c


def pad_rows(parts, total):
    have = sum(p.shape[0] for p in parts)
    if have < total:
        parts = parts + [jnp.zeros((total - have, parts[0].shape[1]), parts[0].dtype)]
    return jnp.concatenate(parts, axis=0)


def rows16(rows, width):
    idx = lax.broadcasted_iota(jnp.int32, (16, width), 0)
    out = jnp.zeros((16, width), jnp.float32)
    for i, r in enumerate(rows):
        out = jnp.where(idx == i, r, out)
    return out.astype(jnp.bfloat16)


def fwd_kernel(utts, lengths_ref, qkv_ref, ok_ref, out_ref, lse_ref, kaug, vaug):
    sources, _, frames = qkv_ref.shape
    per = frames // BQ
    pad_u = aug_rows(utts)
    step = pl.program_id(0)

    @pl.when(step == 0)
    def _():
        def build(s, c):
            hot = onehot_rows(lengths_ref, utts, pad_u, s * frames, frames)
            ok = ok_ref[s].astype(jnp.float32)
            block = qkv_ref[s]
            one = jnp.ones((1, frames), jnp.float32)
            kT = pad_rows(
                [block[DH : 2 * DH], (1.0 - hot).astype(jnp.bfloat16), rows16([1.0 - ok], frames)], 128
            )
            kaug[pl.ds(pl.multiple_of(s * frames, frames), frames), :] = kT.T
            vT = jnp.concatenate([block[2 * DH :], rows16([one], frames)], axis=0)
            for t in range(frames // BK):
                vaug[s * (frames // BK) + t] = vT[:, t * BK : (t + 1) * BK]
            return c

        lax.fori_loop(0, sources, build, 0)

    block = qkv_ref[step]
    hot_q = onehot_rows(lengths_ref, utts, pad_u, step * frames, frames)
    qT = (block[:DH].astype(jnp.float32) * 0.125)
    one = jnp.ones((1, frames), jnp.float32)
    qaug = pad_rows(
        [qT.astype(jnp.bfloat16), (hot_q * -BIG).astype(jnp.bfloat16), rows16([one * -BIG], frames)], 128
    )
    kT = block[DH : 2 * DH].astype(jnp.float32)
    vT = block[2 * DH :].astype(jnp.float32)
    ok = ok_ref[step] > 0
    s_self = jnp.sum(qT * kT, axis=0, keepdims=True)
    m0 = jnp.where(ok, -3e38, s_self)
    acc0 = jnp.concatenate([jnp.where(ok, 0.0, vT), jnp.where(ok, 0.0, jnp.ones((16, frames), jnp.float32))], axis=0)
    for t in range(per):
        cols = slice(t * BQ, (t + 1) * BQ)
        low, high = key_range(lengths_ref, utts, step * frames + t * BQ, step * frames + (t + 1) * BQ - 1)
        q_b = qaug[:, cols]

        def body(j, carry):
            m, acc = carry
            s = jnp.dot(kaug[pl.ds(pl.multiple_of(j * BK, BK), BK), :], q_b, preferred_element_type=jnp.float32)
            m_new = jnp.maximum(m, jnp.max(s, axis=0, keepdims=True))
            p = jnp.exp(s - m_new).astype(jnp.bfloat16)
            alpha = jnp.exp(m - m_new)
            acc = acc * alpha + jnp.dot(vaug[j], p, preferred_element_type=jnp.float32)
            return m_new, acc

        m, acc = lax.fori_loop(low, high, body, (m0[:, cols], acc0[:, cols]))
        total = acc[DH : DH + 1]
        out_ref[0, :, cols] = (acc[:DH] / total).astype(jnp.bfloat16)
        lse_ref[0, :, cols] = m + jnp.log(total)


def attend(lengths, qkv, ok):
    sources, _, frames = qkv.shape
    total = sources * frames
    utts = lengths.shape[0]
    whole = lambda shape: pl.BlockSpec(shape, lambda i, *_: (0,) * len(shape))
    return pl.pallas_call(
        functools.partial(fwd_kernel, utts),
        out_shape=(
            jax.ShapeDtypeStruct((sources, DH, frames), jnp.bfloat16),
            jax.ShapeDtypeStruct((sources, 1, frames), jnp.float32),
        ),
        grid_spec=pltpu.PrefetchScalarGridSpec(
            num_scalar_prefetch=1,
            grid=(sources,),
            in_specs=[whole(qkv.shape), whole(ok.shape)],
            out_specs=(
                pl.BlockSpec((1, DH, frames), lambda i, *_: (i, 0, 0)),
                pl.BlockSpec((1, 1, frames), lambda i, *_: (i, 0, 0)),
            ),
            scratch_shapes=[
                pltpu.VMEM((total, 128), jnp.bfloat16),
                pltpu.VMEM((total // BK, DH + 16, BK), jnp.bfloat16),
            ],
        ),
        cost_estimate=cost(250),
        name="attend",
    )(lengths, qkv, ok)


def bwd_kernel(utts, chunk, lengths_ref, qkv_ref, ok_ref, o_ref, do_ref, lse_ref, out_ref, kaug, vnat, kT_s, dk, dv):
    sources, _, frames = qkv_ref.shape
    per = frames // BK
    pad_u = aug_rows(utts)
    step = pl.program_id(0)
    f32 = jnp.float32

    @pl.when(step == 0)
    def _():
        def build(s, c):
            hot = onehot_rows(lengths_ref, utts, pad_u, s * frames, frames)
            ok = ok_ref[s]
            block = qkv_ref[s]
            one = jnp.ones((1, frames), f32)
            kT = block[DH : 2 * DH]
            vT = block[2 * DH :]
            kA = pad_rows(
                [kT, (1.0 - hot).astype(jnp.bfloat16), rows16([1.0 - ok.astype(f32), one, one, one], frames)], 128
            )
            rows = pl.ds(pl.multiple_of(s * frames, frames), frames)
            kaug[rows, :] = kA.T
            vnat[rows, :] = pad_rows([vT, rows16([one, one, one], frames)], 128).T
            qT = block[:DH].astype(f32) * 0.125
            do = do_ref[s, chunk * DH : (chunk + 1) * DH, :].astype(f32)
            s_self = jnp.sum(qT * kT.astype(f32), axis=0, keepdims=True)
            delta = jnp.sum(do * o_ref[s].astype(f32), axis=0, keepdims=True)
            p_self = jnp.where(ok > 0, 0.0, jnp.exp(s_self - lse_ref[s]))
            ds_self = p_self * (jnp.sum(do * vT.astype(f32), axis=0, keepdims=True) - delta)
            dk0 = ds_self * qT
            dv0 = p_self * do
            for t in range(per):
                cols = slice(t * BK, (t + 1) * BK)
                kT_s[s * per + t] = kT[:, cols]
                dk[s * per + t] = dk0[:, cols]
                dv[s * per + t] = dv0[:, cols]
            return c

        lax.fori_loop(0, sources, build, 0)

    block = qkv_ref[step]
    one = jnp.ones((1, frames), f32)
    hot_q = onehot_rows(lengths_ref, utts, pad_u, step * frames, frames)
    qT = block[:DH].astype(f32) * 0.125
    qTb = qT.astype(jnp.bfloat16)
    kT = block[DH : 2 * DH].astype(f32)
    vT = block[2 * DH :].astype(f32)
    ok = ok_ref[step]
    dob = do_ref[step, chunk * DH : (chunk + 1) * DH, :]
    do = dob.astype(f32)
    lse = lse_ref[step]
    delta = jnp.sum(do * o_ref[step].astype(f32), axis=0, keepdims=True)
    l3 = [-r.astype(f32) for r in split3(lse)]
    d3 = [-r.astype(f32) for r in split3(delta)]
    qaug = pad_rows([qTb, (hot_q * -BIG).astype(jnp.bfloat16), rows16([one * -BIG] + l3, frames)], 128)
    doaug = pad_rows([dob, rows16(d3, frames)], 128)
    s_self = jnp.sum(qT * kT, axis=0, keepdims=True)
    p_self = jnp.where(ok > 0, 0.0, jnp.exp(s_self - lse))
    ds_self = p_self * (jnp.sum(do * vT, axis=0, keepdims=True) - delta)
    dq0 = ds_self * kT
    nt = (((1,), (1,)), ((), ()))
    for t in range(frames // BQ):
        cols = slice(t * BQ, (t + 1) * BQ)
        low, high = key_range(lengths_ref, utts, step * frames + t * BQ, step * frames + (t + 1) * BQ - 1)
        q_a = qaug[:, cols]
        q_b = qTb[:, cols]
        do_a = doaug[:, cols]
        do_b = dob[:, cols]

        def body(j, dq):
            rows = pl.ds(pl.multiple_of(j * BK, BK), BK)
            s = jnp.dot(kaug[rows, :], q_a, preferred_element_type=f32)
            dp = jnp.dot(vnat[rows, :], do_a, preferred_element_type=f32)
            p = jnp.exp(s)
            ds = (p * dp).astype(jnp.bfloat16)
            dv[j] += lax.dot_general(do_b, p.astype(jnp.bfloat16), nt, preferred_element_type=f32)
            dk[j] += lax.dot_general(q_b, ds, nt, preferred_element_type=f32)
            return dq + jnp.dot(kT_s[j], ds, preferred_element_type=f32)

        dq = lax.fori_loop(low, high, body, dq0[:, cols])
        out_ref[step, :DH, cols] = (dq * 0.125).astype(jnp.bfloat16)

    @pl.when(step == sources - 1)
    def _():
        def finish(s, c):
            for t in range(per):
                cols = slice(t * BK, (t + 1) * BK)
                out_ref[s, DH : 2 * DH, cols] = dk[s * per + t].astype(jnp.bfloat16)
                out_ref[s, 2 * DH :, cols] = dv[s * per + t].astype(jnp.bfloat16)
            return c

        lax.fori_loop(0, sources, finish, 0)


def attend_back(lengths, qkv, ok, out, grad, lse, chunk):
    sources, _, frames = qkv.shape
    total = sources * frames
    utts = lengths.shape[0]
    whole = lambda shape: pl.BlockSpec(shape, lambda i, *_: (0,) * len(shape))
    return pl.pallas_call(
        functools.partial(bwd_kernel, utts, chunk),
        out_shape=jax.ShapeDtypeStruct(qkv.shape, jnp.bfloat16),
        grid_spec=pltpu.PrefetchScalarGridSpec(
            num_scalar_prefetch=1,
            grid=(sources,),
            in_specs=[whole(a.shape) for a in (qkv, ok, out, grad, lse)],
            out_specs=whole(qkv.shape),
            scratch_shapes=[
                pltpu.VMEM((total, 128), jnp.bfloat16),
                pltpu.VMEM((total, 128), jnp.bfloat16),
                pltpu.VMEM((total // BK, DH, BK), jnp.bfloat16),
                pltpu.VMEM((total // BK, DH, BK), jnp.float32),
                pltpu.VMEM((total // BK, DH, BK), jnp.float32),
            ],
        ),
        cost_estimate=cost(320),
        name="attend_back",
    )(lengths, qkv, ok, out, grad, lse)


FF_TILE = 512
EPS = 1e-06


def dot(left, right):
    return jnp.dot(left, right, preferred_element_type=jnp.float32)


def dot_nt(left, right):
    return lax.dot_general(left, right, (((1,), (1,)), ((), ())), preferred_element_type=jnp.float32)


def norm_stats(x):
    mean = jnp.mean(x, axis=1, keepdims=True)
    centred = x - mean
    rstd = lax.rsqrt(jnp.mean(centred * centred, axis=1, keepdims=True) + EPS)
    return centred * rstd, rstd


def norm_back(grad, normed, rstd):
    first = jnp.mean(grad, axis=1, keepdims=True)
    second = jnp.mean(grad * normed, axis=1, keepdims=True)
    return rstd * (grad - first - normed * second)


def mods_operand(mods_ref):
    rows = mods_ref[...]
    return pad_rows(list(split3(rows)), 128)


def table_rows(utts):
    return -(-utts // 8) * 8


def sum_rows(hot, utts_pad, frames):
    idx = lax.broadcasted_iota(jnp.int32, (16, frames), 0)
    ones = jnp.where(idx == 0, 1.0, 0.0).astype(jnp.bfloat16)
    return jnp.concatenate([hot.astype(jnp.bfloat16), ones], axis=0)


def mid_kernel(
    dims,
    lengths_ref,
    ids_ref,
    *refs,
):
    seq_ways, heads_local, utts, ff = dims
    att_refs = refs[:heads_local]
    (
        hidden_ref,
        mods_ref,
        cot_ref,
        loss_ref,
        w_out_ref,
        b_out_ref,
        w_up_ref,
        b_up_ref,
        w_down_ref,
        b_down_ref,
    ) = refs[heads_local : heads_local + 10]
    outs = refs[heads_local + 10 :]
    output_ref, after_grad_ref, small_ref, gatt_ref = outs[:4]
    refs_out = outs[4:6]
    (
        attT,
        attn_proj,
        after,
        nf,
        nfT,
        gff,
        ff_acc,
        gnf_acc,
        sums,
        cols,
        madd,
        grads,
        sems,
    ) = outs[6:]
    f32, bf16 = jnp.float32, jnp.bfloat16
    step = pl.program_id(0)
    steps = pl.num_programs(0)
    core = ids_ref[0]
    rank = ids_ref[1]
    frames, width = hidden_ref.shape
    up_rows = width // seq_ways
    down_rows = FF_TILE
    z_ways = seq_ways // 2
    parts = grads.shape[1]
    pad_u = table_rows(utts)
    ff_total = ff
    up_part = ff_total // width * up_rows // parts
    down_block = ff_total // seq_ways
    down_part = down_block // parts
    out_part = up_rows // parts

    def mod(index):
        return dot(cols[...], madd[:, index * width : (index + 1) * width])

    def grad_out():
        loss = cols[:, 48:49].astype(f32)
        return cot_ref[...].astype(f32) * loss

    @pl.when(step == 0)
    def _():
        hot = onehot_rows(lengths_ref, utts, 16, rank * frames, frames)
        hotb = hot.astype(bf16)
        idx = lax.broadcasted_iota(jnp.int32, (16, frames), 0)
        loss = jnp.where(idx == 0, loss_ref[...].astype(f32), 0.0).astype(bf16)
        cols[...] = pad_rows([hotb, hotb, hotb, loss], 128).T
        sums[...] = sum_rows(hot, 16, frames)
        madd[...] = mods_operand(mods_ref)
        for c in range(heads_local):
            for s in range(seq_ways):
                attT[(c * seq_ways + s) * DH : (c * seq_ways + s + 1) * DH, :] = att_refs[c][s]
        proj = dot(attT[...].T, w_out_ref[...]) + b_out_ref[...].astype(f32)
        attn_proj[...] = proj
        mixed = hidden_ref[...] + mod(0) * proj
        after[...] = mixed
        normed, _ = norm_stats(mixed)
        value = (normed * (1.0 + mod(2)) + mod(1)).astype(bf16)
        nf[...] = value
        nfT[...] = value.T
        gff[...] = (grad_out() * mod(3)).astype(bf16)
        small_ref[4 * pad_u :, :] = jnp.zeros((8, width), f32)

    up = dot(nf[...], w_up_ref[...]) + b_up_ref[...].astype(f32)
    inner = 0.7978845608028654 * (up + 0.044715 * (up * up * up))
    tanh = jnp.tanh(inner)
    cdf = 0.5 * (1.0 + tanh)
    act = (up * cdf).astype(bf16)
    slope = cdf + 0.5 * up * (1.0 - tanh * tanh) * (
        0.7978845608028654 * (1.0 + (3 * 0.044715) * (up * up))
    )
    ff_part = dot(act, w_down_ref[...])
    gup = (dot_nt(gff[...], w_down_ref[...]) * slope).astype(bf16)
    gnf_part = dot_nt(gup, w_up_ref[...])

    @pl.when(step == 0)
    def _():
        ff_acc[...] = ff_part
        gnf_acc[...] = gnf_part

    @pl.when(step > 0)
    def _():
        ff_acc[...] += ff_part
        gnf_acc[...] += gnf_part

    halves = width // FF_TILE
    chunk = step // halves
    half = step % halves
    col = pl.ds(pl.multiple_of(half * FF_TILE, FF_TILE), FF_TILE)
    per_chunk = up_rows // up_part
    small_ref[pl.ds(4 * pad_u + 2 + chunk, 1), col] = dot(sums[16:32, :], gup)[:1]
    grad_w_up = dot(nfT[...], gup).astype(bf16)
    for s in range(seq_ways):
        side = jnp.where(core == s % 2, 0, 1)
        for h in range(per_chunk):
            lo = s * up_rows + h * up_part
            grads[side, chunk * per_chunk + h, s // 2, 0:up_part, col] = grad_w_up[lo : lo + up_part]
    grad_w_down = dot(act.T, gff[...]).astype(bf16)
    blocks = FF_TILE // down_block
    copies = []
    for b in range(blocks):
        s = step * blocks + b
        side = jnp.where(core == s % 2, 0, 1)
        for k in range(parts):
            lo = b * down_block + k * down_part
            grads[side, k, s // 2, up_part : up_part + down_part, :] = grad_w_down[lo : lo + down_part]

    def region_copy(side, where, index):
        return pltpu.make_async_copy(
            grads.at[side].at[where], refs_out[side].at[where], sems.at[side, index]
        )

    def up_copy(side, j):
        where = (
            pl.ds((j // halves) * per_chunk, per_chunk),
            slice(None),
            pl.ds(0, up_part),
            pl.ds(pl.multiple_of((j % halves) * FF_TILE, FF_TILE), FF_TILE),
        )
        return region_copy(side, where, j)

    def down_copy(side, z, index):
        return region_copy(side, (slice(None), pl.ds(z, 1), pl.ds(up_part, down_part)), index)

    def out_copy(side):
        where = (slice(None), slice(None), pl.ds(up_part + down_part, out_part))
        return region_copy(side, where, ff_total // FF_TILE + z_ways)

    base = ff_total // FF_TILE
    for side in range(2):
        up_copy(side, step).start()
    for b in range(blocks):
        s = step * blocks + b
        for side in range(2):

            @pl.when(lax.rem(s + core, 2) == side)
            def _():
                down_copy(side, s // 2, base + s // 2).start()

    @pl.when(step == steps - 1)
    def _():
        ff_out = ff_acc[...] + b_down_ref[...].astype(f32)
        mixed = after[...]
        go = grad_out()
        output_ref[...] = (mixed + mod(3) * ff_out).astype(bf16)
        rows = sums[...]
        small_ref[3 * pad_u : 4 * pad_u, :] = dot(rows, (go * ff_out).astype(bf16))[:pad_u]
        normed, rstd = norm_stats(mixed)
        gnf = gnf_acc[...]
        small_ref[pad_u : 2 * pad_u, :] = dot(rows, gnf.astype(bf16))[:pad_u]
        small_ref[2 * pad_u : 3 * pad_u, :] = dot(rows, (gnf * normed).astype(bf16))[:pad_u]
        g_after = go + norm_back(gnf * (1.0 + mod(2)), normed, rstd)
        after_grad_ref[...] = g_after
        small_ref[0:pad_u, :] = dot(rows, (g_after * attn_proj[...]).astype(bf16))[:pad_u]
        gattn = (g_after * mod(0)).astype(bf16)
        small_ref[4 * pad_u : 4 * pad_u + 1, :] = dot(rows, gattn)[16:17]
        small_ref[4 * pad_u + 1 : 4 * pad_u + 2, :] = dot(rows, gff[...])[16:17]
        gattT = dot_nt(w_out_ref[...], gattn).astype(bf16)
        for c in range(heads_local):
            for s in range(seq_ways):
                lo = (c * seq_ways + s) * DH
                gatt_ref[s, c * DH : (c + 1) * DH, :] = gattT[lo : lo + DH]
        grad_w_out = dot(attT[...], gattn).astype(bf16)
        for s in range(seq_ways):
            side = jnp.where(core == s % 2, 0, 1)
            for k in range(parts):
                lo = s * up_rows + k * out_part
                grads[side, k, s // 2, up_part + down_part : up_part + down_part + out_part, :] = grad_w_out[
                    lo : lo + out_part
                ]
        for side in range(2):
            out_copy(side).start()
        for side in range(2):
            for j in range(ff_total // FF_TILE):
                up_copy(side, j).wait()
            for z in range(z_ways):
                down_copy(side, z, base + z).wait()
            out_copy(side).wait()


def mid_block(
    lengths, ids, att, hidden, mods, cot, loss, w_out, b_out, w_up, b_up, w_down, b_down, parts
):
    frames, width = hidden.shape
    heads_local = len(att)
    seq_ways = att[0].shape[0]
    ff = w_up.shape[1]
    up_rows = width // seq_ways
    rows = (ff // width * up_rows + ff // seq_ways + up_rows) // parts
    utts = lengths.shape[0]
    f32, bf16 = jnp.float32, jnp.bfloat16
    steps = ff // FF_TILE

    def whole(shape):
        return pl.BlockSpec(shape, lambda j, *_: (0,) * len(shape), pipeline_mode=pl.Buffered(1))

    hbm = pl.BlockSpec(memory_space=pl.ANY)
    gshape = (parts, seq_ways // 2, rows, width)
    out_shape = [
        jax.ShapeDtypeStruct((frames, width), bf16),
        jax.ShapeDtypeStruct((frames, width), f32),
        jax.ShapeDtypeStruct((4 * table_rows(utts) + 8, width), f32),
    ]
    out_shape += [jax.ShapeDtypeStruct((seq_ways, heads_local * DH, frames), bf16)]
    out_specs = [whole(o.shape) for o in out_shape] + [hbm] * 2
    out_shape += [jax.ShapeDtypeStruct(gshape, bf16)] * 2
    ins = list(att) + [hidden, mods, cot, loss, w_out, b_out]
    return pl.pallas_call(
        functools.partial(mid_kernel, (seq_ways, heads_local, utts, ff)),
        out_shape=out_shape,
        grid_spec=pltpu.PrefetchScalarGridSpec(
            num_scalar_prefetch=2,
            grid=(steps,),
            in_specs=[whole(a.shape) for a in ins]
            + [
                pl.BlockSpec((width, FF_TILE), lambda j, *_: (0, j)),
                pl.BlockSpec((1, FF_TILE), lambda j, *_: (0, j)),
                pl.BlockSpec((FF_TILE, width), lambda j, *_: (j, 0)),
                whole((1, width)),
            ],
            out_specs=out_specs,
            scratch_shapes=[
                pltpu.VMEM((width, frames), bf16),
                pltpu.VMEM((frames, width), f32),
                pltpu.VMEM((frames, width), f32),
                pltpu.VMEM((frames, width), bf16),
                pltpu.VMEM((width, frames), bf16),
                pltpu.VMEM((frames, width), bf16),
                pltpu.VMEM((frames, width), f32),
                pltpu.VMEM((frames, width), f32),
                pltpu.VMEM((32, frames), bf16),
                pltpu.VMEM((frames, 128), bf16),
                pltpu.VMEM((128, 4 * width), bf16),
                pltpu.VMEM((2,) + gshape, bf16),
                pltpu.SemaphoreType.DMA((2, steps + seq_ways // 2 + 1)),
            ],
        ),
        compiler_params=pltpu.CompilerParams(vmem_limit_bytes=63 << 20),
        cost_estimate=cost(500),
        name="mid_block",
    )(lengths, ids, *ins, w_up, b_up, w_down, b_down)


def whole_block(shape):
    return pl.BlockSpec(shape, lambda *_: (0,) * len(shape), pipeline_mode=pl.Buffered(1))


def segment_rows(lengths_ref, drop_ref, utts, base, width):
    col = base + lax.broadcasted_iota(jnp.int32, (1, width), 1)
    start = jnp.int32(0)
    kept = jnp.zeros((1, width), jnp.float32)
    place = jnp.zeros((1, width), jnp.int32)
    for u in range(utts):
        end = start + lengths_ref[u]
        inside = (col >= start) & (col < end)
        kept = jnp.where(inside, (1 - drop_ref[u]).astype(jnp.float32), kept)
        place = jnp.where(inside, col - start, place)
        start = end
    return kept, place.astype(jnp.float32)


def rotary_rows(place, half):
    index = lax.broadcasted_iota(jnp.int32, (half, 1), 0).astype(jnp.float32)
    inverse = jnp.exp(index * (-9.210340371976184 / half))
    angles = inverse * place
    return jnp.cos(angles), jnp.sin(angles)


def frame_columns(hot, extra):
    hotb = hot.astype(jnp.bfloat16)
    idx = lax.broadcasted_iota(jnp.int32, hot.shape, 0)
    last = jnp.where(idx == 0, extra, 0.0).astype(jnp.bfloat16)
    return pad_rows([hotb, hotb, hotb, last], 128).T


def head_kernel(
    utts,
    lengths_ref,
    ids_ref,
    drop_ref,
    tokens_ref,
    skip_ref,
    cond_ref,
    mods_ref,
    w_skip_ref,
    b_skip_ref,
    hidden_ref,
    joinedT_ref,
    naT_ref,
    na_ref,
    cols,
):
    f32, bf16 = jnp.float32, jnp.bfloat16
    step = pl.program_id(0)
    frames, width = tokens_ref.shape
    rank = ids_ref[1]

    @pl.when(step == 0)
    def _():
        hot = onehot_rows(lengths_ref, utts, 16, rank * frames, frames)
        kept, _ = segment_rows(lengths_ref, drop_ref, utts, rank * frames, frames)
        cols[...] = frame_columns(hot, kept)
        keep = cols[:, 48:49].astype(f32)
        mixed = (tokens_ref[...].astype(f32) + keep * cond_ref[...].astype(f32)).astype(bf16)
        joinedT_ref[0:width, :] = mixed.T
        hidden_ref[...] = dot(mixed, w_skip_ref[...]) + b_skip_ref[...].astype(f32)

    @pl.when(step == 1)
    def _():
        skip = skip_ref[...]
        joinedT_ref[width : 2 * width, :] = skip.T
        hidden = hidden_ref[...] + dot(skip, w_skip_ref[...])
        hidden_ref[...] = hidden
        madd = mods_operand(mods_ref)
        shift = dot(cols[...], madd[:, :width])
        scale = dot(cols[...], madd[:, width:])
        normed, _ = norm_stats(hidden)
        value = (normed * (1.0 + scale) + shift).astype(bf16)
        na_ref[...] = value
        naT_ref[...] = value.T


def head_block(lengths, ids, drop, tokens, skip, cond, mods, w_skip, b_skip):
    frames, width = tokens.shape
    utts = lengths.shape[0]
    f32, bf16 = jnp.float32, jnp.bfloat16

    def whole(shape):
        return pl.BlockSpec(shape, lambda j, *_: (0,) * len(shape), pipeline_mode=pl.Buffered(1))

    out_shape = [
        jax.ShapeDtypeStruct((frames, width), f32),
        jax.ShapeDtypeStruct((2 * width, frames), bf16),
        jax.ShapeDtypeStruct((width, frames), bf16),
        jax.ShapeDtypeStruct((frames, width), bf16),
    ]
    return pl.pallas_call(
        functools.partial(head_kernel, utts),
        out_shape=out_shape,
        grid_spec=pltpu.PrefetchScalarGridSpec(
            num_scalar_prefetch=3,
            grid=(2,),
            in_specs=[whole(a.shape) for a in (tokens, skip, cond, mods)]
            + [pl.BlockSpec((width, width), lambda j, *_: (j, 0)), whole((1, width))],
            out_specs=[whole(o.shape) for o in out_shape],
            scratch_shapes=[pltpu.VMEM((frames, 128), bf16)],
        ),
        compiler_params=pltpu.CompilerParams(vmem_limit_bytes=48 << 20),
        cost_estimate=cost(100),
        name="head_block",
    )(lengths, ids, drop, tokens, skip, cond, mods, w_skip, b_skip)


def turn_heads(tensor, cosine, sine):
    half = DH // 2
    first, second = tensor[:, :half], tensor[:, half:]
    return jnp.concatenate([first * cosine - second * sine, second * cosine + first * sine], axis=1)


def qkv_kernel(utts, seq_ways, lengths_ref, ids_ref, drop_ref, na_ref, w_ref, b_ref, out_ref, trig):
    f32, bf16 = jnp.float32, jnp.bfloat16
    part = pl.program_id(0)
    frames = na_ref.shape[0]

    @pl.when(part == 0)
    def _():
        _, place = segment_rows(lengths_ref, drop_ref, utts, ids_ref[1] * frames, frames)
        cosine, sine = rotary_rows(place, DH // 2)
        trig[0] = cosine
        trig[1] = sine

    raw = dot(na_ref[...], w_ref[...]) + b_ref[...].astype(f32)
    rawT = raw.T.reshape(seq_ways, DH, frames)
    turned = part < 2
    cosine = jnp.where(turned, trig[0], 1.0)[None]
    sine = jnp.where(turned, trig[1], 0.0)[None]
    out_ref[:, pl.ds(pl.multiple_of(part * DH, DH), DH), :] = turn_heads(rawT, cosine, sine).astype(bf16)


def qkv_block(lengths, ids, drop, na, w_qkv, b_qkv, chunk, seq_ways):
    frames, width = na.shape
    cols = seq_ways * DH
    chunks = width // cols
    utts = lengths.shape[0]

    def whole(shape):
        return pl.BlockSpec(shape, lambda j, *_: (0,) * len(shape), pipeline_mode=pl.Buffered(1))

    shape = (seq_ways, 3 * DH, frames)
    return pl.pallas_call(
        functools.partial(qkv_kernel, utts, seq_ways),
        out_shape=jax.ShapeDtypeStruct(shape, jnp.bfloat16),
        grid_spec=pltpu.PrefetchScalarGridSpec(
            num_scalar_prefetch=3,
            grid=(3,),
            in_specs=[
                whole(na.shape),
                pl.BlockSpec((width, cols), lambda j, *_: (0, j * chunks + chunk)),
                pl.BlockSpec((1, cols), lambda j, *_: (0, j * chunks + chunk)),
            ],
            out_specs=whole(shape),
            scratch_shapes=[pltpu.VMEM((2, DH // 2, frames), jnp.float32)],
        ),
        cost_estimate=cost(75),
        name="qkv_block",
    )(lengths, ids, drop, na, w_qkv, b_qkv)


def back_kernel(utts, seq_ways, chunk, lengths_ref, ids_ref, drop_ref, grad_ref, naT_ref, w_ref, *refs):
    first = chunk == 0
    acc_in = None if first else refs[0]
    acc_ref, bias_ref, keep_ref, send_ref, trig, grads, sems = refs[0 if first else 3 :]
    f32, bf16 = jnp.float32, jnp.bfloat16
    part = pl.program_id(0)
    width, frames = naT_ref.shape
    core = ids_ref[0]
    parts = keep_ref.shape[0]
    own = width // seq_ways
    rows = own // parts

    @pl.when(part == 0)
    def _():
        _, place = segment_rows(lengths_ref, drop_ref, utts, ids_ref[1] * frames, frames)
        cosine, sine = rotary_rows(place, DH // 2)
        trig[0] = cosine
        trig[1] = sine

    turned = part < 2
    cosine = jnp.where(turned, trig[0], 1.0)[None]
    sine = jnp.where(turned, trig[1], 0.0)[None]
    raw = grad_ref[:, pl.ds(pl.multiple_of(part * DH, DH), DH), :].astype(f32)
    gpT = turn_heads(raw, cosine, -sine).astype(bf16).reshape(seq_ways * DH, frames)
    gna = dot(w_ref[...], gpT)

    @pl.when(part == 0)
    def _():
        acc_ref[...] = gna if first else acc_in[...] + gna

    @pl.when(part > 0)
    def _():
        acc_ref[...] += gna

    ones = jnp.ones((8, frames), bf16)
    bias_ref[0] = dot_nt(ones, gpT)
    grad_w = dot_nt(naT_ref[...], gpT).astype(bf16)
    cols = seq_ways * DH
    at = pl.ds(pl.multiple_of(part * rows, rows), rows)
    for s in range(seq_ways):
        side = jnp.where(core == s % 2, 0, 1)
        for k in range(parts):
            lo = s * own + k * rows
            grads[side, k, s // 2, at, :] = grad_w[lo : lo + rows]

    def copy(side, p):
        where = (slice(None), slice(None), pl.ds(pl.multiple_of(p * rows, rows), rows))
        return pltpu.make_async_copy(
            grads.at[side].at[where],
            (keep_ref, send_ref)[side].at[(*where, pl.ds(chunk * cols, cols))],
            sems.at[side, p],
        )

    for side in (1, 0):
        copy(side, part).start()

    @pl.when(part == 2)
    def _():
        for side in (1, 0):
            for p in range(3):
                copy(side, p).wait()


def back_block(lengths, ids, drop, grad, naT, w_qkv, before, chunk, parts):
    seq_ways, _, frames = grad.shape
    width = naT.shape[0]
    cols = seq_ways * DH
    chunks = width // cols
    utts = lengths.shape[0]
    f32, bf16 = jnp.float32, jnp.bfloat16
    rows = width // seq_ways // parts

    def whole(shape):
        return pl.BlockSpec(shape, lambda j, *_: (0,) * len(shape), pipeline_mode=pl.Buffered(1))

    gspec = pl.BlockSpec(memory_space=pl.ANY)
    gshape = jax.ShapeDtypeStruct((parts, seq_ways // 2, 3 * rows, width), bf16)
    ins = [grad, naT, w_qkv, *before]
    in_specs = [whole(grad.shape), whole(naT.shape)]
    in_specs += [pl.BlockSpec((width, cols), lambda j, *_: (0, j * chunks + chunk))]
    aliases = {}
    if before:
        in_specs += [whole(before[0].shape), gspec, gspec]
        aliases = {7: 2, 8: 3}
    return pl.pallas_call(
        functools.partial(back_kernel, utts, seq_ways, chunk),
        out_shape=[
            jax.ShapeDtypeStruct((width, frames), f32),
            jax.ShapeDtypeStruct((3, 8, cols), f32),
            gshape,
            gshape,
        ],
        grid_spec=pltpu.PrefetchScalarGridSpec(
            num_scalar_prefetch=3,
            grid=(3,),
            in_specs=in_specs,
            out_specs=[
                whole((width, frames)),
                pl.BlockSpec((1, 8, cols), lambda j, *_: (j, 0, 0)),
                gspec,
                gspec,
            ],
            scratch_shapes=[
                pltpu.VMEM((2, DH // 2, frames), f32),
                pltpu.VMEM((2, parts, seq_ways // 2, 3 * rows, cols), bf16),
                pltpu.SemaphoreType.DMA((2, 3)),
            ],
        ),
        compiler_params=pltpu.CompilerParams(vmem_limit_bytes=48 << 20),
        cost_estimate=cost(100),
        input_output_aliases=aliases,
        name="back_block",
    )(lengths, ids, drop, *ins)


def norm_kernel(
    utts, heads_local, lengths_ref, ids_ref, acc_ref, hidden_ref, after_ref, mods_ref, loss_ref, mid_ref, *refs
):
    f32, bf16 = jnp.float32, jnp.bfloat16
    bias_refs, (gh_ref, small_ref) = refs[:heads_local], refs[heads_local:]
    frames, width = hidden_ref.shape
    pad_u = table_rows(utts)
    base = 6 * pad_u
    hot = onehot_rows(lengths_ref, utts, 16, ids_ref[1] * frames, frames)
    cols = frame_columns(hot, jnp.zeros((1, frames), f32))
    madd = mods_operand(mods_ref)
    scale = dot(cols, madd[:, width:])
    gna = acc_ref[...].T
    normed, rstd = norm_stats(hidden_ref[...])
    sums = sum_rows(hot, 16, frames)
    small_ref[0:pad_u, :] = dot(sums, gna.astype(bf16))[:pad_u]
    small_ref[pad_u : 2 * pad_u, :] = dot(sums, (gna * normed).astype(bf16))[:pad_u]
    gh = (after_ref[...] + norm_back(gna * (1.0 + scale), normed, rstd)).astype(bf16)
    gh_ref[...] = gh
    small_ref[2 * pad_u : base, :] = mid_ref[0 : 4 * pad_u, :]
    cols_local = width // heads_local
    for c in range(heads_local):
        for p in range(3):
            small_ref[base + p : base + p + 1, c * cols_local : (c + 1) * cols_local] = bias_refs[c][p, 0:1, :]
    small_ref[base + 3 : base + 4, :] = dot(sums, gh)[16:17]
    small_ref[base + 4 : base + 12, :] = mid_ref[4 * pad_u : 4 * pad_u + 8, :]
    count = jnp.sum(loss_ref[...].astype(f32), axis=1, keepdims=True)
    high = jnp.floor(count / 32.0) * 32.0
    small_ref[base + 12 : base + 13, :] = jnp.broadcast_to(high, (1, width))
    small_ref[base + 13 : base + 16, :] = jnp.broadcast_to(count - high, (3, width))


def norm_block(lengths, ids, acc, hidden, after, mods, loss, mid_small, biases):
    frames, width = hidden.shape
    utts = lengths.shape[0]
    out_shape = [
        jax.ShapeDtypeStruct((frames, width), jnp.bfloat16),
        jax.ShapeDtypeStruct((6 * table_rows(utts) + 16, width), jnp.float32),
    ]
    return pl.pallas_call(
        functools.partial(norm_kernel, utts, len(biases)),
        out_shape=out_shape,
        grid_spec=pltpu.PrefetchScalarGridSpec(
            num_scalar_prefetch=2,
            grid=(1,),
            in_specs=[whole_block(a.shape) for a in (acc, hidden, after, mods, loss, mid_small, *biases)],
            out_specs=[whole_block(o.shape) for o in out_shape],
        ),
        compiler_params=pltpu.CompilerParams(vmem_limit_bytes=48 << 20),
        cost_estimate=cost(50),
        name="norm_block",
    )(lengths, ids, acc, hidden, after, mods, loss, mid_small, *biases)


def skip_kernel(seq_ways, ids_ref, joinedT_ref, gh_ref, keep_ref, send_ref, grads, sems):
    step = pl.program_id(0)
    core = ids_ref[0]
    parts = keep_ref.shape[0]
    width = joinedT_ref.shape[0]
    block = 2 * width // seq_ways
    rows = block // parts
    z_step = seq_ways // 4
    grad_w = dot(joinedT_ref[...], gh_ref[...]).astype(jnp.bfloat16)
    for b in range(width // block):
        side = jnp.where(core == b % 2, 0, 1)
        for k in range(parts):
            lo = b * block + k * rows
            grads[side, k, step * z_step + b // 2] = grad_w[lo : lo + rows]

    def copy(side, at):
        where = (slice(None), pl.ds(at * z_step, z_step))
        return pltpu.make_async_copy(
            grads.at[side].at[where], (keep_ref, send_ref)[side].at[where], sems.at[side, at]
        )

    for side in (1, 0):
        copy(side, step).start()

    @pl.when(step == 1)
    def _():
        for side in (1, 0):
            for at in range(2):
                copy(side, at).wait()


def skip_block(ids, joinedT, gh, seq_ways, parts):
    frames, width = gh.shape
    rows = 2 * width // seq_ways // parts
    gshape = (parts, seq_ways // 2, rows, width)
    return pl.pallas_call(
        functools.partial(skip_kernel, seq_ways),
        out_shape=[jax.ShapeDtypeStruct(gshape, jnp.bfloat16)] * 2,
        grid_spec=pltpu.PrefetchScalarGridSpec(
            num_scalar_prefetch=1,
            grid=(2,),
            in_specs=[pl.BlockSpec((width, frames), lambda j, *_: (j, 0)), whole_block(gh.shape)],
            out_specs=[pl.BlockSpec(memory_space=pl.ANY)] * 2,
            scratch_shapes=[pltpu.VMEM((2,) + gshape, jnp.bfloat16), pltpu.SemaphoreType.DMA((2, 2))],
        ),
        compiler_params=pltpu.CompilerParams(vmem_limit_bytes=32 << 20),
        cost_estimate=cost(50),
        name="skip_block",
    )(ids, joinedT, gh)


def joined_kernel(gh_ref, w_ref, scale_ref, first_ref, second_ref):
    step = pl.program_id(0)
    value = dot_nt(gh_ref[...], w_ref[...]) * scale_ref[0:1, 0:1]

    @pl.when(step == 0)
    def _():
        first_ref[...] = value

    @pl.when(step == 1)
    def _():
        second_ref[...] = value


def joined_block(gh, w_skip, scale):
    frames, width = gh.shape
    out = jax.ShapeDtypeStruct((frames, width), jnp.float32)
    return pl.pallas_call(
        joined_kernel,
        out_shape=[out, out],
        grid_spec=pltpu.PrefetchScalarGridSpec(
            num_scalar_prefetch=0,
            grid=(2,),
            in_specs=[
                whole_block(gh.shape),
                pl.BlockSpec((width, width), lambda j: (j, 0)),
                whole_block(scale.shape),
            ],
            out_specs=[whole_block(out.shape)] * 2,
        ),
        compiler_params=pltpu.CompilerParams(vmem_limit_bytes=32 << 20),
        cost_estimate=cost(50),
        name="joined_block",
    )(gh, w_skip, scale)


def add_bf16(left, right):
    return (left.astype(jnp.float32) + right.astype(jnp.float32)).astype(jnp.bfloat16)


def first_kernel(pairs, splits, ids_ref, *refs):
    ins, outs = refs[: 8 * pairs], list(refs[8 * pairs :])
    for i in range(4):
        own = [outs.pop(0) for _ in range(splits if i < 2 else 1)]
        at = 0
        for p in range(pairs):
            left, right = ins[2 * (i * pairs + p)], ins[2 * (i * pairs + p) + 1]
            rows = left.shape[-2]
            value = add_bf16(left[0, 0, 0], right[0, 0, 0])
            if len(own) == 1:
                own[0][0, :, at : at + rows, :] = value
            else:
                for out in own:
                    out[0] = value[:, at : at + out.shape[2], :]
                    at += out.shape[2]
            at += rows


def first_sum(ids, pairs, splits):
    _, _, _, z_ways, _, width = pairs[0][0].shape
    total = sum(k.shape[4] for k, _ in pairs)
    step = 1 if total > 100 else z_ways

    def source(half, axis, mine, rows):
        def at(g, z, ids):
            bit = ids[axis]
            return half, bit if mine else 1 - bit, g, z, 0, 0

        return pl.BlockSpec((1, 1, 1, step, rows, width), at)

    order = [(0, 2, False), (1, 3, False), (0, 2, True), (1, 3, True)]
    sizes = [*splits, *splits, total, total]
    return pl.pallas_call(
        functools.partial(first_kernel, len(pairs), len(splits)),
        out_shape=[jax.ShapeDtypeStruct((2, z_ways, n, width), jnp.bfloat16) for n in sizes],
        grid_spec=pltpu.PrefetchScalarGridSpec(
            num_scalar_prefetch=1,
            grid=(2, z_ways // step),
            in_specs=[source(*o, a.shape[4]) for o in order for pair in pairs for a in pair],
            out_specs=[pl.BlockSpec((1, step, n, width), lambda g, z, ids: (g, z, 0, 0)) for n in sizes],
        ),
        compiler_params=pltpu.CompilerParams(vmem_limit_bytes=48 << 20),
        cost_estimate=cost(60),
        name="first_sum",
    )(ids, *([a for pair in pairs for a in pair] * 4))


def second_kernel(pieces, ids_ref, *refs):
    for i in range(4):
        keep, *got = refs[(pieces + 1) * i : (pieces + 1) * (i + 1)]
        out = refs[4 * (pieces + 1) + i]
        at = 0
        for g in got:
            rows = g.shape[2]
            out[:, at : at + rows, :] = add_bf16(keep[0, :, at : at + rows, :], g[0])
            at += rows


def second_sum(ids, keep_a, got_a, keep_b, got_b):
    _, z_ways, rows, width = keep_a.shape
    step = z_ways // 2 if rows > 100 else z_ways

    def source(axis, mine, value):
        def at(z, ids):
            bit = ids[axis]
            return bit if mine else 1 - bit, z, 0, 0

        return pl.BlockSpec((1, step, *value.shape[2:]), at)

    order = [(3, False), (2, False), (3, True), (2, True)]
    sides = [[keep_a, *got_a], [keep_b, *got_b]]
    out = jax.ShapeDtypeStruct((z_ways, rows, width), jnp.bfloat16)
    return pl.pallas_call(
        functools.partial(second_kernel, len(got_a)),
        out_shape=[out] * 4,
        grid_spec=pltpu.PrefetchScalarGridSpec(
            num_scalar_prefetch=1,
            grid=(z_ways // step,),
            in_specs=[source(*o, v) for i, o in enumerate(order) for v in sides[i % 2]],
            out_specs=[pl.BlockSpec((step, rows, width), lambda z, ids: (z, 0, 0))] * 4,
        ),
        compiler_params=pltpu.CompilerParams(vmem_limit_bytes=48 << 20),
        cost_estimate=cost(30),
        name="second_sum",
    )(ids, *((sides[0] + sides[1]) * 2))


def third_kernel(ids_ref, keep_a, got_a, keep_b, got_b, *outs):
    for j, out in enumerate(outs):
        at = ids_ref[4] ^ j
        out[0] = add_bf16(keep_a[at], got_a[at])
        out[1] = add_bf16(keep_b[at], got_b[at])


def third_sum(ids, keep_a, got_a, keep_b, got_b):
    z_ways, rows, width = keep_a.shape
    out = jax.ShapeDtypeStruct((2, rows, width), jnp.bfloat16)
    return pl.pallas_call(
        third_kernel,
        out_shape=[out] * z_ways,
        grid_spec=pltpu.PrefetchScalarGridSpec(
            num_scalar_prefetch=1,
            grid=(1,),
            in_specs=[whole_block(keep_a.shape)] * 4,
            out_specs=[whole_block(out.shape)] * z_ways,
        ),
        cost_estimate=cost(10),
        name="third_sum",
    )(ids, keep_a, got_a, keep_b, got_b)


def third_all_kernel(ids_ref, keep_a, got_a, keep_b, got_b, out):
    for z in range(keep_a.shape[0]):
        out[z, 0] = add_bf16(keep_a[z], got_a[z])
        out[z, 1] = add_bf16(keep_b[z], got_b[z])


def third_sum_all(ids, keep_a, got_a, keep_b, got_b):
    z_ways, rows, width = keep_a.shape
    out = jax.ShapeDtypeStruct((z_ways, 2, rows, width), jnp.bfloat16)
    step = max(1, z_ways // 2)
    return pl.pallas_call(
        third_all_kernel,
        out_shape=out,
        grid_spec=pltpu.PrefetchScalarGridSpec(
            num_scalar_prefetch=1,
            grid=(z_ways // step,),
            in_specs=[pl.BlockSpec((step, rows, width), lambda i, *_: (i, 0, 0))] * 4,
            out_specs=pl.BlockSpec((step, 2, rows, width), lambda i, *_: (i, 0, 0, 0)),
        ),
        cost_estimate=cost(10),
        name="third_sum_all",
    )(ids, keep_a, got_a, keep_b, got_b)


def fourth_all_kernel(x, out):
    total = x[0].astype(jnp.float32)
    for z in range(1, x.shape[0]):
        total = total + x[z].astype(jnp.float32)
    out[...] = total.astype(jnp.bfloat16)


def fourth_sum_all(terms):
    return pl.pallas_call(
        fourth_all_kernel,
        out_shape=jax.ShapeDtypeStruct(terms.shape[1:], jnp.bfloat16),
        grid=(1,),
        in_specs=[whole_block(terms.shape)],
        out_specs=whole_block(terms.shape[1:]),
        cost_estimate=cost(10),
        name="fourth_sum_all",
    )(terms)


def fourth_kernel(*refs):
    total = refs[0][...].astype(jnp.float32)
    for r in refs[1:-1]:
        total = total + r[...].astype(jnp.float32)
    refs[-1][...] = total.astype(jnp.bfloat16)


def fourth_sum(terms):
    shape = terms[0].shape
    return pl.pallas_call(
        fourth_kernel,
        out_shape=jax.ShapeDtypeStruct(shape, jnp.bfloat16),
        grid=(1,),
        in_specs=[whole_block(shape)] * len(terms),
        out_specs=whole_block(shape),
        cost_estimate=cost(10),
        name="fourth_sum",
    )(*terms)


def place_kernel(streams, plan, ids_ref, scale_ref, *refs):
    blocks, outs = refs[: 4 * streams], refs[4 * streams :]
    x, y = ids_ref[2], ids_ref[3]
    scale = scale_ref[0:1, 0:1]
    for stream, row, rows, lane, lanes, out, row_of, lane_of in plan:
        for d in range(4):
            own_x, own_y = x ^ (d & 1), y ^ (d >> 1)
            for half in range(2):
                k = own_x * 2 + own_y if half == 0 else 4 + own_y * 2 + own_x
                tile = blocks[4 * stream + d][half, row : row + rows, lane : lane + lanes]
                outs[out][row_of(k), lane_of(k)] = tile.astype(jnp.float32) * scale


def place_blocks(ids, scale, streams, plan, shapes):
    blocks = [b for s in streams for b in s]
    outs = [jax.ShapeDtypeStruct(s, jnp.float32) for s in shapes]
    return pl.pallas_call(
        functools.partial(place_kernel, len(streams), plan),
        out_shape=outs,
        grid_spec=pltpu.PrefetchScalarGridSpec(
            num_scalar_prefetch=1,
            grid=(1,),
            in_specs=[whole_block(a.shape) for a in (scale, *blocks)],
            out_specs=[whole_block(o.shape) for o in outs],
        ),
        compiler_params=pltpu.CompilerParams(vmem_limit_bytes=32 << 20),
        cost_estimate=cost(20),
        name="place_blocks",
    )(ids, scale, *blocks)


def span(start, size):
    return pl.ds(pl.multiple_of(start, size), size)


def ada_kernel(groups, pad_u, numerator, time_ref, *refs):
    f32 = jnp.float32
    parts, (weight_ref, vector_ref, scale_ref) = refs[:groups], refs[groups:]
    table = pl.program_id(0)
    base = 6 * pad_u
    count = parts[0][base + 12 : base + 13, 0:1] + parts[0][base + 13 : base + 14, 0:1]
    for p in parts[1:]:
        count = count + p[base + 12 : base + 13, 0:1] + p[base + 13 : base + 14, 0:1]
    scale = numerator / count
    rows = jnp.concatenate([p[pl.ds(pl.multiple_of(table * pad_u, 8), pad_u), :] for p in parts], axis=0) * scale
    vector_ref[pl.ds(table, 1), :] = jnp.sum(rows, axis=0, keepdims=True)
    operand = jnp.concatenate(list(split3(rows)), axis=0)
    weight_ref[...] = dot(time_ref[...], operand)

    @pl.when(table == 0)
    def _():
        total = parts[0][base : base + 16, :]
        for p in parts[1:]:
            total = total + p[base : base + 16, :]
        vector_ref[8:24, :] = total * scale
        scale_ref[...] = jnp.broadcast_to(scale, scale_ref.shape)


def ada_block(time3, parts, utts, numerator):
    pad_u = table_rows(utts)
    width = parts[0].shape[1]
    own = time3.shape[0]
    f32 = jnp.float32
    return pl.pallas_call(
        functools.partial(ada_kernel, len(parts), pad_u, numerator),
        out_shape=[
            jax.ShapeDtypeStruct((own, 6 * width), f32),
            jax.ShapeDtypeStruct((24, width), f32),
            jax.ShapeDtypeStruct((8, 128), f32),
        ],
        grid=(6,),
        in_specs=[whole_block(time3.shape)] + [whole_block(p.shape) for p in parts],
        out_specs=[
            pl.BlockSpec((own, width), lambda j: (0, j)),
            whole_block((24, width)),
            whole_block((8, 128)),
        ],
        cost_estimate=cost(50),
        name="ada_block",
    )(time3, *parts)


def sum_exchange(value, axis, bit):
    ways = lax.axis_size(axis)
    return lax.ppermute(value, axis, [(i, i ^ bit) for i in range(ways)])


def axis_bits(ways):
    return [1 << i for i in range(ways.bit_length() - 1)]


def reduce_stages(ids, blocks, splits, whole_z):
    batch_ways = lax.axis_size("batch")
    x_bit, y_bit = 1, 1 << ((batch_ways.bit_length() - 1) // 2)
    pairs = []
    for keep, send in blocks:
        shape = (2, 2, 2) + keep.shape[1:]
        pairs.append((keep.reshape(shape), sum_exchange(send, "seq", 1).reshape(shape)))
    *sends, keep_a, keep_b = first_sum(ids, pairs, splits)
    sends = follow(sends, (yield sends))
    got, token = [[], []], None
    for i in range(len(splits)):
        pieces = follow([sends[i], sends[len(splits) + i]], token)
        for side, bit in enumerate((x_bit, y_bit)):
            got[side].append(sum_exchange(pieces[side], "batch", bit))
        token = yield [got[0][i], got[1][i]]
    got_a, got_b = (follow(g, token) for g in got)
    send_a, send_b, keep_a, keep_b = second_sum(ids, keep_a, got_a, keep_b, got_b)
    send_a, send_b = follow([send_a, send_b], (yield [send_a, send_b]))
    got = [sum_exchange(send_a, "batch", y_bit), sum_exchange(send_b, "batch", x_bit)]
    got_a, got_b = follow(got, (yield got))
    if whole_z:
        ways = lax.axis_size("seq")
        groups = [list(range(c, ways, 2)) for c in range(2)]
        away = [third_sum_all(ids, keep_a, got_a, keep_b, got_b)]
        away = follow(away, (yield away))
        got = [lax.all_to_all(away[0], "seq", 0, 0, axis_index_groups=groups, tiled=True)]
        got = follow(got, (yield got))
        block = fourth_sum_all(got[0])
    else:
        own, *away = third_sum(ids, keep_a, got_a, keep_b, got_b)
        away = follow(away, (yield away))
        got = [sum_exchange(a, "seq", 2 * (j + 1)) for j, a in enumerate(away)]
        got = follow(got, (yield got))
        block = fourth_sum([own] + got)
    for bit in axis_bits(batch_ways):
        if bit not in (x_bit, y_bit):
            block = add_bf16(block, sum_exchange(block, "batch", bit))
    (block,) = follow([block], (yield [block]))
    yield [block] + [sum_exchange(block, "batch", bit) for bit in (x_bit, y_bit, x_bit | y_bit)]


def advance(stages, steps, token=None):
    value = next(stages) if token is None else stages.send(token)
    for _ in range(steps - 1):
        value = next(stages)
    return value


def last_stage(stages, token=None):
    value = stages.send(token)
    for value in stages:
        pass
    return value


def follow(values, token):
    return values if token is None else [after(v, token) for v in values]


def after(value, *others):
    return lax.optimization_barrier((value,) + others)[0]


def gather_groups(value):
    away = value.astype(jnp.bfloat16)
    others = [sum_exchange(away, "batch", i) for i in range(1, lax.axis_size("batch"))]
    return [value] + [other.astype(value.dtype) for other in others]


def sum_z(value, tokens):
    away = after(value.astype(jnp.bfloat16), *tokens)
    for j in range(1, lax.axis_size("seq") // 2):
        value = value + sum_exchange(away, "seq", 2 * j).astype(jnp.float32)
    return value


def shards(
    tokens_in,
    skip_in,
    condition,
    cotangent,
    time_embed,
    lengths,
    key_mask,
    drop_mask,
    loss_mask,
    w_skip,
    b_skip,
    w_ada,
    b_ada,
    w_qkv,
    b_qkv,
    w_out,
    b_out,
    w_up,
    b_up,
    w_down,
    b_down,
):
    f32, bf16 = jnp.float32, jnp.bfloat16
    seq_ways, batch_ways = lax.axis_size("seq"), lax.axis_size("batch")
    seq_rank = lax.axis_index("seq")
    frames, width = tokens_in.shape[1:]
    group_frames = frames * seq_ways
    heads_local = HEADS // seq_ways
    utts = lengths.shape[1]
    lengths_row, drop = lengths[0], drop_mask[0]
    batch_rank = lax.axis_index("batch")
    side = 1 << ((batch_ways.bit_length() - 1) // 2)
    ids = [lax.rem(seq_rank, 2), seq_rank, lax.rem(batch_rank, 2), lax.rem(batch_rank // side, 2), seq_rank // 2]
    ids = jnp.stack(ids).astype(jnp.int32)
    ok = key_mask.reshape(seq_ways, 1, frames)
    exchange = functools.partial(lax.all_to_all, axis_name="seq", split_axis=0, concat_axis=0, tiled=True)

    time_act = jax.nn.silu(time_embed[0]).astype(bf16)
    time_rows = jnp.pad(time_act, ((0, 16 - utts), (0, 0)))

    def modulation(first, last):
        return jnp.dot(time_rows, w_ada[:, first:last], preferred_element_type=f32) + b_ada[
            first:last
        ].astype(f32)

    mods_a = modulation(0, 2 * width)
    hidden, joinedT, naT, na = head_block(
        lengths_row, ids, drop, tokens_in[0], skip_in[0], condition[0], mods_a, w_skip, b_skip[None]
    )
    mods_rest = modulation(2 * width, 6 * width)
    received = []
    for c in range(heads_local):
        packed = qkv_block(lengths_row, ids, drop, na, w_qkv, b_qkv[None], c, seq_ways)
        if c == 0:
            na = after(na, mods_rest)
        received.append(exchange(packed))

    own = width // seq_ways
    pad_u = table_rows(utts)
    time_own = lax.dynamic_slice_in_dim(jnp.concatenate(gather_groups(time_rows[:pad_u])), seq_rank * own, own, axis=1)
    time3 = jnp.tile(time_own.T, (1, 3))

    received[0] = after(received[0], mods_rest)
    head_out, log_totals, returned = [], [], []
    for c in range(heads_local):
        out, log_total = attend(lengths_row, received[c], ok)
        head_out.append(out)
        log_totals.append(log_total)
        returned.append(exchange(after(out, *returned)))
        if c < heads_local - 1:
            received[c + 1] = after(received[c + 1], out, time3)
    mid = mid_block(
        lengths_row,
        ids,
        returned,
        hidden,
        mods_rest,
        cotangent[0],
        loss_mask,
        w_out,
        b_out[None],
        w_up,
        b_up[None],
        w_down,
        b_down[None],
        PARTS,
    )
    output, after_grad, mid_small, grad_att, keep, send = mid
    grad_heads = exchange(grad_att)
    front = keep.shape[2] * 4 // 9 // 16 * 16
    feed = reduce_stages(ids, [(keep, send)], [front, keep.shape[2] - front], True)

    ahead = next(feed)
    grad_local = []
    for c in range(heads_local):
        operand = after(grad_heads, *ahead)
        moving = feed.send(grad if c else None) if c < 2 else []
        grad = attend_back(lengths_row, received[c], ok, head_out[c], operand, log_totals[c], c)
        grad_local.append(exchange(after(grad, *moving)))
        ahead = [grad]
    if heads_local == 1:
        next(feed)
    ahead = ahead + advance(feed, 1, ahead[0])
    before, biases = (), []
    for c in range(heads_local):
        acc, bias, keep, send = back_block(
            lengths_row, ids, drop, after(grad_local[c], *ahead), naT, w_qkv, before, c, PARTS
        )
        before = (acc, keep, send)
        biases.append(bias)
        ahead = next(feed) and advance(feed, 1, acc) if c == 0 else []
    gh, small = norm_block(lengths_row, ids, acc, hidden, after_grad, mods_a, loss_mask, mid_small, biases)
    small = small + sum_exchange(small, "seq", 1)
    skip_keep, skip_send = skip_block(ids, joinedT, gh, seq_ways, PARTS)
    blocks = [(skip_keep, skip_send), (keep, send)]
    rest = reduce_stages(ids, blocks, [5 * own // PARTS], False)
    moving = next(feed)
    small = sum_z(small, moving + advance(rest, 3))
    next(rest)
    moving = next(rest)
    groups = gather_groups(after(small, *moving, *next(feed)))
    numerator = float(group_frames * batch_ways)
    grad_w_ada, vectors, scale = ada_block(time3, groups, utts, numerator)
    grad_tokens, grad_skip = joined_block(gh, w_skip, scale)
    feed = last_stage(feed, groups[-1])
    next(rest)
    rest.send(grad_tokens)
    rest = last_stage(rest)

    ff = w_up.shape[1]
    chunks = ff // width
    up_part = chunks * own // PARTS
    down_part = ff // seq_ways // PARTS
    out_part = own // PARTS
    per_chunk = own // up_part
    whole_lanes = lambda k: span(0, width)
    grad_w_up, grad_w_down, grad_w_out = place_blocks(
        ids,
        scale,
        [feed],
        [
            (
                *(0, 0, up_part, 0, width, 0),
                lambda k: span(lax.rem(k, per_chunk) * up_part, up_part),
                lambda k: span(k // per_chunk * width, width),
            ),
            (0, up_part, down_part, 0, width, 1, lambda k: span(k * down_part, down_part), whole_lanes),
            (0, up_part + down_part, out_part, 0, width, 2, lambda k: span(k * out_part, out_part), whole_lanes),
        ],
        [(own, ff), (ff // seq_ways, width), (own, width)],
    )
    skip_part = 2 * own // PARTS
    grad_w_skip, grad_w_qkv = place_blocks(
        ids,
        after(scale, grad_w_down),
        [rest],
        [(0, 0, skip_part, 0, width, 0, lambda k: span(k * skip_part, skip_part), whole_lanes)]
        + [
            (
                *(0, skip_part + p * out_part, out_part, 0, width, 1),
                lambda k: span(k * out_part, out_part),
                lambda k, at=p * width: span(at, width),
            )
            for p in range(3)
        ],
        [(2 * own, width), (own, 3 * width)],
    )

    def own_slice(vector):
        vector = vector.reshape(-1)
        size = vector.shape[0] // seq_ways
        return lax.dynamic_slice_in_dim(vector, seq_rank * size, size)

    grad_b_ada = own_slice(vectors[:6])
    grad_b_qkv = own_slice(vectors[8:11])
    grad_b_skip = own_slice(vectors[11])
    grad_b_out = own_slice(vectors[12])
    grad_b_down = own_slice(vectors[13])
    grad_b_up = own_slice(vectors[14 : 14 + chunks])
    return (
        output[None],
        grad_tokens[None],
        grad_skip[None],
        grad_w_skip,
        grad_b_skip,
        grad_w_ada,
        grad_b_ada,
        grad_w_qkv,
        grad_b_qkv,
        grad_w_out,
        grad_b_out,
        grad_w_up,
        grad_b_up,
        grad_w_down,
        grad_b_down,
    )


def solution(mesh):
    in_specs = (
        P("batch", "seq", None),
        P("batch", "seq", None),
        P("batch", "seq", None),
        P("batch", "seq", None),
        P("batch", None, None),
        P("batch", None),
        P("batch", None),
        P("batch", None),
        P("batch", "seq"),
        P(),
        P(),
        P(),
        P(),
        P(),
        P(),
        P(),
        P(),
        P(),
        P(),
        P(),
        P(),
    )
    out_specs = (
        P("batch", "seq", None),
        P("batch", "seq", None),
        P("batch", "seq", None),
        P("seq", None),
        P("seq"),
        P("seq", None),
        P("seq"),
        P("seq", None),
        P("seq"),
        P("seq", None),
        P("seq"),
        P("seq", None),
        P("seq"),
        P("seq", None),
        P("seq"),
    )
    return jax.shard_map(shards, mesh=mesh, in_specs=in_specs, out_specs=out_specs, check_vma=False)
```

```python
import functools

import jax
import jax.numpy as jnp
from jax import lax
from jax.experimental import pallas as pl
from jax.experimental.pallas import tpu as pltpu
from jax.sharding import PartitionSpec as P

HEADS = 16
HEAD_DIM = 64
PARTS = 8
BIG = 1e30
DH = 64
BQ = 512
BK = 512


def cost(weight):
    return pl.CostEstimate(flops=weight * 100000000, bytes_accessed=weight * 100000, transcendentals=0)


def onehot_rows(lengths_ref, utts, rows, base, width):
    row = lax.broadcasted_iota(jnp.int32, (rows, width), 0)
    col = base + lax.broadcasted_iota(jnp.int32, (rows, width), 1)
    start = jnp.int32(0)
    hot = jnp.zeros((rows, width), jnp.float32)
    for u in range(utts):
        end = start + lengths_ref[u]
        hot = jnp.where((row == u) & (col >= start) & (col < end), 1.0, hot)
        start = end
    return hot


def key_range(lengths_ref, utts, first, last):
    start = jnp.int32(0)
    low, high = jnp.int32(0), jnp.int32(0)
    for u in range(utts):
        end = start + lengths_ref[u]
        low = jnp.where((start <= first) & (first < end), start, low)
        high = jnp.where((start <= last) & (last < end), end, high)
        start = end
    return low // BK, (high + BK - 1) // BK


def aug_rows(utts):
    return -(-utts // 16) * 16


def split3(row):
    a = row.astype(jnp.bfloat16)
    rest = row - a.astype(jnp.float32)
    b = rest.astype(jnp.bfloat16)
    c = (rest - b.astype(jnp.float32)).astype(jnp.bfloat16)
    return a, b, c


def pad_rows(parts, total):
    have = sum(p.shape[0] for p in parts)
    if have < total:
        parts = parts + [jnp.zeros((total - have, parts[0].shape[1]), parts[0].dtype)]
    return jnp.concatenate(parts, axis=0)


def rows16(rows, width):
    idx = lax.broadcasted_iota(jnp.int32, (16, width), 0)
    out = jnp.zeros((16, width), jnp.float32)
    for i, r in enumerate(rows):
        out = jnp.where(idx == i, r, out)
    return out.astype(jnp.bfloat16)


def fwd_kernel(utts, lengths_ref, qkv_ref, ok_ref, out_ref, lse_ref, kaug, vaug):
    sources, _, frames = qkv_ref.shape
    per = frames // BQ
    pad_u = aug_rows(utts)
    step = pl.program_id(0)

    @pl.when(step == 0)
    def _():
        def build(s, c):
            hot = onehot_rows(lengths_ref, utts, pad_u, s * frames, frames)
            ok = ok_ref[s].astype(jnp.float32)
            block = qkv_ref[s]
            one = jnp.ones((1, frames), jnp.float32)
            kT = pad_rows(
                [block[DH : 2 * DH], (1.0 - hot).astype(jnp.bfloat16), rows16([1.0 - ok], frames)], 128
            )
            kaug[pl.ds(pl.multiple_of(s * frames, frames), frames), :] = kT.T
            vT = jnp.concatenate([block[2 * DH :], rows16([one], frames)], axis=0)
            for t in range(frames // BK):
                vaug[s * (frames // BK) + t] = vT[:, t * BK : (t + 1) * BK]
            return c

        lax.fori_loop(0, sources, build, 0)

    block = qkv_ref[step]
    hot_q = onehot_rows(lengths_ref, utts, pad_u, step * frames, frames)
    qT = (block[:DH].astype(jnp.float32) * 0.125)
    one = jnp.ones((1, frames), jnp.float32)
    qaug = pad_rows(
        [qT.astype(jnp.bfloat16), (hot_q * -BIG).astype(jnp.bfloat16), rows16([one * -BIG], frames)], 128
    )
    kT = block[DH : 2 * DH].astype(jnp.float32)
    vT = block[2 * DH :].astype(jnp.float32)
    ok = ok_ref[step] > 0
    s_self = jnp.sum(qT * kT, axis=0, keepdims=True)
    m0 = jnp.where(ok, -3e38, s_self)
    acc0 = jnp.concatenate([jnp.where(ok, 0.0, vT), jnp.where(ok, 0.0, jnp.ones((16, frames), jnp.float32))], axis=0)
    for t in range(per):
        cols = slice(t * BQ, (t + 1) * BQ)
        low, high = key_range(lengths_ref, utts, step * frames + t * BQ, step * frames + (t + 1) * BQ - 1)
        q_b = qaug[:, cols]

        def body(j, carry):
            m, acc = carry
            s = jnp.dot(kaug[pl.ds(pl.multiple_of(j * BK, BK), BK), :], q_b, preferred_element_type=jnp.float32)
            m_new = jnp.maximum(m, jnp.max(s, axis=0, keepdims=True))
            p = jnp.exp(s - m_new).astype(jnp.bfloat16)
            alpha = jnp.exp(m - m_new)
            acc = acc * alpha + jnp.dot(vaug[j], p, preferred_element_type=jnp.float32)
            return m_new, acc

        m, acc = lax.fori_loop(low, high, body, (m0[:, cols], acc0[:, cols]))
        total = acc[DH : DH + 1]
        out_ref[0, :, cols] = (acc[:DH] / total).astype(jnp.bfloat16)
        lse_ref[0, :, cols] = m + jnp.log(total)


def attend(lengths, qkv, ok):
    sources, _, frames = qkv.shape
    total = sources * frames
    utts = lengths.shape[0]
    whole = lambda shape: pl.BlockSpec(shape, lambda i, *_: (0,) * len(shape))
    return pl.pallas_call(
        functools.partial(fwd_kernel, utts),
        out_shape=(
            jax.ShapeDtypeStruct((sources, DH, frames), jnp.bfloat16),
            jax.ShapeDtypeStruct((sources, 1, frames), jnp.float32),
        ),
        grid_spec=pltpu.PrefetchScalarGridSpec(
            num_scalar_prefetch=1,
            grid=(sources,),
            in_specs=[whole(qkv.shape), whole(ok.shape)],
            out_specs=(
                pl.BlockSpec((1, DH, frames), lambda i, *_: (i, 0, 0)),
                pl.BlockSpec((1, 1, frames), lambda i, *_: (i, 0, 0)),
            ),
            scratch_shapes=[
                pltpu.VMEM((total, 128), jnp.bfloat16),
                pltpu.VMEM((total // BK, DH + 16, BK), jnp.bfloat16),
            ],
        ),
        cost_estimate=cost(250),
        name="attend",
    )(lengths, qkv, ok)


def bwd_kernel(utts, chunk, lengths_ref, qkv_ref, ok_ref, o_ref, do_ref, lse_ref, out_ref, kaug, vnat, kT_s, dk, dv):
    sources, _, frames = qkv_ref.shape
    per = frames // BK
    pad_u = aug_rows(utts)
    step = pl.program_id(0)
    f32 = jnp.float32

    @pl.when(step == 0)
    def _():
        def build(s, c):
            hot = onehot_rows(lengths_ref, utts, pad_u, s * frames, frames)
            ok = ok_ref[s]
            block = qkv_ref[s]
            one = jnp.ones((1, frames), f32)
            kT = block[DH : 2 * DH]
            vT = block[2 * DH :]
            kA = pad_rows(
                [kT, (1.0 - hot).astype(jnp.bfloat16), rows16([1.0 - ok.astype(f32), one, one, one], frames)], 128
            )
            rows = pl.ds(pl.multiple_of(s * frames, frames), frames)
            kaug[rows, :] = kA.T
            vnat[rows, :] = pad_rows([vT, rows16([one, one, one], frames)], 128).T
            qT = block[:DH].astype(f32) * 0.125
            do = do_ref[s, chunk * DH : (chunk + 1) * DH, :].astype(f32)
            s_self = jnp.sum(qT * kT.astype(f32), axis=0, keepdims=True)
            delta = jnp.sum(do * o_ref[s].astype(f32), axis=0, keepdims=True)
            p_self = jnp.where(ok > 0, 0.0, jnp.exp(s_self - lse_ref[s]))
            ds_self = p_self * (jnp.sum(do * vT.astype(f32), axis=0, keepdims=True) - delta)
            dk0 = ds_self * qT
            dv0 = p_self * do
            for t in range(per):
                cols = slice(t * BK, (t + 1) * BK)
                kT_s[s * per + t] = kT[:, cols]
                dk[s * per + t] = dk0[:, cols]
                dv[s * per + t] = dv0[:, cols]
            return c

        lax.fori_loop(0, sources, build, 0)

    block = qkv_ref[step]
    one = jnp.ones((1, frames), f32)
    hot_q = onehot_rows(lengths_ref, utts, pad_u, step * frames, frames)
    qT = block[:DH].astype(f32) * 0.125
    qTb = qT.astype(jnp.bfloat16)
    kT = block[DH : 2 * DH].astype(f32)
    vT = block[2 * DH :].astype(f32)
    ok = ok_ref[step]
    dob = do_ref[step, chunk * DH : (chunk + 1) * DH, :]
    do = dob.astype(f32)
    lse = lse_ref[step]
    delta = jnp.sum(do * o_ref[step].astype(f32), axis=0, keepdims=True)
    l3 = [-r.astype(f32) for r in split3(lse)]
    d3 = [-r.astype(f32) for r in split3(delta)]
    qaug = pad_rows([qTb, (hot_q * -BIG).astype(jnp.bfloat16), rows16([one * -BIG] + l3, frames)], 128)
    doaug = pad_rows([dob, rows16(d3, frames)], 128)
    s_self = jnp.sum(qT * kT, axis=0, keepdims=True)
    p_self = jnp.where(ok > 0, 0.0, jnp.exp(s_self - lse))
    ds_self = p_self * (jnp.sum(do * vT, axis=0, keepdims=True) - delta)
    dq0 = ds_self * kT
    nt = (((1,), (1,)), ((), ()))
    for t in range(frames // BQ):
        cols = slice(t * BQ, (t + 1) * BQ)
        low, high = key_range(lengths_ref, utts, step * frames + t * BQ, step * frames + (t + 1) * BQ - 1)
        q_a = qaug[:, cols]
        q_b = qTb[:, cols]
        do_a = doaug[:, cols]
        do_b = dob[:, cols]

        def body(j, dq):
            rows = pl.ds(pl.multiple_of(j * BK, BK), BK)
            s = jnp.dot(kaug[rows, :], q_a, preferred_element_type=f32)
            dp = jnp.dot(vnat[rows, :], do_a, preferred_element_type=f32)
            p = jnp.exp(s)
            ds = (p * dp).astype(jnp.bfloat16)
            dv[j] += lax.dot_general(do_b, p.astype(jnp.bfloat16), nt, preferred_element_type=f32)
            dk[j] += lax.dot_general(q_b, ds, nt, preferred_element_type=f32)
            return dq + jnp.dot(kT_s[j], ds, preferred_element_type=f32)

        dq = lax.fori_loop(low, high, body, dq0[:, cols])
        out_ref[step, :DH, cols] = (dq * 0.125).astype(jnp.bfloat16)

    @pl.when(step == sources - 1)
    def _():
        def finish(s, c):
            for t in range(per):
                cols = slice(t * BK, (t + 1) * BK)
                out_ref[s, DH : 2 * DH, cols] = dk[s * per + t].astype(jnp.bfloat16)
                out_ref[s, 2 * DH :, cols] = dv[s * per + t].astype(jnp.bfloat16)
            return c

        lax.fori_loop(0, sources, finish, 0)


def attend_back(lengths, qkv, ok, out, grad, lse, chunk):
    sources, _, frames = qkv.shape
    total = sources * frames
    utts = lengths.shape[0]
    whole = lambda shape: pl.BlockSpec(shape, lambda i, *_: (0,) * len(shape))
    return pl.pallas_call(
        functools.partial(bwd_kernel, utts, chunk),
        out_shape=jax.ShapeDtypeStruct(qkv.shape, jnp.bfloat16),
        grid_spec=pltpu.PrefetchScalarGridSpec(
            num_scalar_prefetch=1,
            grid=(sources,),
            in_specs=[whole(a.shape) for a in (qkv, ok, out, grad, lse)],
            out_specs=whole(qkv.shape),
            scratch_shapes=[
                pltpu.VMEM((total, 128), jnp.bfloat16),
                pltpu.VMEM((total, 128), jnp.bfloat16),
                pltpu.VMEM((total // BK, DH, BK), jnp.bfloat16),
                pltpu.VMEM((total // BK, DH, BK), jnp.float32),
                pltpu.VMEM((total // BK, DH, BK), jnp.float32),
            ],
        ),
        cost_estimate=cost(320),
        name="attend_back",
    )(lengths, qkv, ok, out, grad, lse)


FF_TILE = 512
EPS = 1e-06


def dot(left, right):
    return jnp.dot(left, right, preferred_element_type=jnp.float32)


def dot_nt(left, right):
    return lax.dot_general(left, right, (((1,), (1,)), ((), ())), preferred_element_type=jnp.float32)


def norm_stats(x):
    mean = jnp.mean(x, axis=1, keepdims=True)
    centred = x - mean
    rstd = lax.rsqrt(jnp.mean(centred * centred, axis=1, keepdims=True) + EPS)
    return centred * rstd, rstd


def norm_back(grad, normed, rstd):
    first = jnp.mean(grad, axis=1, keepdims=True)
    second = jnp.mean(grad * normed, axis=1, keepdims=True)
    return rstd * (grad - first - normed * second)


def mods_operand(mods_ref):
    rows = mods_ref[...]
    return pad_rows(list(split3(rows)), 128)


def table_rows(utts):
    return -(-utts // 8) * 8


def sum_rows(hot, utts_pad, frames):
    idx = lax.broadcasted_iota(jnp.int32, (16, frames), 0)
    ones = jnp.where(idx == 0, 1.0, 0.0).astype(jnp.bfloat16)
    return jnp.concatenate([hot.astype(jnp.bfloat16), ones], axis=0)


def mid_kernel(
    dims,
    lengths_ref,
    ids_ref,
    *refs,
):
    seq_ways, heads_local, utts, ff = dims
    att_refs = refs[:heads_local]
    (
        hidden_ref,
        mods_ref,
        cot_ref,
        loss_ref,
        w_out_ref,
        b_out_ref,
        w_up_ref,
        b_up_ref,
        w_down_ref,
        b_down_ref,
    ) = refs[heads_local : heads_local + 10]
    outs = refs[heads_local + 10 :]
    output_ref, after_grad_ref, small_ref, gatt_ref = outs[:4]
    refs_out = outs[4:6]
    (
        attT,
        attn_proj,
        after,
        nf,
        nfT,
        gff,
        ff_acc,
        gnf_acc,
        sums,
        cols,
        madd,
        grads,
        sems,
    ) = outs[6:]
    f32, bf16 = jnp.float32, jnp.bfloat16
    step = pl.program_id(0)
    steps = pl.num_programs(0)
    core = ids_ref[0]
    rank = ids_ref[1]
    frames, width = hidden_ref.shape
    up_rows = width // seq_ways
    down_rows = FF_TILE
    z_ways = seq_ways // 2
    parts = grads.shape[1]
    pad_u = table_rows(utts)
    ff_total = ff
    up_part = ff_total // width * up_rows // parts
    down_block = ff_total // seq_ways
    down_part = down_block // parts
    out_part = up_rows // parts

    def mod(index):
        return dot(cols[...], madd[:, index * width : (index + 1) * width])

    def grad_out():
        loss = cols[:, 48:49].astype(f32)
        return cot_ref[...].astype(f32) * loss

    @pl.when(step == 0)
    def _():
        hot = onehot_rows(lengths_ref, utts, 16, rank * frames, frames)
        hotb = hot.astype(bf16)
        idx = lax.broadcasted_iota(jnp.int32, (16, frames), 0)
        loss = jnp.where(idx == 0, loss_ref[...].astype(f32), 0.0).astype(bf16)
        cols[...] = pad_rows([hotb, hotb, hotb, loss], 128).T
        sums[...] = sum_rows(hot, 16, frames)
        madd[...] = mods_operand(mods_ref)
        for c in range(heads_local):
            for s in range(seq_ways):
                attT[(c * seq_ways + s) * DH : (c * seq_ways + s + 1) * DH, :] = att_refs[c][s]
        proj = dot(attT[...].T, w_out_ref[...]) + b_out_ref[...].astype(f32)
        attn_proj[...] = proj
        mixed = hidden_ref[...] + mod(0) * proj
        after[...] = mixed
        normed, _ = norm_stats(mixed)
        value = (normed * (1.0 + mod(2)) + mod(1)).astype(bf16)
        nf[...] = value
        nfT[...] = value.T
        gff[...] = (grad_out() * mod(3)).astype(bf16)
        small_ref[4 * pad_u :, :] = jnp.zeros((8, width), f32)

    up = dot(nf[...], w_up_ref[...]) + b_up_ref[...].astype(f32)
    inner = 0.7978845608028654 * (up + 0.044715 * (up * up * up))
    tanh = jnp.tanh(inner)
    cdf = 0.5 * (1.0 + tanh)
    act = (up * cdf).astype(bf16)
    slope = cdf + 0.5 * up * (1.0 - tanh * tanh) * (
        0.7978845608028654 * (1.0 + (3 * 0.044715) * (up * up))
    )
    ff_part = dot(act, w_down_ref[...])
    gup = (dot_nt(gff[...], w_down_ref[...]) * slope).astype(bf16)
    gnf_part = dot_nt(gup, w_up_ref[...])

    @pl.when(step == 0)
    def _():
        ff_acc[...] = ff_part
        gnf_acc[...] = gnf_part

    @pl.when(step > 0)
    def _():
        ff_acc[...] += ff_part
        gnf_acc[...] += gnf_part

    halves = width // FF_TILE
    chunk = step // halves
    half = step % halves
    col = pl.ds(pl.multiple_of(half * FF_TILE, FF_TILE), FF_TILE)
    per_chunk = up_rows // up_part
    small_ref[pl.ds(4 * pad_u + 2 + chunk, 1), col] = dot(sums[16:32, :], gup)[:1]
    grad_w_up = dot(nfT[...], gup).astype(bf16)
    for s in range(seq_ways):
        side = jnp.where(core == s % 2, 0, 1)
        for h in range(per_chunk):
            lo = s * up_rows + h * up_part
            grads[side, chunk * per_chunk + h, s // 2, 0:up_part, col] = grad_w_up[lo : lo + up_part]
    grad_w_down = dot(act.T, gff[...]).astype(bf16)
    blocks = FF_TILE // down_block
    copies = []
    for b in range(blocks):
        s = step * blocks + b
        side = jnp.where(core == s % 2, 0, 1)
        for k in range(parts):
            lo = b * down_block + k * down_part
            grads[side, k, s // 2, up_part : up_part + down_part, :] = grad_w_down[lo : lo + down_part]

    def region_copy(side, where, index):
        return pltpu.make_async_copy(
            grads.at[side].at[where], refs_out[side].at[where], sems.at[side, index]
        )

    def up_copy(side, j):
        where = (
            pl.ds((j // halves) * per_chunk, per_chunk),
            slice(None),
            pl.ds(0, up_part),
            pl.ds(pl.multiple_of((j % halves) * FF_TILE, FF_TILE), FF_TILE),
        )
        return region_copy(side, where, j)

    def down_copy(side, z, index):
        return region_copy(side, (slice(None), pl.ds(z, 1), pl.ds(up_part, down_part)), index)

    def out_copy(side):
        where = (slice(None), slice(None), pl.ds(up_part + down_part, out_part))
        return region_copy(side, where, ff_total // FF_TILE + z_ways)

    base = ff_total // FF_TILE
    for side in range(2):
        up_copy(side, step).start()
    for b in range(blocks):
        s = step * blocks + b
        for side in range(2):

            @pl.when(lax.rem(s + core, 2) == side)
            def _():
                down_copy(side, s // 2, base + s // 2).start()

    @pl.when(step == steps - 1)
    def _():
        ff_out = ff_acc[...] + b_down_ref[...].astype(f32)
        mixed = after[...]
        go = grad_out()
        output_ref[...] = (mixed + mod(3) * ff_out).astype(bf16)
        rows = sums[...]
        small_ref[3 * pad_u : 4 * pad_u, :] = dot(rows, (go * ff_out).astype(bf16))[:pad_u]
        normed, rstd = norm_stats(mixed)
        gnf = gnf_acc[...]
        small_ref[pad_u : 2 * pad_u, :] = dot(rows, gnf.astype(bf16))[:pad_u]
        small_ref[2 * pad_u : 3 * pad_u, :] = dot(rows, (gnf * normed).astype(bf16))[:pad_u]
        g_after = go + norm_back(gnf * (1.0 + mod(2)), normed, rstd)
        after_grad_ref[...] = g_after
        small_ref[0:pad_u, :] = dot(rows, (g_after * attn_proj[...]).astype(bf16))[:pad_u]
        gattn = (g_after * mod(0)).astype(bf16)
        small_ref[4 * pad_u : 4 * pad_u + 1, :] = dot(rows, gattn)[16:17]
        small_ref[4 * pad_u + 1 : 4 * pad_u + 2, :] = dot(rows, gff[...])[16:17]
        gattT = dot_nt(w_out_ref[...], gattn).astype(bf16)
        for c in range(heads_local):
            for s in range(seq_ways):
                lo = (c * seq_ways + s) * DH
                gatt_ref[s, c * DH : (c + 1) * DH, :] = gattT[lo : lo + DH]
        grad_w_out = dot(attT[...], gattn).astype(bf16)
        for s in range(seq_ways):
            side = jnp.where(core == s % 2, 0, 1)
            for k in range(parts):
                lo = s * up_rows + k * out_part
                grads[side, k, s // 2, up_part + down_part : up_part + down_part + out_part, :] = grad_w_out[
                    lo : lo + out_part
                ]
        for side in range(2):
            out_copy(side).start()
        for side in range(2):
            for j in range(ff_total // FF_TILE):
                up_copy(side, j).wait()
            for z in range(z_ways):
                down_copy(side, z, base + z).wait()
            out_copy(side).wait()


def mid_block(
    lengths, ids, att, hidden, mods, cot, loss, w_out, b_out, w_up, b_up, w_down, b_down, parts
):
    frames, width = hidden.shape
    heads_local = len(att)
    seq_ways = att[0].shape[0]
    ff = w_up.shape[1]
    up_rows = width // seq_ways
    rows = (ff // width * up_rows + ff // seq_ways + up_rows) // parts
    utts = lengths.shape[0]
    f32, bf16 = jnp.float32, jnp.bfloat16
    steps = ff // FF_TILE

    def whole(shape):
        return pl.BlockSpec(shape, lambda j, *_: (0,) * len(shape), pipeline_mode=pl.Buffered(1))

    hbm = pl.BlockSpec(memory_space=pl.ANY)
    gshape = (parts, seq_ways // 2, rows, width)
    out_shape = [
        jax.ShapeDtypeStruct((frames, width), bf16),
        jax.ShapeDtypeStruct((frames, width), f32),
        jax.ShapeDtypeStruct((4 * table_rows(utts) + 8, width), f32),
    ]
    out_shape += [jax.ShapeDtypeStruct((seq_ways, heads_local * DH, frames), bf16)]
    out_specs = [whole(o.shape) for o in out_shape] + [hbm] * 2
    out_shape += [jax.ShapeDtypeStruct(gshape, bf16)] * 2
    ins = list(att) + [hidden, mods, cot, loss, w_out, b_out]
    return pl.pallas_call(
        functools.partial(mid_kernel, (seq_ways, heads_local, utts, ff)),
        out_shape=out_shape,
        grid_spec=pltpu.PrefetchScalarGridSpec(
            num_scalar_prefetch=2,
            grid=(steps,),
            in_specs=[whole(a.shape) for a in ins]
            + [
                pl.BlockSpec((width, FF_TILE), lambda j, *_: (0, j)),
                pl.BlockSpec((1, FF_TILE), lambda j, *_: (0, j)),
                pl.BlockSpec((FF_TILE, width), lambda j, *_: (j, 0)),
                whole((1, width)),
            ],
            out_specs=out_specs,
            scratch_shapes=[
                pltpu.VMEM((width, frames), bf16),
                pltpu.VMEM((frames, width), f32),
                pltpu.VMEM((frames, width), f32),
                pltpu.VMEM((frames, width), bf16),
                pltpu.VMEM((width, frames), bf16),
                pltpu.VMEM((frames, width), bf16),
                pltpu.VMEM((frames, width), f32),
                pltpu.VMEM((frames, width), f32),
                pltpu.VMEM((32, frames), bf16),
                pltpu.VMEM((frames, 128), bf16),
                pltpu.VMEM((128, 4 * width), bf16),
                pltpu.VMEM((2,) + gshape, bf16),
                pltpu.SemaphoreType.DMA((2, steps + seq_ways // 2 + 1)),
            ],
        ),
        compiler_params=pltpu.CompilerParams(vmem_limit_bytes=63 << 20),
        cost_estimate=cost(500),
        name="mid_block",
    )(lengths, ids, *ins, w_up, b_up, w_down, b_down)


def whole_block(shape):
    return pl.BlockSpec(shape, lambda *_: (0,) * len(shape), pipeline_mode=pl.Buffered(1))


def segment_rows(lengths_ref, drop_ref, utts, base, width):
    col = base + lax.broadcasted_iota(jnp.int32, (1, width), 1)
    start = jnp.int32(0)
    kept = jnp.zeros((1, width), jnp.float32)
    place = jnp.zeros((1, width), jnp.int32)
    for u in range(utts):
        end = start + lengths_ref[u]
        inside = (col >= start) & (col < end)
        kept = jnp.where(inside, (1 - drop_ref[u]).astype(jnp.float32), kept)
        place = jnp.where(inside, col - start, place)
        start = end
    return kept, place.astype(jnp.float32)


def rotary_rows(place, half):
    index = lax.broadcasted_iota(jnp.int32, (half, 1), 0).astype(jnp.float32)
    inverse = jnp.exp(index * (-9.210340371976184 / half))
    angles = inverse * place
    return jnp.cos(angles), jnp.sin(angles)


def frame_columns(hot, extra):
    hotb = hot.astype(jnp.bfloat16)
    idx = lax.broadcasted_iota(jnp.int32, hot.shape, 0)
    last = jnp.where(idx == 0, extra, 0.0).astype(jnp.bfloat16)
    return pad_rows([hotb, hotb, hotb, last], 128).T


def head_kernel(
    utts,
    lengths_ref,
    ids_ref,
    drop_ref,
    tokens_ref,
    skip_ref,
    cond_ref,
    mods_ref,
    w_skip_ref,
    b_skip_ref,
    hidden_ref,
    joinedT_ref,
    naT_ref,
    na_ref,
    cols,
):
    f32, bf16 = jnp.float32, jnp.bfloat16
    step = pl.program_id(0)
    frames, width = tokens_ref.shape
    rank = ids_ref[1]

    @pl.when(step == 0)
    def _():
        hot = onehot_rows(lengths_ref, utts, 16, rank * frames, frames)
        kept, _ = segment_rows(lengths_ref, drop_ref, utts, rank * frames, frames)
        cols[...] = frame_columns(hot, kept)
        keep = cols[:, 48:49].astype(f32)
        mixed = (tokens_ref[...].astype(f32) + keep * cond_ref[...].astype(f32)).astype(bf16)
        joinedT_ref[0:width, :] = mixed.T
        hidden_ref[...] = dot(mixed, w_skip_ref[...]) + b_skip_ref[...].astype(f32)

    @pl.when(step == 1)
    def _():
        skip = skip_ref[...]
        joinedT_ref[width : 2 * width, :] = skip.T
        hidden = hidden_ref[...] + dot(skip, w_skip_ref[...])
        hidden_ref[...] = hidden
        madd = mods_operand(mods_ref)
        shift = dot(cols[...], madd[:, :width])
        scale = dot(cols[...], madd[:, width:])
        normed, _ = norm_stats(hidden)
        value = (normed * (1.0 + scale) + shift).astype(bf16)
        na_ref[...] = value
        naT_ref[...] = value.T


def head_block(lengths, ids, drop, tokens, skip, cond, mods, w_skip, b_skip):
    frames, width = tokens.shape
    utts = lengths.shape[0]
    f32, bf16 = jnp.float32, jnp.bfloat16

    def whole(shape):
        return pl.BlockSpec(shape, lambda j, *_: (0,) * len(shape), pipeline_mode=pl.Buffered(1))

    out_shape = [
        jax.ShapeDtypeStruct((frames, width), f32),
        jax.ShapeDtypeStruct((2 * width, frames), bf16),
        jax.ShapeDtypeStruct((width, frames), bf16),
        jax.ShapeDtypeStruct((frames, width), bf16),
    ]
    return pl.pallas_call(
        functools.partial(head_kernel, utts),
        out_shape=out_shape,
        grid_spec=pltpu.PrefetchScalarGridSpec(
            num_scalar_prefetch=3,
            grid=(2,),
            in_specs=[whole(a.shape) for a in (tokens, skip, cond, mods)]
            + [pl.BlockSpec((width, width), lambda j, *_: (j, 0)), whole((1, width))],
            out_specs=[whole(o.shape) for o in out_shape],
            scratch_shapes=[pltpu.VMEM((frames, 128), bf16)],
        ),
        compiler_params=pltpu.CompilerParams(vmem_limit_bytes=48 << 20),
        cost_estimate=cost(100),
        name="head_block",
    )(lengths, ids, drop, tokens, skip, cond, mods, w_skip, b_skip)


def turn_heads(tensor, cosine, sine):
    half = DH // 2
    first, second = tensor[:, :half], tensor[:, half:]
    return jnp.concatenate([first * cosine - second * sine, second * cosine + first * sine], axis=1)


def qkv_kernel(utts, seq_ways, lengths_ref, ids_ref, drop_ref, na_ref, w_ref, b_ref, out_ref, trig):
    f32, bf16 = jnp.float32, jnp.bfloat16
    part = pl.program_id(0)
    frames = na_ref.shape[0]

    @pl.when(part == 0)
    def _():
        _, place = segment_rows(lengths_ref, drop_ref, utts, ids_ref[1] * frames, frames)
        cosine, sine = rotary_rows(place, DH // 2)
        trig[0] = cosine
        trig[1] = sine

    raw = dot(na_ref[...], w_ref[...]) + b_ref[...].astype(f32)
    rawT = raw.T.reshape(seq_ways, DH, frames)
    turned = part < 2
    cosine = jnp.where(turned, trig[0], 1.0)[None]
    sine = jnp.where(turned, trig[1], 0.0)[None]
    out_ref[:, pl.ds(pl.multiple_of(part * DH, DH), DH), :] = turn_heads(rawT, cosine, sine).astype(bf16)


def qkv_block(lengths, ids, drop, na, w_qkv, b_qkv, chunk, seq_ways):
    frames, width = na.shape
    cols = seq_ways * DH
    chunks = width // cols
    utts = lengths.shape[0]

    def whole(shape):
        return pl.BlockSpec(shape, lambda j, *_: (0,) * len(shape), pipeline_mode=pl.Buffered(1))

    shape = (seq_ways, 3 * DH, frames)
    return pl.pallas_call(
        functools.partial(qkv_kernel, utts, seq_ways),
        out_shape=jax.ShapeDtypeStruct(shape, jnp.bfloat16),
        grid_spec=pltpu.PrefetchScalarGridSpec(
            num_scalar_prefetch=3,
            grid=(3,),
            in_specs=[
                whole(na.shape),
                pl.BlockSpec((width, cols), lambda j, *_: (0, j * chunks + chunk)),
                pl.BlockSpec((1, cols), lambda j, *_: (0, j * chunks + chunk)),
            ],
            out_specs=whole(shape),
            scratch_shapes=[pltpu.VMEM((2, DH // 2, frames), jnp.float32)],
        ),
        cost_estimate=cost(75),
        name="qkv_block",
    )(lengths, ids, drop, na, w_qkv, b_qkv)


def back_kernel(utts, seq_ways, chunk, lengths_ref, ids_ref, drop_ref, grad_ref, naT_ref, w_ref, *refs):
    first = chunk == 0
    acc_in = None if first else refs[0]
    acc_ref, bias_ref, keep_ref, send_ref, trig, grads, sems = refs[0 if first else 3 :]
    f32, bf16 = jnp.float32, jnp.bfloat16
    part = pl.program_id(0)
    width, frames = naT_ref.shape
    core = ids_ref[0]
    parts = keep_ref.shape[0]
    own = width // seq_ways
    rows = own // parts

    @pl.when(part == 0)
    def _():
        _, place = segment_rows(lengths_ref, drop_ref, utts, ids_ref[1] * frames, frames)
        cosine, sine = rotary_rows(place, DH // 2)
        trig[0] = cosine
        trig[1] = sine

    turned = part < 2
    cosine = jnp.where(turned, trig[0], 1.0)[None]
    sine = jnp.where(turned, trig[1], 0.0)[None]
    raw = grad_ref[:, pl.ds(pl.multiple_of(part * DH, DH), DH), :].astype(f32)
    gpT = turn_heads(raw, cosine, -sine).astype(bf16).reshape(seq_ways * DH, frames)
    gna = dot(w_ref[...], gpT)

    @pl.when(part == 0)
    def _():
        acc_ref[...] = gna if first else acc_in[...] + gna

    @pl.when(part > 0)
    def _():
        acc_ref[...] += gna

    ones = jnp.ones((8, frames), bf16)
    bias_ref[0] = dot_nt(ones, gpT)
    grad_w = dot_nt(naT_ref[...], gpT).astype(bf16)
    cols = seq_ways * DH
    at = pl.ds(pl.multiple_of(part * rows, rows), rows)
    for s in range(seq_ways):
        side = jnp.where(core == s % 2, 0, 1)
        for k in range(parts):
            lo = s * own + k * rows
            grads[side, k, s // 2, at, :] = grad_w[lo : lo + rows]

    def copy(side, p):
        where = (slice(None), slice(None), pl.ds(pl.multiple_of(p * rows, rows), rows))
        return pltpu.make_async_copy(
            grads.at[side].at[where],
            (keep_ref, send_ref)[side].at[(*where, pl.ds(chunk * cols, cols))],
            sems.at[side, p],
        )

    for side in (1, 0):
        copy(side, part).start()

    @pl.when(part == 2)
    def _():
        for side in (1, 0):
            for p in range(3):
                copy(side, p).wait()


def back_block(lengths, ids, drop, grad, naT, w_qkv, before, chunk, parts):
    seq_ways, _, frames = grad.shape
    width = naT.shape[0]
    cols = seq_ways * DH
    chunks = width // cols
    utts = lengths.shape[0]
    f32, bf16 = jnp.float32, jnp.bfloat16
    rows = width // seq_ways // parts

    def whole(shape):
        return pl.BlockSpec(shape, lambda j, *_: (0,) * len(shape), pipeline_mode=pl.Buffered(1))

    gspec = pl.BlockSpec(memory_space=pl.ANY)
    gshape = jax.ShapeDtypeStruct((parts, seq_ways // 2, 3 * rows, width), bf16)
    ins = [grad, naT, w_qkv, *before]
    in_specs = [whole(grad.shape), whole(naT.shape)]
    in_specs += [pl.BlockSpec((width, cols), lambda j, *_: (0, j * chunks + chunk))]
    aliases = {}
    if before:
        in_specs += [whole(before[0].shape), gspec, gspec]
        aliases = {7: 2, 8: 3}
    return pl.pallas_call(
        functools.partial(back_kernel, utts, seq_ways, chunk),
        out_shape=[
            jax.ShapeDtypeStruct((width, frames), f32),
            jax.ShapeDtypeStruct((3, 8, cols), f32),
            gshape,
            gshape,
        ],
        grid_spec=pltpu.PrefetchScalarGridSpec(
            num_scalar_prefetch=3,
            grid=(3,),
            in_specs=in_specs,
            out_specs=[
                whole((width, frames)),
                pl.BlockSpec((1, 8, cols), lambda j, *_: (j, 0, 0)),
                gspec,
                gspec,
            ],
            scratch_shapes=[
                pltpu.VMEM((2, DH // 2, frames), f32),
                pltpu.VMEM((2, parts, seq_ways // 2, 3 * rows, cols), bf16),
                pltpu.SemaphoreType.DMA((2, 3)),
            ],
        ),
        compiler_params=pltpu.CompilerParams(vmem_limit_bytes=48 << 20),
        cost_estimate=cost(100),
        input_output_aliases=aliases,
        name="back_block",
    )(lengths, ids, drop, *ins)


def norm_kernel(
    utts, heads_local, lengths_ref, ids_ref, acc_ref, hidden_ref, after_ref, mods_ref, loss_ref, mid_ref, *refs
):
    f32, bf16 = jnp.float32, jnp.bfloat16
    bias_refs, (gh_ref, small_ref) = refs[:heads_local], refs[heads_local:]
    frames, width = hidden_ref.shape
    pad_u = table_rows(utts)
    base = 6 * pad_u
    hot = onehot_rows(lengths_ref, utts, 16, ids_ref[1] * frames, frames)
    cols = frame_columns(hot, jnp.zeros((1, frames), f32))
    madd = mods_operand(mods_ref)
    scale = dot(cols, madd[:, width:])
    gna = acc_ref[...].T
    normed, rstd = norm_stats(hidden_ref[...])
    sums = sum_rows(hot, 16, frames)
    small_ref[0:pad_u, :] = dot(sums, gna.astype(bf16))[:pad_u]
    small_ref[pad_u : 2 * pad_u, :] = dot(sums, (gna * normed).astype(bf16))[:pad_u]
    gh = (after_ref[...] + norm_back(gna * (1.0 + scale), normed, rstd)).astype(bf16)
    gh_ref[...] = gh
    small_ref[2 * pad_u : base, :] = mid_ref[0 : 4 * pad_u, :]
    cols_local = width // heads_local
    for c in range(heads_local):
        for p in range(3):
            small_ref[base + p : base + p + 1, c * cols_local : (c + 1) * cols_local] = bias_refs[c][p, 0:1, :]
    small_ref[base + 3 : base + 4, :] = dot(sums, gh)[16:17]
    small_ref[base + 4 : base + 12, :] = mid_ref[4 * pad_u : 4 * pad_u + 8, :]
    count = jnp.sum(loss_ref[...].astype(f32), axis=1, keepdims=True)
    high = jnp.floor(count / 32.0) * 32.0
    small_ref[base + 12 : base + 13, :] = jnp.broadcast_to(high, (1, width))
    small_ref[base + 13 : base + 16, :] = jnp.broadcast_to(count - high, (3, width))


def norm_block(lengths, ids, acc, hidden, after, mods, loss, mid_small, biases):
    frames, width = hidden.shape
    utts = lengths.shape[0]
    out_shape = [
        jax.ShapeDtypeStruct((frames, width), jnp.bfloat16),
        jax.ShapeDtypeStruct((6 * table_rows(utts) + 16, width), jnp.float32),
    ]
    return pl.pallas_call(
        functools.partial(norm_kernel, utts, len(biases)),
        out_shape=out_shape,
        grid_spec=pltpu.PrefetchScalarGridSpec(
            num_scalar_prefetch=2,
            grid=(1,),
            in_specs=[whole_block(a.shape) for a in (acc, hidden, after, mods, loss, mid_small, *biases)],
            out_specs=[whole_block(o.shape) for o in out_shape],
        ),
        compiler_params=pltpu.CompilerParams(vmem_limit_bytes=48 << 20),
        cost_estimate=cost(50),
        name="norm_block",
    )(lengths, ids, acc, hidden, after, mods, loss, mid_small, *biases)


def skip_kernel(seq_ways, ids_ref, joinedT_ref, gh_ref, keep_ref, send_ref, grads, sems):
    step = pl.program_id(0)
    core = ids_ref[0]
    parts = keep_ref.shape[0]
    width = joinedT_ref.shape[0]
    block = 2 * width // seq_ways
    rows = block // parts
    z_step = seq_ways // 4
    grad_w = dot(joinedT_ref[...], gh_ref[...]).astype(jnp.bfloat16)
    for b in range(width // block):
        side = jnp.where(core == b % 2, 0, 1)
        for k in range(parts):
            lo = b * block + k * rows
            grads[side, k, step * z_step + b // 2] = grad_w[lo : lo + rows]

    def copy(side, at):
        where = (slice(None), pl.ds(at * z_step, z_step))
        return pltpu.make_async_copy(
            grads.at[side].at[where], (keep_ref, send_ref)[side].at[where], sems.at[side, at]
        )

    for side in (1, 0):
        copy(side, step).start()

    @pl.when(step == 1)
    def _():
        for side in (1, 0):
            for at in range(2):
                copy(side, at).wait()


def skip_block(ids, joinedT, gh, seq_ways, parts):
    frames, width = gh.shape
    rows = 2 * width // seq_ways // parts
    gshape = (parts, seq_ways // 2, rows, width)
    return pl.pallas_call(
        functools.partial(skip_kernel, seq_ways),
        out_shape=[jax.ShapeDtypeStruct(gshape, jnp.bfloat16)] * 2,
        grid_spec=pltpu.PrefetchScalarGridSpec(
            num_scalar_prefetch=1,
            grid=(2,),
            in_specs=[pl.BlockSpec((width, frames), lambda j, *_: (j, 0)), whole_block(gh.shape)],
            out_specs=[pl.BlockSpec(memory_space=pl.ANY)] * 2,
            scratch_shapes=[pltpu.VMEM((2,) + gshape, jnp.bfloat16), pltpu.SemaphoreType.DMA((2, 2))],
        ),
        compiler_params=pltpu.CompilerParams(vmem_limit_bytes=32 << 20),
        cost_estimate=cost(50),
        name="skip_block",
    )(ids, joinedT, gh)


def joined_kernel(gh_ref, w_ref, scale_ref, first_ref, second_ref):
    step = pl.program_id(0)
    value = dot_nt(gh_ref[...], w_ref[...]) * scale_ref[0:1, 0:1]

    @pl.when(step == 0)
    def _():
        first_ref[...] = value

    @pl.when(step == 1)
    def _():
        second_ref[...] = value


def joined_block(gh, w_skip, scale):
    frames, width = gh.shape
    out = jax.ShapeDtypeStruct((frames, width), jnp.float32)
    return pl.pallas_call(
        joined_kernel,
        out_shape=[out, out],
        grid_spec=pltpu.PrefetchScalarGridSpec(
            num_scalar_prefetch=0,
            grid=(2,),
            in_specs=[
                whole_block(gh.shape),
                pl.BlockSpec((width, width), lambda j: (j, 0)),
                whole_block(scale.shape),
            ],
            out_specs=[whole_block(out.shape)] * 2,
        ),
        compiler_params=pltpu.CompilerParams(vmem_limit_bytes=32 << 20),
        cost_estimate=cost(50),
        name="joined_block",
    )(gh, w_skip, scale)


def add_bf16(left, right):
    return (left.astype(jnp.float32) + right.astype(jnp.float32)).astype(jnp.bfloat16)


def first_kernel(pairs, splits, ids_ref, *refs):
    ins, outs = refs[: 8 * pairs], list(refs[8 * pairs :])
    for i in range(4):
        own = [outs.pop(0) for _ in range(splits if i < 2 else 1)]
        at = 0
        for p in range(pairs):
            left, right = ins[2 * (i * pairs + p)], ins[2 * (i * pairs + p) + 1]
            rows = left.shape[-2]
            value = add_bf16(left[0, 0, 0], right[0, 0, 0])
            if len(own) == 1:
                own[0][0, :, at : at + rows, :] = value
            else:
                for out in own:
                    out[0] = value[:, at : at + out.shape[2], :]
                    at += out.shape[2]
            at += rows


def first_sum(ids, pairs, splits):
    _, _, _, z_ways, _, width = pairs[0][0].shape
    total = sum(k.shape[4] for k, _ in pairs)
    step = 1 if total > 100 else z_ways

    def source(half, axis, mine, rows):
        def at(g, z, ids):
            bit = ids[axis]
            return half, bit if mine else 1 - bit, g, z, 0, 0

        return pl.BlockSpec((1, 1, 1, step, rows, width), at)

    order = [(0, 2, False), (1, 3, False), (0, 2, True), (1, 3, True)]
    sizes = [*splits, *splits, total, total]
    return pl.pallas_call(
        functools.partial(first_kernel, len(pairs), len(splits)),
        out_shape=[jax.ShapeDtypeStruct((2, z_ways, n, width), jnp.bfloat16) for n in sizes],
        grid_spec=pltpu.PrefetchScalarGridSpec(
            num_scalar_prefetch=1,
            grid=(2, z_ways // step),
            in_specs=[source(*o, a.shape[4]) for o in order for pair in pairs for a in pair],
            out_specs=[pl.BlockSpec((1, step, n, width), lambda g, z, ids: (g, z, 0, 0)) for n in sizes],
        ),
        compiler_params=pltpu.CompilerParams(vmem_limit_bytes=48 << 20),
        cost_estimate=cost(60),
        name="first_sum",
    )(ids, *([a for pair in pairs for a in pair] * 4))


def second_kernel(keeps, pieces, ids_ref, *refs):
    for i in range(4):
        own = refs[(keeps + pieces) * i : (keeps + pieces) * (i + 1)]
        out = refs[4 * (keeps + pieces) + i]
        at = 0
        for p in range(pieces):
            got = own[keeps + p]
            rows = got.shape[2]
            left = own[p][0] if keeps > 1 else own[0][0, :, at : at + rows, :]
            out[:, at : at + rows, :] = add_bf16(left, got[0])
            at += rows


def second_sum(ids, keep_a, got_a, keep_b, got_b):
    _, z_ways, _, width = keep_a[0].shape
    rows = sum(g.shape[2] for g in got_a)
    step = z_ways // 2 if rows > 100 else z_ways

    def source(axis, mine, value):
        def at(z, ids):
            bit = ids[axis]
            return bit if mine else 1 - bit, z, 0, 0

        return pl.BlockSpec((1, step, *value.shape[2:]), at)

    order = [(3, False), (2, False), (3, True), (2, True)]
    sides = [[*keep_a, *got_a], [*keep_b, *got_b]]
    out = jax.ShapeDtypeStruct((z_ways, rows, width), jnp.bfloat16)
    return pl.pallas_call(
        functools.partial(second_kernel, len(keep_a), len(got_a)),
        out_shape=[out] * 4,
        grid_spec=pltpu.PrefetchScalarGridSpec(
            num_scalar_prefetch=1,
            grid=(z_ways // step,),
            in_specs=[source(*o, v) for i, o in enumerate(order) for v in sides[i % 2]],
            out_specs=[pl.BlockSpec((step, rows, width), lambda z, ids: (z, 0, 0))] * 4,
        ),
        compiler_params=pltpu.CompilerParams(vmem_limit_bytes=48 << 20),
        cost_estimate=cost(30),
        name="second_sum",
    )(ids, *((sides[0] + sides[1]) * 2))


def third_kernel(ids_ref, keep_a, got_a, keep_b, got_b, *outs):
    for j, out in enumerate(outs):
        at = ids_ref[4] ^ j
        out[0] = add_bf16(keep_a[at], got_a[at])
        out[1] = add_bf16(keep_b[at], got_b[at])


def third_sum(ids, keep_a, got_a, keep_b, got_b):
    z_ways, rows, width = keep_a.shape
    out = jax.ShapeDtypeStruct((2, rows, width), jnp.bfloat16)
    return pl.pallas_call(
        third_kernel,
        out_shape=[out] * z_ways,
        grid_spec=pltpu.PrefetchScalarGridSpec(
            num_scalar_prefetch=1,
            grid=(1,),
            in_specs=[whole_block(keep_a.shape)] * 4,
            out_specs=[whole_block(out.shape)] * z_ways,
        ),
        cost_estimate=cost(10),
        name="third_sum",
    )(ids, keep_a, got_a, keep_b, got_b)


def third_all_kernel(ids_ref, keep_a, got_a, keep_b, got_b, out):
    rows = keep_a.shape[1]
    for z in range(keep_a.shape[0]):
        out[z, 0, :rows, :] = add_bf16(keep_a[z], got_a[z])
        out[z, 1, :rows, :] = add_bf16(keep_b[z], got_b[z])


def third_sum_all(ids, keep_a, got_a, keep_b, got_b, room):
    z_ways, rows, width = keep_a.shape
    out = jax.ShapeDtypeStruct((z_ways, 2, rows + room, width), jnp.bfloat16)
    step = max(1, z_ways // 2)
    return pl.pallas_call(
        third_all_kernel,
        out_shape=out,
        grid_spec=pltpu.PrefetchScalarGridSpec(
            num_scalar_prefetch=1,
            grid=(z_ways // step,),
            in_specs=[pl.BlockSpec((step, rows, width), lambda i, *_: (i, 0, 0))] * 4,
            out_specs=pl.BlockSpec((step, 2, rows + room, width), lambda i, *_: (i, 0, 0, 0)),
        ),
        cost_estimate=cost(10),
        name="third_sum_all",
    )(ids, keep_a, got_a, keep_b, got_b)


def put_kernel(small_ref, big_ref, out_ref, held, sems):
    room = held.shape[1]
    z_ways, rows = out_ref.shape[0], out_ref.shape[2] - room
    for half in range(2):
        held[half] = small_ref[half * room : (half + 1) * room, :].astype(jnp.bfloat16)
    copies = [
        pltpu.make_async_copy(held, out_ref.at[z, :, pl.ds(rows, room), :], sems.at[z]) for z in range(z_ways)
    ]
    for copy in copies:
        copy.start()
    for copy in copies:
        copy.wait()


def put_rows(big, small):
    room = small.shape[0] // 2
    hbm = pl.BlockSpec(memory_space=pl.ANY)
    return pl.pallas_call(
        put_kernel,
        out_shape=jax.ShapeDtypeStruct(big.shape, big.dtype),
        grid=(1,),
        in_specs=[whole_block(small.shape), hbm],
        out_specs=hbm,
        scratch_shapes=[
            pltpu.VMEM((2, room, big.shape[3]), jnp.bfloat16),
            pltpu.SemaphoreType.DMA((big.shape[0],)),
        ],
        input_output_aliases={1: 0},
        cost_estimate=cost(10),
        name="put_rows",
    )(small, big)


def fourth_all_kernel(x, out, small):
    rows = out.shape[1]
    room = small.shape[0] // 2
    total = x[0].astype(jnp.float32)
    for z in range(1, x.shape[0]):
        total = total + x[z].astype(jnp.float32)
    out[...] = total[:, :rows].astype(jnp.bfloat16)
    for half in range(2):
        small[half * room : (half + 1) * room, :] = total[half, rows:]


def fourth_sum_all(terms, room):
    _, _, rows, width = terms.shape
    outs = [
        jax.ShapeDtypeStruct((2, rows - room, width), jnp.bfloat16),
        jax.ShapeDtypeStruct((2 * room, width), jnp.float32),
    ]
    return pl.pallas_call(
        fourth_all_kernel,
        out_shape=outs,
        grid=(1,),
        in_specs=[whole_block(terms.shape)],
        out_specs=[whole_block(o.shape) for o in outs],
        cost_estimate=cost(10),
        name="fourth_sum_all",
    )(terms)


def fourth_kernel(*refs):
    total = refs[0][...].astype(jnp.float32)
    for r in refs[1:-1]:
        total = total + r[...].astype(jnp.float32)
    refs[-1][...] = total.astype(jnp.bfloat16)


def fourth_sum(terms):
    shape = terms[0].shape
    return pl.pallas_call(
        fourth_kernel,
        out_shape=jax.ShapeDtypeStruct(shape, jnp.bfloat16),
        grid=(1,),
        in_specs=[whole_block(shape)] * len(terms),
        out_specs=whole_block(shape),
        cost_estimate=cost(10),
        name="fourth_sum",
    )(*terms)


def place_kernel(streams, plan, ids_ref, scale_ref, *refs):
    blocks, outs = refs[: 4 * streams], refs[4 * streams :]
    x, y = ids_ref[2], ids_ref[3]
    scale = scale_ref[0:1, 0:1]
    for stream, row, rows, lane, lanes, out, row_of, lane_of in plan:
        for d in range(4):
            own_x, own_y = x ^ (d & 1), y ^ (d >> 1)
            for half in range(2):
                k = own_x * 2 + own_y if half == 0 else 4 + own_y * 2 + own_x
                tile = blocks[4 * stream + d][half, row : row + rows, lane : lane + lanes]
                outs[out][row_of(k), lane_of(k)] = tile.astype(jnp.float32) * scale


def place_blocks(ids, scale, streams, plan, shapes):
    blocks = [b for s in streams for b in s]
    outs = [jax.ShapeDtypeStruct(s, jnp.float32) for s in shapes]
    return pl.pallas_call(
        functools.partial(place_kernel, len(streams), plan),
        out_shape=outs,
        grid_spec=pltpu.PrefetchScalarGridSpec(
            num_scalar_prefetch=1,
            grid=(1,),
            in_specs=[whole_block(a.shape) for a in (scale, *blocks)],
            out_specs=[whole_block(o.shape) for o in outs],
        ),
        compiler_params=pltpu.CompilerParams(vmem_limit_bytes=32 << 20),
        cost_estimate=cost(20),
        name="place_blocks",
    )(ids, scale, *blocks)


def span(start, size):
    return pl.ds(pl.multiple_of(start, size), size)


def ada_kernel(groups, pad_u, numerator, time_ref, *refs):
    f32 = jnp.float32
    parts, (weight_ref, vector_ref, scale_ref) = refs[:groups], refs[groups:]
    table = pl.program_id(0)
    base = 6 * pad_u
    count = parts[0][base + 12 : base + 13, 0:1] + parts[0][base + 13 : base + 14, 0:1]
    for p in parts[1:]:
        count = count + p[base + 12 : base + 13, 0:1] + p[base + 13 : base + 14, 0:1]
    scale = numerator / count
    rows = jnp.concatenate([p[pl.ds(pl.multiple_of(table * pad_u, 8), pad_u), :] for p in parts], axis=0) * scale
    vector_ref[pl.ds(table, 1), :] = jnp.sum(rows, axis=0, keepdims=True)
    operand = jnp.concatenate(list(split3(rows)), axis=0)
    weight_ref[...] = dot(time_ref[...], operand)

    @pl.when(table == 0)
    def _():
        total = parts[0][base : base + 16, :]
        for p in parts[1:]:
            total = total + p[base : base + 16, :]
        vector_ref[8:24, :] = total * scale
        scale_ref[...] = jnp.broadcast_to(scale, scale_ref.shape)


def ada_block(time3, parts, utts, numerator):
    pad_u = table_rows(utts)
    width = parts[0].shape[1]
    own = time3.shape[0]
    f32 = jnp.float32
    return pl.pallas_call(
        functools.partial(ada_kernel, len(parts), pad_u, numerator),
        out_shape=[
            jax.ShapeDtypeStruct((own, 6 * width), f32),
            jax.ShapeDtypeStruct((24, width), f32),
            jax.ShapeDtypeStruct((8, 128), f32),
        ],
        grid=(6,),
        in_specs=[whole_block(time3.shape)] + [whole_block(p.shape) for p in parts],
        out_specs=[
            pl.BlockSpec((own, width), lambda j: (0, j)),
            whole_block((24, width)),
            whole_block((8, 128)),
        ],
        cost_estimate=cost(50),
        name="ada_block",
    )(time3, *parts)


def sum_exchange(value, axis, bit):
    ways = lax.axis_size(axis)
    return lax.ppermute(value, axis, [(i, i ^ bit) for i in range(ways)])


def axis_bits(ways):
    return [1 << i for i in range(ways.bit_length() - 1)]


def reduce_stages(ids, blocks, splits, room=0):
    batch_ways = lax.axis_size("batch")
    x_bit, y_bit = 1, 1 << ((batch_ways.bit_length() - 1) // 2)
    side_a, side_b, keeps_a, keeps_b = [], [], [], []
    for block, split in zip(blocks, splits):
        keep, send = block(side_a + side_b) if callable(block) else block
        shape = (2, 2, 2) + keep.shape[1:]
        pair = (keep.reshape(shape), sum_exchange(send, "seq", 1).reshape(shape))
        *sends, keep_a, keep_b = first_sum(ids, [pair], split)
        side_a += sends[: len(split)]
        side_b += sends[len(split) :]
        keeps_a.append(keep_a)
        keeps_b.append(keep_b)
    pieces = len(side_a)
    sends = follow(side_a + side_b, (yield side_a + side_b))
    got, token = [[], []], None
    for i in range(pieces):
        moved = follow([sends[i], sends[pieces + i]], token)
        for side, bit in enumerate((x_bit, y_bit)):
            got[side].append(sum_exchange(moved[side], "batch", bit))
        token = yield [got[0][i], got[1][i]]
    got_a, got_b = (follow(g, token) for g in got)
    send_a, send_b, keep_a, keep_b = second_sum(ids, keeps_a, got_a, keeps_b, got_b)
    send_a, send_b = follow([send_a, send_b], (yield [send_a, send_b]))
    got = [sum_exchange(send_a, "batch", y_bit), sum_exchange(send_b, "batch", x_bit)]
    got_a, got_b = follow(got, (yield got))
    extra = []
    if room:
        ways = lax.axis_size("seq")
        groups = [list(range(c, ways, 2)) for c in range(2)]
        away = third_sum_all(ids, keep_a, got_a, keep_b, got_b, room)
        away = put_rows(away, (yield [away]))
        got = [lax.all_to_all(away, "seq", 0, 0, axis_index_groups=groups, tiled=True)]
        got = follow(got, (yield got))
        block, *extra = fourth_sum_all(got[0], room)
    else:
        own, *away = third_sum(ids, keep_a, got_a, keep_b, got_b)
        away = follow(away, (yield away))
        got = [sum_exchange(a, "seq", 2 * (j + 1)) for j, a in enumerate(away)]
        got = follow(got, (yield got))
        block = fourth_sum([own] + got)
    for bit in axis_bits(batch_ways):
        if bit not in (x_bit, y_bit):
            block = add_bf16(block, sum_exchange(block, "batch", bit))
    (block,) = follow([block], (yield [block, *extra]))
    yield [block] + [sum_exchange(block, "batch", bit) for bit in (x_bit, y_bit, x_bit | y_bit)]


def advance(stages, steps, token=None):
    value = next(stages) if token is None else stages.send(token)
    for _ in range(steps - 1):
        value = next(stages)
    return value


def last_stage(stages, token=None):
    value = stages.send(token)
    for value in stages:
        pass
    return value


def follow(values, token):
    return values if token is None else [after(v, token) for v in values]


def after(value, *others):
    return lax.optimization_barrier((value,) + others)[0]


def gather_groups(value):
    away = value.astype(jnp.bfloat16)
    others = [sum_exchange(away, "batch", i) for i in range(1, lax.axis_size("batch"))]
    return [value] + [other.astype(value.dtype) for other in others]


def shards(
    tokens_in,
    skip_in,
    condition,
    cotangent,
    time_embed,
    lengths,
    key_mask,
    drop_mask,
    loss_mask,
    w_skip,
    b_skip,
    w_ada,
    b_ada,
    w_qkv,
    b_qkv,
    w_out,
    b_out,
    w_up,
    b_up,
    w_down,
    b_down,
):
    f32, bf16 = jnp.float32, jnp.bfloat16
    seq_ways, batch_ways = lax.axis_size("seq"), lax.axis_size("batch")
    seq_rank = lax.axis_index("seq")
    frames, width = tokens_in.shape[1:]
    group_frames = frames * seq_ways
    heads_local = HEADS // seq_ways
    utts = lengths.shape[1]
    lengths_row, drop = lengths[0], drop_mask[0]
    batch_rank = lax.axis_index("batch")
    side = 1 << ((batch_ways.bit_length() - 1) // 2)
    ids = [lax.rem(seq_rank, 2), seq_rank, lax.rem(batch_rank, 2), lax.rem(batch_rank // side, 2), seq_rank // 2]
    ids = jnp.stack(ids).astype(jnp.int32)
    ok = key_mask.reshape(seq_ways, 1, frames)
    exchange = functools.partial(lax.all_to_all, axis_name="seq", split_axis=0, concat_axis=0, tiled=True)

    time_act = jax.nn.silu(time_embed[0]).astype(bf16)
    time_rows = jnp.pad(time_act, ((0, 16 - utts), (0, 0)))

    def modulation(first, last):
        return jnp.dot(time_rows, w_ada[:, first:last], preferred_element_type=f32) + b_ada[
            first:last
        ].astype(f32)

    mods_a = modulation(0, 2 * width)
    hidden, joinedT, naT, na = head_block(
        lengths_row, ids, drop, tokens_in[0], skip_in[0], condition[0], mods_a, w_skip, b_skip[None]
    )
    mods_rest = modulation(2 * width, 6 * width)
    received = []
    for c in range(heads_local):
        packed = qkv_block(lengths_row, ids, drop, na, w_qkv, b_qkv[None], c, seq_ways)
        if c == 0:
            na = after(na, mods_rest)
        received.append(exchange(packed))

    own = width // seq_ways
    pad_u = table_rows(utts)
    time_own = lax.dynamic_slice_in_dim(jnp.concatenate(gather_groups(time_rows[:pad_u])), seq_rank * own, own, axis=1)
    time3 = jnp.tile(time_own.T, (1, 3))

    received[0] = after(received[0], mods_rest)
    head_out, log_totals, returned = [], [], []
    for c in range(heads_local):
        out, log_total = attend(lengths_row, received[c], ok)
        head_out.append(out)
        log_totals.append(log_total)
        returned.append(exchange(after(out, *returned)))
        if c < heads_local - 1:
            received[c + 1] = after(received[c + 1], out, time3)
    mid = mid_block(
        lengths_row,
        ids,
        returned,
        hidden,
        mods_rest,
        cotangent[0],
        loss_mask,
        w_out,
        b_out[None],
        w_up,
        b_up[None],
        w_down,
        b_down[None],
        PARTS,
    )
    output, after_grad, mid_small, grad_att, keep, send = mid
    grad_heads = exchange(grad_att)
    front = keep.shape[2] * 4 // 9 // 16 * 16
    feed = reduce_stages(ids, [(keep, send)], [[front, keep.shape[2] - front]], 3 * pad_u + 8)

    ahead = next(feed)
    grad_local = []
    for c in range(heads_local):
        operand = after(grad_heads, *ahead)
        moving = feed.send(grad if c else None) if c < 2 else []
        grad = attend_back(lengths_row, received[c], ok, head_out[c], operand, log_totals[c], c)
        grad_local.append(exchange(after(grad, *moving)))
        ahead = [grad]
    if heads_local == 1:
        next(feed)
    ahead = ahead + advance(feed, 1, ahead[0])
    before, biases = (), []
    for c in range(heads_local):
        acc, bias, keep, send = back_block(
            lengths_row, ids, drop, after(grad_local[c], *ahead), naT, w_qkv, before, c, PARTS
        )
        before = (acc, keep, send)
        biases.append(bias)
        ahead = next(feed) and advance(feed, 1, acc) if c == 0 else []
    gh, small = norm_block(lengths_row, ids, acc, hidden, after_grad, mods_a, loss_mask, mid_small, biases)
    small = small + sum_exchange(small, "seq", 1)
    blocks = [(keep, send), lambda sends: skip_block(ids, joinedT, after(gh, *sends), seq_ways, PARTS)]
    rest = reduce_stages(ids, blocks, [[3 * own // PARTS], [2 * own // PARTS]])
    feed.send(small)
    third = advance(rest, 6)
    brought = next(rest)
    _, small = feed.send(third[0])
    feed = last_stage(feed, third[0])
    groups = gather_groups(after(small, *brought, *feed[1:]))
    numerator = float(group_frames * batch_ways)
    grad_w_ada, vectors, scale = ada_block(time3, groups, utts, numerator)
    grad_tokens, grad_skip = joined_block(gh, w_skip, scale)
    next(rest)
    rest = last_stage(rest)

    ff = w_up.shape[1]
    chunks = ff // width
    up_part = chunks * own // PARTS
    down_part = ff // seq_ways // PARTS
    out_part = own // PARTS
    per_chunk = own // up_part
    whole_lanes = lambda k: span(0, width)
    grad_w_up, grad_w_down, grad_w_out = place_blocks(
        ids,
        scale,
        [feed],
        [
            (
                *(0, 0, up_part, 0, width, 0),
                lambda k: span(lax.rem(k, per_chunk) * up_part, up_part),
                lambda k: span(k // per_chunk * width, width),
            ),
            (0, up_part, down_part, 0, width, 1, lambda k: span(k * down_part, down_part), whole_lanes),
            (0, up_part + down_part, out_part, 0, width, 2, lambda k: span(k * out_part, out_part), whole_lanes),
        ],
        [(own, ff), (ff // seq_ways, width), (own, width)],
    )
    skip_part = 2 * own // PARTS
    grad_w_skip, grad_w_qkv = place_blocks(
        ids,
        after(scale, grad_w_down),
        [rest],
        [(0, 3 * out_part, skip_part, 0, width, 0, lambda k: span(k * skip_part, skip_part), whole_lanes)]
        + [
            (
                *(0, p * out_part, out_part, 0, width, 1),
                lambda k: span(k * out_part, out_part),
                lambda k, at=p * width: span(at, width),
            )
            for p in range(3)
        ],
        [(2 * own, width), (own, 3 * width)],
    )

    def own_slice(vector):
        vector = vector.reshape(-1)
        size = vector.shape[0] // seq_ways
        return lax.dynamic_slice_in_dim(vector, seq_rank * size, size)

    grad_b_ada = own_slice(vectors[:6])
    grad_b_qkv = own_slice(vectors[8:11])
    grad_b_skip = own_slice(vectors[11])
    grad_b_out = own_slice(vectors[12])
    grad_b_down = own_slice(vectors[13])
    grad_b_up = own_slice(vectors[14 : 14 + chunks])
    return (
        output[None],
        grad_tokens[None],
        grad_skip[None],
        grad_w_skip,
        grad_b_skip,
        grad_w_ada,
        grad_b_ada,
        grad_w_qkv,
        grad_b_qkv,
        grad_w_out,
        grad_b_out,
        grad_w_up,
        grad_b_up,
        grad_w_down,
        grad_b_down,
    )


def solution(mesh):
    in_specs = (
        P("batch", "seq", None),
        P("batch", "seq", None),
        P("batch", "seq", None),
        P("batch", "seq", None),
        P("batch", None, None),
        P("batch", None),
        P("batch", None),
        P("batch", None),
        P("batch", "seq"),
        P(),
        P(),
        P(),
        P(),
        P(),
        P(),
        P(),
        P(),
        P(),
        P(),
        P(),
        P(),
    )
    out_specs = (
        P("batch", "seq", None),
        P("batch", "seq", None),
        P("batch", "seq", None),
        P("seq", None),
        P("seq"),
        P("seq", None),
        P("seq"),
        P("seq", None),
        P("seq"),
        P("seq", None),
        P("seq"),
        P("seq", None),
        P("seq"),
        P("seq", None),
        P("seq"),
    )
    return jax.shard_map(shards, mesh=mesh, in_specs=in_specs, out_specs=out_specs, check_vma=False)
```

```python
import functools

import jax
import jax.numpy as jnp
from jax import lax
from jax.experimental import pallas as pl
from jax.experimental.pallas import tpu as pltpu
from jax.sharding import PartitionSpec as P

HEADS = 16
HEAD_DIM = 64
PARTS = 8
BIG = 1e30
DH = 64
BQ = 512
BK = 512


def cost(weight):
    return pl.CostEstimate(flops=weight * 100000000, bytes_accessed=weight * 100000, transcendentals=0)


def onehot_rows(lengths_ref, utts, rows, base, width):
    row = lax.broadcasted_iota(jnp.int32, (rows, width), 0)
    col = base + lax.broadcasted_iota(jnp.int32, (rows, width), 1)
    start = jnp.int32(0)
    hot = jnp.zeros((rows, width), jnp.float32)
    for u in range(utts):
        end = start + lengths_ref[u]
        hot = jnp.where((row == u) & (col >= start) & (col < end), 1.0, hot)
        start = end
    return hot


def key_range(lengths_ref, utts, first, last):
    start = jnp.int32(0)
    low, high = jnp.int32(0), jnp.int32(0)
    for u in range(utts):
        end = start + lengths_ref[u]
        low = jnp.where((start <= first) & (first < end), start, low)
        high = jnp.where((start <= last) & (last < end), end, high)
        start = end
    return low // BK, (high + BK - 1) // BK


def aug_rows(utts):
    return -(-utts // 16) * 16


def split3(row):
    a = row.astype(jnp.bfloat16)
    rest = row - a.astype(jnp.float32)
    b = rest.astype(jnp.bfloat16)
    c = (rest - b.astype(jnp.float32)).astype(jnp.bfloat16)
    return a, b, c


def pad_rows(parts, total):
    have = sum(p.shape[0] for p in parts)
    if have < total:
        parts = parts + [jnp.zeros((total - have, parts[0].shape[1]), parts[0].dtype)]
    return jnp.concatenate(parts, axis=0)


def rows16(rows, width):
    idx = lax.broadcasted_iota(jnp.int32, (16, width), 0)
    out = jnp.zeros((16, width), jnp.float32)
    for i, r in enumerate(rows):
        out = jnp.where(idx == i, r, out)
    return out.astype(jnp.bfloat16)


def fwd_kernel(utts, lengths_ref, qkv_ref, ok_ref, out_ref, lse_ref, kaug, vaug):
    sources, _, frames = qkv_ref.shape
    per = frames // BQ
    pad_u = aug_rows(utts)
    step = pl.program_id(0)

    @pl.when(step == 0)
    def _():
        def build(s, c):
            hot = onehot_rows(lengths_ref, utts, pad_u, s * frames, frames)
            ok = ok_ref[s].astype(jnp.float32)
            block = qkv_ref[s]
            one = jnp.ones((1, frames), jnp.float32)
            kT = pad_rows(
                [block[DH : 2 * DH], (1.0 - hot).astype(jnp.bfloat16), rows16([1.0 - ok], frames)], 128
            )
            kaug[pl.ds(pl.multiple_of(s * frames, frames), frames), :] = kT.T
            vT = jnp.concatenate([block[2 * DH :], rows16([one], frames)], axis=0)
            for t in range(frames // BK):
                vaug[s * (frames // BK) + t] = vT[:, t * BK : (t + 1) * BK]
            return c

        lax.fori_loop(0, sources, build, 0)

    block = qkv_ref[step]
    hot_q = onehot_rows(lengths_ref, utts, pad_u, step * frames, frames)
    qT = (block[:DH].astype(jnp.float32) * 0.125)
    one = jnp.ones((1, frames), jnp.float32)
    qaug = pad_rows(
        [qT.astype(jnp.bfloat16), (hot_q * -BIG).astype(jnp.bfloat16), rows16([one * -BIG], frames)], 128
    )
    kT = block[DH : 2 * DH].astype(jnp.float32)
    vT = block[2 * DH :].astype(jnp.float32)
    ok = ok_ref[step] > 0
    s_self = jnp.sum(qT * kT, axis=0, keepdims=True)
    m0 = jnp.where(ok, -3e38, s_self)
    acc0 = jnp.concatenate([jnp.where(ok, 0.0, vT), jnp.where(ok, 0.0, jnp.ones((16, frames), jnp.float32))], axis=0)
    for t in range(per):
        cols = slice(t * BQ, (t + 1) * BQ)
        low, high = key_range(lengths_ref, utts, step * frames + t * BQ, step * frames + (t + 1) * BQ - 1)
        q_b = qaug[:, cols]

        def body(j, carry):
            m, acc = carry
            s = jnp.dot(kaug[pl.ds(pl.multiple_of(j * BK, BK), BK), :], q_b, preferred_element_type=jnp.float32)
            m_new = jnp.maximum(m, jnp.max(s, axis=0, keepdims=True))
            p = jnp.exp(s - m_new).astype(jnp.bfloat16)
            alpha = jnp.exp(m - m_new)
            acc = acc * alpha + jnp.dot(vaug[j], p, preferred_element_type=jnp.float32)
            return m_new, acc

        m, acc = lax.fori_loop(low, high, body, (m0[:, cols], acc0[:, cols]))
        total = acc[DH : DH + 1]
        out_ref[0, :, cols] = (acc[:DH] / total).astype(jnp.bfloat16)
        lse_ref[0, :, cols] = m + jnp.log(total)


def attend(lengths, qkv, ok):
    sources, _, frames = qkv.shape
    total = sources * frames
    utts = lengths.shape[0]
    whole = lambda shape: pl.BlockSpec(shape, lambda i, *_: (0,) * len(shape))
    return pl.pallas_call(
        functools.partial(fwd_kernel, utts),
        out_shape=(
            jax.ShapeDtypeStruct((sources, DH, frames), jnp.bfloat16),
            jax.ShapeDtypeStruct((sources, 1, frames), jnp.float32),
        ),
        grid_spec=pltpu.PrefetchScalarGridSpec(
            num_scalar_prefetch=1,
            grid=(sources,),
            in_specs=[whole(qkv.shape), whole(ok.shape)],
            out_specs=(
                pl.BlockSpec((1, DH, frames), lambda i, *_: (i, 0, 0)),
                pl.BlockSpec((1, 1, frames), lambda i, *_: (i, 0, 0)),
            ),
            scratch_shapes=[
                pltpu.VMEM((total, 128), jnp.bfloat16),
                pltpu.VMEM((total // BK, DH + 16, BK), jnp.bfloat16),
            ],
        ),
        cost_estimate=cost(250),
        name="attend",
    )(lengths, qkv, ok)


def bwd_kernel(utts, chunk, lengths_ref, qkv_ref, ok_ref, o_ref, do_ref, lse_ref, out_ref, kaug, vnat, kT_s, dk, dv):
    sources, _, frames = qkv_ref.shape
    per = frames // BK
    pad_u = aug_rows(utts)
    step = pl.program_id(0)
    f32 = jnp.float32

    @pl.when(step == 0)
    def _():
        def build(s, c):
            hot = onehot_rows(lengths_ref, utts, pad_u, s * frames, frames)
            ok = ok_ref[s]
            block = qkv_ref[s]
            one = jnp.ones((1, frames), f32)
            kT = block[DH : 2 * DH]
            vT = block[2 * DH :]
            kA = pad_rows(
                [kT, (1.0 - hot).astype(jnp.bfloat16), rows16([1.0 - ok.astype(f32), one, one, one], frames)], 128
            )
            rows = pl.ds(pl.multiple_of(s * frames, frames), frames)
            kaug[rows, :] = kA.T
            vnat[rows, :] = pad_rows([vT, rows16([one, one, one], frames)], 128).T
            qT = block[:DH].astype(f32) * 0.125
            do = do_ref[s, chunk * DH : (chunk + 1) * DH, :].astype(f32)
            s_self = jnp.sum(qT * kT.astype(f32), axis=0, keepdims=True)
            delta = jnp.sum(do * o_ref[s].astype(f32), axis=0, keepdims=True)
            p_self = jnp.where(ok > 0, 0.0, jnp.exp(s_self - lse_ref[s]))
            ds_self = p_self * (jnp.sum(do * vT.astype(f32), axis=0, keepdims=True) - delta)
            dk0 = ds_self * qT
            dv0 = p_self * do
            for t in range(per):
                cols = slice(t * BK, (t + 1) * BK)
                kT_s[s * per + t] = kT[:, cols]
                dk[s * per + t] = dk0[:, cols]
                dv[s * per + t] = dv0[:, cols]
            return c

        lax.fori_loop(0, sources, build, 0)

    block = qkv_ref[step]
    one = jnp.ones((1, frames), f32)
    hot_q = onehot_rows(lengths_ref, utts, pad_u, step * frames, frames)
    qT = block[:DH].astype(f32) * 0.125
    qTb = qT.astype(jnp.bfloat16)
    kT = block[DH : 2 * DH].astype(f32)
    vT = block[2 * DH :].astype(f32)
    ok = ok_ref[step]
    dob = do_ref[step, chunk * DH : (chunk + 1) * DH, :]
    do = dob.astype(f32)
    lse = lse_ref[step]
    delta = jnp.sum(do * o_ref[step].astype(f32), axis=0, keepdims=True)
    l3 = [-r.astype(f32) for r in split3(lse)]
    d3 = [-r.astype(f32) for r in split3(delta)]
    qaug = pad_rows([qTb, (hot_q * -BIG).astype(jnp.bfloat16), rows16([one * -BIG] + l3, frames)], 128)
    doaug = pad_rows([dob, rows16(d3, frames)], 128)
    s_self = jnp.sum(qT * kT, axis=0, keepdims=True)
    p_self = jnp.where(ok > 0, 0.0, jnp.exp(s_self - lse))
    ds_self = p_self * (jnp.sum(do * vT, axis=0, keepdims=True) - delta)
    dq0 = ds_self * kT
    nt = (((1,), (1,)), ((), ()))
    for t in range(frames // BQ):
        cols = slice(t * BQ, (t + 1) * BQ)
        low, high = key_range(lengths_ref, utts, step * frames + t * BQ, step * frames + (t + 1) * BQ - 1)
        q_a = qaug[:, cols]
        q_b = qTb[:, cols]
        do_a = doaug[:, cols]
        do_b = dob[:, cols]

        def body(j, dq):
            rows = pl.ds(pl.multiple_of(j * BK, BK), BK)
            s = jnp.dot(kaug[rows, :], q_a, preferred_element_type=f32)
            dp = jnp.dot(vnat[rows, :], do_a, preferred_element_type=f32)
            p = jnp.exp(s)
            ds = (p * dp).astype(jnp.bfloat16)
            dv[j] += lax.dot_general(do_b, p.astype(jnp.bfloat16), nt, preferred_element_type=f32)
            dk[j] += lax.dot_general(q_b, ds, nt, preferred_element_type=f32)
            return dq + jnp.dot(kT_s[j], ds, preferred_element_type=f32)

        dq = lax.fori_loop(low, high, body, dq0[:, cols])
        out_ref[step, :DH, cols] = (dq * 0.125).astype(jnp.bfloat16)

    @pl.when(step == sources - 1)
    def _():
        def finish(s, c):
            for t in range(per):
                cols = slice(t * BK, (t + 1) * BK)
                out_ref[s, DH : 2 * DH, cols] = dk[s * per + t].astype(jnp.bfloat16)
                out_ref[s, 2 * DH :, cols] = dv[s * per + t].astype(jnp.bfloat16)
            return c

        lax.fori_loop(0, sources, finish, 0)


def attend_back(lengths, qkv, ok, out, grad, lse, chunk):
    sources, _, frames = qkv.shape
    total = sources * frames
    utts = lengths.shape[0]
    whole = lambda shape: pl.BlockSpec(shape, lambda i, *_: (0,) * len(shape))
    return pl.pallas_call(
        functools.partial(bwd_kernel, utts, chunk),
        out_shape=jax.ShapeDtypeStruct(qkv.shape, jnp.bfloat16),
        grid_spec=pltpu.PrefetchScalarGridSpec(
            num_scalar_prefetch=1,
            grid=(sources,),
            in_specs=[whole(a.shape) for a in (qkv, ok, out, grad, lse)],
            out_specs=whole(qkv.shape),
            scratch_shapes=[
                pltpu.VMEM((total, 128), jnp.bfloat16),
                pltpu.VMEM((total, 128), jnp.bfloat16),
                pltpu.VMEM((total // BK, DH, BK), jnp.bfloat16),
                pltpu.VMEM((total // BK, DH, BK), jnp.float32),
                pltpu.VMEM((total // BK, DH, BK), jnp.float32),
            ],
        ),
        cost_estimate=cost(320),
        name="attend_back",
    )(lengths, qkv, ok, out, grad, lse)


FF_TILE = 512
EPS = 1e-06


def dot(left, right):
    return jnp.dot(left, right, preferred_element_type=jnp.float32)


def dot_nt(left, right):
    return lax.dot_general(left, right, (((1,), (1,)), ((), ())), preferred_element_type=jnp.float32)


def norm_stats(x):
    mean = jnp.mean(x, axis=1, keepdims=True)
    centred = x - mean
    rstd = lax.rsqrt(jnp.mean(centred * centred, axis=1, keepdims=True) + EPS)
    return centred * rstd, rstd


def norm_back(grad, normed, rstd):
    first = jnp.mean(grad, axis=1, keepdims=True)
    second = jnp.mean(grad * normed, axis=1, keepdims=True)
    return rstd * (grad - first - normed * second)


def mods_operand(mods_ref):
    rows = mods_ref[...]
    return pad_rows(list(split3(rows)), 128)


def table_rows(utts):
    return -(-utts // 8) * 8


def sum_rows(hot, utts_pad, frames):
    idx = lax.broadcasted_iota(jnp.int32, (16, frames), 0)
    ones = jnp.where(idx == 0, 1.0, 0.0).astype(jnp.bfloat16)
    return jnp.concatenate([hot.astype(jnp.bfloat16), ones], axis=0)


def mid_kernel(
    dims,
    lengths_ref,
    ids_ref,
    *refs,
):
    seq_ways, heads_local, utts, ff = dims
    att_refs = refs[:heads_local]
    (
        hidden_ref,
        mods_ref,
        cot_ref,
        loss_ref,
        w_out_ref,
        b_out_ref,
        w_up_ref,
        b_up_ref,
        w_down_ref,
        b_down_ref,
    ) = refs[heads_local : heads_local + 10]
    outs = refs[heads_local + 10 :]
    output_ref, after_grad_ref, small_ref, gatt_ref = outs[:4]
    refs_out = outs[4:6]
    (
        attT,
        attn_proj,
        after,
        nf,
        nfT,
        gff,
        ff_acc,
        gnf_acc,
        sums,
        cols,
        madd,
        grads,
        sems,
    ) = outs[6:]
    f32, bf16 = jnp.float32, jnp.bfloat16
    step = pl.program_id(0)
    steps = pl.num_programs(0)
    core = ids_ref[0]
    rank = ids_ref[1]
    frames, width = hidden_ref.shape
    up_rows = width // seq_ways
    down_rows = FF_TILE
    z_ways = seq_ways // 2
    parts = grads.shape[1]
    pad_u = table_rows(utts)
    ff_total = ff
    up_part = ff_total // width * up_rows // parts
    down_block = ff_total // seq_ways
    down_part = down_block // parts
    out_part = up_rows // parts

    def mod(index):
        return dot(cols[...], madd[:, index * width : (index + 1) * width])

    def grad_out():
        loss = cols[:, 48:49].astype(f32)
        return cot_ref[...].astype(f32) * loss

    @pl.when(step == 0)
    def _():
        hot = onehot_rows(lengths_ref, utts, 16, rank * frames, frames)
        hotb = hot.astype(bf16)
        idx = lax.broadcasted_iota(jnp.int32, (16, frames), 0)
        loss = jnp.where(idx == 0, loss_ref[...].astype(f32), 0.0).astype(bf16)
        cols[...] = pad_rows([hotb, hotb, hotb, loss], 128).T
        sums[...] = sum_rows(hot, 16, frames)
        madd[...] = mods_operand(mods_ref)
        for c in range(heads_local):
            for s in range(seq_ways):
                attT[(c * seq_ways + s) * DH : (c * seq_ways + s + 1) * DH, :] = att_refs[c][s]
        proj = dot(attT[...].T, w_out_ref[...]) + b_out_ref[...].astype(f32)
        attn_proj[...] = proj
        mixed = hidden_ref[...] + mod(0) * proj
        after[...] = mixed
        normed, _ = norm_stats(mixed)
        value = (normed * (1.0 + mod(2)) + mod(1)).astype(bf16)
        nf[...] = value
        nfT[...] = value.T
        gff[...] = (grad_out() * mod(3)).astype(bf16)
        small_ref[4 * pad_u :, :] = jnp.zeros((8, width), f32)

    up = dot(nf[...], w_up_ref[...]) + b_up_ref[...].astype(f32)
    inner = 0.7978845608028654 * (up + 0.044715 * (up * up * up))
    tanh = jnp.tanh(inner)
    cdf = 0.5 * (1.0 + tanh)
    act = (up * cdf).astype(bf16)
    slope = cdf + 0.5 * up * (1.0 - tanh * tanh) * (
        0.7978845608028654 * (1.0 + (3 * 0.044715) * (up * up))
    )
    ff_part = dot(act, w_down_ref[...])
    gup = (dot_nt(gff[...], w_down_ref[...]) * slope).astype(bf16)
    gnf_part = dot_nt(gup, w_up_ref[...])

    @pl.when(step == 0)
    def _():
        ff_acc[...] = ff_part
        gnf_acc[...] = gnf_part

    @pl.when(step > 0)
    def _():
        ff_acc[...] += ff_part
        gnf_acc[...] += gnf_part

    halves = width // FF_TILE
    chunk = step // halves
    half = step % halves
    col = pl.ds(pl.multiple_of(half * FF_TILE, FF_TILE), FF_TILE)
    per_chunk = up_rows // up_part
    small_ref[pl.ds(4 * pad_u + 2 + chunk, 1), col] = dot(sums[16:32, :], gup)[:1]
    grad_w_up = dot(nfT[...], gup).astype(bf16)
    for s in range(seq_ways):
        side = jnp.where(core == s % 2, 0, 1)
        for h in range(per_chunk):
            lo = s * up_rows + h * up_part
            grads[side, chunk * per_chunk + h, s // 2, 0:up_part, col] = grad_w_up[lo : lo + up_part]
    grad_w_down = dot(act.T, gff[...]).astype(bf16)
    blocks = FF_TILE // down_block
    copies = []
    for b in range(blocks):
        s = step * blocks + b
        side = jnp.where(core == s % 2, 0, 1)
        for k in range(parts):
            lo = b * down_block + k * down_part
            grads[side, k, s // 2, up_part : up_part + down_part, :] = grad_w_down[lo : lo + down_part]

    def region_copy(side, where, index):
        return pltpu.make_async_copy(
            grads.at[side].at[where], refs_out[side].at[where], sems.at[side, index]
        )

    def up_copy(side, j):
        where = (
            pl.ds((j // halves) * per_chunk, per_chunk),
            slice(None),
            pl.ds(0, up_part),
            pl.ds(pl.multiple_of((j % halves) * FF_TILE, FF_TILE), FF_TILE),
        )
        return region_copy(side, where, j)

    def down_copy(side, z, index):
        return region_copy(side, (slice(None), pl.ds(z, 1), pl.ds(up_part, down_part)), index)

    def out_copy(side):
        where = (slice(None), slice(None), pl.ds(up_part + down_part, out_part))
        return region_copy(side, where, ff_total // FF_TILE + z_ways)

    base = ff_total // FF_TILE
    for side in range(2):
        up_copy(side, step).start()
    for b in range(blocks):
        s = step * blocks + b
        for side in range(2):

            @pl.when(lax.rem(s + core, 2) == side)
            def _():
                down_copy(side, s // 2, base + s // 2).start()

    @pl.when(step == steps - 1)
    def _():
        ff_out = ff_acc[...] + b_down_ref[...].astype(f32)
        mixed = after[...]
        go = grad_out()
        output_ref[...] = (mixed + mod(3) * ff_out).astype(bf16)
        rows = sums[...]
        small_ref[3 * pad_u : 4 * pad_u, :] = dot(rows, (go * ff_out).astype(bf16))[:pad_u]
        normed, rstd = norm_stats(mixed)
        gnf = gnf_acc[...]
        small_ref[pad_u : 2 * pad_u, :] = dot(rows, gnf.astype(bf16))[:pad_u]
        small_ref[2 * pad_u : 3 * pad_u, :] = dot(rows, (gnf * normed).astype(bf16))[:pad_u]
        g_after = go + norm_back(gnf * (1.0 + mod(2)), normed, rstd)
        after_grad_ref[...] = g_after
        small_ref[0:pad_u, :] = dot(rows, (g_after * attn_proj[...]).astype(bf16))[:pad_u]
        gattn = (g_after * mod(0)).astype(bf16)
        small_ref[4 * pad_u : 4 * pad_u + 1, :] = dot(rows, gattn)[16:17]
        small_ref[4 * pad_u + 1 : 4 * pad_u + 2, :] = dot(rows, gff[...])[16:17]
        gattT = dot_nt(w_out_ref[...], gattn).astype(bf16)
        for c in range(heads_local):
            for s in range(seq_ways):
                lo = (c * seq_ways + s) * DH
                gatt_ref[s, c * DH : (c + 1) * DH, :] = gattT[lo : lo + DH]
        grad_w_out = dot(attT[...], gattn).astype(bf16)
        for s in range(seq_ways):
            side = jnp.where(core == s % 2, 0, 1)
            for k in range(parts):
                lo = s * up_rows + k * out_part
                grads[side, k, s // 2, up_part + down_part : up_part + down_part + out_part, :] = grad_w_out[
                    lo : lo + out_part
                ]
        for side in range(2):
            out_copy(side).start()
        for side in range(2):
            for j in range(ff_total // FF_TILE):
                up_copy(side, j).wait()
            for z in range(z_ways):
                down_copy(side, z, base + z).wait()
            out_copy(side).wait()


def mid_block(
    lengths, ids, att, hidden, mods, cot, loss, w_out, b_out, w_up, b_up, w_down, b_down, parts
):
    frames, width = hidden.shape
    heads_local = len(att)
    seq_ways = att[0].shape[0]
    ff = w_up.shape[1]
    up_rows = width // seq_ways
    rows = (ff // width * up_rows + ff // seq_ways + up_rows) // parts
    utts = lengths.shape[0]
    f32, bf16 = jnp.float32, jnp.bfloat16
    steps = ff // FF_TILE

    def whole(shape):
        return pl.BlockSpec(shape, lambda j, *_: (0,) * len(shape), pipeline_mode=pl.Buffered(1))

    hbm = pl.BlockSpec(memory_space=pl.ANY)
    gshape = (parts, seq_ways // 2, rows, width)
    out_shape = [
        jax.ShapeDtypeStruct((frames, width), bf16),
        jax.ShapeDtypeStruct((frames, width), f32),
        jax.ShapeDtypeStruct((4 * table_rows(utts) + 8, width), f32),
    ]
    out_shape += [jax.ShapeDtypeStruct((seq_ways, heads_local * DH, frames), bf16)]
    out_specs = [whole(o.shape) for o in out_shape] + [hbm] * 2
    out_shape += [jax.ShapeDtypeStruct(gshape, bf16)] * 2
    ins = list(att) + [hidden, mods, cot, loss, w_out, b_out]
    return pl.pallas_call(
        functools.partial(mid_kernel, (seq_ways, heads_local, utts, ff)),
        out_shape=out_shape,
        grid_spec=pltpu.PrefetchScalarGridSpec(
            num_scalar_prefetch=2,
            grid=(steps,),
            in_specs=[whole(a.shape) for a in ins]
            + [
                pl.BlockSpec((width, FF_TILE), lambda j, *_: (0, j)),
                pl.BlockSpec((1, FF_TILE), lambda j, *_: (0, j)),
                pl.BlockSpec((FF_TILE, width), lambda j, *_: (j, 0)),
                whole((1, width)),
            ],
            out_specs=out_specs,
            scratch_shapes=[
                pltpu.VMEM((width, frames), bf16),
                pltpu.VMEM((frames, width), f32),
                pltpu.VMEM((frames, width), f32),
                pltpu.VMEM((frames, width), bf16),
                pltpu.VMEM((width, frames), bf16),
                pltpu.VMEM((frames, width), bf16),
                pltpu.VMEM((frames, width), f32),
                pltpu.VMEM((frames, width), f32),
                pltpu.VMEM((32, frames), bf16),
                pltpu.VMEM((frames, 128), bf16),
                pltpu.VMEM((128, 4 * width), bf16),
                pltpu.VMEM((2,) + gshape, bf16),
                pltpu.SemaphoreType.DMA((2, steps + seq_ways // 2 + 1)),
            ],
        ),
        compiler_params=pltpu.CompilerParams(vmem_limit_bytes=63 << 20),
        cost_estimate=cost(500),
        name="mid_block",
    )(lengths, ids, *ins, w_up, b_up, w_down, b_down)


def whole_block(shape):
    return pl.BlockSpec(shape, lambda *_: (0,) * len(shape), pipeline_mode=pl.Buffered(1))


def segment_rows(lengths_ref, drop_ref, utts, base, width):
    col = base + lax.broadcasted_iota(jnp.int32, (1, width), 1)
    start = jnp.int32(0)
    kept = jnp.zeros((1, width), jnp.float32)
    place = jnp.zeros((1, width), jnp.int32)
    for u in range(utts):
        end = start + lengths_ref[u]
        inside = (col >= start) & (col < end)
        kept = jnp.where(inside, (1 - drop_ref[u]).astype(jnp.float32), kept)
        place = jnp.where(inside, col - start, place)
        start = end
    return kept, place.astype(jnp.float32)


def rotary_rows(place, half):
    index = lax.broadcasted_iota(jnp.int32, (half, 1), 0).astype(jnp.float32)
    inverse = jnp.exp(index * (-9.210340371976184 / half))
    angles = inverse * place
    return jnp.cos(angles), jnp.sin(angles)


def frame_columns(hot, extra):
    hotb = hot.astype(jnp.bfloat16)
    idx = lax.broadcasted_iota(jnp.int32, hot.shape, 0)
    last = jnp.where(idx == 0, extra, 0.0).astype(jnp.bfloat16)
    return pad_rows([hotb, hotb, hotb, last], 128).T


def head_kernel(
    utts,
    lengths_ref,
    ids_ref,
    drop_ref,
    tokens_ref,
    skip_ref,
    cond_ref,
    mods_ref,
    w_skip_ref,
    b_skip_ref,
    hidden_ref,
    joinedT_ref,
    naT_ref,
    na_ref,
    cols,
):
    f32, bf16 = jnp.float32, jnp.bfloat16
    step = pl.program_id(0)
    frames, width = tokens_ref.shape
    rank = ids_ref[1]

    @pl.when(step == 0)
    def _():
        hot = onehot_rows(lengths_ref, utts, 16, rank * frames, frames)
        kept, _ = segment_rows(lengths_ref, drop_ref, utts, rank * frames, frames)
        cols[...] = frame_columns(hot, kept)
        keep = cols[:, 48:49].astype(f32)
        mixed = (tokens_ref[...].astype(f32) + keep * cond_ref[...].astype(f32)).astype(bf16)
        joinedT_ref[0:width, :] = mixed.T
        hidden_ref[...] = dot(mixed, w_skip_ref[...]) + b_skip_ref[...].astype(f32)

    @pl.when(step == 1)
    def _():
        skip = skip_ref[...]
        joinedT_ref[width : 2 * width, :] = skip.T
        hidden = hidden_ref[...] + dot(skip, w_skip_ref[...])
        hidden_ref[...] = hidden
        madd = mods_operand(mods_ref)
        shift = dot(cols[...], madd[:, :width])
        scale = dot(cols[...], madd[:, width:])
        normed, _ = norm_stats(hidden)
        value = (normed * (1.0 + scale) + shift).astype(bf16)
        na_ref[...] = value
        naT_ref[...] = value.T


def head_block(lengths, ids, drop, tokens, skip, cond, mods, w_skip, b_skip):
    frames, width = tokens.shape
    utts = lengths.shape[0]
    f32, bf16 = jnp.float32, jnp.bfloat16

    def whole(shape):
        return pl.BlockSpec(shape, lambda j, *_: (0,) * len(shape), pipeline_mode=pl.Buffered(1))

    out_shape = [
        jax.ShapeDtypeStruct((frames, width), f32),
        jax.ShapeDtypeStruct((2 * width, frames), bf16),
        jax.ShapeDtypeStruct((width, frames), bf16),
        jax.ShapeDtypeStruct((frames, width), bf16),
    ]
    return pl.pallas_call(
        functools.partial(head_kernel, utts),
        out_shape=out_shape,
        grid_spec=pltpu.PrefetchScalarGridSpec(
            num_scalar_prefetch=3,
            grid=(2,),
            in_specs=[whole(a.shape) for a in (tokens, skip, cond, mods)]
            + [pl.BlockSpec((width, width), lambda j, *_: (j, 0)), whole((1, width))],
            out_specs=[whole(o.shape) for o in out_shape],
            scratch_shapes=[pltpu.VMEM((frames, 128), bf16)],
        ),
        compiler_params=pltpu.CompilerParams(vmem_limit_bytes=48 << 20),
        cost_estimate=cost(100),
        name="head_block",
    )(lengths, ids, drop, tokens, skip, cond, mods, w_skip, b_skip)


def turn_heads(tensor, cosine, sine):
    half = DH // 2
    first, second = tensor[:, :half], tensor[:, half:]
    return jnp.concatenate([first * cosine - second * sine, second * cosine + first * sine], axis=1)


def qkv_kernel(utts, seq_ways, lengths_ref, ids_ref, drop_ref, na_ref, w_ref, b_ref, out_ref, trig):
    f32, bf16 = jnp.float32, jnp.bfloat16
    part = pl.program_id(0)
    frames = na_ref.shape[0]

    @pl.when(part == 0)
    def _():
        _, place = segment_rows(lengths_ref, drop_ref, utts, ids_ref[1] * frames, frames)
        cosine, sine = rotary_rows(place, DH // 2)
        trig[0] = cosine
        trig[1] = sine

    raw = dot(na_ref[...], w_ref[...]) + b_ref[...].astype(f32)
    rawT = raw.T.reshape(seq_ways, DH, frames)
    turned = part < 2
    cosine = jnp.where(turned, trig[0], 1.0)[None]
    sine = jnp.where(turned, trig[1], 0.0)[None]
    out_ref[:, pl.ds(pl.multiple_of(part * DH, DH), DH), :] = turn_heads(rawT, cosine, sine).astype(bf16)


def qkv_block(lengths, ids, drop, na, w_qkv, b_qkv, chunk, seq_ways):
    frames, width = na.shape
    cols = seq_ways * DH
    chunks = width // cols
    utts = lengths.shape[0]

    def whole(shape):
        return pl.BlockSpec(shape, lambda j, *_: (0,) * len(shape), pipeline_mode=pl.Buffered(1))

    shape = (seq_ways, 3 * DH, frames)
    return pl.pallas_call(
        functools.partial(qkv_kernel, utts, seq_ways),
        out_shape=jax.ShapeDtypeStruct(shape, jnp.bfloat16),
        grid_spec=pltpu.PrefetchScalarGridSpec(
            num_scalar_prefetch=3,
            grid=(3,),
            in_specs=[
                whole(na.shape),
                pl.BlockSpec((width, cols), lambda j, *_: (0, j * chunks + chunk)),
                pl.BlockSpec((1, cols), lambda j, *_: (0, j * chunks + chunk)),
            ],
            out_specs=whole(shape),
            scratch_shapes=[pltpu.VMEM((2, DH // 2, frames), jnp.float32)],
        ),
        cost_estimate=cost(75),
        name="qkv_block",
    )(lengths, ids, drop, na, w_qkv, b_qkv)


def back_kernel(utts, seq_ways, chunk, lengths_ref, ids_ref, drop_ref, grad_ref, naT_ref, w_ref, *refs):
    first = chunk == 0
    acc_in = None if first else refs[0]
    acc_ref, bias_ref, keep_ref, send_ref, trig, grads, sems = refs[0 if first else 3 :]
    f32, bf16 = jnp.float32, jnp.bfloat16
    part = pl.program_id(0)
    width, frames = naT_ref.shape
    core = ids_ref[0]
    parts = keep_ref.shape[0]
    own = width // seq_ways
    rows = own // parts

    @pl.when(part == 0)
    def _():
        _, place = segment_rows(lengths_ref, drop_ref, utts, ids_ref[1] * frames, frames)
        cosine, sine = rotary_rows(place, DH // 2)
        trig[0] = cosine
        trig[1] = sine

    turned = part < 2
    cosine = jnp.where(turned, trig[0], 1.0)[None]
    sine = jnp.where(turned, trig[1], 0.0)[None]
    raw = grad_ref[:, pl.ds(pl.multiple_of(part * DH, DH), DH), :].astype(f32)
    gpT = turn_heads(raw, cosine, -sine).astype(bf16).reshape(seq_ways * DH, frames)
    gna = dot(w_ref[...], gpT)

    @pl.when(part == 0)
    def _():
        acc_ref[...] = gna if first else acc_in[...] + gna

    @pl.when(part > 0)
    def _():
        acc_ref[...] += gna

    ones = jnp.ones((8, frames), bf16)
    bias_ref[0] = dot_nt(ones, gpT)
    grad_w = dot_nt(naT_ref[...], gpT).astype(bf16)
    cols = seq_ways * DH
    at = pl.ds(pl.multiple_of(part * rows, rows), rows)
    for s in range(seq_ways):
        side = jnp.where(core == s % 2, 0, 1)
        for k in range(parts):
            lo = s * own + k * rows
            grads[side, k, s // 2, at, :] = grad_w[lo : lo + rows]

    def copy(side, p):
        where = (slice(None), slice(None), pl.ds(pl.multiple_of(p * rows, rows), rows))
        return pltpu.make_async_copy(
            grads.at[side].at[where],
            (keep_ref, send_ref)[side].at[(*where, pl.ds(chunk * cols, cols))],
            sems.at[side, p],
        )

    for side in (1, 0):
        copy(side, part).start()

    @pl.when(part == 2)
    def _():
        for side in (1, 0):
            for p in range(3):
                copy(side, p).wait()


def back_block(lengths, ids, drop, grad, naT, w_qkv, before, chunk, parts):
    seq_ways, _, frames = grad.shape
    width = naT.shape[0]
    cols = seq_ways * DH
    chunks = width // cols
    utts = lengths.shape[0]
    f32, bf16 = jnp.float32, jnp.bfloat16
    rows = width // seq_ways // parts

    def whole(shape):
        return pl.BlockSpec(shape, lambda j, *_: (0,) * len(shape), pipeline_mode=pl.Buffered(1))

    gspec = pl.BlockSpec(memory_space=pl.ANY)
    gshape = jax.ShapeDtypeStruct((parts, seq_ways // 2, 3 * rows, width), bf16)
    ins = [grad, naT, w_qkv, *before]
    in_specs = [whole(grad.shape), whole(naT.shape)]
    in_specs += [pl.BlockSpec((width, cols), lambda j, *_: (0, j * chunks + chunk))]
    aliases = {}
    if before:
        in_specs += [whole(before[0].shape), gspec, gspec]
        aliases = {7: 2, 8: 3}
    return pl.pallas_call(
        functools.partial(back_kernel, utts, seq_ways, chunk),
        out_shape=[
            jax.ShapeDtypeStruct((width, frames), f32),
            jax.ShapeDtypeStruct((3, 8, cols), f32),
            gshape,
            gshape,
        ],
        grid_spec=pltpu.PrefetchScalarGridSpec(
            num_scalar_prefetch=3,
            grid=(3,),
            in_specs=in_specs,
            out_specs=[
                whole((width, frames)),
                pl.BlockSpec((1, 8, cols), lambda j, *_: (j, 0, 0)),
                gspec,
                gspec,
            ],
            scratch_shapes=[
                pltpu.VMEM((2, DH // 2, frames), f32),
                pltpu.VMEM((2, parts, seq_ways // 2, 3 * rows, cols), bf16),
                pltpu.SemaphoreType.DMA((2, 3)),
            ],
        ),
        compiler_params=pltpu.CompilerParams(vmem_limit_bytes=48 << 20),
        cost_estimate=cost(100),
        input_output_aliases=aliases,
        name="back_block",
    )(lengths, ids, drop, *ins)


def norm_kernel(
    utts, heads_local, lengths_ref, ids_ref, acc_ref, hidden_ref, after_ref, mods_ref, loss_ref, mid_ref, *refs
):
    f32, bf16 = jnp.float32, jnp.bfloat16
    bias_refs, (gh_ref, small_ref) = refs[:heads_local], refs[heads_local:]
    frames, width = hidden_ref.shape
    pad_u = table_rows(utts)
    base = 6 * pad_u
    hot = onehot_rows(lengths_ref, utts, 16, ids_ref[1] * frames, frames)
    cols = frame_columns(hot, jnp.zeros((1, frames), f32))
    madd = mods_operand(mods_ref)
    scale = dot(cols, madd[:, width:])
    gna = acc_ref[...].T
    normed, rstd = norm_stats(hidden_ref[...])
    sums = sum_rows(hot, 16, frames)
    small_ref[0:pad_u, :] = dot(sums, gna.astype(bf16))[:pad_u]
    small_ref[pad_u : 2 * pad_u, :] = dot(sums, (gna * normed).astype(bf16))[:pad_u]
    gh = (after_ref[...] + norm_back(gna * (1.0 + scale), normed, rstd)).astype(bf16)
    gh_ref[...] = gh
    small_ref[2 * pad_u : base, :] = mid_ref[0 : 4 * pad_u, :]
    cols_local = width // heads_local
    for c in range(heads_local):
        for p in range(3):
            small_ref[base + p : base + p + 1, c * cols_local : (c + 1) * cols_local] = bias_refs[c][p, 0:1, :]
    small_ref[base + 3 : base + 4, :] = dot(sums, gh)[16:17]
    small_ref[base + 4 : base + 12, :] = mid_ref[4 * pad_u : 4 * pad_u + 8, :]
    count = jnp.sum(loss_ref[...].astype(f32), axis=1, keepdims=True)
    high = jnp.floor(count / 32.0) * 32.0
    small_ref[base + 12 : base + 13, :] = jnp.broadcast_to(high, (1, width))
    small_ref[base + 13 : base + 16, :] = jnp.broadcast_to(count - high, (3, width))


def norm_block(lengths, ids, acc, hidden, after, mods, loss, mid_small, biases):
    frames, width = hidden.shape
    utts = lengths.shape[0]
    out_shape = [
        jax.ShapeDtypeStruct((frames, width), jnp.bfloat16),
        jax.ShapeDtypeStruct((6 * table_rows(utts) + 16, width), jnp.float32),
    ]
    return pl.pallas_call(
        functools.partial(norm_kernel, utts, len(biases)),
        out_shape=out_shape,
        grid_spec=pltpu.PrefetchScalarGridSpec(
            num_scalar_prefetch=2,
            grid=(1,),
            in_specs=[whole_block(a.shape) for a in (acc, hidden, after, mods, loss, mid_small, *biases)],
            out_specs=[whole_block(o.shape) for o in out_shape],
        ),
        compiler_params=pltpu.CompilerParams(vmem_limit_bytes=48 << 20),
        cost_estimate=cost(50),
        name="norm_block",
    )(lengths, ids, acc, hidden, after, mods, loss, mid_small, *biases)


def skip_kernel(seq_ways, ids_ref, joinedT_ref, gh_ref, keep_ref, send_ref, grads, sems):
    step = pl.program_id(0)
    core = ids_ref[0]
    parts = keep_ref.shape[0]
    width = joinedT_ref.shape[0]
    block = 2 * width // seq_ways
    rows = block // parts
    z_step = seq_ways // 4
    grad_w = dot(joinedT_ref[...], gh_ref[...]).astype(jnp.bfloat16)
    for b in range(width // block):
        side = jnp.where(core == b % 2, 0, 1)
        for k in range(parts):
            lo = b * block + k * rows
            grads[side, k, step * z_step + b // 2] = grad_w[lo : lo + rows]

    def copy(side, at):
        where = (slice(None), pl.ds(at * z_step, z_step))
        return pltpu.make_async_copy(
            grads.at[side].at[where], (keep_ref, send_ref)[side].at[where], sems.at[side, at]
        )

    for side in (1, 0):
        copy(side, step).start()

    @pl.when(step == 1)
    def _():
        for side in (1, 0):
            for at in range(2):
                copy(side, at).wait()


def skip_block(ids, joinedT, gh, seq_ways, parts):
    frames, width = gh.shape
    rows = 2 * width // seq_ways // parts
    gshape = (parts, seq_ways // 2, rows, width)
    return pl.pallas_call(
        functools.partial(skip_kernel, seq_ways),
        out_shape=[jax.ShapeDtypeStruct(gshape, jnp.bfloat16)] * 2,
        grid_spec=pltpu.PrefetchScalarGridSpec(
            num_scalar_prefetch=1,
            grid=(2,),
            in_specs=[pl.BlockSpec((width, frames), lambda j, *_: (j, 0)), whole_block(gh.shape)],
            out_specs=[pl.BlockSpec(memory_space=pl.ANY)] * 2,
            scratch_shapes=[pltpu.VMEM((2,) + gshape, jnp.bfloat16), pltpu.SemaphoreType.DMA((2, 2))],
        ),
        compiler_params=pltpu.CompilerParams(vmem_limit_bytes=32 << 20),
        cost_estimate=cost(50),
        name="skip_block",
    )(ids, joinedT, gh)


def joined_kernel(gh_ref, w_ref, scale_ref, first_ref, second_ref):
    step = pl.program_id(0)
    value = dot_nt(gh_ref[...], w_ref[...]) * scale_ref[0:1, 0:1]

    @pl.when(step == 0)
    def _():
        first_ref[...] = value

    @pl.when(step == 1)
    def _():
        second_ref[...] = value


def joined_block(gh, w_skip, scale):
    frames, width = gh.shape
    out = jax.ShapeDtypeStruct((frames, width), jnp.float32)
    return pl.pallas_call(
        joined_kernel,
        out_shape=[out, out],
        grid_spec=pltpu.PrefetchScalarGridSpec(
            num_scalar_prefetch=0,
            grid=(2,),
            in_specs=[
                whole_block(gh.shape),
                pl.BlockSpec((width, width), lambda j: (j, 0)),
                whole_block(scale.shape),
            ],
            out_specs=[whole_block(out.shape)] * 2,
        ),
        compiler_params=pltpu.CompilerParams(vmem_limit_bytes=32 << 20),
        cost_estimate=cost(50),
        name="joined_block",
    )(gh, w_skip, scale)


def add_bf16(left, right):
    return (left.astype(jnp.float32) + right.astype(jnp.float32)).astype(jnp.bfloat16)


def first_kernel(pairs, splits, ids_ref, *refs):
    ins, outs = refs[: 8 * pairs], list(refs[8 * pairs :])
    for i in range(4):
        own = [outs.pop(0) for _ in range(splits if i < 2 else 1)]
        at = 0
        for p in range(pairs):
            left, right = ins[2 * (i * pairs + p)], ins[2 * (i * pairs + p) + 1]
            rows = left.shape[-2]
            value = add_bf16(left[0, 0, 0], right[0, 0, 0])
            if len(own) == 1:
                own[0][0, :, at : at + rows, :] = value
            else:
                for out in own:
                    out[0] = value[:, at : at + out.shape[2], :]
                    at += out.shape[2]
            at += rows


def first_sum(ids, pairs, splits):
    _, _, _, z_ways, _, width = pairs[0][0].shape
    total = sum(k.shape[4] for k, _ in pairs)
    step = z_ways // 2 if total > 100 else z_ways

    def source(half, axis, mine, rows):
        def at(g, z, ids):
            bit = ids[axis]
            return half, bit if mine else 1 - bit, g, z, 0, 0

        return pl.BlockSpec((1, 1, 1, step, rows, width), at)

    order = [(0, 2, False), (1, 3, False), (0, 2, True), (1, 3, True)]
    sizes = [*splits, *splits, total, total]
    return pl.pallas_call(
        functools.partial(first_kernel, len(pairs), len(splits)),
        out_shape=[jax.ShapeDtypeStruct((2, z_ways, n, width), jnp.bfloat16) for n in sizes],
        grid_spec=pltpu.PrefetchScalarGridSpec(
            num_scalar_prefetch=1,
            grid=(2, z_ways // step),
            in_specs=[source(*o, a.shape[4]) for o in order for pair in pairs for a in pair],
            out_specs=[pl.BlockSpec((1, step, n, width), lambda g, z, ids: (g, z, 0, 0)) for n in sizes],
        ),
        compiler_params=pltpu.CompilerParams(vmem_limit_bytes=48 << 20),
        cost_estimate=cost(60),
        name="first_sum",
    )(ids, *([a for pair in pairs for a in pair] * 4))


def second_kernel(pieces, ids_ref, *refs):
    for i in range(4):
        keep, *got = refs[(pieces + 1) * i : (pieces + 1) * (i + 1)]
        out = refs[4 * (pieces + 1) + i]
        at = 0
        for g in got:
            rows = g.shape[2]
            out[:, at : at + rows, :] = add_bf16(keep[0, :, at : at + rows, :], g[0])
            at += rows


def second_sum(ids, keep_a, got_a, keep_b, got_b):
    _, z_ways, rows, width = keep_a.shape
    step = z_ways // 2 if rows > 100 else z_ways

    def source(axis, mine, value):
        def at(z, ids):
            bit = ids[axis]
            return bit if mine else 1 - bit, z, 0, 0

        return pl.BlockSpec((1, step, *value.shape[2:]), at)

    order = [(3, False), (2, False), (3, True), (2, True)]
    sides = [[keep_a, *got_a], [keep_b, *got_b]]
    out = jax.ShapeDtypeStruct((z_ways, rows, width), jnp.bfloat16)
    return pl.pallas_call(
        functools.partial(second_kernel, len(got_a)),
        out_shape=[out] * 4,
        grid_spec=pltpu.PrefetchScalarGridSpec(
            num_scalar_prefetch=1,
            grid=(z_ways // step,),
            in_specs=[source(*o, v) for i, o in enumerate(order) for v in sides[i % 2]],
            out_specs=[pl.BlockSpec((step, rows, width), lambda z, ids: (z, 0, 0))] * 4,
        ),
        compiler_params=pltpu.CompilerParams(vmem_limit_bytes=48 << 20),
        cost_estimate=cost(30),
        name="second_sum",
    )(ids, *((sides[0] + sides[1]) * 2))


def third_kernel(ids_ref, keep_a, got_a, keep_b, got_b, *outs):
    for j, out in enumerate(outs):
        at = ids_ref[4] ^ j
        out[0] = add_bf16(keep_a[at], got_a[at])
        out[1] = add_bf16(keep_b[at], got_b[at])


def third_sum(ids, keep_a, got_a, keep_b, got_b):
    z_ways, rows, width = keep_a.shape
    out = jax.ShapeDtypeStruct((2, rows, width), jnp.bfloat16)
    return pl.pallas_call(
        third_kernel,
        out_shape=[out] * z_ways,
        grid_spec=pltpu.PrefetchScalarGridSpec(
            num_scalar_prefetch=1,
            grid=(1,),
            in_specs=[whole_block(keep_a.shape)] * 4,
            out_specs=[whole_block(out.shape)] * z_ways,
        ),
        cost_estimate=cost(10),
        name="third_sum",
    )(ids, keep_a, got_a, keep_b, got_b)


def third_all_kernel(ids_ref, keep_a, got_a, keep_b, got_b, out):
    for z in range(keep_a.shape[0]):
        out[z, 0] = add_bf16(keep_a[z], got_a[z])
        out[z, 1] = add_bf16(keep_b[z], got_b[z])


def third_sum_all(ids, keep_a, got_a, keep_b, got_b):
    z_ways, rows, width = keep_a.shape
    out = jax.ShapeDtypeStruct((z_ways, 2, rows, width), jnp.bfloat16)
    step = max(1, z_ways // 2)
    return pl.pallas_call(
        third_all_kernel,
        out_shape=out,
        grid_spec=pltpu.PrefetchScalarGridSpec(
            num_scalar_prefetch=1,
            grid=(z_ways // step,),
            in_specs=[pl.BlockSpec((step, rows, width), lambda i, *_: (i, 0, 0))] * 4,
            out_specs=pl.BlockSpec((step, 2, rows, width), lambda i, *_: (i, 0, 0, 0)),
        ),
        cost_estimate=cost(10),
        name="third_sum_all",
    )(ids, keep_a, got_a, keep_b, got_b)


def fourth_all_kernel(x, out):
    total = x[0].astype(jnp.float32)
    for z in range(1, x.shape[0]):
        total = total + x[z].astype(jnp.float32)
    out[...] = total.astype(jnp.bfloat16)


def fourth_sum_all(terms):
    return pl.pallas_call(
        fourth_all_kernel,
        out_shape=jax.ShapeDtypeStruct(terms.shape[1:], jnp.bfloat16),
        grid=(1,),
        in_specs=[whole_block(terms.shape)],
        out_specs=whole_block(terms.shape[1:]),
        cost_estimate=cost(10),
        name="fourth_sum_all",
    )(terms)


def fourth_kernel(*refs):
    total = refs[0][...].astype(jnp.float32)
    for r in refs[1:-1]:
        total = total + r[...].astype(jnp.float32)
    refs[-1][...] = total.astype(jnp.bfloat16)


def fourth_sum(terms):
    shape = terms[0].shape
    return pl.pallas_call(
        fourth_kernel,
        out_shape=jax.ShapeDtypeStruct(shape, jnp.bfloat16),
        grid=(1,),
        in_specs=[whole_block(shape)] * len(terms),
        out_specs=whole_block(shape),
        cost_estimate=cost(10),
        name="fourth_sum",
    )(*terms)


def place_kernel(streams, plan, ids_ref, scale_ref, *refs):
    blocks, outs = refs[: 4 * streams], refs[4 * streams :]
    x, y = ids_ref[2], ids_ref[3]
    scale = scale_ref[0:1, 0:1]
    for stream, row, rows, lane, lanes, out, row_of, lane_of in plan:
        for d in range(4):
            own_x, own_y = x ^ (d & 1), y ^ (d >> 1)
            for half in range(2):
                k = own_x * 2 + own_y if half == 0 else 4 + own_y * 2 + own_x
                tile = blocks[4 * stream + d][half, row : row + rows, lane : lane + lanes]
                outs[out][row_of(k), lane_of(k)] = tile.astype(jnp.float32) * scale


def place_blocks(ids, scale, streams, plan, shapes):
    blocks = [b for s in streams for b in s]
    outs = [jax.ShapeDtypeStruct(s, jnp.float32) for s in shapes]
    return pl.pallas_call(
        functools.partial(place_kernel, len(streams), plan),
        out_shape=outs,
        grid_spec=pltpu.PrefetchScalarGridSpec(
            num_scalar_prefetch=1,
            grid=(1,),
            in_specs=[whole_block(a.shape) for a in (scale, *blocks)],
            out_specs=[whole_block(o.shape) for o in outs],
        ),
        compiler_params=pltpu.CompilerParams(vmem_limit_bytes=32 << 20),
        cost_estimate=cost(20),
        name="place_blocks",
    )(ids, scale, *blocks)


def span(start, size):
    return pl.ds(pl.multiple_of(start, size), size)


def ada_kernel(groups, pad_u, numerator, time_ref, *refs):
    f32 = jnp.float32
    parts, (weight_ref, vector_ref, scale_ref) = refs[:groups], refs[groups:]
    table = pl.program_id(0)
    base = 6 * pad_u
    count = parts[0][base + 12 : base + 13, 0:1] + parts[0][base + 13 : base + 14, 0:1]
    for p in parts[1:]:
        count = count + p[base + 12 : base + 13, 0:1] + p[base + 13 : base + 14, 0:1]
    scale = numerator / count
    rows = jnp.concatenate([p[pl.ds(pl.multiple_of(table * pad_u, 8), pad_u), :] for p in parts], axis=0) * scale
    vector_ref[pl.ds(table, 1), :] = jnp.sum(rows, axis=0, keepdims=True)
    operand = jnp.concatenate(list(split3(rows)), axis=0)
    weight_ref[...] = dot(time_ref[...], operand)

    @pl.when(table == 0)
    def _():
        total = parts[0][base : base + 16, :]
        for p in parts[1:]:
            total = total + p[base : base + 16, :]
        vector_ref[8:24, :] = total * scale
        scale_ref[...] = jnp.broadcast_to(scale, scale_ref.shape)


def ada_block(time3, parts, utts, numerator):
    pad_u = table_rows(utts)
    width = parts[0].shape[1]
    own = time3.shape[0]
    f32 = jnp.float32
    return pl.pallas_call(
        functools.partial(ada_kernel, len(parts), pad_u, numerator),
        out_shape=[
            jax.ShapeDtypeStruct((own, 6 * width), f32),
            jax.ShapeDtypeStruct((24, width), f32),
            jax.ShapeDtypeStruct((8, 128), f32),
        ],
        grid=(6,),
        in_specs=[whole_block(time3.shape)] + [whole_block(p.shape) for p in parts],
        out_specs=[
            pl.BlockSpec((own, width), lambda j: (0, j)),
            whole_block((24, width)),
            whole_block((8, 128)),
        ],
        cost_estimate=cost(50),
        name="ada_block",
    )(time3, *parts)


def sum_exchange(value, axis, bit):
    ways = lax.axis_size(axis)
    return lax.ppermute(value, axis, [(i, i ^ bit) for i in range(ways)])


def axis_bits(ways):
    return [1 << i for i in range(ways.bit_length() - 1)]


def reduce_stages(ids, blocks, splits, whole_z):
    batch_ways = lax.axis_size("batch")
    x_bit, y_bit = 1, 1 << ((batch_ways.bit_length() - 1) // 2)
    pairs = []
    for keep, send in blocks:
        shape = (2, 2, 2) + keep.shape[1:]
        pairs.append((keep.reshape(shape), sum_exchange(send, "seq", 1).reshape(shape)))
    *sends, keep_a, keep_b = first_sum(ids, pairs, splits)
    sends = follow(sends, (yield sends))
    got, token = [[], []], None
    for i in range(len(splits)):
        pieces = follow([sends[i], sends[len(splits) + i]], token)
        for side, bit in enumerate((x_bit, y_bit)):
            got[side].append(sum_exchange(pieces[side], "batch", bit))
        token = yield [got[0][i], got[1][i]]
    got_a, got_b = (follow(g, token) for g in got)
    send_a, send_b, keep_a, keep_b = second_sum(ids, keep_a, got_a, keep_b, got_b)
    send_a, send_b = follow([send_a, send_b], (yield [send_a, send_b]))
    got = [sum_exchange(send_a, "batch", y_bit), sum_exchange(send_b, "batch", x_bit)]
    got_a, got_b = follow(got, (yield got))
    if whole_z:
        ways = lax.axis_size("seq")
        groups = [list(range(c, ways, 2)) for c in range(2)]
        away = [third_sum_all(ids, keep_a, got_a, keep_b, got_b)]
        away = follow(away, (yield away))
        got = [lax.all_to_all(away[0], "seq", 0, 0, axis_index_groups=groups, tiled=True)]
        got = follow(got, (yield got))
        block = fourth_sum_all(got[0])
    else:
        own, *away = third_sum(ids, keep_a, got_a, keep_b, got_b)
        away = follow(away, (yield away))
        got = [sum_exchange(a, "seq", 2 * (j + 1)) for j, a in enumerate(away)]
        got = follow(got, (yield got))
        block = fourth_sum([own] + got)
    for bit in axis_bits(batch_ways):
        if bit not in (x_bit, y_bit):
            block = add_bf16(block, sum_exchange(block, "batch", bit))
    (block,) = follow([block], (yield [block]))
    yield [block] + [sum_exchange(block, "batch", bit) for bit in (x_bit, y_bit, x_bit | y_bit)]


def advance(stages, steps, token=None):
    value = next(stages) if token is None else stages.send(token)
    for _ in range(steps - 1):
        value = next(stages)
    return value


def last_stage(stages, token=None):
    value = stages.send(token)
    for value in stages:
        pass
    return value


def follow(values, token):
    return values if token is None else [after(v, token) for v in values]


def after(value, *others):
    return lax.optimization_barrier((value,) + others)[0]


def gather_groups(value):
    away = value.astype(jnp.bfloat16)
    others = [sum_exchange(away, "batch", i) for i in range(1, lax.axis_size("batch"))]
    return [value] + [other.astype(value.dtype) for other in others]


def sum_z(value, tokens):
    away = after(value.astype(jnp.bfloat16), *tokens)
    for j in range(1, lax.axis_size("seq") // 2):
        value = value + sum_exchange(away, "seq", 2 * j).astype(jnp.float32)
    return value


def shards(
    tokens_in,
    skip_in,
    condition,
    cotangent,
    time_embed,
    lengths,
    key_mask,
    drop_mask,
    loss_mask,
    w_skip,
    b_skip,
    w_ada,
    b_ada,
    w_qkv,
    b_qkv,
    w_out,
    b_out,
    w_up,
    b_up,
    w_down,
    b_down,
):
    f32, bf16 = jnp.float32, jnp.bfloat16
    seq_ways, batch_ways = lax.axis_size("seq"), lax.axis_size("batch")
    seq_rank = lax.axis_index("seq")
    frames, width = tokens_in.shape[1:]
    group_frames = frames * seq_ways
    heads_local = HEADS // seq_ways
    utts = lengths.shape[1]
    lengths_row, drop = lengths[0], drop_mask[0]
    batch_rank = lax.axis_index("batch")
    side = 1 << ((batch_ways.bit_length() - 1) // 2)
    ids = [lax.rem(seq_rank, 2), seq_rank, lax.rem(batch_rank, 2), lax.rem(batch_rank // side, 2), seq_rank // 2]
    ids = jnp.stack(ids).astype(jnp.int32)
    ok = key_mask.reshape(seq_ways, 1, frames)
    exchange = functools.partial(lax.all_to_all, axis_name="seq", split_axis=0, concat_axis=0, tiled=True)

    time_act = jax.nn.silu(time_embed[0]).astype(bf16)
    time_rows = jnp.pad(time_act, ((0, 16 - utts), (0, 0)))

    def modulation(first, last):
        return jnp.dot(time_rows, w_ada[:, first:last], preferred_element_type=f32) + b_ada[
            first:last
        ].astype(f32)

    mods_a = modulation(0, 2 * width)
    hidden, joinedT, naT, na = head_block(
        lengths_row, ids, drop, tokens_in[0], skip_in[0], condition[0], mods_a, w_skip, b_skip[None]
    )
    mods_rest = modulation(2 * width, 6 * width)
    received = []
    for c in range(heads_local):
        packed = qkv_block(lengths_row, ids, drop, na, w_qkv, b_qkv[None], c, seq_ways)
        if c == 0:
            na = after(na, mods_rest)
        received.append(exchange(packed))

    own = width // seq_ways
    pad_u = table_rows(utts)
    time_own = lax.dynamic_slice_in_dim(jnp.concatenate(gather_groups(time_rows[:pad_u])), seq_rank * own, own, axis=1)
    time3 = jnp.tile(time_own.T, (1, 3))

    received[0] = after(received[0], mods_rest)
    head_out, log_totals, returned = [], [], []
    for c in range(heads_local):
        out, log_total = attend(lengths_row, received[c], ok)
        head_out.append(out)
        log_totals.append(log_total)
        returned.append(exchange(after(out, *returned)))
        if c < heads_local - 1:
            received[c + 1] = after(received[c + 1], out, time3)
    mid = mid_block(
        lengths_row,
        ids,
        returned,
        hidden,
        mods_rest,
        cotangent[0],
        loss_mask,
        w_out,
        b_out[None],
        w_up,
        b_up[None],
        w_down,
        b_down[None],
        PARTS,
    )
    output, after_grad, mid_small, grad_att, keep, send = mid
    grad_heads = exchange(grad_att)
    front = keep.shape[2] * 4 // 9 // 16 * 16
    feed = reduce_stages(ids, [(keep, send)], [front, keep.shape[2] - front], True)

    ahead = next(feed)
    grad_local = []
    for c in range(heads_local):
        operand = after(grad_heads, *ahead)
        moving = feed.send(grad if c else None) if c < 2 else []
        grad = attend_back(lengths_row, received[c], ok, head_out[c], operand, log_totals[c], c)
        grad_local.append(exchange(after(grad, *moving)))
        ahead = [grad]
    if heads_local == 1:
        next(feed)
    ahead = ahead + advance(feed, 1, ahead[0])
    before, biases = (), []
    for c in range(heads_local):
        acc, bias, keep, send = back_block(
            lengths_row, ids, drop, after(grad_local[c], *ahead), naT, w_qkv, before, c, PARTS
        )
        before = (acc, keep, send)
        biases.append(bias)
        ahead = next(feed) and advance(feed, 1, acc) if c == 0 else []
    gh, small = norm_block(lengths_row, ids, acc, hidden, after_grad, mods_a, loss_mask, mid_small, biases)
    small = small + sum_exchange(small, "seq", 1)
    skip_keep, skip_send = skip_block(ids, joinedT, gh, seq_ways, PARTS)
    blocks = [(skip_keep, skip_send), (keep, send)]
    rest = reduce_stages(ids, blocks, [5 * own // PARTS], False)
    moving = next(feed)
    small = sum_z(small, moving + advance(rest, 3))
    next(rest)
    moving = next(rest)
    groups = gather_groups(after(small, *moving, *next(feed)))
    numerator = float(group_frames * batch_ways)
    grad_w_ada, vectors, scale = ada_block(time3, groups, utts, numerator)
    grad_tokens, grad_skip = joined_block(gh, w_skip, scale)
    feed = last_stage(feed, groups[-1])
    next(rest)
    rest.send(grad_tokens)
    rest = last_stage(rest)

    ff = w_up.shape[1]
    chunks = ff // width
    up_part = chunks * own // PARTS
    down_part = ff // seq_ways // PARTS
    out_part = own // PARTS
    per_chunk = own // up_part
    whole_lanes = lambda k: span(0, width)
    grad_w_up, grad_w_down, grad_w_out = place_blocks(
        ids,
        scale,
        [feed],
        [
            (
                *(0, 0, up_part, 0, width, 0),
                lambda k: span(lax.rem(k, per_chunk) * up_part, up_part),
                lambda k: span(k // per_chunk * width, width),
            ),
            (0, up_part, down_part, 0, width, 1, lambda k: span(k * down_part, down_part), whole_lanes),
            (0, up_part + down_part, out_part, 0, width, 2, lambda k: span(k * out_part, out_part), whole_lanes),
        ],
        [(own, ff), (ff // seq_ways, width), (own, width)],
    )
    skip_part = 2 * own // PARTS
    grad_w_skip, grad_w_qkv = place_blocks(
        ids,
        after(scale, grad_w_down),
        [rest],
        [(0, 0, skip_part, 0, width, 0, lambda k: span(k * skip_part, skip_part), whole_lanes)]
        + [
            (
                *(0, skip_part + p * out_part, out_part, 0, width, 1),
                lambda k: span(k * out_part, out_part),
                lambda k, at=p * width: span(at, width),
            )
            for p in range(3)
        ],
        [(2 * own, width), (own, 3 * width)],
    )

    def own_slice(vector):
        vector = vector.reshape(-1)
        size = vector.shape[0] // seq_ways
        return lax.dynamic_slice_in_dim(vector, seq_rank * size, size)

    grad_b_ada = own_slice(vectors[:6])
    grad_b_qkv = own_slice(vectors[8:11])
    grad_b_skip = own_slice(vectors[11])
    grad_b_out = own_slice(vectors[12])
    grad_b_down = own_slice(vectors[13])
    grad_b_up = own_slice(vectors[14 : 14 + chunks])
    return (
        output[None],
        grad_tokens[None],
        grad_skip[None],
        grad_w_skip,
        grad_b_skip,
        grad_w_ada,
        grad_b_ada,
        grad_w_qkv,
        grad_b_qkv,
        grad_w_out,
        grad_b_out,
        grad_w_up,
        grad_b_up,
        grad_w_down,
        grad_b_down,
    )


def solution(mesh):
    in_specs = (
        P("batch", "seq", None),
        P("batch", "seq", None),
        P("batch", "seq", None),
        P("batch", "seq", None),
        P("batch", None, None),
        P("batch", None),
        P("batch", None),
        P("batch", None),
        P("batch", "seq"),
        P(),
        P(),
        P(),
        P(),
        P(),
        P(),
        P(),
        P(),
        P(),
        P(),
        P(),
        P(),
    )
    out_specs = (
        P("batch", "seq", None),
        P("batch", "seq", None),
        P("batch", "seq", None),
        P("seq", None),
        P("seq"),
        P("seq", None),
        P("seq"),
        P("seq", None),
        P("seq"),
        P("seq", None),
        P("seq"),
        P("seq", None),
        P("seq"),
        P("seq", None),
        P("seq"),
    )
    return jax.shard_map(shards, mesh=mesh, in_specs=in_specs, out_specs=out_specs, check_vma=False)
```
